32 devices in a mesh: row: 8 (over z, core), sample: 4 (over y, x).
Axes of the slice: x: 2, y: 2, z: 4, core: 2. Of those that a mesh axis runs over, the one named last changes fastest.
Arguments:
- tokens: bfloat16 [2, 12, 512, 768], P(None, 'sample', 'row'), may hold values from -6 to 6
- single: bfloat16 [2, 12, 512, 384], P(None, 'sample', 'row'), may hold values from -6 to 6
- pair: bfloat16 [2, 512, 512, 128], P(None, 'row'), may hold values from -6 to 6
- token_count: int32 [2], replicated, may hold values from 256 to 512, as said below
- pair_mask: int32 [2, 512, 512], P(None, 'row'), may hold values 0 or 1
- cotangent: bfloat16 [2, 12, 512, 768], P(None, 'sample', 'row'), may hold values from -6 to 6
- cond_gain: bfloat16 [2, 384], P(None, 'sample'), may hold values from 0.5 to 1.5
- ada_weight: bfloat16 [4, 384, 768], P(None, 'sample'), may hold values from -0.3125 to 0.3125
- ada_bias: bfloat16 [2, 768], P(None, 'sample'), may hold values from -3 to 3
- zero_weight: bfloat16 [2, 384, 768], P(None, 'sample'), may hold values from -0.3125 to 0.3125
- zero_bias: bfloat16 [2, 768], P(None, 'sample'), may hold values from -4 to 4
- attn_weight: bfloat16 [4, 768, 768], P(None, 'sample'), may hold values from -0.21875 to 0.21875
- query_bias: bfloat16 [768], P('sample'), may hold values from -3 to 3
- out_weight: bfloat16 [768, 768], P('sample'), may hold values from -1.75 to 1.75
- pair_gain: bfloat16 [128], P('sample'), may hold values from 0.25 to 1.75
- pair_weight: bfloat16 [128, 16], P('sample'), may hold values from -0.5 to 0.5
- trans_in: bfloat16 [2, 768, 1536], P(None, 'sample'), may hold values from -0.21875 to 0.21875
- trans_out: bfloat16 [1536, 768], P('sample'), may hold values from -0.3125 to 0.3125
Outputs:
- output: bfloat16 [2, 12, 512, 768], P(None, 'sample', 'row')
- token_grad: float32 [2, 12, 512, 768], P(None, 'sample', 'row')
- cond_gain_grad: float32 [2, 384], P(None, 'sample')
- ada_weight_grad: float32 [4, 384, 768], P(None, 'sample')
- ada_bias_grad: float32 [2, 768], P(None, 'sample')
- zero_weight_grad: float32 [2, 384, 768], P(None, 'sample')
- zero_bias_grad: float32 [2, 768], P(None, 'sample')
- attn_weight_grad: float32 [4, 768, 768], P(None, 'sample')
- query_bias_grad: float32 [768], P('sample')
- out_weight_grad: float32 [768, 768], P('sample')
- pair_gain_grad: float32 [128], P('sample')
- pair_weight_grad: float32 [128, 16], P('sample')
- trans_in_grad: float32 [2, 768, 1536], P(None, 'sample')
- trans_out_grad: float32 [1536, 768], P('sample')
The draws below stay inside these ranges and needn't reach their ends.
Inputs may be any that keep to these rules, and one draw needn't show every extreme that they name: The tokens of complex c are the positions below token_count[c], the rest is padding; each count is 256 or more, and in every draw one complex, at a drawn place, has all 512 tokens.
All inputs are finite; a program needn't handle non-finite values. No bound on the sum of `pair_mask` on one device may be relied on, other than what follows from the above.
Results may differ from the reference program's by a relative error of at most 0.023.
Values may be sent and summed in bfloat16 or wider, within the bound.
A program may use at most 256 MiB of HBM per device.

```python
import jax
import jax.numpy as jnp
from jax import lax

D = 768
CS = 384
CZ = 128
H = 16
HD = 48
FF = 1536
COMPLEXES = 2
L = 512
SAMPLES = 12


def draw_token_count(key, part):
    key_counts = jax.random.fold_in(key, 11)
    key_order = jax.random.fold_in(key, 12)
    others = jax.random.randint(key_counts, (COMPLEXES - 1,), L // 2, L + 1)
    counts = jnp.concatenate([jnp.full((1,), L, dtype=jnp.int32), others.astype(jnp.int32)])
    return counts[jax.random.permutation(key_order, COMPLEXES)]


def row_field(key, width):
    shape = (COMPLEXES, SAMPLES, L, width)
    values = jax.random.truncated_normal(jax.random.fold_in(key, 23), -6.0, 6.0, shape, jnp.float32)
    return values.astype(jnp.bfloat16)


def draw_tokens(key, part):
    return row_field(jax.random.fold_in(key, 31), D)


def draw_single(key, part):
    return row_field(jax.random.fold_in(key, 32), CS)


def set_ends(values, stream_key, low, largest):
    spot = [jax.random.randint(jax.random.fold_in(stream_key, axis), (), 0, length) for axis, length in enumerate(values.shape)]
    main_axis = values.shape.index(max(values.shape))
    neighbour = spot[:main_axis] + [(spot[main_axis] + 1) % values.shape[main_axis]] + spot[main_axis + 1:]
    return values.at[tuple(spot)].set(low).at[tuple(neighbour)].set(largest)


def steps_of(stream_key, shape, split, low, high):
    def one(dim, parts):
        heights = jax.random.uniform(jax.random.fold_in(jax.random.fold_in(stream_key, 6), dim), (parts,), jnp.float32, low / len(split), high / len(split))
        return jnp.repeat(jnp.exp(heights), shape[dim] // parts).reshape((-1,) + (1,) * (len(shape) - dim - 1))

    loudness = one(*split[0])
    for cut in split[1:]:
        loudness = loudness * one(*cut)
    return loudness


def noise(key, dims, deviation, most, split=(), kind=jnp.bfloat16):
    level = steps_of(key, dims, split, -0.22, 0.18) if split else 1.0
    entries = jax.random.normal(key, dims, jnp.float32) * deviation * level
    return jnp.minimum(jnp.maximum(entries, -most), most).astype(kind)


def setup_inputs(seed: int = 0) -> dict:
    splits = jax.random.split(jax.random.key(seed), 19)
    tokens = draw_tokens(jax.random.fold_in(splits[18], 71), 0)
    single = draw_single(jax.random.fold_in(splits[18], 71), 0)
    pair = noise(splits[2], (COMPLEXES, L, L, CZ), 1.0, 6.0, ((1, 8),))
    token_count = draw_token_count(jax.random.fold_in(splits[18], 71), 0)
    pair_mask = set_ends((jax.random.randint(splits[4], (COMPLEXES, L, L), 0, 8) < 7).astype(jnp.int32), jax.random.fold_in(splits[4], 1), 0, 1)
    cotangent = noise(splits[5], (COMPLEXES, SAMPLES, L, D), 1.0, 6.0, ((1, 4), (2, 8)))
    cond_gain = jnp.clip(1.0 + 0.1 * jax.random.normal(splits[6], (2, CS), jnp.float32), 0.5, 1.5).astype(jnp.bfloat16)
    ada_weight = noise(splits[7], (4, CS, D), CS ** -0.5, 0.3125, ((1, 4),))
    ada_bias = noise(splits[8], (2, D), 0.5, 3.0, ((1, 4),))
    zero_weight = noise(splits[9], (2, CS, D), CS ** -0.5, 0.3125, ((1, 4),))
    zero_bias = noise(splits[10], (2, D), 1.0, 4.0, ((1, 4),))
    attn_weight = noise(splits[11], (4, D, D), D ** -0.5, 0.21875, ((1, 4),))
    query_bias = noise(splits[12], (D,), 0.5, 3.0, ((0, 4),))
    out_weight = noise(splits[13], (D, D), (max(D // 64, 1)) ** -0.5, 1.75, ((0, 4),))
    pair_gain = jnp.clip(1.0 + 0.15 * jax.random.normal(splits[14], (CZ,), jnp.float32), 0.25, 1.75).astype(jnp.bfloat16)
    pair_weight = noise(splits[15], (CZ, H), CZ ** -0.5, 0.5, ((0, 4),))
    trans_in = noise(splits[16], (2, D, FF), D ** -0.5, 0.21875, ((1, 4),))
    trans_out = noise(splits[17], (FF, D), (FF // 4) ** -0.5, 0.3125, ((0, 4),))
    return dict(tokens=tokens, single=single, pair=pair, token_count=token_count, pair_mask=pair_mask, cotangent=cotangent, cond_gain=cond_gain, ada_weight=ada_weight, ada_bias=ada_bias, zero_weight=zero_weight, zero_bias=zero_bias, attn_weight=attn_weight, query_bias=query_bias, out_weight=out_weight, pair_gain=pair_gain, pair_weight=pair_weight, trans_in=trans_in, trans_out=trans_out)


EPSILON = 1e-05
MASKED = -1000000000.0
HIGHEST = lax.Precision.HIGHEST

@jax.custom_vjp
def low(v):
    return lax.optimization_barrier(v.astype(jnp.bfloat16)).astype(jnp.float32)

@jax.custom_vjp
def low_back(v):
    return v

def low_keep(v):
    return (low(v), None)

def low_pass(kept, grad):
    return (grad,)

def back_keep(v):
    return (v, None)

def back_low(kept, grad):
    return (low(grad),)
low.defvjp(low_keep, low_pass)
low_back.defvjp(back_keep, back_low)

def norm_rows(value):
    center = value - lax.optimization_barrier(jnp.mean(value, axis=-1, keepdims=True))
    return center * lax.rsqrt(lax.optimization_barrier(jnp.mean(center * center, axis=-1, keepdims=True)) + EPSILON)

def product(left, right):
    return jnp.dot(left, right, precision=HIGHEST)

def adaptive(activation, cond_normed, gain, scale_weight, scale_bias, shift_weight):
    cond_low = low(cond_normed * gain)
    gate_pre = low_back(product(cond_low, scale_weight) + scale_bias)
    mixed = jax.nn.sigmoid(gate_pre) * norm_rows(activation) + product(cond_low, shift_weight)
    return low(low_back(mixed))

def sample_forward(token_rows, cond_rows, params, bias, allowed, valid_rows):
    cond_gain, ada_weight, ada_bias, zero_weight, zero_bias, attn_weight, query_bias, out_weight, pair_gain, pair_weight, trans_in, trans_out = params
    cond_normed = norm_rows(cond_rows)
    normed_in = adaptive(token_rows, cond_normed, cond_gain[0], ada_weight[0], ada_bias[0], ada_weight[1])
    queries = low(low_back(product(normed_in, attn_weight[0]) + query_bias)).reshape(L, H, HD)
    key_rows = low(low_back(product(normed_in, attn_weight[1]))).reshape(L, H, HD)
    value_rows = low(low_back(product(normed_in, attn_weight[2]))).reshape(L, H, HD)
    gate_value = jax.nn.sigmoid(low_back(product(normed_in, attn_weight[3])))
    scores = jnp.einsum('ihd,jhd->hij', queries, key_rows, precision=HIGHEST) * HD ** (-0.5) + bias
    scores = low_back(jnp.where(allowed[None], scores, MASKED))
    attn_prob = jax.nn.softmax(scores, axis=-1)
    attended = low_back(jnp.einsum('hij,jhd->ihd', low(attn_prob), value_rows, precision=HIGHEST)).reshape(L, D)
    gated = low(attended * gate_value)
    attn_branch = low_back(product(gated, out_weight))
    attn_zero = jax.nn.sigmoid(low_back(product(cond_rows, zero_weight[0]) + zero_bias[0]))
    middle = token_rows + valid_rows * attn_zero * attn_branch
    trans_input = adaptive(middle, cond_normed, cond_gain[1], ada_weight[2], ada_bias[1], ada_weight[3])
    first_proj = low_back(product(trans_input, trans_in[0]))
    second_proj = low_back(product(trans_input, trans_in[1]))
    hidden = low(jax.nn.silu(first_proj) * second_proj)
    trans_branch = low_back(product(hidden, trans_out))
    trans_zero = jax.nn.sigmoid(low_back(product(cond_rows, zero_weight[1]) + zero_bias[1]))
    return middle + valid_rows * trans_zero * trans_branch

def complex_forward(token_block, params, cond_block, pair_block, allowed, valid_rows):
    pair_low = low(norm_rows(pair_block) * params[8])
    bias = jnp.einsum('ijc,ch->hij', pair_low, params[9], precision=HIGHEST)

    def one_sample(pieces):
        return sample_forward(pieces[0], pieces[1], params, bias, allowed, valid_rows)
    return lax.map(jax.checkpoint(one_sample), (token_block, cond_block))

def reference(tokens, single, pair, token_count, pair_mask, cotangent, cond_gain, ada_weight, ada_bias, zero_weight, zero_bias, attn_weight, query_bias, out_weight, pair_gain, pair_weight, trans_in, trans_out):
    params = tuple((weight.astype(jnp.float32) for weight in (cond_gain, ada_weight, ada_bias, zero_weight, zero_bias, attn_weight, query_bias, out_weight, pair_gain, pair_weight, trans_in, trans_out)))
    positions = jnp.arange(L, dtype=jnp.int32)

    def one_complex(totals, inputs):
        token_now, single_now, pair_now, count_now, mask_now, cot_now = inputs
        valid_rows = (positions < count_now).astype(jnp.float32)[:, None]
        allowed = (positions[None, :] < count_now) & ((mask_now == 1) | (positions[:, None] == positions[None, :]) | (positions[:, None] >= count_now))
        cond_block = single_now.astype(jnp.float32)
        pair_block = pair_now.astype(jnp.float32)

        def forward(token_block, weights):
            return complex_forward(token_block, weights, cond_block, pair_block, allowed, valid_rows)
        result, pullback = jax.vjp(forward, token_now.astype(jnp.float32), params)
        token_grad, weight_grads = pullback(cot_now.astype(jnp.float32))
        totals = tuple((running + update for running, update in zip(totals, weight_grads)))
        return (totals, (result.astype(jnp.bfloat16), token_grad))
    start = tuple((jnp.zeros_like(weight) for weight in params))
    totals, outputs = lax.scan(one_complex, start, (tokens, single, pair, token_count, pair_mask, cotangent))
    return (outputs[0], outputs[1], totals[0], totals[1], totals[2], totals[3], totals[4], totals[5], totals[6], totals[7], totals[8], totals[9], totals[10], totals[11])
```

```python
import functools

import jax
import jax.numpy as jnp
from jax import lax
from jax.experimental import pallas as pl
from jax.experimental.pallas import tpu as pltpu
from jax.sharding import PartitionSpec as P

EPSILON = 1e-05
MASKED = -1000000000.0
F32 = jnp.float32
BF16 = jnp.bfloat16
VMEM_LIMIT = 58 << 20


def center_rows(value):
    center = value - jnp.mean(value, axis=-1, keepdims=True)
    rstd = lax.rsqrt(jnp.mean(center * center, axis=-1, keepdims=True) + EPSILON)
    return center * rstd, rstd


def dot(left, right):
    return lax.dot_general(left, right, (((1,), (0,)), ((), ())), preferred_element_type=F32)


def dot_nt(left, right):
    return lax.dot_general(left, right, (((1,), (1,)), ((), ())), preferred_element_type=F32)


def dot_tn(left, right):
    return lax.dot_general(left, right, (((0,), (0,)), ((), ())), preferred_element_type=F32)


def params(**extra):
    return pltpu.CompilerParams(vmem_limit_bytes=VMEM_LIMIT, **extra)


def head_windows(heads, head_dim):
    windows, head = [], 0
    while head < heads:
        start = head * head_dim // 128 * 128
        start = min(start, heads * head_dim - 256)
        inside = []
        while head < heads and (head + 1) * head_dim <= start + 256:
            inside.append(head)
            head += 1
        windows.append((start, inside))
    return windows


def head_mask(start, head, head_dim):
    lane = lax.broadcasted_iota(jnp.int32, (1, 256), 1) + start
    return (lane >= head * head_dim) & (lane < (head + 1) * head_dim)


def stack_heads(rows, start, inside, head_dim):
    zero = jnp.zeros_like(rows)
    return jnp.concatenate(
        [jnp.where(head_mask(start, head, head_dim), rows, zero) for head in inside], axis=0
    )


def unstack_heads(stacked, start, inside, head_dim):
    rows = stacked.shape[0] // len(inside)
    total = None
    for place, head in enumerate(inside):
        piece = jnp.where(
            head_mask(start, head, head_dim), stacked[place * rows : (place + 1) * rows], 0.0
        )
        total = piece if total is None else total + piece
    return total


def join_windows(parts, width):
    tiles = [None] * (width // 128)
    for start, value in parts:
        for half in range(2):
            place = start // 128 + half
            piece = value[:, half * 128 : (half + 1) * 128]
            tiles[place] = piece if tiles[place] is None else tiles[place] + piece
    return jnp.concatenate(tiles, axis=1)


def pair_kernel(meta_ref, pair_ref, mask_ref, gain_ref, weight_ref, low_ref, bias_ref):
    complex_id, block = pl.program_id(0), pl.program_id(1)
    rows, length = pair_ref.shape[1], pair_ref.shape[2]
    count = meta_ref[1 + complex_id]
    gain = gain_ref[...]
    weight = weight_ref[...]
    lines = []
    for row in range(rows):
        normed, _ = center_rows(pair_ref[0, row].astype(F32))
        low = (normed * gain).astype(BF16)
        low_ref[0, row] = low
        lines.append(dot_nt(weight, low))
    bias = jnp.stack(lines, axis=1)
    own = meta_ref[0] + block * rows + lax.broadcasted_iota(jnp.int32, (rows, length), 0)
    key = lax.broadcasted_iota(jnp.int32, (rows, length), 1)
    allowed = (key < count) & ((mask_ref[0] == 1) | (own == key) | (own >= count))
    bias_ref[0] = jnp.where(allowed[None], bias, MASKED)


def pair_bias(meta, pair, pair_mask, gain, weight):
    complexes, rows, length, width = pair.shape
    heads = weight.shape[1]
    block = 8
    return pl.pallas_call(
        pair_kernel,
        grid_spec=pltpu.PrefetchScalarGridSpec(
            num_scalar_prefetch=1,
            grid=(complexes, rows // block),
            in_specs=[
                pl.BlockSpec((1, block, length, width), lambda c, b, m: (c, b, 0, 0)),
                pl.BlockSpec((1, block, length), lambda c, b, m: (c, b, 0)),
                pl.BlockSpec((1, width), lambda c, b, m: (0, 0)),
                pl.BlockSpec((heads, width), lambda c, b, m: (0, 0)),
            ],
            out_specs=[
                pl.BlockSpec((1, block, length, width), lambda c, b, m: (c, b, 0, 0)),
                pl.BlockSpec((1, heads, block, length), lambda c, b, m: (c, 0, b, 0)),
            ],
        ),
        out_shape=[
            jax.ShapeDtypeStruct(pair.shape, BF16),
            jax.ShapeDtypeStruct((complexes, heads, rows, length), F32),
        ],
        compiler_params=params(),
        name="pair_bias",
    )(meta, pair, pair_mask, gain.astype(F32).reshape(1, width), weight.T)


def pair_grad_kernel(dbias_ref, low_ref, out_ref):
    first = (pl.program_id(0) == 0) & (pl.program_id(1) == 0)

    @pl.when(first)
    def _():
        out_ref[...] = jnp.zeros_like(out_ref)

    total = out_ref[...]
    for row in range(low_ref.shape[1]):
        total = total + dot(dbias_ref[0, :, row, :].astype(BF16), low_ref[0, row])
    out_ref[...] = total


def pair_grad(dbias, pair_low):
    complexes, rows, length, width = pair_low.shape
    heads = dbias.shape[1]
    block = 8
    return pl.pallas_call(
        pair_grad_kernel,
        grid=(complexes, rows // block),
        in_specs=[
            pl.BlockSpec((1, heads, block, length), lambda c, b: (c, 0, b, 0)),
            pl.BlockSpec((1, block, length, width), lambda c, b: (c, b, 0, 0)),
        ],
        out_specs=pl.BlockSpec((heads, width), lambda c, b: (0, 0)),
        out_shape=jax.ShapeDtypeStruct((heads, width), F32),
        compiler_params=params(),
        name="pair_grad",
    )(dbias, pair_low)


def project_kernel(
    tok_ref, single_ref, gain_ref, ada_ref, bias_ref, attn_ref, qbias_ref,
    normed_ref, query_ref, keyval_ref, gate_ref, hold_ref,
):
    which = pl.program_id(0)

    @pl.when(which == 0)
    def _():
        cond, _ = center_rows(single_ref[...].astype(F32))
        cond = (cond * gain_ref[0:1].astype(F32)).astype(BF16)
        pre = dot(cond, ada_ref[0]) + bias_ref[0:1].astype(F32)
        shift = dot(cond, ada_ref[1])
        normed, _ = center_rows(tok_ref[...].astype(F32))
        normed_in = (jax.nn.sigmoid(pre) * normed + shift).astype(BF16)
        normed_ref[...] = normed_in
        hold_ref[...] = normed_in

    result = dot(hold_ref[...], attn_ref[0])

    @pl.when(which == 0)
    def _():
        query_ref[...] = (result + qbias_ref[...].astype(F32)).astype(BF16)

    @pl.when((which == 1) | (which == 2))
    def _():
        keyval_ref[0] = result.astype(BF16)

    @pl.when(which == 3)
    def _():
        gate_ref[...] = jax.nn.sigmoid(result)


def project(tok, single, gain, ada, ada_bias, attn, query_bias):
    rows, width = tok.shape
    cond = single.shape[1]
    whole = lambda shape: pl.BlockSpec(shape, lambda w: (0,) * len(shape))
    return pl.pallas_call(
        project_kernel,
        grid=(4,),
        in_specs=[
            whole((rows, width)),
            whole((rows, cond)),
            whole((2, cond)),
            pl.BlockSpec((2, cond, width), lambda w: (0, 0, 0)),
            whole((2, width)),
            pl.BlockSpec((1, width, width), lambda w: (w, 0, 0)),
            whole((1, width)),
        ],
        out_specs=[
            whole((rows, width)),
            whole((rows, width)),
            pl.BlockSpec((1, rows, width), lambda w: (jnp.clip(w - 1, 0, 1), 0, 0)),
            whole((rows, width)),
        ],
        out_shape=[
            jax.ShapeDtypeStruct((rows, width), BF16),
            jax.ShapeDtypeStruct((rows, width), BF16),
            jax.ShapeDtypeStruct((2, rows, width), BF16),
            jax.ShapeDtypeStruct((rows, width), F32),
        ],
        scratch_shapes=[pltpu.VMEM((rows, width), BF16)],
        compiler_params=params(),
        name="project",
    )(tok, single, gain, ada, ada_bias, attn, query_bias.reshape(1, width))


def attend_kernel(heads, query_ref, key_ref, value_ref, bias_ref, out_ref, prob_ref):
    rows, width = query_ref.shape[2], query_ref.shape[3]
    length = key_ref.shape[2]
    head_dim = width // heads
    scale = head_dim ** (-0.5)
    parts = []
    for start, inside in head_windows(heads, head_dim):
        count = len(inside)
        lanes = slice(start, start + 256)
        stacked = stack_heads(query_ref[0, 0, :, lanes], start, inside, head_dim)
        scores = dot_nt(stacked, key_ref[0, 0, :, lanes]) * scale
        bias = bias_ref[0, inside[0] : inside[-1] + 1].reshape(count * rows, length)
        scores = scores + bias
        weight = jnp.exp(scores - jnp.max(scores, axis=-1, keepdims=True))
        prob = weight * (1.0 / jnp.sum(weight, axis=-1, keepdims=True))
        low = prob.astype(BF16)
        prob_ref[0, 0, inside[0] : inside[-1] + 1] = low.reshape(count, rows, length)
        mixed = dot(low, value_ref[0, 0, :, lanes])
        parts.append((start, unstack_heads(mixed, start, inside, head_dim)))
    out_ref[0, 0] = join_windows(parts, width)


def attend(query, key, value, bias):
    complexes, samples, rows, width = query.shape
    heads, length = bias.shape[1], bias.shape[3]
    own = pl.BlockSpec((1, 1, rows, width), lambda c, s: (c, s, 0, 0))
    full = pl.BlockSpec((1, 1, length, width), lambda c, s: (c, s, 0, 0))
    return pl.pallas_call(
        functools.partial(attend_kernel, heads),
        grid=(complexes, samples),
        in_specs=[
            own,
            full,
            full,
            pl.BlockSpec((1, heads, rows, length), lambda c, s: (c, 0, 0, 0)),
        ],
        out_specs=[
            own,
            pl.BlockSpec((1, 1, heads, rows, length), lambda c, s: (c, s, 0, 0, 0)),
        ],
        out_shape=[
            jax.ShapeDtypeStruct((complexes, samples, rows, width), F32),
            jax.ShapeDtypeStruct((complexes, samples, heads, rows, length), BF16),
        ],
        compiler_params=params(),
        name="attend",
    )(query, key, value, bias)


def attend_back_kernel(
    heads, prob_ref, grad_ref, query_ref, key_ref, value_ref, dq_ref, dk_ref, dv_ref, dbias_ref
):
    rows, width = query_ref.shape[2], query_ref.shape[3]
    length = key_ref.shape[2]
    head_dim = width // heads
    scale = head_dim ** (-0.5)

    @pl.when(pl.program_id(1) == 0)
    def _():
        dbias_ref[...] = jnp.zeros_like(dbias_ref)

    dq_parts, dk_parts, dv_parts = [], [], []
    for start, inside in head_windows(heads, head_dim):
        count = len(inside)
        lanes = slice(start, start + 256)
        queries = stack_heads(query_ref[0, 0, :, lanes], start, inside, head_dim)
        grads = stack_heads(grad_ref[0, 0, :, lanes], start, inside, head_dim)
        span = slice(inside[0], inside[-1] + 1)
        low = prob_ref[0, 0, span].reshape(count * rows, length)
        prob = low.astype(F32)
        dprob = dot_nt(grads, value_ref[0, 0, :, lanes])
        inner = jnp.sum(prob * dprob, axis=-1, keepdims=True)
        dscore = (prob * (dprob - inner)).astype(BF16)
        dbias_ref[0, span] += dscore.astype(F32).reshape(count, rows, length)
        mixed = dot(dscore, key_ref[0, 0, :, lanes])
        dq_parts.append((start, unstack_heads(mixed, start, inside, head_dim)))
        dk_parts.append((start, dot_tn(dscore, queries)))
        dv_parts.append((start, dot_tn(low, grads)))
    dq_ref[0, 0] = (join_windows(dq_parts, width) * scale).astype(BF16)
    dk_ref[0, 0] = (join_windows(dk_parts, width) * scale).astype(BF16)
    dv_ref[0, 0] = join_windows(dv_parts, width).astype(BF16)


def attend_back(prob, grad, query, key, value):
    complexes, samples, rows, width = query.shape
    heads, length = prob.shape[2], prob.shape[4]
    own = pl.BlockSpec((1, 1, rows, width), lambda c, s: (c, s, 0, 0))
    full = pl.BlockSpec((1, 1, length, width), lambda c, s: (c, s, 0, 0))
    return pl.pallas_call(
        functools.partial(attend_back_kernel, heads),
        grid=(complexes, samples),
        in_specs=[
            pl.BlockSpec((1, 1, heads, rows, length), lambda c, s: (c, s, 0, 0, 0)),
            own,
            own,
            full,
            full,
        ],
        out_specs=[
            own,
            full,
            full,
            pl.BlockSpec((1, heads, rows, length), lambda c, s: (c, 0, 0, 0)),
        ],
        out_shape=[
            jax.ShapeDtypeStruct((complexes, samples, rows, width), BF16),
            jax.ShapeDtypeStruct((complexes, samples, length, width), BF16),
            jax.ShapeDtypeStruct((complexes, samples, length, width), BF16),
            jax.ShapeDtypeStruct((complexes, heads, rows, length), F32),
        ],
        compiler_params=params(),
        name="attend_back",
    )(prob, grad, query, key, value)


def middle_kernel(
    samples, rows_dev, meta_ref,
    att_ref, gate_ref, tok_ref, single_ref, cot_ref,
    gain_ref, ada_ref, ada_bias_ref, zero_ref, zero_bias_ref, out_w_ref, tin_ref, tout_ref,
    out_ref, dmid_ref, datt_ref, dglogit_ref,
    gated_ref, dabranch_ref, dza_ref, dzb_ref, tcond_ref, dtpre_ref, dtin_ref,
    tinput_ref, dfirst_ref, dsecond_ref, hidden_ref, dtbranch_ref, small_ref,
):
    step = pl.program_id(0)
    rows = att_ref.shape[0]
    count = meta_ref[1 + step]
    place = lax.broadcasted_iota(jnp.int32, (rows, 1), 0) % rows_dev + meta_ref[0]
    valid = (place < count).astype(F32)
    att = att_ref[...]
    gate = gate_ref[...]
    single = single_ref[...]
    gated = (att * gate).astype(BF16)
    gated_ref[...] = gated
    branch = dot(gated, out_w_ref[...])
    attn_zero = jax.nn.sigmoid(dot(single, zero_ref[0]) + zero_bias_ref[0:1].astype(F32))
    middle = tok_ref[...].astype(F32) + valid * attn_zero * branch
    cond, _ = center_rows(single.astype(F32))
    tcond = (cond * gain_ref[1:2].astype(F32)).astype(BF16)
    tcond_ref[...] = tcond
    scale = jax.nn.sigmoid(dot(tcond, ada_ref[0]) + ada_bias_ref[1:2].astype(F32))
    shift = dot(tcond, ada_ref[1])
    normed, rstd = center_rows(middle)
    tinput = (scale * normed + shift).astype(BF16)
    tinput_ref[...] = tinput
    first = dot(tinput, tin_ref[0])
    second = dot(tinput, tin_ref[1])
    sig = jax.nn.sigmoid(first)
    hidden = (first * sig * second).astype(BF16)
    hidden_ref[...] = hidden
    tbranch = dot(hidden, tout_ref[...])
    trans_zero = jax.nn.sigmoid(dot(single, zero_ref[1]) + zero_bias_ref[1:2].astype(F32))
    out_ref[...] = (middle + valid * trans_zero * tbranch).astype(BF16)
    grad_out = cot_ref[...].astype(F32)
    gated_out = grad_out * valid
    dtbranch = (gated_out * trans_zero).astype(BF16)
    dtbranch_ref[...] = dtbranch
    dzb = (gated_out * tbranch * trans_zero * (1.0 - trans_zero)).astype(BF16)
    dzb_ref[...] = dzb
    dhidden = dot_nt(dtbranch, tout_ref[...])
    dfirst = (dhidden * second * sig * (1.0 + first * (1.0 - sig))).astype(BF16)
    dsecond = (dhidden * first * sig).astype(BF16)
    dfirst_ref[...] = dfirst
    dsecond_ref[...] = dsecond
    dtin = (dot_nt(dfirst, tin_ref[0]) + dot_nt(dsecond, tin_ref[1])).astype(BF16)
    dtin_ref[...] = dtin
    dtin_full = dtin.astype(F32)
    dtpre = (dtin_full * normed * scale * (1.0 - scale)).astype(BF16)
    dtpre_ref[...] = dtpre
    grad_norm = dtin_full * scale
    tail = grad_norm - jnp.mean(grad_norm, axis=-1, keepdims=True)
    tail = tail - normed * jnp.mean(grad_norm * normed, axis=-1, keepdims=True)
    dmid = grad_out + tail * rstd
    dmid_ref[...] = dmid
    dtcond = dot_nt(dtpre, ada_ref[0]) + dot_nt(dtin, ada_ref[1])
    gated_mid = dmid * valid
    dabranch = (gated_mid * attn_zero).astype(BF16)
    dabranch_ref[...] = dabranch
    dza = (gated_mid * branch * attn_zero * (1.0 - attn_zero)).astype(BF16)
    dza_ref[...] = dza
    dgated = dot_nt(dabranch, out_w_ref[...])
    datt_ref[...] = (dgated * gate).astype(BF16)
    dglogit_ref[...] = (dgated * att * gate * (1.0 - gate)).astype(BF16)

    @pl.when(step == 0)
    def _():
        small_ref[...] = jnp.zeros_like(small_ref)

    width, narrow = att.shape[1], single.shape[1]
    total = lambda value: jnp.sum(value.astype(F32), axis=0, keepdims=True)
    small_ref[0:1, :] += total(dtpre)
    small_ref[1:2, :] += total(dza)
    small_ref[2:3, :] += total(dzb)
    small_ref[3:4, 0:narrow] += total(dtcond * cond)


def middle_pass(
    meta, att, gate, tok, single, cot, gain, ada, ada_bias, zero, zero_bias, out_w, trans_in,
    trans_out, complexes, samples, rows_dev,
):
    rows, width = tok.shape
    narrow = single.shape[1]
    hidden = trans_out.shape[0]
    part = rows // complexes
    wide = pl.BlockSpec((part, width), lambda c, m: (c, 0))
    slim = pl.BlockSpec((part, narrow), lambda c, m: (c, 0))
    long = pl.BlockSpec((part, hidden), lambda c, m: (c, 0))
    once = lambda shape: pl.BlockSpec(
        shape, lambda c, m: (0,) * len(shape), pipeline_mode=pl.Buffered(1)
    )
    shape = lambda cols, kind: jax.ShapeDtypeStruct((rows, cols), kind)
    return pl.pallas_call(
        functools.partial(middle_kernel, samples, rows_dev),
        grid_spec=pltpu.PrefetchScalarGridSpec(
            num_scalar_prefetch=1,
            grid=(complexes,),
            in_specs=[
                wide, wide, wide, slim, wide,
                once(gain.shape),
                pl.BlockSpec((2, narrow, width), lambda c, m: (1, 0, 0), pipeline_mode=pl.Buffered(1)),
                once(ada_bias.shape),
                once(zero.shape),
                once(zero_bias.shape),
                once(out_w.shape),
                once(trans_in.shape),
                once(trans_out.shape),
            ],
            out_specs=[
                wide, wide, wide, wide,
                wide, wide, wide, wide, slim, wide, wide,
                wide, long, long, long, wide,
                once((8, width)),
            ],
        ),
        out_shape=[
            shape(width, BF16), shape(width, F32), shape(width, BF16), shape(width, BF16),
            shape(width, BF16), shape(width, BF16), shape(width, BF16), shape(width, BF16),
            shape(narrow, BF16), shape(width, BF16), shape(width, BF16),
            shape(width, BF16), shape(hidden, BF16), shape(hidden, BF16), shape(hidden, BF16),
            shape(width, BF16),
            jax.ShapeDtypeStruct((8, width), F32),
        ],
        compiler_params=params(),
        name="middle_pass",
    )(meta, att, gate, tok, single, cot, gain, ada, ada_bias, zero, zero_bias, out_w, trans_in, trans_out)


def last_kernel(
    dquery_ref, dkey_ref, dvalue_ref, dglogit_ref, tok_ref, single_ref, dmid_ref,
    gain_ref, ada_ref, ada_bias_ref, attn_ref,
    tgrad_ref, dnormed_ref, dapre_ref, cond_ref, small_ref, acc_ref,
):
    which = pl.program_id(0)

    @pl.when(which == 0)
    def _():
        acc_ref[...] = dot_nt(dquery_ref[...], attn_ref[0])

    @pl.when(which == 1)
    def _():
        acc_ref[...] += dot_nt(dkey_ref[...], attn_ref[0])

    @pl.when(which == 2)
    def _():
        acc_ref[...] += dot_nt(dvalue_ref[...], attn_ref[0])

    @pl.when(which == 3)
    def _():
        dnormed = (acc_ref[...] + dot_nt(dglogit_ref[...], attn_ref[0])).astype(BF16)
        dnormed_ref[...] = dnormed
        cond, _ = center_rows(single_ref[...].astype(F32))
        cond_low = (cond * gain_ref[0:1].astype(F32)).astype(BF16)
        cond_ref[...] = cond_low
        scale = jax.nn.sigmoid(dot(cond_low, ada_ref[0]) + ada_bias_ref[0:1].astype(F32))
        normed, rstd = center_rows(tok_ref[...].astype(F32))
        full = dnormed.astype(F32)
        dapre = (full * normed * scale * (1.0 - scale)).astype(BF16)
        dapre_ref[...] = dapre
        grad_norm = full * scale
        tail = grad_norm - jnp.mean(grad_norm, axis=-1, keepdims=True)
        tail = tail - normed * jnp.mean(grad_norm * normed, axis=-1, keepdims=True)
        tgrad_ref[...] = dmid_ref[...] + tail * rstd
        dcond = dot_nt(dapre, ada_ref[0]) + dot_nt(dnormed, ada_ref[1])
        narrow = cond.shape[1]
        total = lambda value: jnp.sum(value.astype(F32), axis=0, keepdims=True)
        small_ref[...] = jnp.zeros_like(small_ref)
        small_ref[0:1, :] = total(dapre)
        small_ref[1:2, :] = total(dquery_ref[...])
        small_ref[2:3, 0:narrow] = total(dcond * cond)


def last_pass(dquery, dkey, dvalue, dglogit, tok, single, dmid, gain, ada, ada_bias, attn):
    rows, width = tok.shape
    narrow = single.shape[1]
    whole = lambda shape: pl.BlockSpec(shape, lambda w: (0,) * len(shape))
    wide = whole((rows, width))
    shape = lambda cols, kind: jax.ShapeDtypeStruct((rows, cols), kind)
    return pl.pallas_call(
        last_kernel,
        grid=(4,),
        in_specs=[
            wide, wide, wide, wide, wide, whole((rows, narrow)), wide,
            whole(gain.shape),
            pl.BlockSpec((2, narrow, width), lambda w: (0, 0, 0)),
            whole(ada_bias.shape),
            pl.BlockSpec((1, width, width), lambda w: (w, 0, 0)),
        ],
        out_specs=[wide, wide, wide, whole((rows, narrow)), whole((8, width))],
        out_shape=[
            shape(width, F32), shape(width, BF16), shape(width, BF16), shape(narrow, BF16),
            jax.ShapeDtypeStruct((8, width), F32),
        ],
        scratch_shapes=[pltpu.VMEM((rows, width), F32)],
        compiler_params=params(),
        name="last_pass",
    )(dquery, dkey, dvalue, dglogit, tok, single, dmid, gain, ada, ada_bias, attn)


def weight_grad(left, grads):
    return [dot_tn(left, grad).astype(BF16) for grad in grads]


def gather_weights(shards, axes):
    return [
        lax.all_gather(shard, "sample", axis=axis, tiled=True) for shard, axis in zip(shards, axes)
    ]


def local(
    tokens, single, pair, token_count, pair_mask, cotangent, cond_gain, ada_weight, ada_bias,
    zero_weight, zero_bias, attn_weight, query_bias, out_weight, pair_gain, pair_weight,
    trans_in, trans_out,
):
    complexes, samples, rows_dev, width = tokens.shape
    narrow = single.shape[3]
    heads = pair_weight.shape[1]
    length = pair.shape[2]
    own_start = (lax.axis_index("row") * rows_dev).astype(jnp.int32)
    meta = jnp.concatenate([own_start[None], token_count.astype(jnp.int32)])
    full = gather_weights(
        (cond_gain, ada_weight, ada_bias, zero_weight, zero_bias, attn_weight, query_bias,
         out_weight, pair_gain, pair_weight, trans_in, trans_out),
        (1, 1, 1, 1, 1, 1, 0, 0, 0, 0, 1, 0),
    )
    (gain, ada, ada_b, zero, zero_b, attn, query_b, out_w, pgain, pweight, tin, tout) = full
    rows = complexes * samples * rows_dev
    flat = lambda value: value.reshape(rows, value.shape[-1])
    block = lambda value: value.reshape(complexes, samples, rows_dev, width)
    tok, sing, cot = flat(tokens), flat(single), flat(cotangent)

    pair_low, bias = pair_bias(meta, pair, pair_mask, pgain, pweight)
    normed_in, query, keyval, gate = project(tok, sing, gain, ada, ada_b, attn, query_b)
    query = block(query)
    key_all = lax.all_gather(block(keyval[0]), "row", axis=2, tiled=True)
    value_all = lax.all_gather(block(keyval[1]), "row", axis=2, tiled=True)
    att, prob = attend(query, key_all, value_all, bias)
    (
        output, dmid, datt, dglogit, gated, dabranch, dza, dzb, tcond, dtpre, dtin, tinput,
        dfirst, dsecond, hidden, dtbranch, small_mid,
    ) = middle_pass(
        meta, flat(att), gate, tok, sing, cot, gain, ada, ada_b, zero, zero_b, out_w, tin, tout,
        complexes, samples, rows_dev,
    )
    dquery, dkey, dvalue, dbias = attend_back(prob, block(datt), query, key_all, value_all)
    dkey_own = lax.psum_scatter(dkey, "row", scatter_dimension=2, tiled=True)
    dvalue_own = lax.psum_scatter(dvalue, "row", scatter_dimension=2, tiled=True)
    pair_sum = pair_grad(dbias, pair_low)
    dquery, dkey_own, dvalue_own = flat(dquery), flat(dkey_own), flat(dvalue_own)
    tgrad, dnormed, dapre, cond, small_last = last_pass(
        dquery, dkey_own, dvalue_own, dglogit, tok, sing, dmid, gain, ada, ada_b, attn
    )
    ada_grad = jnp.stack(weight_grad(cond, [dapre, dnormed]) + weight_grad(tcond, [dtpre, dtin]))
    zero_grad = jnp.stack(weight_grad(sing, [dza, dzb]))
    attn_grad = jnp.stack(weight_grad(normed_in, [dquery, dkey_own, dvalue_own, dglogit]))
    out_grad = weight_grad(gated, [dabranch])[0]
    tin_grad = jnp.stack(weight_grad(tinput, [dfirst, dsecond]))
    tout_grad = weight_grad(hidden, [dtbranch])[0]

    def reduce(value, axis):
        part = lax.psum_scatter(value, "sample", scatter_dimension=axis, tiled=True)
        return lax.psum(part, "row").astype(F32)

    small = jnp.concatenate(
        [small_mid.reshape(-1), small_last.reshape(-1), pair_sum.reshape(-1)]
    )
    small = lax.psum(small, ("row", "sample"))
    mid_size = small_mid.size
    small_mid = small[:mid_size].reshape(small_mid.shape)
    small_last = small[mid_size : 2 * mid_size].reshape(small_last.shape)
    pair_sum = small[2 * mid_size :].reshape(pair_sum.shape)
    spot = lax.axis_index("sample")

    def own_part(value, axis):
        size = value.shape[axis] // lax.axis_size("sample")
        return lax.dynamic_slice_in_dim(value, spot * size, size, axis)

    gain_grad = own_part(jnp.stack([small_last[2, :narrow], small_mid[3, :narrow]]), 1)
    ada_bias_grad = own_part(jnp.stack([small_last[0], small_mid[0]]), 1)
    zero_bias_grad = own_part(small_mid[1:3], 1)
    query_bias_grad = own_part(small_last[1], 0)
    pair_gain_grad = own_part(
        jnp.sum(pweight.astype(F32).T * pair_sum, axis=0) / pgain.astype(F32), 0
    )
    pair_weight_grad = own_part(pair_sum.T, 0)
    return (
        output.reshape(tokens.shape),
        tgrad.reshape(tokens.shape),
        gain_grad,
        reduce(ada_grad, 1),
        ada_bias_grad,
        reduce(zero_grad, 1),
        zero_bias_grad,
        reduce(attn_grad, 1),
        query_bias_grad,
        reduce(out_grad, 0),
        pair_gain_grad,
        pair_weight_grad,
        reduce(tin_grad, 1),
        reduce(tout_grad, 0),
    )


def solution(mesh):
    rowwise = P(None, "sample", "row", None)
    return jax.shard_map(
        local,
        mesh=mesh,
        in_specs=(
            rowwise,
            rowwise,
            P(None, "row", None, None),
            P(),
            P(None, "row", None),
            rowwise,
            P(None, "sample"),
            P(None, "sample", None),
            P(None, "sample"),
            P(None, "sample", None),
            P(None, "sample"),
            P(None, "sample", None),
            P("sample"),
            P("sample", None),
            P("sample"),
            P("sample", None),
            P(None, "sample", None),
            P("sample", None),
        ),
        out_specs=(
            rowwise,
            rowwise,
            P(None, "sample"),
            P(None, "sample", None),
            P(None, "sample"),
            P(None, "sample", None),
            P(None, "sample"),
            P(None, "sample", None),
            P("sample"),
            P("sample", None),
            P("sample"),
            P("sample", None),
            P(None, "sample", None),
            P("sample", None),
        ),
        check_vma=False,
    )
```

```python
import functools

import jax
import jax.numpy as jnp
from jax import lax
from jax.experimental import pallas as pl
from jax.experimental.pallas import tpu as pltpu
from jax.sharding import PartitionSpec as P

EPSILON = 1e-05
MASKED = -1000000000.0
F32 = jnp.float32
BF16 = jnp.bfloat16
VMEM_LIMIT = 58 << 20


def center_rows(value):
    center = value - jnp.mean(value, axis=-1, keepdims=True)
    rstd = lax.rsqrt(jnp.mean(center * center, axis=-1, keepdims=True) + EPSILON)
    return center * rstd, rstd


def dot(left, right):
    return lax.dot_general(left, right, (((1,), (0,)), ((), ())), preferred_element_type=F32)


def dot_nt(left, right):
    return lax.dot_general(left, right, (((1,), (1,)), ((), ())), preferred_element_type=F32)


def dot_tn(left, right):
    return lax.dot_general(left, right, (((0,), (0,)), ((), ())), preferred_element_type=F32)


def params(**extra):
    return pltpu.CompilerParams(vmem_limit_bytes=VMEM_LIMIT, **extra)


MESH = pl.DeviceIdType.MESH
ANY = pl.BlockSpec(memory_space=pl.ANY)


class Place:
    def __init__(self, chips, samples):
        self.row = lax.axis_index("row")
        self.chip = self.row // 2
        self.core = self.row % 2
        self.sample = lax.axis_index("sample")
        self.chips, self.samples = chips, samples

    def twin(self):
        return (self.row + 1 - 2 * self.core, self.sample)

    def peer(self, k):
        return (self.row, jnp.bitwise_xor(self.sample, k))

    def up(self):
        return (self.row + 2, self.sample)

    def down(self):
        return (self.row - 2, self.sample)

    def barrier(self, plane, line):
        bar = pltpu.get_barrier_semaphore()

        def greet(device):
            pl.semaphore_signal(bar, inc=1, device_id=device, device_id_type=MESH)

        greet(self.twin())
        if plane:
            for k in range(1, self.samples):
                greet(self.peer(k))
        if line:

            @pl.when(self.chip > 0)
            def _():
                greet(self.down())

            @pl.when(self.chip < self.chips - 1)
            def _():
                greet(self.up())

        count = 1 + (self.samples - 1 if plane else 0)
        if line:
            count = count + jnp.minimum(self.chip, 1) + jnp.minimum(self.chips - 1 - self.chip, 1)
        pl.semaphore_wait(bar, count)


def send(source, target, send_sem, recv_sem, device):
    return pltpu.make_async_remote_copy(
        source, target, send_sem, recv_sem, device_id=device, device_id_type=MESH
    )


def half_of(ref, core):
    if ref.shape[0] > 1:
        size = ref.shape[0] // 2
        return ref.at[pl.ds(core * size, size)]
    size = ref.shape[1] // 2
    return ref.at[:, pl.ds(pl.multiple_of(core * size, 16), size)]


class PlaneGather:
    @staticmethod
    def sems(arrays, samples):
        dma = pltpu.SemaphoreType.DMA
        return [dma((arrays, samples))] * 4 + [dma((arrays, 2))] * 2

    def __init__(self, place, shards, fulls, sems):
        self.place, self.shards, self.fulls = place, shards, fulls
        self.out, self.come, self.swap_out, self.swap_come, self.hop_out, self.hop_come = sems
        self.relayed = place.samples == 4
        self.direct = [1, 2] if self.relayed else list(range(1, place.samples))

    def owner(self, k):
        return jnp.bitwise_xor(self.place.sample, k)

    def half(self, i, k):
        return half_of(self.fulls[i].at[self.owner(k)], self.place.core)

    def copy(self, i, k):
        slot = self.half(i, 0)
        return send(
            half_of(self.shards[i], self.place.core), slot, self.out.at[i, k], self.come.at[i, k],
            self.place.peer(k),
        )

    def hop(self, i, k):
        slot = self.half(i, k)
        size = slot.shape[1] // 2
        piece = slot.at[:, pl.ds((k - 1) * size, size)]
        return send(piece, piece, self.hop_out.at[i, k - 1], self.hop_come.at[i, k - 1], self.place.peer(3 - k))

    def swap(self, i, k):
        slot = self.half(i, k)
        return send(slot, slot, self.swap_out.at[i, k], self.swap_come.at[i, k], self.place.twin())

    def keep(self, i):
        return send(
            self.shards[i], self.fulls[i].at[self.place.sample], self.swap_out.at[i, 0],
            self.swap_come.at[i, 0], self.place.twin(),
        )

    def start(self):
        for i in range(len(self.shards)):
            for k in self.direct:
                self.copy(i, k).start()
            self.keep(i).start()

    def relay(self, i):
        for k in self.direct:
            self.copy(i, k).wait_recv()
            if self.relayed:
                self.hop(i, k).start()
            self.swap(i, k).start()

    def settle(self, i):
        if self.relayed:
            for k in self.direct:
                self.hop(i, k).wait_recv()
            self.swap(i, 3).start()

    def finish(self):
        for i in range(len(self.shards)):
            self.keep(i).wait()
            for k in self.direct:
                self.copy(i, k).wait_send()
                if self.relayed:
                    self.hop(i, k).wait_send()
            for k in range(1, self.place.samples):
                self.swap(i, k).wait()


class LineSpread:
    @staticmethod
    def sems(lines, chips):
        dma = pltpu.SemaphoreType.DMA
        return [dma((lines, chips))] * 6

    def __init__(self, place, line, slot, sems):
        self.place, self.line, self.slot = place, line, slot
        self.up_out, self.up_come, self.down_out, self.down_come, self.swap_out, self.swap_come = sems

    def step(self, upward, t):
        place, last = self.place, self.place.chips - 1
        z = place.chip
        if upward:
            out_chip, has_out = z - t + 1, (z >= t - 1) & (z < last)
            in_chip, has_in = z - t, z >= t
            sems, device = (self.up_out, self.up_come), place.up()
        else:
            out_chip, has_out = z + t - 1, (z + t - 1 <= last) & (z > 0)
            in_chip, has_in = z + t, z + t <= last
            sems, device = (self.down_out, self.down_come), place.down()
        make = lambda chip: send(
            self.slot(chip), self.slot(chip),
            sems[0].at[self.line, t], sems[1].at[self.line, t], device,
        )
        return (has_out, lambda: make(out_chip)), (has_in, in_chip, lambda: make(in_chip))

    def hand_over(self, chip):
        slot = self.slot(chip)
        return send(
            slot, slot, self.swap_out.at[self.line, chip], self.swap_come.at[self.line, chip],
            self.place.twin(),
        )

    def depart(self, t):
        for upward in (True, False):
            (has_out, copy), _ = self.step(upward, t)

            @pl.when(has_out)
            def _():
                copy().start()

    def advance(self, t):
        for upward in (True, False):
            _, (has_in, chip, copy) = self.step(upward, t)

            @pl.when(has_in)
            def _():
                copy().wait_recv()

        if t + 1 < self.place.chips:
            self.depart(t + 1)
        for upward in (True, False):
            _, (has_in, chip, copy) = self.step(upward, t)

            @pl.when(has_in)
            def _():
                self.hand_over(chip).start()

    def finish(self):
        for t in range(1, self.place.chips):
            for upward in (True, False):
                (has_out, copy), (has_in, chip, _) = self.step(upward, t)

                @pl.when(has_out)
                def _():
                    copy().wait_send()

                @pl.when(has_in)
                def _():
                    self.hand_over(chip).wait()


class LineReduce:
    @staticmethod
    def sems(lines, chips):
        dma = pltpu.SemaphoreType.DMA
        return [dma((lines, chips))] * 4

    def __init__(self, place, line, slot, up_buf, down_buf, sems):
        self.place, self.line, self.slot = place, line, slot
        self.bufs = (up_buf, down_buf)
        self.up_out, self.up_come, self.down_out, self.down_come = sems

    def step(self, upward, t):
        place, last = self.place, self.place.chips - 1
        z, distance = place.chip, place.chips - t
        buf = self.bufs[0 if upward else 1]
        if upward:
            block, has_out, has_before = z + distance, z + distance <= last, z > 0
            has_in = (z > 0) & (z - 1 + distance <= last)
            sems, device = (self.up_out, self.up_come), place.up()
        else:
            block, has_out, has_before = z - distance, z - distance >= 0, z < last
            has_in = (z < last) & (z + 1 - distance >= 0)
            sems, device = (self.down_out, self.down_come), place.down()
        copy = lambda chip: send(
            self.slot(chip), buf.at[self.line, t],
            sems[0].at[self.line, t], sems[1].at[self.line, t], device,
        )
        return block, has_out, has_before, has_in, copy, buf

    def advance(self, t):
        for upward in (True, False):
            block, has_out, has_before, _, copy, buf = self.step(upward, t)
            before = self.step(upward, t - 1)[4] if t > 1 else None

            @pl.when(has_out)
            def _():
                if t > 1:

                    @pl.when(has_before)
                    def _():
                        before(block).wait_recv()
                        slot = self.slot(block)
                        slot[...] = (
                            slot[...].astype(F32) + buf[self.line, t - 1].astype(F32)
                        ).astype(slot.dtype)

                copy(block).start()

    def finish(self):
        last_step = self.place.chips - 1
        slot = self.slot(self.place.chip)
        for upward in (True, False):
            _, _, _, has_in, copy, buf = self.step(upward, last_step)

            @pl.when(has_in)
            def _():
                copy(self.place.chip).wait_recv()
                slot[...] = (
                    slot[...].astype(F32) + buf[self.line, last_step].astype(F32)
                ).astype(slot.dtype)

        for t in range(1, self.place.chips):
            for upward in (True, False):
                block, has_out, _, _, copy, _ = self.step(upward, t)

                @pl.when(has_out)
                def _():
                    copy(block).wait_send()


class RowGather:
    @staticmethod
    def sems(lines, chips):
        dma = pltpu.SemaphoreType.DMA
        return [dma((lines, 2))] * 3 + LineSpread.sems(lines, chips)

    def __init__(self, place, part, full, line, sems):
        self.place, self.part, self.full, self.index = place, part, full, line
        self.spot = (line // part.shape[2], line % part.shape[2])
        self.local, self.swap_out, self.swap_come = sems[:3]
        self.rows = part.shape[3]
        self.line = LineSpread(place, line, self.chip_slot, sems[3:])

    def chip_slot(self, chip):
        size = 2 * self.rows
        rows = pl.ds(pl.multiple_of(chip * size, size), size)
        return self.full.at[(self.place.core,) + self.spot + (rows,)]

    def own_slot(self, role):
        rows = pl.ds(pl.multiple_of(self.place.row * self.rows, self.rows), self.rows)
        return self.full.at[(role,) + self.spot + (rows,)]

    def keep(self, role):
        return pltpu.make_async_copy(
            self.part.at[(role,) + self.spot], self.own_slot(role), self.local.at[self.index, role]
        )

    def first_swap(self, role):
        return send(
            self.part.at[(role,) + self.spot], self.own_slot(role),
            self.swap_out.at[self.index, role], self.swap_come.at[self.index, role], self.place.twin(),
        )

    def start(self):
        for role in range(2):
            self.keep(role).start()
            self.first_swap(role).start()

    def begin(self):
        for role in range(2):
            self.keep(role).wait()
            self.first_swap(role).wait()
        self.line.depart(1)


def gather_kernel(arrays, chips, samples, *refs):
    shards, fulls = refs[:arrays], refs[arrays : 2 * arrays]
    place = Place(chips, samples)
    move = PlaneGather(place, shards, fulls, refs[2 * arrays :])
    place.barrier(True, False)
    move.start()
    for i in range(arrays):
        move.relay(i)
        if i:
            move.settle(i - 1)
    move.settle(arrays - 1)
    move.finish()


def gather_weights(shards, collective_id):
    samples, chips = lax.axis_size("sample"), lax.axis_size("row") // 2
    count = len(shards)
    return pl.pallas_call(
        functools.partial(gather_kernel, count, chips, samples),
        in_specs=[ANY] * count,
        out_specs=[ANY] * count,
        out_shape=[jax.ShapeDtypeStruct((samples,) + s.shape, s.dtype) for s in shards],
        scratch_shapes=PlaneGather.sems(count, samples),
        compiler_params=pltpu.CompilerParams(collective_id=collective_id, has_side_effects=True),
        name="gather_weights",
    )(*shards)


def gather_rows_kernel(chips, samples, part_ref, full_ref, *sems):
    place = Place(chips, samples)
    lines = part_ref.shape[1] * part_ref.shape[2]
    moves = [RowGather(place, part_ref, full_ref, line, sems) for line in range(lines)]
    place.barrier(False, True)
    for move in moves:
        move.start()
    for move in moves:
        move.begin()
    for t in range(1, chips):
        for move in moves:
            move.line.advance(t)
    for move in moves:
        move.line.finish()


def gather_rows(part, collective_id):
    samples, chips = lax.axis_size("sample"), lax.axis_size("row") // 2
    two, complexes, own, rows, width = part.shape
    full = (two, complexes, own, rows * 2 * chips, width)
    return pl.pallas_call(
        functools.partial(gather_rows_kernel, chips, samples),
        in_specs=[pl.BlockSpec(memory_space=pltpu.VMEM)],
        out_specs=ANY,
        out_shape=jax.ShapeDtypeStruct(full, part.dtype),
        scratch_shapes=RowGather.sems(complexes * own, chips),
        compiler_params=params(collective_id=collective_id, has_side_effects=True),
        name="gather_rows",
    )(part)


class RowReduce:
    @staticmethod
    def scratch(complexes, samples_own, length, rows, width, chips):
        dma = pltpu.SemaphoreType.DMA
        hop = pltpu.VMEM((complexes, chips, samples_own, 2 * rows, width), BF16)
        return [
            pltpu.VMEM((complexes, samples_own, length, width), BF16), hop, hop,
        ] + [dma((complexes,))] * 5 + LineReduce.sems(complexes, chips)

    def __init__(self, place, part, own, which, scratch):
        self.place, self.part, self.own, self.which = place, part, own, which
        self.sums, up_buf, down_buf = scratch[:3]
        self.swap_out, self.swap_come, self.last_out, self.last_come, self.keep_sem = scratch[3:8]
        self.rows = own.shape[3]
        self.line = LineReduce(place, which, self.chip_slot, up_buf, down_buf, scratch[8:])

    def chip_slot(self, chip):
        size = 2 * self.rows
        return self.sums.at[self.which, :, pl.ds(pl.multiple_of(chip * size, size), size)]

    def first_swap(self):
        return send(
            self.part.at[1 - self.place.core, self.which], self.sums.at[self.which],
            self.swap_out.at[self.which], self.swap_come.at[self.which], self.place.twin(),
        )

    def begin(self):
        self.first_swap().wait_recv()
        for sample in range(self.part.shape[2]):
            mine = self.part[self.place.core, self.which, sample].astype(F32)
            self.sums[self.which, sample] = (
                mine + self.sums[self.which, sample].astype(F32)
            ).astype(BF16)

    def result(self, core):
        spot = self.place.row - self.place.core + core
        spot = pl.ds(pl.multiple_of(spot * self.rows, self.rows), self.rows)
        return self.sums.at[self.which, :, spot]

    def last_copies(self):
        target = self.own.at[self.place.core, self.which]
        return (
            send(
                self.result(1 - self.place.core), target,
                self.last_out.at[self.which], self.last_come.at[self.which], self.place.twin(),
            ),
            pltpu.make_async_copy(self.result(self.place.core), target, self.keep_sem.at[self.which]),
        )

    def finish(self):
        self.line.finish()
        for copy in self.last_copies():
            copy.start()

    def drain(self):
        self.first_swap().wait_send()
        for copy in self.last_copies():
            copy.wait()


def reduce_rows_kernel(chips, samples, part_ref, own_ref, *scratch):
    place = Place(chips, samples)
    moves = [
        RowReduce(place, part_ref, own_ref, which, scratch) for which in range(part_ref.shape[1])
    ]
    place.barrier(False, True)
    for move in moves:
        move.first_swap().start()
    for move in moves:
        move.begin()
        move.line.advance(1)
    for t in range(2, chips):
        for move in moves:
            move.line.advance(t)
    for move in moves:
        move.finish()
    for move in moves:
        move.drain()


def reduce_rows(part, collective_id):
    samples, chips = lax.axis_size("sample"), lax.axis_size("row") // 2
    two, complexes, own, length, width = part.shape
    rows = length // (2 * chips)
    return pl.pallas_call(
        functools.partial(reduce_rows_kernel, chips, samples),
        in_specs=[pl.BlockSpec(memory_space=pltpu.VMEM)],
        out_specs=ANY,
        out_shape=jax.ShapeDtypeStruct((two, complexes, own, rows, width), part.dtype),
        scratch_shapes=RowReduce.scratch(complexes, own, length, rows, width, chips),
        compiler_params=params(collective_id=collective_id, has_side_effects=True),
        name="reduce_rows",
    )(part)


class PlaneReduce:
    @staticmethod
    def scratch(samples, rows, width):
        dma = pltpu.SemaphoreType.DMA
        half = rows // 2
        return [
            pltpu.VMEM((samples, half, width), BF16), pltpu.VMEM((samples, half, width), BF16),
        ] + [dma((samples,))] * 4

    def __init__(self, place, grads, plane, scratch):
        self.place, self.grads, self.plane = place, grads, plane
        self.sums, self.come_buf, self.swap_out, self.swap_come, self.out, self.come = scratch
        self.half = grads.shape[1] // 2

    def shard(self, k):
        return jnp.bitwise_xor(self.place.sample, k)

    def half_rows(self, core):
        return pl.ds(pl.multiple_of(core * self.half, 16), self.half)

    def swap(self, k):
        return send(
            self.grads.at[self.shard(k), self.half_rows(1 - self.place.core)],
            self.sums.at[self.shard(k)],
            self.swap_out.at[k], self.swap_come.at[k], self.place.twin(),
        )

    def copy(self, k):
        return send(
            self.sums.at[self.shard(k)], self.come_buf.at[k], self.out.at[k], self.come.at[k],
            self.place.peer(k),
        )

    def order(self):
        return list(range(1, self.place.samples)) + [0]

    def start(self):
        for k in self.order():
            self.swap(k).start()

    def depart(self, k):
        self.swap(k).wait_recv()
        mine = self.grads[self.shard(k), self.half_rows(self.place.core)].astype(F32)
        slot = self.sums.at[self.shard(k)]
        slot[...] = (mine + slot[...].astype(F32)).astype(BF16)
        if k:
            self.copy(k).start()

    def finish(self):
        value = self.sums[self.place.sample].astype(F32)
        for k in range(1, self.place.samples):
            self.copy(k).wait_recv()
            value = value + self.come_buf[k].astype(F32)
        self.plane[...] = value.astype(BF16)

    def drain(self):
        for k in self.order():
            self.swap(k).wait_send()
            if k:
                self.copy(k).wait_send()


class LineTotal:
    @staticmethod
    def scratch(rows, width, chips):
        hop = pltpu.VMEM((1, chips, rows // 2 // chips, width), BF16)
        return [hop, hop] + LineReduce.sems(1, chips) + LineSpread.sems(1, chips)

    def __init__(self, place, plane, total, scratch):
        self.place, self.plane, self.total = place, plane, total
        self.half = total.shape[0] // 2
        self.size = self.half // place.chips
        self.reduce = LineReduce(place, 0, self.block, scratch[0], scratch[1], scratch[2:6])
        self.spread = LineSpread(place, 0, self.slot, scratch[6:])

    def block(self, chip):
        return self.plane.at[pl.ds(pl.multiple_of(chip * self.size, 16), self.size)]

    def slot(self, chip):
        start = self.place.core * self.half + chip * self.size
        return self.total.at[pl.ds(pl.multiple_of(start, 16), self.size)]

    def turn(self):
        self.reduce.finish()
        own = self.slot(self.place.chip)
        own[...] = self.block(self.place.chip)[...]
        self.spread.depart(1)
        self.spread.hand_over(self.place.chip).start()

    def finish(self):
        self.spread.finish()
        self.spread.hand_over(self.place.chip).wait()


def reduce_grads_kernel(chips, samples, grads_ref, total_ref, *scratch):
    place = Place(chips, samples)
    count = len(PlaneReduce.scratch(samples, 32, 128))
    plane_buf = scratch[0]
    plane = PlaneReduce(place, grads_ref, plane_buf, scratch[1 : 1 + count])
    line = LineTotal(place, plane_buf, total_ref, scratch[1 + count :])
    place.barrier(True, True)
    plane.start()
    for k in plane.order():
        plane.depart(k)
    plane.finish()
    for t in range(1, chips):
        line.reduce.advance(t)
    line.turn()
    for t in range(1, chips):
        line.spread.advance(t)
    line.finish()
    plane.drain()


def reduce_grads(grads, collective_id):
    chips = lax.axis_size("row") // 2
    samples, rows, width = grads.shape
    return pl.pallas_call(
        functools.partial(reduce_grads_kernel, chips, samples),
        in_specs=[pl.BlockSpec(memory_space=pltpu.VMEM)],
        out_specs=pl.BlockSpec(memory_space=pltpu.VMEM),
        out_shape=jax.ShapeDtypeStruct((rows, width), BF16),
        scratch_shapes=[pltpu.VMEM((rows // 2, width), BF16)]
        + PlaneReduce.scratch(samples, rows, width)
        + LineTotal.scratch(rows, width, chips),
        compiler_params=params(collective_id=collective_id, has_side_effects=True),
        name="reduce_grads",
    )(grads)


def joined(ref, which=0):
    samples, _, rows, cols = ref.shape
    return ref[:, which].reshape(samples * rows, cols)


def head_windows(heads, head_dim):
    windows, head = [], 0
    while head < heads:
        start = head * head_dim // 128 * 128
        start = min(start, heads * head_dim - 256)
        inside = []
        while head < heads and (head + 1) * head_dim <= start + 256:
            inside.append(head)
            head += 1
        windows.append((start, inside))
    return windows


def head_mask(start, head, head_dim):
    lane = lax.broadcasted_iota(jnp.int32, (1, 256), 1) + start
    return (lane >= head * head_dim) & (lane < (head + 1) * head_dim)


def stack_heads(rows, start, inside, head_dim):
    zero = jnp.zeros_like(rows)
    return jnp.concatenate(
        [jnp.where(head_mask(start, head, head_dim), rows, zero) for head in inside], axis=0
    )


def unstack_heads(stacked, start, inside, head_dim):
    rows = stacked.shape[0] // len(inside)
    total = None
    for place, head in enumerate(inside):
        piece = jnp.where(
            head_mask(start, head, head_dim), stacked[place * rows : (place + 1) * rows], 0.0
        )
        total = piece if total is None else total + piece
    return total


def join_windows(parts, width):
    tiles = [None] * (width // 128)
    for start, value in parts:
        for half in range(2):
            place = start // 128 + half
            piece = value[:, half * 128 : (half + 1) * 128]
            tiles[place] = piece if tiles[place] is None else tiles[place] + piece
    return jnp.concatenate(tiles, axis=1)


def pair_kernel(meta_ref, pair_ref, mask_ref, gain_ref, weight_ref, low_ref, bias_ref):
    complex_id, block = pl.program_id(0), pl.program_id(1)
    rows, length = pair_ref.shape[1], pair_ref.shape[2]
    count = meta_ref[1 + complex_id]
    gain = gain_ref[...]
    weight = weight_ref[...]
    lines = []
    for row in range(rows):
        normed, _ = center_rows(pair_ref[0, row].astype(F32))
        low = (normed * gain).astype(BF16)
        low_ref[0, row] = low
        lines.append(dot_nt(weight, low))
    bias = jnp.stack(lines, axis=1)
    own = meta_ref[0] + block * rows + lax.broadcasted_iota(jnp.int32, (rows, length), 0)
    key = lax.broadcasted_iota(jnp.int32, (rows, length), 1)
    allowed = (key < count) & ((mask_ref[0] == 1) | (own == key) | (own >= count))
    bias_ref[0] = jnp.where(allowed[None], bias, MASKED)


def pair_bias(meta, pair, pair_mask, gain, weight):
    complexes, rows, length, width = pair.shape
    heads = weight.shape[1]
    block = 8
    return pl.pallas_call(
        pair_kernel,
        grid_spec=pltpu.PrefetchScalarGridSpec(
            num_scalar_prefetch=1,
            grid=(complexes, rows // block),
            in_specs=[
                pl.BlockSpec((1, block, length, width), lambda c, b, m: (c, b, 0, 0)),
                pl.BlockSpec((1, block, length), lambda c, b, m: (c, b, 0)),
                pl.BlockSpec((1, width), lambda c, b, m: (0, 0)),
                pl.BlockSpec((heads, width), lambda c, b, m: (0, 0)),
            ],
            out_specs=[
                pl.BlockSpec((1, block, length, width), lambda c, b, m: (c, b, 0, 0)),
                pl.BlockSpec((1, heads, block, length), lambda c, b, m: (c, 0, b, 0)),
            ],
        ),
        out_shape=[
            jax.ShapeDtypeStruct(pair.shape, BF16),
            jax.ShapeDtypeStruct((complexes, heads, rows, length), F32),
        ],
        compiler_params=params(),
        name="pair_bias",
    )(meta, pair, pair_mask, gain.astype(F32).reshape(1, width), weight.T)


def pair_grad_kernel(dbias_ref, low_ref, out_ref):
    first = (pl.program_id(0) == 0) & (pl.program_id(1) == 0)

    @pl.when(first)
    def _():
        out_ref[...] = jnp.zeros_like(out_ref)

    total = out_ref[...]
    for row in range(low_ref.shape[1]):
        total = total + dot(dbias_ref[0, :, row, :].astype(BF16), low_ref[0, row])
    out_ref[...] = total


def pair_grad(dbias, pair_low):
    complexes, rows, length, width = pair_low.shape
    heads = dbias.shape[1]
    block = 8
    return pl.pallas_call(
        pair_grad_kernel,
        grid=(complexes, rows // block),
        in_specs=[
            pl.BlockSpec((1, heads, block, length), lambda c, b: (c, 0, b, 0)),
            pl.BlockSpec((1, block, length, width), lambda c, b: (c, b, 0, 0)),
        ],
        out_specs=pl.BlockSpec((heads, width), lambda c, b: (0, 0)),
        out_shape=jax.ShapeDtypeStruct((heads, width), F32),
        compiler_params=params(),
        name="pair_grad",
    )(dbias, pair_low)


def project_kernel(
    tok_ref, single_ref, gain_ref, ada_ref, bias_ref, attn_ref, qbias_ref,
    normed_ref, query_ref, keyval_ref, gate_ref, hold_ref,
):
    which = pl.program_id(0)

    @pl.when(which == 0)
    def _():
        cond, _ = center_rows(single_ref[...].astype(F32))
        cond = (cond * gain_ref[0:1].astype(F32)).astype(BF16)
        pre = dot(cond, joined(ada_ref, 0)) + bias_ref[0:1].astype(F32)
        shift = dot(cond, joined(ada_ref, 1))
        normed, _ = center_rows(tok_ref[...].astype(F32))
        normed_in = (jax.nn.sigmoid(pre) * normed + shift).astype(BF16)
        normed_ref[...] = normed_in
        hold_ref[...] = normed_in

    result = dot(hold_ref[...], joined(attn_ref))

    @pl.when(which == 0)
    def _():
        query_ref[...] = (result + qbias_ref[...].astype(F32)).astype(BF16)

    @pl.when((which == 1) | (which == 2))
    def _():
        keyval_ref[0] = result.astype(BF16)

    @pl.when(which == 3)
    def _():
        gate_ref[...] = jax.nn.sigmoid(result)


def project(tok, single, gain, ada, ada_bias, attn, query_bias):
    rows, width = tok.shape
    cond = single.shape[1]
    whole = lambda shape: pl.BlockSpec(shape, lambda w: (0,) * len(shape))
    return pl.pallas_call(
        project_kernel,
        grid=(4,),
        in_specs=[
            whole((rows, width)),
            whole((rows, cond)),
            whole((2, cond)),
            pl.BlockSpec((ada.shape[0], 2) + ada.shape[2:], lambda w: (0, 0, 0, 0)),
            whole((2, width)),
            pl.BlockSpec((attn.shape[0], 1) + attn.shape[2:], lambda w: (0, w, 0, 0)),
            whole((1, width)),
        ],
        out_specs=[
            whole((rows, width)),
            whole((rows, width)),
            pl.BlockSpec((1, rows, width), lambda w: (jnp.clip(w - 1, 0, 1), 0, 0)),
            whole((rows, width)),
        ],
        out_shape=[
            jax.ShapeDtypeStruct((rows, width), BF16),
            jax.ShapeDtypeStruct((rows, width), BF16),
            jax.ShapeDtypeStruct((2, rows, width), BF16),
            jax.ShapeDtypeStruct((rows, width), F32),
        ],
        scratch_shapes=[pltpu.VMEM((rows, width), BF16)],
        compiler_params=params(),
        name="project",
    )(tok, single, gain, ada, ada_bias, attn, query_bias.reshape(1, width))


def attend_kernel(heads, query_ref, keyval_ref, bias_ref, out_ref, prob_ref):
    rows, width = query_ref.shape[2], query_ref.shape[3]
    length = keyval_ref.shape[3]
    head_dim = width // heads
    scale = head_dim ** (-0.5)
    parts = []
    for start, inside in head_windows(heads, head_dim):
        count = len(inside)
        lanes = slice(start, start + 256)
        stacked = stack_heads(query_ref[0, 0, :, lanes], start, inside, head_dim)
        scores = dot_nt(stacked, keyval_ref[0, 0, 0, :, lanes]) * scale
        bias = bias_ref[0, inside[0] : inside[-1] + 1].reshape(count * rows, length)
        scores = scores + bias
        weight = jnp.exp(scores - jnp.max(scores, axis=-1, keepdims=True))
        prob = weight * (1.0 / jnp.sum(weight, axis=-1, keepdims=True))
        low = prob.astype(BF16)
        prob_ref[0, 0, inside[0] : inside[-1] + 1] = low.reshape(count, rows, length)
        mixed = dot(low, keyval_ref[1, 0, 0, :, lanes])
        parts.append((start, unstack_heads(mixed, start, inside, head_dim)))
    out_ref[0, 0] = join_windows(parts, width)


def attend(query, keyval, bias):
    complexes, samples, rows, width = query.shape
    heads, length = bias.shape[1], bias.shape[3]
    own = pl.BlockSpec((1, 1, rows, width), lambda c, s: (c, s, 0, 0))
    full = pl.BlockSpec((2, 1, 1, length, width), lambda c, s: (0, c, s, 0, 0))
    return pl.pallas_call(
        functools.partial(attend_kernel, heads),
        grid=(complexes, samples),
        in_specs=[
            own,
            full,
            pl.BlockSpec((1, heads, rows, length), lambda c, s: (c, 0, 0, 0)),
        ],
        out_specs=[
            own,
            pl.BlockSpec((1, 1, heads, rows, length), lambda c, s: (c, s, 0, 0, 0)),
        ],
        out_shape=[
            jax.ShapeDtypeStruct((complexes, samples, rows, width), F32),
            jax.ShapeDtypeStruct((complexes, samples, heads, rows, length), BF16),
        ],
        compiler_params=params(),
        name="attend",
    )(query, keyval, bias)


def attend_back_kernel(
    heads, prob_ref, grad_ref, query_ref, keyval_ref, dq_ref, dkeyval_ref, dbias_ref
):
    rows, width = query_ref.shape[2], query_ref.shape[3]
    length = keyval_ref.shape[3]
    head_dim = width // heads
    scale = head_dim ** (-0.5)

    @pl.when(pl.program_id(1) == 0)
    def _():
        dbias_ref[...] = jnp.zeros_like(dbias_ref)

    dq_parts, dk_parts, dv_parts = [], [], []
    for start, inside in head_windows(heads, head_dim):
        count = len(inside)
        lanes = slice(start, start + 256)
        queries = stack_heads(query_ref[0, 0, :, lanes], start, inside, head_dim)
        grads = stack_heads(grad_ref[0, 0, :, lanes], start, inside, head_dim)
        span = slice(inside[0], inside[-1] + 1)
        low = prob_ref[0, 0, span].reshape(count * rows, length)
        prob = low.astype(F32)
        dprob = dot_nt(grads, keyval_ref[1, 0, 0, :, lanes])
        inner = jnp.sum(prob * dprob, axis=-1, keepdims=True)
        dscore = (prob * (dprob - inner)).astype(BF16)
        dbias_ref[0, span] += dscore.astype(F32).reshape(count, rows, length)
        mixed = dot(dscore, keyval_ref[0, 0, 0, :, lanes])
        dq_parts.append((start, unstack_heads(mixed, start, inside, head_dim)))
        dk_parts.append((start, dot_tn(dscore, queries)))
        dv_parts.append((start, dot_tn(low, grads)))
    dq_ref[0, 0] = (join_windows(dq_parts, width) * scale).astype(BF16)
    dkeyval_ref[0, 0, 0] = (join_windows(dk_parts, width) * scale).astype(BF16)
    dkeyval_ref[1, 0, 0] = join_windows(dv_parts, width).astype(BF16)


def attend_back(prob, grad, query, keyval):
    complexes, samples, rows, width = query.shape
    heads, length = prob.shape[2], prob.shape[4]
    own = pl.BlockSpec((1, 1, rows, width), lambda c, s: (c, s, 0, 0))
    full = pl.BlockSpec((2, 1, 1, length, width), lambda c, s: (0, c, s, 0, 0))
    return pl.pallas_call(
        functools.partial(attend_back_kernel, heads),
        grid=(complexes, samples),
        in_specs=[
            pl.BlockSpec((1, 1, heads, rows, length), lambda c, s: (c, s, 0, 0, 0)),
            own,
            own,
            full,
        ],
        out_specs=[
            own,
            full,
            pl.BlockSpec((1, heads, rows, length), lambda c, s: (c, 0, 0, 0)),
        ],
        out_shape=[
            jax.ShapeDtypeStruct((complexes, samples, rows, width), BF16),
            jax.ShapeDtypeStruct((2, complexes, samples, length, width), BF16),
            jax.ShapeDtypeStruct((complexes, heads, rows, length), F32),
        ],
        compiler_params=params(),
        name="attend_back",
    )(prob, grad, query, keyval)


def middle_kernel(
    samples, rows_dev, meta_ref,
    att_ref, gate_ref, tok_ref, single_ref, cot_ref,
    gain_ref, ada_ref, ada_bias_ref, zero_ref, zero_bias_ref, out_w_ref, tin_ref, tout_ref,
    out_ref, dmid_ref, datt_ref, dglogit_ref,
    gated_ref, dabranch_ref, dza_ref, dzb_ref, tcond_ref, dtpre_ref, dtin_ref,
    tinput_ref, dfirst_ref, dsecond_ref, hidden_ref, dtbranch_ref, small_ref,
):
    step = pl.program_id(0)
    rows = att_ref.shape[0]
    count = meta_ref[1 + step]
    place = lax.broadcasted_iota(jnp.int32, (rows, 1), 0) % rows_dev + meta_ref[0]
    valid = (place < count).astype(F32)
    att = att_ref[...]
    gate = gate_ref[...]
    single = single_ref[...]
    gated = (att * gate).astype(BF16)
    gated_ref[...] = gated
    branch = dot(gated, joined(out_w_ref))
    attn_zero = jax.nn.sigmoid(dot(single, joined(zero_ref, 0)) + zero_bias_ref[0:1].astype(F32))
    middle = tok_ref[...].astype(F32) + valid * attn_zero * branch
    cond, _ = center_rows(single.astype(F32))
    tcond = (cond * gain_ref[1:2].astype(F32)).astype(BF16)
    tcond_ref[...] = tcond
    scale = jax.nn.sigmoid(dot(tcond, joined(ada_ref, 0)) + ada_bias_ref[1:2].astype(F32))
    shift = dot(tcond, joined(ada_ref, 1))
    normed, rstd = center_rows(middle)
    tinput = (scale * normed + shift).astype(BF16)
    tinput_ref[...] = tinput
    first = dot(tinput, joined(tin_ref, 0))
    second = dot(tinput, joined(tin_ref, 1))
    sig = jax.nn.sigmoid(first)
    hidden = (first * sig * second).astype(BF16)
    hidden_ref[...] = hidden
    tbranch = dot(hidden, joined(tout_ref))
    trans_zero = jax.nn.sigmoid(dot(single, joined(zero_ref, 1)) + zero_bias_ref[1:2].astype(F32))
    out_ref[...] = (middle + valid * trans_zero * tbranch).astype(BF16)
    grad_out = cot_ref[...].astype(F32)
    gated_out = grad_out * valid
    dtbranch = (gated_out * trans_zero).astype(BF16)
    dtbranch_ref[...] = dtbranch
    dzb = (gated_out * tbranch * trans_zero * (1.0 - trans_zero)).astype(BF16)
    dzb_ref[...] = dzb
    dhidden = dot_nt(dtbranch, joined(tout_ref))
    dfirst = (dhidden * second * sig * (1.0 + first * (1.0 - sig))).astype(BF16)
    dsecond = (dhidden * first * sig).astype(BF16)
    dfirst_ref[...] = dfirst
    dsecond_ref[...] = dsecond
    dtin = (dot_nt(dfirst, joined(tin_ref, 0)) + dot_nt(dsecond, joined(tin_ref, 1))).astype(BF16)
    dtin_ref[...] = dtin
    dtin_full = dtin.astype(F32)
    dtpre = (dtin_full * normed * scale * (1.0 - scale)).astype(BF16)
    dtpre_ref[...] = dtpre
    grad_norm = dtin_full * scale
    tail = grad_norm - jnp.mean(grad_norm, axis=-1, keepdims=True)
    tail = tail - normed * jnp.mean(grad_norm * normed, axis=-1, keepdims=True)
    dmid = grad_out + tail * rstd
    dmid_ref[...] = dmid
    dtcond = dot_nt(dtpre, joined(ada_ref, 0)) + dot_nt(dtin, joined(ada_ref, 1))
    gated_mid = dmid * valid
    dabranch = (gated_mid * attn_zero).astype(BF16)
    dabranch_ref[...] = dabranch
    dza = (gated_mid * branch * attn_zero * (1.0 - attn_zero)).astype(BF16)
    dza_ref[...] = dza
    dgated = dot_nt(dabranch, joined(out_w_ref))
    datt_ref[...] = (dgated * gate).astype(BF16)
    dglogit_ref[...] = (dgated * att * gate * (1.0 - gate)).astype(BF16)

    @pl.when(step == 0)
    def _():
        small_ref[...] = jnp.zeros_like(small_ref)

    width, narrow = att.shape[1], single.shape[1]
    total = lambda value: jnp.sum(value.astype(F32), axis=0, keepdims=True)
    small_ref[0:1, :] += total(dtpre)
    small_ref[1:2, :] += total(dza)
    small_ref[2:3, :] += total(dzb)
    small_ref[3:4, 0:narrow] += total(dtcond * cond)


def middle_pass(
    meta, att, gate, tok, single, cot, gain, ada, ada_bias, zero, zero_bias, out_w, trans_in,
    trans_out, complexes, samples, rows_dev,
):
    rows, width = tok.shape
    narrow = single.shape[1]
    hidden = trans_out.shape[0] * trans_out.shape[2]
    part = rows // complexes
    wide = pl.BlockSpec((part, width), lambda c, m: (c, 0))
    slim = pl.BlockSpec((part, narrow), lambda c, m: (c, 0))
    long = pl.BlockSpec((part, hidden), lambda c, m: (c, 0))
    once = lambda shape: pl.BlockSpec(
        shape, lambda c, m: (0,) * len(shape), pipeline_mode=pl.Buffered(1)
    )
    shape = lambda cols, kind: jax.ShapeDtypeStruct((rows, cols), kind)
    return pl.pallas_call(
        functools.partial(middle_kernel, samples, rows_dev),
        grid_spec=pltpu.PrefetchScalarGridSpec(
            num_scalar_prefetch=1,
            grid=(complexes,),
            in_specs=[
                wide, wide, wide, slim, wide,
                once(gain.shape),
                pl.BlockSpec(
                    (ada.shape[0], 2) + ada.shape[2:], lambda c, m: (0, 1, 0, 0),
                    pipeline_mode=pl.Buffered(1),
                ),
                once(ada_bias.shape),
                once(zero.shape),
                once(zero_bias.shape),
                once(out_w.shape),
                once(trans_in.shape),
                once(trans_out.shape),
            ],
            out_specs=[
                wide, wide, wide, wide,
                wide, wide, wide, wide, slim, wide, wide,
                wide, long, long, long, wide,
                once((8, width)),
            ],
        ),
        out_shape=[
            shape(width, BF16), shape(width, F32), shape(width, BF16), shape(width, BF16),
            shape(width, BF16), shape(width, BF16), shape(width, BF16), shape(width, BF16),
            shape(narrow, BF16), shape(width, BF16), shape(width, BF16),
            shape(width, BF16), shape(hidden, BF16), shape(hidden, BF16), shape(hidden, BF16),
            shape(width, BF16),
            jax.ShapeDtypeStruct((8, width), F32),
        ],
        compiler_params=params(),
        name="middle_pass",
    )(meta, att, gate, tok, single, cot, gain, ada, ada_bias, zero, zero_bias, out_w, trans_in, trans_out)


def last_kernel(
    dquery_ref, dkeyval_ref, dglogit_ref, tok_ref, single_ref, dmid_ref,
    gain_ref, ada_ref, ada_bias_ref, attn_ref,
    tgrad_ref, dnormed_ref, dapre_ref, cond_ref, small_ref, acc_ref,
):
    which = pl.program_id(0)

    @pl.when(which == 0)
    def _():
        acc_ref[...] = dot_nt(dquery_ref[...], joined(attn_ref))

    @pl.when(which == 1)
    def _():
        acc_ref[...] += dot_nt(dkeyval_ref[0], joined(attn_ref))

    @pl.when(which == 2)
    def _():
        acc_ref[...] += dot_nt(dkeyval_ref[1], joined(attn_ref))

    @pl.when(which == 3)
    def _():
        dnormed = (acc_ref[...] + dot_nt(dglogit_ref[...], joined(attn_ref))).astype(BF16)
        dnormed_ref[...] = dnormed
        cond, _ = center_rows(single_ref[...].astype(F32))
        cond_low = (cond * gain_ref[0:1].astype(F32)).astype(BF16)
        cond_ref[...] = cond_low
        scale = jax.nn.sigmoid(dot(cond_low, joined(ada_ref, 0)) + ada_bias_ref[0:1].astype(F32))
        normed, rstd = center_rows(tok_ref[...].astype(F32))
        full = dnormed.astype(F32)
        dapre = (full * normed * scale * (1.0 - scale)).astype(BF16)
        dapre_ref[...] = dapre
        grad_norm = full * scale
        tail = grad_norm - jnp.mean(grad_norm, axis=-1, keepdims=True)
        tail = tail - normed * jnp.mean(grad_norm * normed, axis=-1, keepdims=True)
        tgrad_ref[...] = dmid_ref[...] + tail * rstd
        dcond = dot_nt(dapre, joined(ada_ref, 0)) + dot_nt(dnormed, joined(ada_ref, 1))
        narrow = cond.shape[1]
        total = lambda value: jnp.sum(value.astype(F32), axis=0, keepdims=True)
        small_ref[...] = jnp.zeros_like(small_ref)
        small_ref[0:1, :] = total(dapre)
        small_ref[1:2, :] = total(dquery_ref[...])
        small_ref[2:3, 0:narrow] = total(dcond * cond)


def last_pass(dquery, dkeyval, dglogit, tok, single, dmid, gain, ada, ada_bias, attn):
    rows, width = tok.shape
    narrow = single.shape[1]
    whole = lambda shape: pl.BlockSpec(shape, lambda w: (0,) * len(shape))
    wide = whole((rows, width))
    shape = lambda cols, kind: jax.ShapeDtypeStruct((rows, cols), kind)
    return pl.pallas_call(
        last_kernel,
        grid=(4,),
        in_specs=[
            wide, whole(dkeyval.shape), wide, wide, whole((rows, narrow)), wide,
            whole(gain.shape),
            pl.BlockSpec((ada.shape[0], 2) + ada.shape[2:], lambda w: (0, 0, 0, 0)),
            whole(ada_bias.shape),
            pl.BlockSpec((attn.shape[0], 1) + attn.shape[2:], lambda w: (0, w, 0, 0)),
        ],
        out_specs=[wide, wide, wide, whole((rows, narrow)), whole((8, width))],
        out_shape=[
            shape(width, F32), shape(width, BF16), shape(width, BF16), shape(narrow, BF16),
            jax.ShapeDtypeStruct((8, width), F32),
        ],
        scratch_shapes=[pltpu.VMEM((rows, width), F32)],
        compiler_params=params(),
        name="last_pass",
    )(dquery, dkeyval, dglogit, tok, single, dmid, gain, ada, ada_bias, attn)


def grad_rows(samples, chips, parts):
    unit = 32 * chips
    return -(-sum(parts) // unit) * unit


def store_grads(out_ref, start, left, grads):
    samples, _, width = out_ref.shape
    turned = left.T
    rows = turned.shape[0] // samples
    for grad in grads:
        value = dot(turned, grad).astype(BF16)
        out_ref[:, start : start + rows] = value.reshape(samples, rows, width)
        start += rows
    return start


def pad_grads(out_ref, start):
    samples, rows, width = out_ref.shape
    if start < rows:
        out_ref[:, start:] = jnp.zeros((samples, rows - start, width), BF16)


def late_grads_kernel(
    tcond, dtpre, dtin, single, dza, dzb, gated, dabranch, tinput, dfirst, dsecond, hidden,
    dtbranch, out_ref,
):
    width = out_ref.shape[2]
    start = store_grads(out_ref, 0, tcond[...], [dtpre[...], dtin[...]])
    start = store_grads(out_ref, start, single[...], [dza[...], dzb[...]])
    start = store_grads(out_ref, start, gated[...], [dabranch[...]])
    halves = [
        ref[:, lane : lane + width] for ref in (dfirst, dsecond) for lane in range(0, dfirst.shape[1], width)
    ]
    start = store_grads(out_ref, start, tinput[...], halves)
    start = store_grads(out_ref, start, hidden[...], [dtbranch[...]])
    pad_grads(out_ref, start)


def early_grads_kernel(
    cond, dapre, dnormed, normed_in, dquery, dkeyval, dglogit, small_mid, small_last, pair_sum,
    out_ref,
):
    samples, rows, width = out_ref.shape
    start = store_grads(out_ref, 0, cond[...], [dapre[...], dnormed[...]])
    start = store_grads(
        out_ref, start, normed_in[...], [dquery[...], dkeyval[0], dkeyval[1], dglogit[...]]
    )
    pairs = jnp.concatenate(
        [pair_sum[...], jnp.zeros((pair_sum.shape[0], width - pair_sum.shape[1]), F32)], axis=1
    )
    small = jnp.concatenate([small_mid[...], small_last[...], pairs], axis=0).astype(BF16)
    for sample in range(samples):
        out_ref[sample, start : start + small.shape[0]] = small
    pad_grads(out_ref, start + small.shape[0])


def grads_call(kernel, samples, rows, width, operands, name):
    return pl.pallas_call(
        kernel,
        out_shape=jax.ShapeDtypeStruct((samples, rows, width), BF16),
        compiler_params=params(),
        name=name,
    )(*operands)


def pack_small(parts):
    flat = jnp.concatenate([part.reshape(-1) for part in parts])
    size = -(-flat.size // 4096) * 4096
    return jnp.pad(flat, (0, size - flat.size)).reshape(1, size // 128, 128)


def unpack_small(block, parts, axes):
    samples = block.shape[0]
    flat = block.reshape(samples, -1)
    whole, start = [], 0
    for part, axis in zip(parts, axes):
        piece = flat[:, start : start + part.size].reshape((samples,) + part.shape)
        start += part.size
        piece = jnp.moveaxis(piece, 0, axis)
        shape = list(part.shape)
        shape[axis] *= samples
        whole.append(piece.reshape(shape))
    return whole


def local(
    tokens, single, pair, token_count, pair_mask, cotangent, cond_gain, ada_weight, ada_bias,
    zero_weight, zero_bias, attn_weight, query_bias, out_weight, pair_gain, pair_weight,
    trans_in, trans_out,
):
    complexes, samples_own, rows_dev, width = tokens.shape
    narrow = single.shape[3]
    heads = pair_weight.shape[1]
    samples, chips = lax.axis_size("sample"), lax.axis_size("row") // 2
    own_start = (lax.axis_index("row") * rows_dev).astype(jnp.int32)
    meta = jnp.concatenate([own_start[None], token_count.astype(jnp.int32)])

    small_parts = (cond_gain, ada_bias, zero_bias, query_bias, pair_gain, pair_weight)
    packed, ada, attn, zero, out_w, tin, tout = gather_weights(
        [pack_small(small_parts), ada_weight, attn_weight, zero_weight, out_weight[None], trans_in,
         trans_out[None]],
        0,
    )
    gain, ada_b, zero_b, query_b, pgain, pweight = unpack_small(packed, small_parts, (1, 1, 1, 0, 0, 0))

    rows = complexes * samples_own * rows_dev
    flat = lambda value: value.reshape(rows, value.shape[-1])
    block = lambda value: value.reshape(complexes, samples_own, rows_dev, width)
    tok, sing, cot = flat(tokens), flat(single), flat(cotangent)

    pair_low, bias = pair_bias(meta, pair, pair_mask, pgain, pweight)
    normed_in, query, keyval, gate = project(tok, sing, gain, ada, ada_b, attn, query_b)
    query = block(query)
    keyval = gather_rows(keyval.reshape(2, complexes, samples_own, rows_dev, width), 1)
    att, prob = attend(query, keyval, bias)
    (
        output, dmid, datt, dglogit, gated, dabranch, dza, dzb, tcond, dtpre, dtin, tinput,
        dfirst, dsecond, hidden, dtbranch, small_mid,
    ) = middle_pass(
        meta, flat(att), gate, tok, sing, cot, gain, ada, ada_b, zero, zero_b, out_w, tin, tout,
        complexes, samples_own, rows_dev,
    )
    dquery, dkeyval, dbias = attend_back(prob, block(datt), query, keyval)
    dkeyval = reduce_rows(dkeyval, 2).reshape(2, rows, width)
    pair_sum = pair_grad(dbias, pair_low)
    dquery = flat(dquery)
    tgrad, dnormed, dapre, cond, small_last = last_pass(
        dquery, dkeyval, dglogit, tok, sing, dmid, gain, ada, ada_b, attn
    )
    slim, wide = narrow // samples, width // samples
    late_parts = [slim] * 4 + [wide] * 5 + [tout.shape[2]]
    early_parts = [slim] * 2 + [wide] * 4 + [16 + heads]
    late = grads_call(
        late_grads_kernel, samples, grad_rows(samples, chips, late_parts), width,
        (tcond, dtpre, dtin, sing, dza, dzb, gated, dabranch, tinput, dfirst, dsecond, hidden, dtbranch),
        "late_grads",
    )
    early = grads_call(
        early_grads_kernel, samples, grad_rows(samples, chips, early_parts), width,
        (cond, dapre, dnormed, normed_in, dquery, dkeyval, dglogit, small_mid, small_last, pair_sum),
        "early_grads",
    )
    late = reduce_grads(late, 3)
    early = reduce_grads(early, 4)

    def pieces(total, parts):
        out, start = [], 0
        for size in parts:
            out.append(total[start : start + size].astype(F32))
            start += size
        return out

    late = pieces(late, late_parts)
    early = pieces(early, early_parts)
    small = early[6]
    small_mid, small_last, pair_sum = small[:8], small[8:16], small[16:, : pair_weight.shape[0] * samples]
    spot = lax.axis_index("sample")

    def own_part(value, axis):
        size = value.shape[axis] // samples
        return lax.dynamic_slice_in_dim(value, spot * size, size, axis)

    gain_grad = own_part(jnp.stack([small_last[2, :narrow], small_mid[3, :narrow]]), 1)
    ada_bias_grad = own_part(jnp.stack([small_last[0], small_mid[0]]), 1)
    zero_bias_grad = own_part(small_mid[1:3], 1)
    query_bias_grad = own_part(small_last[1], 0)
    pair_gain_grad = own_part(
        jnp.sum(pweight.astype(F32).T * pair_sum, axis=0) / pgain.astype(F32), 0
    )
    pair_weight_grad = own_part(pair_sum.T, 0)
    return (
        output.reshape(tokens.shape),
        tgrad.reshape(tokens.shape),
        gain_grad,
        jnp.stack([early[0], early[1], late[0], late[1]]),
        ada_bias_grad,
        jnp.stack([late[2], late[3]]),
        zero_bias_grad,
        jnp.stack(early[2:6]),
        query_bias_grad,
        late[4],
        pair_gain_grad,
        pair_weight_grad,
        jnp.stack([jnp.concatenate(late[5:7], axis=1), jnp.concatenate(late[7:9], axis=1)]),
        late[9],
    )


def solution(mesh):
    rowwise = P(None, "sample", "row", None)
    return jax.shard_map(
        local,
        mesh=mesh,
        in_specs=(
            rowwise,
            rowwise,
            P(None, "row", None, None),
            P(),
            P(None, "row", None),
            rowwise,
            P(None, "sample"),
            P(None, "sample", None),
            P(None, "sample"),
            P(None, "sample", None),
            P(None, "sample"),
            P(None, "sample", None),
            P("sample"),
            P("sample", None),
            P("sample"),
            P("sample", None),
            P(None, "sample", None),
            P("sample", None),
        ),
        out_specs=(
            rowwise,
            rowwise,
            P(None, "sample"),
            P(None, "sample", None),
            P(None, "sample"),
            P(None, "sample", None),
            P(None, "sample"),
            P(None, "sample", None),
            P("sample"),
            P("sample", None),
            P("sample"),
            P("sample", None),
            P(None, "sample", None),
            P("sample", None),
        ),
        check_vma=False,
    )
```

```python
import functools

import jax
import jax.numpy as jnp
from jax import lax
from jax.experimental import pallas as pl
from jax.experimental.pallas import tpu as pltpu
from jax.sharding import PartitionSpec as P

EPSILON = 1e-05
MASKED = -1000000000.0
F32 = jnp.float32
BF16 = jnp.bfloat16
VMEM_LIMIT = 60 << 20


def center_rows(value):
    center = value - jnp.mean(value, axis=-1, keepdims=True)
    rstd = lax.rsqrt(jnp.mean(center * center, axis=-1, keepdims=True) + EPSILON)
    return center * rstd, rstd


def dot(left, right):
    return lax.dot_general(left, right, (((1,), (0,)), ((), ())), preferred_element_type=F32)


def dot_nt(left, right):
    return lax.dot_general(left, right, (((1,), (1,)), ((), ())), preferred_element_type=F32)


def dot_tn(left, right):
    return lax.dot_general(left, right, (((0,), (0,)), ((), ())), preferred_element_type=F32)


def params(**extra):
    return pltpu.CompilerParams(vmem_limit_bytes=VMEM_LIMIT, **extra)


MESH = pl.DeviceIdType.MESH
ANY = pl.BlockSpec(memory_space=pl.ANY)


class Place:
    def __init__(self, chips, samples):
        self.row = lax.axis_index("row")
        self.chip = self.row // 2
        self.core = self.row % 2
        self.sample = lax.axis_index("sample")
        self.chips, self.samples = chips, samples

    def twin(self):
        return (self.row + 1 - 2 * self.core, self.sample)

    def peer(self, k):
        return (self.row, jnp.bitwise_xor(self.sample, k))

    def up(self):
        return (self.row + 2, self.sample)

    def down(self):
        return (self.row - 2, self.sample)

    def along(self, k):
        return (jnp.bitwise_xor(self.row, 2 * k), self.sample)

    def barrier(self, plane, line, whole_line=False):
        bar = pltpu.get_barrier_semaphore()

        def greet(device):
            pl.semaphore_signal(bar, inc=1, device_id=device, device_id_type=MESH)

        greet(self.twin())
        if plane:
            for k in range(1, self.samples):
                greet(self.peer(k))
        if line and not whole_line:

            @pl.when(self.chip > 0)
            def _():
                greet(self.down())

            @pl.when(self.chip < self.chips - 1)
            def _():
                greet(self.up())

        count = 1 + (self.samples - 1 if plane else 0)
        if whole_line:
            for k in range(1, self.chips):
                greet(self.along(k))
            count = count + self.chips - 1
        elif line:
            count = count + jnp.minimum(self.chip, 1) + jnp.minimum(self.chips - 1 - self.chip, 1)
        pl.semaphore_wait(bar, count)


def send(source, target, send_sem, recv_sem, device):
    return pltpu.make_async_remote_copy(
        source, target, send_sem, recv_sem, device_id=device, device_id_type=MESH
    )


def half_of(ref, core):
    if ref.shape[0] > 1:
        size = ref.shape[0] // 2
        return ref.at[pl.ds(core * size, size)]
    size = ref.shape[1] // 2
    return ref.at[:, pl.ds(pl.multiple_of(core * size, 16), size)]


class PlaneGather:
    @staticmethod
    def sems(arrays, samples):
        dma = pltpu.SemaphoreType.DMA
        return [dma((arrays, samples))] * 4 + [dma((arrays, 2))] * 2

    def __init__(self, place, shards, fulls, sems):
        self.place, self.shards, self.fulls = place, shards, fulls
        self.out, self.come, self.swap_out, self.swap_come, self.hop_out, self.hop_come = sems
        self.relayed = place.samples == 4
        self.direct = [1, 2] if self.relayed else list(range(1, place.samples))

    def owner(self, k):
        return jnp.bitwise_xor(self.place.sample, k)

    def half(self, i, k):
        return half_of(self.fulls[i].at[self.owner(k)], self.place.core)

    def copy(self, i, k):
        slot = self.half(i, 0)
        return send(
            half_of(self.shards[i], self.place.core), slot, self.out.at[i, k], self.come.at[i, k],
            self.place.peer(k),
        )

    def hop(self, i, k):
        slot = self.half(i, k)
        size = slot.shape[1] // 2
        piece = slot.at[:, pl.ds((k - 1) * size, size)]
        return send(piece, piece, self.hop_out.at[i, k - 1], self.hop_come.at[i, k - 1], self.place.peer(3 - k))

    def swap(self, i, k):
        slot = self.half(i, k)
        return send(slot, slot, self.swap_out.at[i, k], self.swap_come.at[i, k], self.place.twin())

    def keep(self, i):
        return send(
            self.shards[i], self.fulls[i].at[self.place.sample], self.swap_out.at[i, 0],
            self.swap_come.at[i, 0], self.place.twin(),
        )

    def start(self, i):
        for k in self.direct:
            self.copy(i, k).start()
        self.keep(i).start()

    def relay(self, i):
        for k in self.direct:
            self.copy(i, k).wait_recv()
            if self.relayed:
                self.hop(i, k).start()
            self.swap(i, k).start()

    def settle(self, i):
        if self.relayed:
            for k in self.direct:
                self.hop(i, k).wait_recv()
            self.swap(i, 3).start()

    def arrive(self, i):
        self.keep(i).wait_recv()
        for k in range(1, self.place.samples):
            self.swap(i, k).wait_recv()

    def finish(self, arrived=()):
        for i in range(len(self.shards)):
            if i not in arrived:
                self.arrive(i)
            self.keep(i).wait_send()
            for k in self.direct:
                self.copy(i, k).wait_send()
                if self.relayed:
                    self.hop(i, k).wait_send()
            for k in range(1, self.place.samples):
                self.swap(i, k).wait_send()


class LineSpread:
    @staticmethod
    def sems(lines, chips):
        dma = pltpu.SemaphoreType.DMA
        return [dma((lines, chips))] * 6

    def __init__(self, place, line, slot, sems):
        self.place, self.line, self.slot = place, line, slot
        self.up_out, self.up_come, self.down_out, self.down_come, self.swap_out, self.swap_come = sems

    def step(self, upward, t):
        place, last = self.place, self.place.chips - 1
        z = place.chip
        if upward:
            out_chip, has_out = z - t + 1, (z >= t - 1) & (z < last)
            in_chip, has_in = z - t, z >= t
            sems, device = (self.up_out, self.up_come), place.up()
        else:
            out_chip, has_out = z + t - 1, (z + t - 1 <= last) & (z > 0)
            in_chip, has_in = z + t, z + t <= last
            sems, device = (self.down_out, self.down_come), place.down()
        make = lambda chip: send(
            self.slot(chip), self.slot(chip),
            sems[0].at[self.line, t], sems[1].at[self.line, t], device,
        )
        return (has_out, lambda: make(out_chip)), (has_in, in_chip, lambda: make(in_chip))

    def hand_over(self, chip):
        slot = self.slot(chip)
        return send(
            slot, slot, self.swap_out.at[self.line, chip], self.swap_come.at[self.line, chip],
            self.place.twin(),
        )

    def depart(self, t):
        for upward in (True, False):
            (has_out, copy), _ = self.step(upward, t)

            @pl.when(has_out)
            def _():
                copy().start()

    def advance(self, t):
        for upward in (True, False):
            _, (has_in, chip, copy) = self.step(upward, t)

            @pl.when(has_in)
            def _():
                copy().wait_recv()

        if t + 1 < self.place.chips:
            self.depart(t + 1)
        for upward in (True, False):
            _, (has_in, chip, copy) = self.step(upward, t)

            @pl.when(has_in)
            def _():
                self.hand_over(chip).start()

    def finish(self):
        for t in range(1, self.place.chips):
            for upward in (True, False):
                (has_out, copy), (has_in, chip, _) = self.step(upward, t)

                @pl.when(has_out)
                def _():
                    copy().wait_send()

                @pl.when(has_in)
                def _():
                    self.hand_over(chip).wait()


class LineReduce:
    @staticmethod
    def sems(lines, chips):
        dma = pltpu.SemaphoreType.DMA
        return [dma((lines, chips))] * 4

    def __init__(self, place, line, slot, up_buf, down_buf, sems):
        self.place, self.line, self.slot = place, line, slot
        self.bufs = (up_buf, down_buf)
        self.up_out, self.up_come, self.down_out, self.down_come = sems

    def step(self, upward, t):
        place, last = self.place, self.place.chips - 1
        z, distance = place.chip, place.chips - t
        buf = self.bufs[0 if upward else 1]
        if upward:
            block, has_out, has_before = z + distance, z + distance <= last, z > 0
            has_in = (z > 0) & (z - 1 + distance <= last)
            sems, device = (self.up_out, self.up_come), place.up()
        else:
            block, has_out, has_before = z - distance, z - distance >= 0, z < last
            has_in = (z < last) & (z + 1 - distance >= 0)
            sems, device = (self.down_out, self.down_come), place.down()
        copy = lambda chip: send(
            self.slot(chip), buf.at[self.line, t - 1],
            sems[0].at[self.line, t], sems[1].at[self.line, t], device,
        )
        return block, has_out, has_before, has_in, copy, buf

    def advance(self, t):
        for upward in (True, False):
            block, has_out, has_before, _, copy, buf = self.step(upward, t)
            before = self.step(upward, t - 1)[4] if t > 1 else None

            @pl.when(has_out)
            def _():
                if t > 1:

                    @pl.when(has_before)
                    def _():
                        before(block).wait_recv()
                        slot = self.slot(block)
                        slot[...] = (
                            slot[...].astype(F32) + buf[self.line, t - 2].astype(F32)
                        ).astype(slot.dtype)

                copy(block).start()

    def finish(self):
        last_step = self.place.chips - 1
        slot = self.slot(self.place.chip)
        for upward in (True, False):
            _, _, _, has_in, copy, buf = self.step(upward, last_step)

            @pl.when(has_in)
            def _():
                copy(self.place.chip).wait_recv()
                slot[...] = (
                    slot[...].astype(F32) + buf[self.line, last_step - 1].astype(F32)
                ).astype(slot.dtype)

        for t in range(1, self.place.chips):
            for upward in (True, False):
                block, has_out, _, _, copy, _ = self.step(upward, t)

                @pl.when(has_out)
                def _():
                    copy(block).wait_send()


class RowGather:
    @staticmethod
    def sems(lines, chips):
        return [pltpu.SemaphoreType.DMA((lines,))] + LineSpread.sems(lines, chips)

    def __init__(self, place, part, full, line, sems):
        self.place, self.part, self.full, self.index = place, part, full, line
        self.spot = (line // part.shape[1], line % part.shape[1])
        self.keep_sem = sems[0]
        self.rows = part.shape[2]
        self.line = LineSpread(place, line, self.slot, sems[1:])

    def slot(self, chip):
        start = (2 * chip + self.place.core) * self.rows
        return self.full.at[self.spot + (pl.ds(pl.multiple_of(start, 16), self.rows),)]

    def keep(self):
        return pltpu.make_async_copy(
            self.part.at[self.spot], self.slot(self.place.chip), self.keep_sem.at[self.index]
        )

    def start(self):
        self.keep().start()

    def begin(self):
        self.keep().wait()
        self.line.depart(1)
        self.line.hand_over(self.place.chip).start()

    def finish(self):
        self.line.finish()
        self.line.hand_over(self.place.chip).wait()


class RowReduce:
    @staticmethod
    def scratch(complexes, samples_own, length, rows, width, chips):
        dma = pltpu.SemaphoreType.DMA
        hop = pltpu.VMEM((complexes, chips - 1, samples_own, rows, width), BF16)
        return [
            pltpu.VMEM((complexes, samples_own, chips, rows, width), BF16), hop, hop,
        ] + [dma((complexes,))] * 3 + LineReduce.sems(complexes, chips)

    def __init__(self, place, part, own, which, scratch):
        self.place, self.part, self.own, self.which = place, part, own, which
        self.sums, up_buf, down_buf = scratch[:3]
        self.swap_out, self.swap_come, self.keep_sem = scratch[3:6]
        self.line = LineReduce(place, which, self.slot, up_buf, down_buf, scratch[6:])

    def slot(self, chip):
        return self.sums.at[self.which, :, chip]

    def first_swap(self):
        return send(
            self.part.at[self.which, :, :, 1 - self.place.core], self.sums.at[self.which],
            self.swap_out.at[self.which], self.swap_come.at[self.which], self.place.twin(),
        )

    def begin(self):
        self.first_swap().wait_recv()
        for sample in range(self.part.shape[1]):
            for chip in range(self.place.chips):
                mine = self.part[self.which, sample, chip, self.place.core].astype(F32)
                self.sums[self.which, sample, chip] = (
                    mine + self.sums[self.which, sample, chip].astype(F32)
                ).astype(BF16)

    def keep(self):
        return pltpu.make_async_copy(
            self.slot(self.place.chip), self.own.at[self.which], self.keep_sem.at[self.which]
        )

    def finish(self):
        self.line.finish()
        self.keep().start()

    def drain(self):
        self.first_swap().wait_send()
        self.keep().wait()


def reduce_rows_kernel(chips, samples, part_ref, own_ref, *scratch):
    place = Place(chips, samples)
    moves = [
        RowReduce(place, part_ref, own_ref, which, scratch) for which in range(part_ref.shape[0])
    ]
    place.barrier(False, True)
    for move in moves:
        move.first_swap().start()
    for move in moves:
        move.begin()
        move.line.advance(1)
    for t in range(2, chips):
        for move in moves:
            move.line.advance(t)
    for move in moves:
        move.finish()
    for move in moves:
        move.drain()


def reduce_rows(part, collective_id):
    samples, chips = lax.axis_size("sample"), lax.axis_size("row") // 2
    complexes, own, length, width = part.shape
    rows = length // (2 * chips)
    return pl.pallas_call(
        functools.partial(reduce_rows_kernel, chips, samples),
        in_specs=[pl.BlockSpec(memory_space=pltpu.VMEM)],
        out_specs=ANY,
        out_shape=jax.ShapeDtypeStruct((complexes, own, rows, width), part.dtype),
        scratch_shapes=RowReduce.scratch(complexes, own, length, rows, width, chips),
        compiler_params=params(collective_id=collective_id, has_side_effects=True),
        name="reduce_rows",
    )(part.reshape(complexes, own, chips, 2, rows, width))


class PlaneReduce:
    @staticmethod
    def scratch(samples, rows, width):
        dma = pltpu.SemaphoreType.DMA
        half = rows // 2
        return [
            pltpu.VMEM((samples, half, width), BF16),
            pltpu.VMEM((2 * samples - 2, half // 2, width), BF16),
            pltpu.VMEM((half, width), BF16),
        ] + [dma((samples,))] * 3 + [dma((2 * samples,))] * 2

    def __init__(self, place, grads, plane, scratch):
        self.place, self.grads, self.plane = place, grads, plane
        self.sums, self.come_buf, self.mine = scratch[:3]
        self.swap_out, self.swap_come, self.load_sem, self.out, self.come = scratch[3:]
        self.half = grads.shape[1] // 2
        self.relayed = place.samples == 4
        self.order = [3, 1, 2, 0] if self.relayed else list(range(1, place.samples)) + [0]

    def shard(self, k):
        return jnp.bitwise_xor(self.place.sample, k)

    def half_rows(self, core):
        return pl.ds(pl.multiple_of(core * self.half, 16), self.half)

    def part(self, k, which):
        return self.sums.at[self.shard(k), pl.ds(which * (self.half // 2), self.half // 2)]

    def swap(self, k):
        return send(
            self.grads.at[self.shard(k), self.half_rows(1 - self.place.core)],
            self.sums.at[self.shard(k)],
            self.swap_out.at[k], self.swap_come.at[k], self.place.twin(),
        )

    def load(self, k):
        return pltpu.make_async_copy(
            self.grads.at[self.shard(k), self.half_rows(self.place.core)],
            self.mine, self.load_sem.at[k],
        )

    def copy(self, k, which, peer, slot):
        return send(
            self.part(k, which), self.come_buf.at[slot], self.out.at[slot], self.come.at[slot],
            self.place.peer(peer),
        )

    def copies(self, k):
        if not self.relayed:
            return [self.copy(k, which, k, 2 * (k - 1) + which) for which in range(2)] if k else []
        return {
            3: lambda: [self.copy(3, 0, 1, 1), self.copy(3, 1, 2, 4)],
            1: lambda: [self.copy(1, 0, 1, 0)],
            2: lambda: [self.copy(2, 1, 2, 3)],
            0: lambda: [],
        }[k]()

    def onward(self):
        return [(self.copy(2, 0, 2, 2), 1, (2, 0)), (self.copy(1, 1, 1, 5), 4, (1, 1))]

    def arrived(self, slot):
        self.copy(0, 0, 1, slot).wait_recv()
        return self.come_buf[slot].astype(F32)

    def start(self):
        for k in self.order:
            self.swap(k).start()
        self.load(self.order[0]).start()

    def depart(self, k):
        place = self.order.index(k)
        self.load(k).wait()
        self.swap(k).wait_recv()
        slot = self.sums.at[self.shard(k)]
        slot[...] = (self.mine[...].astype(F32) + slot[...].astype(F32)).astype(BF16)
        for copy in self.copies(k):
            copy.start()
        if place + 1 < len(self.order):
            self.load(self.order[place + 1]).start()

    def hop(self):
        if self.relayed:
            for copy, slot, piece in self.onward():
                ref = self.part(*piece)
                ref[...] = (ref[...].astype(F32) + self.arrived(slot)).astype(BF16)
                copy.start()

    def finish(self):
        size = self.half // 2
        for which in range(2):
            value = self.part(0, which)[...].astype(F32)
            if self.relayed:
                slots = [3 * which, 3 * which + 2]
            else:
                slots = [2 * (k - 1) + which for k in range(1, self.place.samples)]
            for slot in slots:
                value = value + self.arrived(slot)
            self.plane[which * size : (which + 1) * size] = value.astype(BF16)

    def drain(self):
        for k in self.order:
            self.swap(k).wait_send()
            for copy in self.copies(k):
                copy.wait_send()
        if self.relayed:
            for copy, _, _ in self.onward():
                copy.wait_send()


class LineTotal:
    @staticmethod
    def scratch(size, width, chips):
        hop = pltpu.VMEM((1, chips - 1, size // chips, width), BF16)
        return [hop, hop] + LineReduce.sems(1, chips) + LineSpread.sems(1, chips)

    def __init__(self, place, plane, total, start, size, scratch):
        self.place, self.plane, self.total, self.start = place, plane, total, start
        self.half = total.shape[0] // 2
        self.size = size // place.chips
        self.reduce = LineReduce(place, 0, self.block, scratch[0], scratch[1], scratch[2:6])
        self.spread = LineSpread(place, 0, self.slot, scratch[6:])

    def block(self, chip):
        return self.plane.at[pl.ds(pl.multiple_of(self.start + chip * self.size, 16), self.size)]

    def slot(self, chip):
        start = self.place.core * self.half + self.start + chip * self.size
        return self.total.at[pl.ds(pl.multiple_of(start, 16), self.size)]

    @property
    def steps(self):
        return 2 * self.place.chips - 1

    def advance(self, t):
        if t < self.place.chips:
            self.reduce.advance(t)
            return
        t -= self.place.chips - 1
        if t == 1:
            self.reduce.finish()
            own = self.slot(self.place.chip)
            own[...] = self.block(self.place.chip)[...]
            self.spread.depart(1)
            self.spread.hand_over(self.place.chip).start()
        else:
            self.spread.advance(t - 1)

    def finish(self):
        self.spread.advance(self.place.chips - 1)
        self.spread.finish()
        self.spread.hand_over(self.place.chip).wait()


class DirectTotal:
    steps = 4

    @staticmethod
    def scratch(size, width, chips):
        dma = pltpu.SemaphoreType.DMA
        return [pltpu.VMEM((chips - 1, size // chips, width), BF16)] + [dma((chips,))] * 6

    def __init__(self, place, plane, total, start, size, scratch):
        self.place, self.plane, self.total, self.start = place, plane, total, start
        self.half = total.shape[0] // 2
        self.size = size // place.chips
        self.buf = scratch[0]
        self.out, self.come, self.back_out, self.back_come, self.swap_out, self.swap_come = scratch[1:]

    def chip(self, k):
        return jnp.bitwise_xor(self.place.chip, k)

    def block(self, chip):
        return self.plane.at[pl.ds(pl.multiple_of(self.start + chip * self.size, 16), self.size)]

    def slot(self, chip):
        start = self.place.core * self.half + self.start + chip * self.size
        return self.total.at[pl.ds(pl.multiple_of(start, 16), self.size)]

    def there(self, k):
        return send(
            self.block(self.chip(k)), self.buf.at[k - 1], self.out.at[k], self.come.at[k],
            self.place.along(k),
        )

    def back(self, k):
        own = self.slot(self.place.chip)
        return send(own, own, self.back_out.at[k], self.back_come.at[k], self.place.along(k))

    def swap(self, k):
        slot = self.slot(self.chip(k))
        return send(slot, slot, self.swap_out.at[k], self.swap_come.at[k], self.place.twin())

    def advance(self, t):
        peers = range(1, self.place.chips)
        if t == 1:
            for k in peers:
                self.there(k).start()
        elif t == 2:
            value = self.block(self.place.chip)[...].astype(F32)
            for k in peers:
                self.there(k).wait_recv()
                value = value + self.buf[k - 1].astype(F32)
            own = self.slot(self.place.chip)
            own[...] = value.astype(BF16)
            for k in peers:
                self.back(k).start()
            self.swap(0).start()
        else:
            for k in peers:
                self.back(k).wait_recv()
                self.swap(k).start()

    def finish(self):
        for k in range(1, self.place.chips):
            self.there(k).wait_send()
            self.back(k).wait_send()
        for k in range(self.place.chips):
            self.swap(k).wait()


def reduce_grads_kernel(chips, samples, grads_ref, total_ref, *scratch):
    place = Place(chips, samples)
    count = len(PlaneReduce.scratch(samples, 64, 128))
    plane_buf = scratch[0]
    plane = PlaneReduce(place, grads_ref, plane_buf, scratch[1 : 1 + count])
    line = LineTotal(place, plane_buf, total_ref, 0, plane_buf.shape[0], scratch[1 + count :])
    place.barrier(True, True)
    plane.start()
    for k in plane.order:
        plane.depart(k)
    plane.hop()
    plane.finish()
    for t in range(1, 2 * chips - 1):
        line.advance(t)
    line.finish()
    plane.drain()


def reduce_grads(grads, collective_id):
    chips = lax.axis_size("row") // 2
    samples, rows, width = grads.shape
    return pl.pallas_call(
        functools.partial(reduce_grads_kernel, chips, samples),
        in_specs=[pl.BlockSpec(memory_space=pltpu.VMEM)],
        out_specs=pl.BlockSpec(memory_space=pltpu.VMEM),
        out_shape=jax.ShapeDtypeStruct((rows, width), BF16),
        scratch_shapes=[pltpu.VMEM((rows // 2, width), BF16)]
        + PlaneReduce.scratch(samples, rows, width)
        + LineTotal.scratch(rows // 2, width, chips),
        compiler_params=params(collective_id=collective_id, has_side_effects=True),
        name="reduce_grads",
    )(grads)


def joined(ref, which=0):
    samples, _, rows, cols = ref.shape
    return ref[:, which].reshape(samples * rows, cols)


def head_windows(heads, head_dim):
    windows, head = [], 0
    while head < heads:
        start = head * head_dim // 128 * 128
        start = min(start, heads * head_dim - 256)
        inside = []
        while head < heads and (head + 1) * head_dim <= start + 256:
            inside.append(head)
            head += 1
        windows.append((start, inside))
    return windows


def head_mask(start, head, head_dim):
    lane = lax.broadcasted_iota(jnp.int32, (1, 256), 1) + start
    return (lane >= head * head_dim) & (lane < (head + 1) * head_dim)


def stack_heads(rows, start, inside, head_dim):
    zero = jnp.zeros_like(rows)
    return jnp.concatenate(
        [jnp.where(head_mask(start, head, head_dim), rows, zero) for head in inside], axis=0
    )


def unstack_heads(stacked, start, inside, head_dim):
    rows = stacked.shape[0] // len(inside)
    total = None
    for place, head in enumerate(inside):
        piece = jnp.where(
            head_mask(start, head, head_dim), stacked[place * rows : (place + 1) * rows], 0.0
        )
        total = piece if total is None else total + piece
    return total


def join_windows(parts, width):
    tiles = [None] * (width // 128)
    for start, value in parts:
        for half in range(2):
            place = start // 128 + half
            piece = value[:, half * 128 : (half + 1) * 128]
            tiles[place] = piece if tiles[place] is None else tiles[place] + piece
    return jnp.concatenate(tiles, axis=1)


PACK_ROWS, PACK_LANES = 64, 256


def pack_small(cond_gain, ada_bias, zero_bias, query_bias, pair_gain, pair_weight):
    line = lambda ref: jnp.pad(
        ref[...].astype(F32), ((0, 0), (0, PACK_LANES - ref.shape[1]))
    )
    rows = [line(ref) for ref in (cond_gain, ada_bias, zero_bias, query_bias, pair_gain, pair_weight)]
    left = PACK_ROWS - 8 - pair_weight.shape[0]
    return jnp.concatenate(rows + [jnp.zeros((left, PACK_LANES), F32)], axis=0).astype(BF16)


def unpack_small(packed, narrow, width, pair_width, heads):
    samples = packed.shape[0]
    thin = pair_width // samples

    def spread(size):
        count = size // samples
        total = None
        for sample in range(samples):
            lane = lax.broadcasted_iota(jnp.int32, (PACK_LANES, size), 0)
            spot = lax.broadcasted_iota(jnp.int32, (PACK_LANES, size), 1)
            move = ((spot == lane + count * sample) & (lane < count)).astype(BF16)
            piece = dot(packed[sample, 0:16], move)
            total = piece if total is None else total + piece
        return total

    gains = jnp.pad(spread(narrow)[0:2], ((0, 0), (0, width - narrow)))
    vec = jnp.concatenate([gains, spread(width)[2:7], jnp.zeros((1, width), F32)], axis=0)
    weight = [packed[sample].astype(F32)[8 : 8 + thin, 0:128] for sample in range(samples)]
    return vec, spread(pair_width)[7:8], jnp.concatenate(weight, axis=0).T[0:heads]


def pair_block(count_ref, first_row, complex_id, start, pair_ref, mask_ref, gain, weight, low_ref, bias_ref):
    rows, length = pair_ref.shape[1], pair_ref.shape[2]
    count = count_ref[complex_id]
    lines = []
    for row in range(rows):
        normed, _ = center_rows(pair_ref[0, row].astype(F32))
        low = (normed * gain).astype(BF16)
        low_ref[0, row] = low
        lines.append(dot_nt(weight, low))
    bias = jnp.stack(lines, axis=1)
    own = first_row + start + lax.broadcasted_iota(jnp.int32, (rows, length), 0)
    key = lax.broadcasted_iota(jnp.int32, (rows, length), 1)
    allowed = (key < count) & ((mask_ref[0] == 1) | (own == key) | (own >= count))
    bias_ref[0] = jnp.where(allowed[None], bias, MASKED)


PAIR_ROWS = 8


def enter_kernel(arrays, chips, samples, count_ref, tok_ref, single_ref, pair_ref, mask_ref, *refs):
    small, refs = refs[:6], refs[6:]
    shards, refs = refs[: arrays - 1], refs[arrays - 1 :]
    fulls, refs = refs[:arrays], refs[arrays:]
    full_ref, normed_ref, vec_ref, pairw_ref, low_ref, bias_ref = refs[:6]
    own_pack, packed, ada_buf, load_sem = refs[6:10]
    sems = refs[10:]
    place = Place(chips, samples)
    own_pack[0] = pack_small(*small)
    shards = (own_pack,) + shards
    count = len(PlaneGather.sems(arrays, samples))
    move = PlaneGather(place, shards, fulls, sems[:count])
    complexes, own = normed_ref.shape[:2]
    lines = [
        RowGather(place, normed_ref, full_ref, line, sems[count:]) for line in range(complexes * own)
    ]
    rows_dev, width = normed_ref.shape[2:]
    narrow = single_ref.shape[1]
    place.barrier(True, True)
    move.start(0)
    move.start(1)
    move.relay(0)
    move.settle(0)
    move.relay(1)
    for i in range(2, arrays):
        move.start(i)
    move.arrive(0)
    load = pltpu.make_async_copy(fulls[0].at[:, 0], packed, load_sem.at[0])
    load.start()
    load.wait()
    heads = bias_ref.shape[1]
    vec, pair_gain, pair_weight = unpack_small(packed, narrow, width, pair_ref.shape[3], heads)
    vec_ref[...] = vec
    pairw_ref[0:1] = pair_gain
    pairw_ref[8 : 8 + heads] = pair_weight
    per = rows_dev // PAIR_ROWS

    def pair_part(first, last):
        def body(pair_block_ref, mask_block_ref, low_block_ref, bias_block_ref):
            step = first + pl.program_id(0)
            pair_block(
                count_ref, place.row * rows_dev, step // per, step % per * PAIR_ROWS, pair_block_ref, mask_block_ref,
                pairw_ref[0:1], pairw_ref[8 : 8 + heads].astype(BF16), low_block_ref, bias_block_ref,
            )

        length = pair_ref.shape[2]
        spot = lambda b: ((first + b) // per, (first + b) % per)
        block = pl.BlockSpec((1, PAIR_ROWS, length, pair_ref.shape[3]), lambda b: spot(b) + (0, 0))
        pltpu.emit_pipeline(
            body,
            grid=(last - first,),
            in_specs=[block, pl.BlockSpec((1, PAIR_ROWS, length), lambda b: spot(b) + (0,))],
            out_specs=[
                block,
                pl.BlockSpec((1, heads, PAIR_ROWS, length), lambda b: (spot(b)[0], 0, spot(b)[1], 0)),
            ],
        )(pair_ref, mask_ref, low_ref, bias_ref)

    total = complexes * per
    pair_part(0, total // 4)
    move.settle(1)
    move.arrive(1)
    load = pltpu.make_async_copy(fulls[1].at[:, 0:2], ada_buf, load_sem.at[0])
    load.start()
    load.wait()
    cond, _ = center_rows(single_ref[...].astype(F32))
    cond = (cond * vec_ref[0:1, 0:narrow]).astype(BF16)
    pre = dot(cond, joined(ada_buf, 0)) + vec_ref[2:3]
    shift = dot(cond, joined(ada_buf, 1))
    normed, _ = center_rows(tok_ref[...].astype(F32))
    normed_in = (jax.nn.sigmoid(pre) * normed + shift).astype(BF16)
    normed_ref[...] = normed_in.reshape(normed_ref.shape)
    for line in lines:
        line.start()
    for line in lines:
        line.begin()
    between = {
        0: lambda: (pair_part(total // 4, total // 2), move.relay(2), move.relay(3), move.relay(4)),
        1: lambda: (pair_part(total // 2, total * 3 // 4), move.settle(2), move.relay(5)),
        2: lambda: (
            pair_part(total * 3 // 4, total), move.relay(6), move.settle(3), move.settle(4),
            move.settle(5),
        ),
    }
    for t in range(chips):
        if t:
            for line in lines:
                line.line.advance(t)
        if t in between:
            between[t]()
    move.settle(6)
    for line in lines:
        line.finish()
    move.finish(arrived=(0, 1))


def enter(token_count, tok, single, pair, pair_mask, small, shards, complexes, heads):
    samples, chips = lax.axis_size("sample"), lax.axis_size("row") // 2
    pack = jax.ShapeDtypeStruct((1, PACK_ROWS, PACK_LANES), BF16)
    parts = [pack] + list(shards)
    arrays = len(parts)
    width, narrow = tok.shape[1], single.shape[1]
    _, rows, length, pair_width = pair.shape
    own = tok.shape[0] // complexes // rows
    vmem = pl.BlockSpec(memory_space=pltpu.VMEM)
    fulls = [jax.ShapeDtypeStruct((samples,) + s.shape, s.dtype) for s in parts]
    out = pl.pallas_call(
        functools.partial(enter_kernel, arrays, chips, samples),
        in_specs=[pl.BlockSpec(memory_space=pltpu.SMEM), vmem, vmem, ANY, ANY]
        + [vmem] * 6
        + [ANY] * (arrays - 1),
        out_specs=[ANY] * arrays + [ANY, vmem, vmem, vmem, ANY, ANY],
        out_shape=fulls
        + [
            jax.ShapeDtypeStruct((complexes, own, length, width), BF16),
            jax.ShapeDtypeStruct((complexes, own, rows, width), BF16),
            jax.ShapeDtypeStruct((8, width), F32),
            jax.ShapeDtypeStruct((8 + heads, pair_width), F32),
            jax.ShapeDtypeStruct(pair.shape, BF16),
            jax.ShapeDtypeStruct((complexes, heads, rows, length), F32),
        ],
        scratch_shapes=[
            pltpu.VMEM(pack.shape, BF16),
            pltpu.VMEM((samples,) + pack.shape[1:], BF16),
            pltpu.VMEM((samples, 2) + shards[0].shape[1:], BF16),
            pltpu.SemaphoreType.DMA((1,)),
        ]
        + PlaneGather.sems(arrays, samples)
        + RowGather.sems(complexes * own, chips),
        compiler_params=params(collective_id=0, has_side_effects=True),
        name="enter",
    )(token_count, tok, single, pair, pair_mask, *small, *shards)
    return out[:arrays], out[arrays:]


def pair_grad_kernel(dbias_ref, low_ref, out_ref):
    first = (pl.program_id(0) == 0) & (pl.program_id(1) == 0)

    @pl.when(first)
    def _():
        out_ref[...] = jnp.zeros_like(out_ref)

    total = out_ref[...]
    for row in range(low_ref.shape[1]):
        total = total + dot(dbias_ref[0, :, row, :].astype(BF16), low_ref[0, row])
    out_ref[...] = total


def pair_grad(dbias, pair_low):
    complexes, rows, length, width = pair_low.shape
    heads = dbias.shape[1]
    block = 8
    return pl.pallas_call(
        pair_grad_kernel,
        grid=(complexes, rows // block),
        in_specs=[
            pl.BlockSpec((1, heads, block, length), lambda c, b: (c, 0, b, 0)),
            pl.BlockSpec((1, block, length, width), lambda c, b: (c, b, 0, 0)),
        ],
        out_specs=pl.BlockSpec((heads, width), lambda c, b: (0, 0)),
        out_shape=jax.ShapeDtypeStruct((heads, width), F32),
        compiler_params=params(),
        name="pair_grad",
    )(dbias, pair_low)


def attend_kernel(
    heads, rows_ref, full_ref, attn_ref, vec_ref, bias_ref, out_ref, prob_ref, query_ref,
    gate_ref, keyval_ref,
):
    width = rows_ref.shape[3]
    rows, length = rows_ref.shape[2], full_ref.shape[2]
    head_dim = width // heads
    scale = head_dim ** (-0.5)
    own = rows_ref[0, 0]
    query = dot(own, joined(attn_ref, 0)) + vec_ref[6:7]
    query_ref[0, 0] = query.astype(BF16)
    gate_ref[0, 0] = jax.nn.sigmoid(dot(own, joined(attn_ref, 3)))
    full = full_ref[0, 0]
    for which in range(2):
        keyval_ref[which, 0, 0] = dot(full, joined(attn_ref, 1 + which)).astype(BF16)
    parts = []
    for start, inside in head_windows(heads, head_dim):
        count = len(inside)
        lanes = slice(start, start + 256)
        stacked = stack_heads(query_ref[0, 0, :, lanes], start, inside, head_dim)
        scores = dot_nt(stacked, keyval_ref[0, 0, 0, :, lanes]) * scale
        bias = bias_ref[0, inside[0] : inside[-1] + 1].reshape(count * rows, length)
        scores = scores + bias
        weight = jnp.exp(scores - jnp.max(scores, axis=-1, keepdims=True))
        prob = weight * (1.0 / jnp.sum(weight, axis=-1, keepdims=True))
        low = prob.astype(BF16)
        prob_ref[0, 0, inside[0] : inside[-1] + 1] = low.reshape(count, rows, length)
        mixed = dot(low, keyval_ref[1, 0, 0, :, lanes])
        parts.append((start, unstack_heads(mixed, start, inside, head_dim)))
    out_ref[0, 0] = join_windows(parts, width)


def attend(normed, full, attn, vec, bias):
    complexes, samples, rows, width = normed.shape
    heads, length = bias.shape[1], bias.shape[3]
    own = pl.BlockSpec((1, 1, rows, width), lambda c, s: (c, s, 0, 0))
    return pl.pallas_call(
        functools.partial(attend_kernel, heads),
        grid=(complexes, samples),
        in_specs=[
            own,
            pl.BlockSpec((1, 1, length, width), lambda c, s: (c, s, 0, 0)),
            pl.BlockSpec(attn.shape, lambda c, s: (0,) * 4, pipeline_mode=pl.Buffered(1)),
            pl.BlockSpec(vec.shape, lambda c, s: (0, 0)),
            pl.BlockSpec((1, heads, rows, length), lambda c, s: (c, 0, 0, 0)),
        ],
        out_specs=[
            own,
            pl.BlockSpec((1, 1, heads, rows, length), lambda c, s: (c, s, 0, 0, 0)),
            own,
            own,
            pl.BlockSpec((2, 1, 1, length, width), lambda c, s: (0, c, s, 0, 0)),
        ],
        out_shape=[
            jax.ShapeDtypeStruct((complexes, samples, rows, width), F32),
            jax.ShapeDtypeStruct((complexes, samples, heads, rows, length), BF16),
            jax.ShapeDtypeStruct((complexes, samples, rows, width), BF16),
            jax.ShapeDtypeStruct((complexes, samples, rows, width), F32),
            jax.ShapeDtypeStruct((2, complexes, samples, length, width), BF16),
        ],
        compiler_params=params(),
        name="attend",
    )(normed, full, attn, vec, bias)


def attend_back_step(
    heads, prob_ref, grad_ref, query_ref, key_ref, value_ref, full_ref, key_w, value_w,
    dq_ref, dfull_ref, dbias_ref, dkey_w_ref, dvalue_w_ref,
):
    rows, width = query_ref.shape
    length = key_ref.shape[0]
    head_dim = width // heads
    scale = head_dim ** (-0.5)
    dq_parts, dk_parts, dv_parts = [], [], []
    for start, inside in head_windows(heads, head_dim):
        count = len(inside)
        lanes = slice(start, start + 256)
        queries = stack_heads(query_ref[:, lanes], start, inside, head_dim)
        grads = stack_heads(grad_ref[:, lanes], start, inside, head_dim)
        span = slice(inside[0], inside[-1] + 1)
        low = prob_ref[span].reshape(count * rows, length)
        prob = low.astype(F32)
        dprob = dot_nt(grads, value_ref[:, lanes])
        inner = jnp.sum(prob * dprob, axis=-1, keepdims=True)
        dscore = (prob * (dprob - inner)).astype(BF16)
        dbias_ref[span] += dscore.astype(F32).reshape(count, rows, length)
        mixed = dot(dscore, key_ref[:, lanes])
        dq_parts.append((start, unstack_heads(mixed, start, inside, head_dim)))
        dk_parts.append((start, dot_tn(dscore, queries)))
        dv_parts.append((start, dot_tn(low, grads)))
    dq_ref[...] = (join_windows(dq_parts, width) * scale).astype(BF16)
    dkey = (join_windows(dk_parts, width) * scale).astype(BF16)
    dvalue = join_windows(dv_parts, width).astype(BF16)
    dfull_ref[...] = (dot_nt(dkey, key_w) + dot_nt(dvalue, value_w)).astype(BF16).reshape(
        dfull_ref.shape
    )
    turned = full_ref[...].T
    dkey_w_ref[...] += dot(turned, dkey)
    dvalue_w_ref[...] += dot(turned, dvalue)


def attend_back_kernel(
    heads, prob_ref, grad_ref, query_ref, keyval_ref, full_ref, key_w_ref, value_w_ref,
    dq_ref, dfull_ref, dbias_ref, dkey_w_ref, dvalue_w_ref,
):
    @pl.when(pl.program_id(1) == 0)
    def _():
        dbias_ref[...] = jnp.zeros_like(dbias_ref)

    @pl.when((pl.program_id(0) == 0) & (pl.program_id(1) == 0))
    def _():
        dkey_w_ref[...] = jnp.zeros_like(dkey_w_ref)
        dvalue_w_ref[...] = jnp.zeros_like(dvalue_w_ref)

    attend_back_step(
        heads, prob_ref.at[0, 0], grad_ref.at[0, 0], query_ref.at[0, 0], keyval_ref.at[0, 0, 0],
        keyval_ref.at[1, 0, 0], full_ref.at[0, 0], joined(key_w_ref), joined(value_w_ref),
        dq_ref.at[0, 0], dfull_ref.at[0, 0], dbias_ref.at[0], dkey_w_ref, dvalue_w_ref,
    )


def attend_back(prob, grad, query, keyval, full, attn):
    complexes, samples, rows, width = query.shape
    heads, length = prob.shape[2], prob.shape[4]
    own = pl.BlockSpec((1, 1, rows, width), lambda c, s: (c, s, 0, 0))
    long = pl.BlockSpec((1, 1, length, width), lambda c, s: (c, s, 0, 0))
    weight = lambda which: pl.BlockSpec(
        (attn.shape[0], 1) + attn.shape[2:], lambda c, s: (0, which, 0, 0),
        pipeline_mode=pl.Buffered(1),
    )
    square = pl.BlockSpec((width, width), lambda c, s: (0, 0))
    return pl.pallas_call(
        functools.partial(attend_back_kernel, heads),
        grid=(complexes, samples),
        in_specs=[
            pl.BlockSpec((1, 1, heads, rows, length), lambda c, s: (c, s, 0, 0, 0)),
            own,
            own,
            pl.BlockSpec((2, 1, 1, length, width), lambda c, s: (0, c, s, 0, 0)),
            long,
            weight(1),
            weight(2),
        ],
        out_specs=[
            own,
            long,
            pl.BlockSpec((1, heads, rows, length), lambda c, s: (c, 0, 0, 0)),
            square,
            square,
        ],
        out_shape=[
            jax.ShapeDtypeStruct((complexes, samples, rows, width), BF16),
            jax.ShapeDtypeStruct((complexes, samples, length, width), BF16),
            jax.ShapeDtypeStruct((complexes, heads, rows, length), F32),
            jax.ShapeDtypeStruct((width, width), F32),
            jax.ShapeDtypeStruct((width, width), F32),
        ],
        compiler_params=params(),
        name="attend_back",
    )(prob, grad, query, keyval, full, attn, attn)


def middle_kernel(
    rows_dev, count_ref,
    att_ref, gate_ref, tok_ref, single_ref, cot_ref,
    vec_ref, ada_ref, zero_ref, out_w_ref, tin_ref, tout_ref,
    out_ref, dmid_ref, datt_ref, dglogit_ref,
    gated_ref, dabranch_ref, dza_ref, dzb_ref, tcond_ref, dtpre_ref, dtin_ref,
    tinput_ref, dfirst_ref, dsecond_ref, hidden_ref, dtbranch_ref, small_ref,
):
    step = pl.program_id(0)
    rows = att_ref.shape[0]
    count = count_ref[step]
    place = lax.broadcasted_iota(jnp.int32, (rows, 1), 0) % rows_dev
    place = place + lax.axis_index("row") * rows_dev
    valid = (place < count).astype(F32)
    att = att_ref[...]
    gate = gate_ref[...]
    single = single_ref[...]
    gated = (att * gate).astype(BF16)
    gated_ref[...] = gated
    branch = dot(gated, joined(out_w_ref))
    attn_zero = jax.nn.sigmoid(dot(single, joined(zero_ref, 0)) + vec_ref[4:5])
    middle = tok_ref[...].astype(F32) + valid * attn_zero * branch
    cond, _ = center_rows(single.astype(F32))
    tcond = (cond * vec_ref[1:2, 0 : single.shape[1]]).astype(BF16)
    tcond_ref[...] = tcond
    scale = jax.nn.sigmoid(dot(tcond, joined(ada_ref, 0)) + vec_ref[3:4])
    shift = dot(tcond, joined(ada_ref, 1))
    normed, rstd = center_rows(middle)
    tinput = (scale * normed + shift).astype(BF16)
    tinput_ref[...] = tinput
    first = dot(tinput, joined(tin_ref, 0))
    second = dot(tinput, joined(tin_ref, 1))
    sig = jax.nn.sigmoid(first)
    hidden = (first * sig * second).astype(BF16)
    hidden_ref[...] = hidden
    tbranch = dot(hidden, joined(tout_ref))
    trans_zero = jax.nn.sigmoid(dot(single, joined(zero_ref, 1)) + vec_ref[5:6])
    out_ref[...] = (middle + valid * trans_zero * tbranch).astype(BF16)
    grad_out = cot_ref[...].astype(F32)
    gated_out = grad_out * valid
    dtbranch = (gated_out * trans_zero).astype(BF16)
    dtbranch_ref[...] = dtbranch
    dzb = (gated_out * tbranch * trans_zero * (1.0 - trans_zero)).astype(BF16)
    dzb_ref[...] = dzb
    dhidden = dot_nt(dtbranch, joined(tout_ref))
    dfirst = (dhidden * second * sig * (1.0 + first * (1.0 - sig))).astype(BF16)
    dsecond = (dhidden * first * sig).astype(BF16)
    dfirst_ref[...] = dfirst
    dsecond_ref[...] = dsecond
    dtin = (dot_nt(dfirst, joined(tin_ref, 0)) + dot_nt(dsecond, joined(tin_ref, 1))).astype(BF16)
    dtin_ref[...] = dtin
    dtin_full = dtin.astype(F32)
    dtpre = (dtin_full * normed * scale * (1.0 - scale)).astype(BF16)
    dtpre_ref[...] = dtpre
    grad_norm = dtin_full * scale
    tail = grad_norm - jnp.mean(grad_norm, axis=-1, keepdims=True)
    tail = tail - normed * jnp.mean(grad_norm * normed, axis=-1, keepdims=True)
    dmid = grad_out + tail * rstd
    dmid_ref[...] = dmid
    dtcond = dot_nt(dtpre, joined(ada_ref, 0)) + dot_nt(dtin, joined(ada_ref, 1))
    gated_mid = dmid * valid
    dabranch = (gated_mid * attn_zero).astype(BF16)
    dabranch_ref[...] = dabranch
    dza = (gated_mid * branch * attn_zero * (1.0 - attn_zero)).astype(BF16)
    dza_ref[...] = dza
    dgated = dot_nt(dabranch, joined(out_w_ref))
    datt_ref[...] = (dgated * gate).astype(BF16)
    dglogit_ref[...] = (dgated * att * gate * (1.0 - gate)).astype(BF16)

    @pl.when(step == 0)
    def _():
        small_ref[...] = jnp.zeros_like(small_ref)

    width, narrow = att.shape[1], single.shape[1]
    total = lambda value: jnp.sum(value.astype(F32), axis=0, keepdims=True)
    small_ref[0:1, :] += total(dtpre)
    small_ref[1:2, :] += total(dza)
    small_ref[2:3, :] += total(dzb)
    small_ref[3:4, 0:narrow] += total(dtcond * cond)


def middle_pass(
    token_count, att, gate, tok, single, cot, vec, ada, zero, out_w, trans_in, trans_out, complexes,
    rows_dev,
):
    rows, width = tok.shape
    narrow = single.shape[1]
    hidden = trans_out.shape[0] * trans_out.shape[2]
    part = rows // complexes
    wide = pl.BlockSpec((part, width), lambda c, m: (c, 0))
    slim = pl.BlockSpec((part, narrow), lambda c, m: (c, 0))
    long = pl.BlockSpec((part, hidden), lambda c, m: (c, 0))
    once = lambda shape: pl.BlockSpec(
        shape, lambda c, m: (0,) * len(shape), pipeline_mode=pl.Buffered(1)
    )
    shape = lambda cols, kind: jax.ShapeDtypeStruct((rows, cols), kind)
    return pl.pallas_call(
        functools.partial(middle_kernel, rows_dev),
        grid_spec=pltpu.PrefetchScalarGridSpec(
            num_scalar_prefetch=1,
            grid=(complexes,),
            in_specs=[
                wide, wide, wide, slim, wide,
                once(vec.shape),
                pl.BlockSpec(
                    (ada.shape[0], 2) + ada.shape[2:], lambda c, m: (0, 1, 0, 0),
                    pipeline_mode=pl.Buffered(1),
                ),
                once(zero.shape),
                once(out_w.shape),
                once(trans_in.shape),
                once(trans_out.shape),
            ],
            out_specs=[
                wide, wide, wide, wide,
                wide, wide, wide, wide, slim, wide, wide,
                wide, long, long, long, wide,
                once((8, width)),
            ],
        ),
        out_shape=[
            shape(width, BF16), shape(width, F32), shape(width, BF16), shape(width, BF16),
            shape(width, BF16), shape(width, BF16), shape(width, BF16), shape(width, BF16),
            shape(narrow, BF16), shape(width, BF16), shape(width, BF16),
            shape(width, BF16), shape(hidden, BF16), shape(hidden, BF16), shape(hidden, BF16),
            shape(width, BF16),
            jax.ShapeDtypeStruct((8, width), F32),
        ],
        compiler_params=params(),
        name="middle_pass",
    )(token_count, att, gate, tok, single, cot, vec, ada, zero, out_w, trans_in, trans_out)


def last_kernel(
    dquery_ref, dfull_ref, dglogit_ref, tok_ref, single_ref, dmid_ref,
    vec_ref, ada_ref, query_w_ref, gate_w_ref,
    tgrad_ref, dnormed_ref, dapre_ref, cond_ref, small_ref,
):
    total = lambda value: jnp.sum(value.astype(F32), axis=0, keepdims=True)
    dnormed = (
        dot_nt(dquery_ref[...], joined(query_w_ref))
        + dot_nt(dglogit_ref[...], joined(gate_w_ref))
        + dfull_ref[...].astype(F32)
    ).astype(BF16)
    dnormed_ref[...] = dnormed
    cond, _ = center_rows(single_ref[...].astype(F32))
    cond_low = (cond * vec_ref[0:1, 0 : cond.shape[1]]).astype(BF16)
    cond_ref[...] = cond_low
    scale = jax.nn.sigmoid(dot(cond_low, joined(ada_ref, 0)) + vec_ref[2:3])
    normed, rstd = center_rows(tok_ref[...].astype(F32))
    full = dnormed.astype(F32)
    dapre = (full * normed * scale * (1.0 - scale)).astype(BF16)
    dapre_ref[...] = dapre
    grad_norm = full * scale
    tail = grad_norm - jnp.mean(grad_norm, axis=-1, keepdims=True)
    tail = tail - normed * jnp.mean(grad_norm * normed, axis=-1, keepdims=True)
    tgrad_ref[...] = dmid_ref[...] + tail * rstd
    dcond = dot_nt(dapre, joined(ada_ref, 0)) + dot_nt(dnormed, joined(ada_ref, 1))
    narrow = cond.shape[1]
    small_ref[...] = jnp.zeros_like(small_ref)
    small_ref[0:1, :] = total(dapre)
    small_ref[1:2, :] = total(dquery_ref[...])
    small_ref[2:3, 0:narrow] = total(dcond * cond)


def last_pass(dquery, dfull, dglogit, tok, single, dmid, vec, ada, attn):
    rows, width = tok.shape
    narrow = single.shape[1]
    whole = lambda shape: pl.BlockSpec(shape, lambda w: (0,) * len(shape))
    wide = whole((rows, width))
    shape = lambda cols, kind: jax.ShapeDtypeStruct((rows, cols), kind)
    weight = lambda which: pl.BlockSpec(
        (attn.shape[0], 1) + attn.shape[2:], lambda w: (0, which, 0, 0)
    )
    return pl.pallas_call(
        last_kernel,
        grid=(1,),
        in_specs=[
            wide, wide, wide, wide, whole((rows, narrow)), wide,
            whole(vec.shape),
            pl.BlockSpec((ada.shape[0], 2) + ada.shape[2:], lambda w: (0, 0, 0, 0)),
            weight(0),
            weight(3),
        ],
        out_specs=[wide, wide, wide, whole((rows, narrow)), whole((8, width))],
        out_shape=[
            shape(width, F32), shape(width, BF16), shape(width, BF16), shape(narrow, BF16),
            jax.ShapeDtypeStruct((8, width), F32),
        ],
        compiler_params=params(),
        name="last_pass",
    )(dquery, dfull, dglogit, tok, single, dmid, vec, ada, attn, attn)


def return_kernel(
    heads, chips, samples, grads_ref, prob_ref, grad_ref, query_ref, keyval_ref, full_ref, attn_ref,
    low_ref, normed_ref,
    dq_ref, own_ref, pair_ref, wide_plane, plane_ref, query_plane_ref,
    dfull, dbias, weight_buf, dkey_w_ref, dvalue_w_ref, query_grads_buf, pair_acc,
    load_sem, *scratch,
):
    place = Place(chips, samples)
    complexes, own = query_ref.shape[:2]
    rows, width = query_ref.shape[2:]
    length = full_ref.shape[2]
    count = len(PlaneReduce.scratch(samples, 64, 128))
    cut = 2 * wide_plane.shape[0]
    wide = PlaneReduce(place, grads_ref.at[:, pl.ds(0, cut)], wide_plane, scratch[:count])
    rest = grads_ref.shape[1] - cut
    plane = PlaneReduce(
        place, grads_ref.at[:, pl.ds(cut, rest)], plane_ref, scratch[count : 2 * count]
    )
    query_plane = PlaneReduce(
        place, query_grads_buf, query_plane_ref, scratch[2 * count : 3 * count]
    )
    scratch = scratch[3 * count :]
    moves = [
        RowReduce(place, dfull, own_ref, which, scratch) for which in range(complexes)
    ]
    place.barrier(True, True)
    wide.start()
    plane.start()
    load = pltpu.make_async_copy(attn_ref.at[:, 1:3], weight_buf, load_sem.at[0])
    load.start()
    dkey_w_ref[...] = jnp.zeros_like(dkey_w_ref)
    dvalue_w_ref[...] = jnp.zeros_like(dvalue_w_ref)
    dbias[...] = jnp.zeros_like(dbias)
    load.wait()

    def hooked(step, hooks):
        for at, actions in hooks.items():

            @pl.when(step == at)
            def _():
                for action in actions:
                    action()

    def back(prob_block, grad_block, query_block, keyval_block, full_block):
        step = pl.program_id(0)
        which, sample = step // own, step % own
        attend_back_step(
            heads, prob_block.at[0, 0], grad_block.at[0, 0], query_block.at[0, 0],
            keyval_block.at[0, 0, 0], keyval_block.at[1, 0, 0], full_block.at[0, 0],
            joined(weight_buf, 0), joined(weight_buf, 1), dq_ref.at[which, sample],
            dfull.at[which, sample], dbias.at[which], dkey_w_ref, dvalue_w_ref,
        )
        hooked(step, back_hooks)

    back_hooks = {}
    final = complexes * own - 1

    def then(at, action):
        back_hooks.setdefault(min(at, final), []).append(action)

    half_order = (len(plane.order) + 1) // 2
    for at, k in enumerate(plane.order):
        then(at // half_order, functools.partial(wide.depart, k))
        then(own - 1 + at // half_order, functools.partial(plane.depart, k))
    then(own - 1, lambda: moves[0].first_swap().start())
    then(own, moves[0].begin)
    for t in range(1, chips):
        then(own + t - 1, functools.partial(moves[0].line.advance, t))
    then(own + 1, wide.hop)
    then(final, lambda: moves[1].first_swap().start())

    spot = lambda b: (b // own, b % own)
    rows_block = pl.BlockSpec((1, 1, rows, width), lambda b: spot(b) + (0, 0))
    pltpu.emit_pipeline(
        back,
        grid=(complexes * own,),
        in_specs=[
            pl.BlockSpec((1, 1, heads, rows, length), lambda b: spot(b) + (0, 0, 0)),
            rows_block,
            rows_block,
            pl.BlockSpec((2, 1, 1, length, width), lambda b: (0,) + spot(b) + (0, 0)),
            pl.BlockSpec((1, 1, length, width), lambda b: spot(b) + (0, 0)),
        ],
    )(prob_ref, grad_ref, query_ref, keyval_ref, full_ref)
    query_grads(
        normed_ref[...], dq_ref[...].reshape(complexes * own * rows, width), dkey_w_ref[...],
        dvalue_w_ref[...], query_grads_buf,
    )
    query_plane.start()

    pair_acc[...] = jnp.zeros_like(pair_acc)
    per = rows // PAIR_ROWS

    def pair_part(first, last):
        def body(low_block):
            step = first + pl.program_id(0)
            which, start = step // per, pl.multiple_of(step % per * PAIR_ROWS, PAIR_ROWS)
            lines = dbias[which, :, pl.ds(start, PAIR_ROWS), :]
            lines = lines.reshape(heads * PAIR_ROWS, length).astype(BF16)
            line = lax.broadcasted_iota(jnp.int32, (heads * PAIR_ROWS, 1), 0) % PAIR_ROWS
            total = pair_acc[...]
            for row in range(PAIR_ROWS):
                total = total + jnp.where(line == row, dot(lines, low_block[0, row]), 0.0)
            pair_acc[...] = total

        pltpu.emit_pipeline(
            body,
            grid=(last - first,),
            in_specs=[
                pl.BlockSpec(
                    (1, PAIR_ROWS, length, low_ref.shape[3]),
                    lambda b: ((first + b) // per, (first + b) % per, 0, 0),
                )
            ],
        )(low_ref)

    total = complexes * per
    marks = [total * t // chips for t in range(chips + 1)]
    moves[1].begin()
    moves[1].line.advance(1)
    plane.hop()
    for k in query_plane.order:
        query_plane.depart(k)
    wide.finish()
    moves[0].finish()
    for t in range(chips):
        pair_part(marks[t], marks[t + 1])
        if t + 2 < chips:
            moves[1].line.advance(t + 2)
        if t == 1:
            query_plane.hop()
    pair_ref[...] = jnp.sum(pair_acc[...].reshape(heads, PAIR_ROWS, pair_acc.shape[1]), axis=1)
    plane.finish()
    moves[1].finish()
    query_plane.finish()
    for move in moves:
        move.drain()
    for part in (wide, plane, query_plane):
        part.drain()


def return_pass(grads, cut, prob, grad, query, keyval, full, attn, pair_low, normed, query_rows):
    samples, chips = lax.axis_size("sample"), lax.axis_size("row") // 2
    complexes, own, rows, width = query.shape
    heads, length = prob.shape[2], prob.shape[4]
    vmem = pl.BlockSpec(memory_space=pltpu.VMEM)
    half = (grads.shape[1] - cut) // 2
    return pl.pallas_call(
        functools.partial(return_kernel, heads, chips, samples),
        in_specs=[ANY] * 8 + [vmem],
        out_specs=[vmem, ANY, vmem, vmem, vmem, vmem],
        out_shape=[
            jax.ShapeDtypeStruct(query.shape, BF16),
            jax.ShapeDtypeStruct(query.shape, BF16),
            jax.ShapeDtypeStruct((heads, pair_low.shape[3]), F32),
            jax.ShapeDtypeStruct((cut // 2, width), BF16),
            jax.ShapeDtypeStruct((half, width), BF16),
            jax.ShapeDtypeStruct((query_rows // 2, width), BF16),
        ],
        scratch_shapes=[
            pltpu.VMEM((complexes, own, chips, 2, rows, width), BF16),
            pltpu.VMEM((complexes, heads, rows, length), F32),
            pltpu.VMEM((attn.shape[0], 2) + attn.shape[2:], BF16),
            pltpu.VMEM((width, width), F32),
            pltpu.VMEM((width, width), F32),
            pltpu.VMEM((samples, query_rows, width), BF16),
            pltpu.VMEM((heads * PAIR_ROWS, pair_low.shape[3]), F32),
            pltpu.SemaphoreType.DMA((1,)),
        ]
        + PlaneReduce.scratch(samples, cut, width)
        + PlaneReduce.scratch(samples, 2 * half, width)
        + PlaneReduce.scratch(samples, query_rows, width)
        + RowReduce.scratch(complexes, own, length, rows, width, chips),
        compiler_params=params(collective_id=5, has_side_effects=True),
        name="return_pass",
    )(grads, prob, grad, query, keyval, full, attn, pair_low, normed)


def leave_kernel(
    chips, samples, most_ref, late_ref, query_ref, dquery_ref, dfull_ref, dglogit_ref, tok_ref, single_ref,
    dmid_ref, vec_ref, ada_ref, attn_ref, small_mid, pair_sum,
    tgrad_ref, most_total, late_total, query_total, last_total,
    most_plane, late_plane, query_plane, last_grads_buf, last_plane, dnormed_ref, dapre_ref, cond_ref,
    small_ref, load_sem, *scratch,
):
    place = Place(chips, samples)
    count = len(PlaneReduce.scratch(samples, 64, 128))
    plane = PlaneReduce(place, last_grads_buf, last_plane, scratch[:count])
    scratch = scratch[count:]
    pieces = [
        (LineTotal, most_plane, most_total), (LineTotal, late_plane, late_total),
        (LineTotal, query_plane, query_total),
        (DirectTotal, last_plane, last_total),
    ]
    lines = []
    for kind, buf, total in pieces:
        count = len(kind.scratch(16 * chips, 128, chips))
        lines.append(kind(place, buf, total, 0, buf.shape[0], scratch[:count]))
        scratch = scratch[count:]
    most, late, query, last = lines
    loads = [
        pltpu.make_async_copy(late_ref, late_plane, load_sem.at[0]),
        pltpu.make_async_copy(query_ref, query_plane, load_sem.at[1]),
        pltpu.make_async_copy(most_ref, most_plane, load_sem.at[2]),
    ]
    for load in loads:
        load.start()
    place.barrier(True, True, True)
    for load in loads:
        load.wait()
    groups = [(most, 0), (late, 1), (query, 2), (last, 4)]
    clock = [0]

    def tick():
        t = clock[0] = clock[0] + 1
        for line, behind in groups:
            step = t - behind
            if 1 <= step < line.steps:
                line.advance(step)
            elif step == line.steps:
                line.finish()

    tick()
    last_kernel(
        dquery_ref, dfull_ref, dglogit_ref, tok_ref, single_ref, dmid_ref, vec_ref, ada_ref,
        attn_ref.at[:, 0:1], attn_ref.at[:, 3:4], tgrad_ref, dnormed_ref, dapre_ref, cond_ref,
        small_ref,
    )
    tick()
    last_grads(
        cond_ref[...], dapre_ref[...], dnormed_ref[...], small_mid[...], small_ref[...],
        pair_sum[...], last_grads_buf,
    )
    plane.start()
    tick()
    for k in plane.order:
        plane.depart(k)
    tick()
    plane.hop()
    plane.finish()
    while clock[0] < max(line.steps + behind for line, behind in groups):
        tick()
    plane.drain()


def leave(most, late, query, dquery, dfull, dglogit, tok, single, dmid, vec, ada, attn, small_mid, pair_sum,
          last_rows):
    samples, chips = lax.axis_size("sample"), lax.axis_size("row") // 2
    rows, width = tok.shape
    narrow = single.shape[1]
    halves = [most.shape[0], late.shape[0], query.shape[0], last_rows // 2]
    vmem = pl.BlockSpec(memory_space=pltpu.VMEM)
    return pl.pallas_call(
        functools.partial(leave_kernel, chips, samples),
        in_specs=[ANY] * 3 + [vmem] * 11,
        out_specs=[vmem] * 5,
        out_shape=[jax.ShapeDtypeStruct((rows, width), F32)]
        + [jax.ShapeDtypeStruct((2 * half, width), BF16) for half in halves],
        scratch_shapes=[
            pltpu.VMEM(most.shape, BF16),
            pltpu.VMEM(late.shape, BF16),
            pltpu.VMEM(query.shape, BF16),
            pltpu.VMEM((samples, last_rows, width), BF16),
            pltpu.VMEM((last_rows // 2, width), BF16),
            pltpu.VMEM((rows, width), BF16),
            pltpu.VMEM((rows, width), BF16),
            pltpu.VMEM((rows, narrow), BF16),
            pltpu.VMEM((8, width), F32),
            pltpu.SemaphoreType.DMA((3,)),
        ]
        + PlaneReduce.scratch(samples, last_rows, width)
        + LineTotal.scratch(halves[0], width, chips)
        + LineTotal.scratch(halves[1], width, chips)
        + LineTotal.scratch(halves[2], width, chips)
        + DirectTotal.scratch(halves[3], width, chips),
        compiler_params=params(collective_id=6, has_side_effects=True),
        name="leave",
    )(most, late, query, dquery, dfull, dglogit, tok, single, dmid, vec, ada, attn, small_mid, pair_sum)


def grad_rows(samples, chips, parts):
    unit = 32 * chips
    return -(-sum(parts) // unit) * unit


def store_grads(out_ref, start, left, grads):
    samples, _, width = out_ref.shape
    turned = left.T
    rows = turned.shape[0] // samples
    for grad in grads:
        value = dot(turned, grad).astype(BF16)
        out_ref[:, start : start + rows] = value.reshape(samples, rows, width)
        start += rows
    return start


def pad_grads(out_ref, start):
    samples, rows, width = out_ref.shape
    if start < rows:
        out_ref[:, start:] = jnp.zeros((samples, rows - start, width), BF16)


def late_grads_kernel(
    tcond, dtpre, dtin, single, dza, dzb, gated, dabranch, tinput, dfirst, dsecond, hidden,
    dtbranch, normed_in, dglogit, out_ref,
):
    width = out_ref.shape[2]
    halves = [
        ref[:, lane : lane + width] for ref in (dfirst, dsecond) for lane in range(0, dfirst.shape[1], width)
    ]
    start = store_grads(out_ref, 0, tinput[...], halves)
    start = store_grads(out_ref, start, hidden[...], [dtbranch[...]])
    start = store_grads(out_ref, start, tcond[...], [dtpre[...], dtin[...]])
    start = store_grads(out_ref, start, single[...], [dza[...], dzb[...]])
    start = store_grads(out_ref, start, gated[...], [dabranch[...]])
    start = store_grads(out_ref, start, normed_in[...], [dglogit[...]])
    pad_grads(out_ref, start)


def store_ready(out_ref, start, ready):
    samples, _, width = out_ref.shape
    for value in ready:
        size = value.shape[0] // samples
        out_ref[:, start : start + size] = value.astype(BF16).reshape(samples, size, width)
        start += size
    return start


def query_grads(normed_in, dquery, dkey_w, dvalue_w, out_ref):
    start = store_grads(out_ref, 0, normed_in, [dquery])
    pad_grads(out_ref, store_ready(out_ref, start, [dkey_w, dvalue_w]))


def last_grads(cond, dapre, dnormed, small_mid, small_last, pair_sum, out_ref):
    samples, rows, width = out_ref.shape
    start = store_grads(out_ref, 0, cond, [dapre, dnormed])
    pairs = jnp.concatenate(
        [pair_sum, jnp.zeros((pair_sum.shape[0], width - pair_sum.shape[1]), F32)], axis=1
    )
    small = jnp.concatenate([small_mid, small_last, pairs], axis=0).astype(BF16)
    for sample in range(samples):
        out_ref[sample, start : start + small.shape[0]] = small
    pad_grads(out_ref, start + small.shape[0])


def query_grads_kernel(normed_in, dquery, dkey_w, dvalue_w, out_ref):
    query_grads(normed_in[...], dquery[...], dkey_w[...], dvalue_w[...], out_ref)


def last_grads_kernel(cond, dapre, dnormed, small_mid, small_last, pair_sum, out_ref):
    last_grads(
        cond[...], dapre[...], dnormed[...], small_mid[...], small_last[...], pair_sum[...], out_ref
    )


def grads_call(kernel, samples, rows, width, operands, name):
    return pl.pallas_call(
        kernel,
        out_shape=jax.ShapeDtypeStruct((samples, rows, width), BF16),
        compiler_params=params(),
        name=name,
    )(*operands)


def deal_kernel(
    most, late, early, last, pairw,
    gain_ref, ada_ref, ada_bias_ref, zero_ref, zero_bias_ref, attn_ref, query_bias_ref, out_ref,
    pair_gain_ref, pair_weight_ref, tin_ref, tout_ref,
):
    slim, wide = ada_ref.shape[1], attn_ref.shape[1]
    width = ada_ref.shape[2]
    spot = lax.axis_index("sample")
    part = lambda ref, start, size: ref[start : start + size].astype(F32)
    for which in range(2):
        for lane in range(2):
            tin_ref[which, :, lane * width : (lane + 1) * width] = part(
                most, (2 * which + lane) * wide, wide
            )
    tout_ref[...] = part(most, 4 * wide, tout_ref.shape[0])
    for which in range(2):
        ada_ref[which] = part(last, which * slim, slim)
        ada_ref[2 + which] = part(late, which * slim, slim)
        zero_ref[which] = part(late, (2 + which) * slim, slim)
    out_ref[...] = part(late, 4 * slim, wide)
    for which in range(3):
        attn_ref[which] = part(early, which * wide, wide)
    attn_ref[3] = part(late, 4 * slim + wide, wide)
    heads, thin = pair_weight_ref.shape[1], pair_weight_ref.shape[0]
    small = last[2 * slim : 2 * slim + 16]
    pairs = last[2 * slim + 16 : 2 * slim + 16 + heads, 0 : pairw.shape[1]]

    def choose(size, count):
        row = lax.broadcasted_iota(jnp.int32, (size, count), 0)
        lane = lax.broadcasted_iota(jnp.int32, (size, count), 1)
        return (row == lane + spot * count).astype(BF16)

    lines = dot(small, choose(width, wide))
    narrow = slim * (width // wide)
    slims = dot(small[:, 0:narrow], choose(narrow, slim))
    ada_bias_ref[0:1] = lines[8:9]
    ada_bias_ref[1:2] = lines[0:1]
    zero_bias_ref[...] = lines[1:3]
    query_bias_ref[...] = lines[9:10]
    gain_ref[0:1] = slims[10:11]
    gain_ref[1:2] = slims[3:4]
    turn = lax.broadcasted_iota(jnp.int32, (thin, pairw.shape[1]), 0)
    lane = lax.broadcasted_iota(jnp.int32, (thin, pairw.shape[1]), 1)
    pair_weight_ref[...] = dot_nt((lane == turn + spot * thin).astype(BF16), pairs)
    gains = jnp.sum(pairw[8 : 8 + heads] * pairs.astype(F32), axis=0, keepdims=True) / pairw[0:1]
    pair_gain_ref[...] = lax.dot_general(
        gains, choose(pairw.shape[1], thin).astype(F32), (((1,), (0,)), ((), ())),
        precision=lax.Precision.HIGHEST, preferred_element_type=F32,
    )


def deal(most, late, early, last, pairw, shapes):
    return pl.pallas_call(
        deal_kernel,
        out_shape=[jax.ShapeDtypeStruct(shape, F32) for shape in shapes],
        compiler_params=params(),
        name="deal",
    )(most, late, early, last, pairw)


def local(
    tokens, single, pair, token_count, pair_mask, cotangent, cond_gain, ada_weight, ada_bias,
    zero_weight, zero_bias, attn_weight, query_bias, out_weight, pair_gain, pair_weight,
    trans_in, trans_out,
):
    complexes, samples_own, rows_dev, width = tokens.shape
    narrow = single.shape[3]
    heads, length = pair_weight.shape[1], pair.shape[2]
    samples, chips = lax.axis_size("sample"), lax.axis_size("row") // 2
    rows = complexes * samples_own * rows_dev
    flat = lambda value: value.reshape(rows, value.shape[-1])
    block = lambda value: value.reshape(complexes, samples_own, rows_dev, width)
    tok, sing, cot = flat(tokens), flat(single), flat(cotangent)
    small = (cond_gain, ada_bias, zero_bias, query_bias[None], pair_gain[None], pair_weight)
    weights, (full, normed_in, vec, pairw, pair_low, bias) = enter(
        token_count, tok, sing, pair, pair_mask, small,
        [ada_weight, attn_weight, zero_weight, out_weight[None], trans_in, trans_out[None]],
        complexes, heads,
    )
    _, ada, attn, zero, out_w, tin, tout = weights
    att, prob, query, gate, keyval = attend(normed_in, full, attn, vec, bias)
    normed_in = flat(normed_in)
    (
        output, dmid, datt, dglogit, gated, dabranch, dza, dzb, tcond, dtpre, dtin, tinput,
        dfirst, dsecond, hidden, dtbranch, small_mid,
    ) = middle_pass(
        token_count, flat(att), flat(gate), tok, sing, cot, vec, ada, zero, out_w, tin, tout,
        complexes, rows_dev,
    )
    slim, wide = narrow // samples, width // samples
    late_parts = [wide] * 4 + [tout.shape[2]] + [slim] * 4 + [wide] * 2
    query_parts = [wide] * 3
    last_parts = [slim] * 2 + [16 + heads]
    late_rows, query_rows, last_rows = (
        grad_rows(samples, chips, parts) for parts in (late_parts, query_parts, last_parts)
    )
    late = grads_call(
        late_grads_kernel, samples, late_rows, width,
        (tcond, dtpre, dtin, sing, dza, dzb, gated, dabranch, tinput, dfirst, dsecond, hidden, dtbranch,
         normed_in, dglogit),
        "late_grads",
    )
    datt = block(datt)
    if length <= 512:
        dquery, dfull, pair_sum, most, late, early = return_pass(
            late, sum(late_parts[:5]), prob, datt, query, keyval, full, attn, pair_low, normed_in, query_rows
        )
        tgrad, most, late, early, last = leave(
            most, late, early, flat(dquery), flat(dfull), dglogit, tok, sing, dmid, vec, ada, attn,
            small_mid, pair_sum, last_rows,
        )
    else:
        dquery, dfull, dbias, dkey_w, dvalue_w = attend_back(prob, datt, query, keyval, full, attn)
        dfull = flat(reduce_rows(dfull, 2))
        pair_sum = pair_grad(dbias, pair_low)
        dquery = flat(dquery)
        tgrad, dnormed, dapre, cond, small_last = last_pass(
            dquery, dfull, dglogit, tok, sing, dmid, vec, ada, attn
        )
        early = grads_call(
            query_grads_kernel, samples, query_rows, width, (normed_in, dquery, dkey_w, dvalue_w),
            "query_grads",
        )
        last = grads_call(
            last_grads_kernel, samples, last_rows, width,
            (cond, dapre, dnormed, small_mid, small_last, pair_sum), "last_grads",
        )
        late = reduce_grads(late, 3)
        most, late = late[: sum(late_parts[:5])], late[sum(late_parts[:5]) :]
        early = reduce_grads(early, 4)
        last = reduce_grads(last, 2)

    shapes = [
        cond_gain.shape, ada_weight.shape, ada_bias.shape, zero_weight.shape, zero_bias.shape,
        attn_weight.shape, (1,) + query_bias.shape, out_weight.shape, (1,) + pair_gain.shape,
        pair_weight.shape, trans_in.shape, trans_out.shape,
    ]
    grads = list(deal(most, late, early, last, pairw, shapes))
    for place in (6, 8):
        grads[place] = grads[place][0]
    return (output.reshape(tokens.shape), tgrad.reshape(tokens.shape), *grads)


def solution(mesh):
    rowwise = P(None, "sample", "row", None)
    return jax.shard_map(
        local,
        mesh=mesh,
        in_specs=(
            rowwise,
            rowwise,
            P(None, "row", None, None),
            P(),
            P(None, "row", None),
            rowwise,
            P(None, "sample"),
            P(None, "sample", None),
            P(None, "sample"),
            P(None, "sample", None),
            P(None, "sample"),
            P(None, "sample", None),
            P("sample"),
            P("sample", None),
            P("sample"),
            P("sample", None),
            P(None, "sample", None),
            P("sample", None),
        ),
        out_specs=(
            rowwise,
            rowwise,
            P(None, "sample"),
            P(None, "sample", None),
            P(None, "sample"),
            P(None, "sample", None),
            P(None, "sample"),
            P(None, "sample", None),
            P("sample"),
            P("sample", None),
            P("sample"),
            P("sample", None),
            P(None, "sample", None),
            P("sample", None),
        ),
        check_vma=False,
    )
```

```python
import functools

import jax
import jax.numpy as jnp
from jax import lax
from jax.experimental import pallas as pl
from jax.experimental.pallas import tpu as pltpu
from jax.sharding import PartitionSpec as P

EPSILON = 1e-05
MASKED = -1000000000.0
F32 = jnp.float32
BF16 = jnp.bfloat16
VMEM_LIMIT = 60 << 20


def center_rows(value):
    center = value - jnp.mean(value, axis=-1, keepdims=True)
    rstd = lax.rsqrt(jnp.mean(center * center, axis=-1, keepdims=True) + EPSILON)
    return center * rstd, rstd


def dot(left, right):
    return lax.dot_general(left, right, (((1,), (0,)), ((), ())), preferred_element_type=F32)


def dot_nt(left, right):
    return lax.dot_general(left, right, (((1,), (1,)), ((), ())), preferred_element_type=F32)


def dot_tn(left, right):
    return lax.dot_general(left, right, (((0,), (0,)), ((), ())), preferred_element_type=F32)


def params(**extra):
    return pltpu.CompilerParams(vmem_limit_bytes=VMEM_LIMIT, **extra)


MESH = pl.DeviceIdType.MESH
ANY = pl.BlockSpec(memory_space=pl.ANY)


class Place:
    def __init__(self, chips, samples):
        self.row = lax.axis_index("row")
        self.chip = self.row // 2
        self.core = self.row % 2
        self.sample = lax.axis_index("sample")
        self.chips, self.samples = chips, samples

    def twin(self):
        return (self.row + 1 - 2 * self.core, self.sample)

    def peer(self, k):
        return (self.row, jnp.bitwise_xor(self.sample, k))

    def up(self):
        return (self.row + 2, self.sample)

    def down(self):
        return (self.row - 2, self.sample)

    def along(self, k):
        return (jnp.bitwise_xor(self.row, 2 * k), self.sample)

    def barrier(self, plane, line, whole_line=False):
        bar = pltpu.get_barrier_semaphore()

        def greet(device):
            pl.semaphore_signal(bar, inc=1, device_id=device, device_id_type=MESH)

        greet(self.twin())
        if plane:
            for k in range(1, self.samples):
                greet(self.peer(k))
        if line and not whole_line:

            @pl.when(self.chip > 0)
            def _():
                greet(self.down())

            @pl.when(self.chip < self.chips - 1)
            def _():
                greet(self.up())

        count = 1 + (self.samples - 1 if plane else 0)
        if whole_line:
            for k in range(1, self.chips):
                greet(self.along(k))
            count = count + self.chips - 1
        elif line:
            count = count + jnp.minimum(self.chip, 1) + jnp.minimum(self.chips - 1 - self.chip, 1)
        pl.semaphore_wait(bar, count)


def send(source, target, send_sem, recv_sem, device):
    return pltpu.make_async_remote_copy(
        source, target, send_sem, recv_sem, device_id=device, device_id_type=MESH
    )


def half_of(ref, core):
    if ref.shape[0] > 1:
        size = ref.shape[0] // 2
        return ref.at[pl.ds(core * size, size)]
    size = ref.shape[1] // 2
    return ref.at[:, pl.ds(pl.multiple_of(core * size, 16), size)]


class PlaneGather:
    @staticmethod
    def sems(arrays, samples):
        dma = pltpu.SemaphoreType.DMA
        return [dma((arrays, samples))] * 4 + [dma((arrays, 2))] * 2

    def __init__(self, place, shards, fulls, sems):
        self.place, self.shards, self.fulls = place, shards, fulls
        self.out, self.come, self.swap_out, self.swap_come, self.hop_out, self.hop_come = sems
        self.relayed = place.samples == 4
        self.direct = [1, 2] if self.relayed else list(range(1, place.samples))

    def owner(self, k):
        return jnp.bitwise_xor(self.place.sample, k)

    def half(self, i, k):
        return half_of(self.fulls[i].at[self.owner(k)], self.place.core)

    def copy(self, i, k):
        slot = self.half(i, 0)
        return send(
            half_of(self.shards[i], self.place.core), slot, self.out.at[i, k], self.come.at[i, k],
            self.place.peer(k),
        )

    def hop(self, i, k):
        slot = self.half(i, k)
        size = slot.shape[1] // 2
        piece = slot.at[:, pl.ds((k - 1) * size, size)]
        return send(piece, piece, self.hop_out.at[i, k - 1], self.hop_come.at[i, k - 1], self.place.peer(3 - k))

    def swap(self, i, k):
        slot = self.half(i, k)
        return send(slot, slot, self.swap_out.at[i, k], self.swap_come.at[i, k], self.place.twin())

    def keep(self, i):
        return send(
            self.shards[i], self.fulls[i].at[self.place.sample], self.swap_out.at[i, 0],
            self.swap_come.at[i, 0], self.place.twin(),
        )

    def start(self, i):
        for k in self.direct:
            self.copy(i, k).start()
        self.keep(i).start()

    def relay(self, i):
        for k in self.direct:
            self.copy(i, k).wait_recv()
            if self.relayed:
                self.hop(i, k).start()
            self.swap(i, k).start()

    def settle(self, i):
        if self.relayed:
            for k in self.direct:
                self.hop(i, k).wait_recv()
            self.swap(i, 3).start()

    def arrive(self, i):
        self.keep(i).wait_recv()
        for k in range(1, self.place.samples):
            self.swap(i, k).wait_recv()

    def finish(self, arrived=()):
        for i in range(len(self.shards)):
            if i not in arrived:
                self.arrive(i)
            self.keep(i).wait_send()
            for k in self.direct:
                self.copy(i, k).wait_send()
                if self.relayed:
                    self.hop(i, k).wait_send()
            for k in range(1, self.place.samples):
                self.swap(i, k).wait_send()


class LineSpread:
    @staticmethod
    def sems(lines, chips):
        dma = pltpu.SemaphoreType.DMA
        return [dma((lines, chips))] * 6

    def __init__(self, place, line, slot, sems):
        self.place, self.line, self.slot = place, line, slot
        self.up_out, self.up_come, self.down_out, self.down_come, self.swap_out, self.swap_come = sems

    def step(self, upward, t):
        place, last = self.place, self.place.chips - 1
        z = place.chip
        if upward:
            out_chip, has_out = z - t + 1, (z >= t - 1) & (z < last)
            in_chip, has_in = z - t, z >= t
            sems, device = (self.up_out, self.up_come), place.up()
        else:
            out_chip, has_out = z + t - 1, (z + t - 1 <= last) & (z > 0)
            in_chip, has_in = z + t, z + t <= last
            sems, device = (self.down_out, self.down_come), place.down()
        make = lambda chip: send(
            self.slot(chip), self.slot(chip),
            sems[0].at[self.line, t], sems[1].at[self.line, t], device,
        )
        return (has_out, lambda: make(out_chip)), (has_in, in_chip, lambda: make(in_chip))

    def hand_over(self, chip):
        slot = self.slot(chip)
        return send(
            slot, slot, self.swap_out.at[self.line, chip], self.swap_come.at[self.line, chip],
            self.place.twin(),
        )

    def depart(self, t):
        for upward in (True, False):
            (has_out, copy), _ = self.step(upward, t)

            @pl.when(has_out)
            def _():
                copy().start()

    def advance(self, t):
        for upward in (True, False):
            _, (has_in, chip, copy) = self.step(upward, t)

            @pl.when(has_in)
            def _():
                copy().wait_recv()

        if t + 1 < self.place.chips:
            self.depart(t + 1)
        for upward in (True, False):
            _, (has_in, chip, copy) = self.step(upward, t)

            @pl.when(has_in)
            def _():
                self.hand_over(chip).start()

    def finish(self):
        for t in range(1, self.place.chips):
            for upward in (True, False):
                (has_out, copy), (has_in, chip, _) = self.step(upward, t)

                @pl.when(has_out)
                def _():
                    copy().wait_send()

                @pl.when(has_in)
                def _():
                    self.hand_over(chip).wait()


class LineReduce:
    @staticmethod
    def sems(lines, chips):
        dma = pltpu.SemaphoreType.DMA
        return [dma((lines, chips))] * 4

    def __init__(self, place, line, slot, up_buf, down_buf, sems):
        self.place, self.line, self.slot = place, line, slot
        self.bufs = (up_buf, down_buf)
        self.up_out, self.up_come, self.down_out, self.down_come = sems

    def step(self, upward, t):
        place, last = self.place, self.place.chips - 1
        z, distance = place.chip, place.chips - t
        buf = self.bufs[0 if upward else 1]
        if upward:
            block, has_out, has_before = z + distance, z + distance <= last, z > 0
            has_in = (z > 0) & (z - 1 + distance <= last)
            sems, device = (self.up_out, self.up_come), place.up()
        else:
            block, has_out, has_before = z - distance, z - distance >= 0, z < last
            has_in = (z < last) & (z + 1 - distance >= 0)
            sems, device = (self.down_out, self.down_come), place.down()
        copy = lambda chip: send(
            self.slot(chip), buf.at[self.line, t - 1],
            sems[0].at[self.line, t], sems[1].at[self.line, t], device,
        )
        return block, has_out, has_before, has_in, copy, buf

    def advance(self, t):
        for upward in (True, False):
            block, has_out, has_before, _, copy, buf = self.step(upward, t)
            before = self.step(upward, t - 1)[4] if t > 1 else None

            @pl.when(has_out)
            def _():
                if t > 1:

                    @pl.when(has_before)
                    def _():
                        before(block).wait_recv()
                        slot = self.slot(block)
                        slot[...] = (
                            slot[...].astype(F32) + buf[self.line, t - 2].astype(F32)
                        ).astype(slot.dtype)

                copy(block).start()

    def finish(self):
        last_step = self.place.chips - 1
        slot = self.slot(self.place.chip)
        for upward in (True, False):
            _, _, _, has_in, copy, buf = self.step(upward, last_step)

            @pl.when(has_in)
            def _():
                copy(self.place.chip).wait_recv()
                slot[...] = (
                    slot[...].astype(F32) + buf[self.line, last_step - 1].astype(F32)
                ).astype(slot.dtype)

        for t in range(1, self.place.chips):
            for upward in (True, False):
                block, has_out, _, _, copy, _ = self.step(upward, t)

                @pl.when(has_out)
                def _():
                    copy(block).wait_send()


class RowGather:
    @staticmethod
    def sems(lines, chips):
        return [pltpu.SemaphoreType.DMA((lines,))] + LineSpread.sems(lines, chips)

    def __init__(self, place, part, full, line, sems):
        self.place, self.part, self.full, self.index = place, part, full, line
        self.spot = (line // part.shape[1], line % part.shape[1])
        self.keep_sem = sems[0]
        self.rows = part.shape[2]
        self.line = LineSpread(place, line, self.slot, sems[1:])

    def slot(self, chip):
        start = (2 * chip + self.place.core) * self.rows
        return self.full.at[self.spot + (pl.ds(pl.multiple_of(start, 16), self.rows),)]

    def keep(self):
        return pltpu.make_async_copy(
            self.part.at[self.spot], self.slot(self.place.chip), self.keep_sem.at[self.index]
        )

    def start(self):
        self.keep().start()

    def begin(self):
        self.keep().wait()
        self.line.depart(1)
        self.line.hand_over(self.place.chip).start()

    def finish(self):
        self.line.finish()
        self.line.hand_over(self.place.chip).wait()


class RowReduce:
    @staticmethod
    def scratch(complexes, samples_own, length, rows, width, chips):
        dma = pltpu.SemaphoreType.DMA
        hop = pltpu.VMEM((complexes, chips - 1, samples_own, rows, width), BF16)
        return [
            pltpu.VMEM((complexes, samples_own, chips, rows, width), BF16), hop, hop,
        ] + [dma((complexes,))] * 3 + LineReduce.sems(complexes, chips)

    def __init__(self, place, part, own, which, scratch):
        self.place, self.part, self.own, self.which = place, part, own, which
        self.sums, up_buf, down_buf = scratch[:3]
        self.swap_out, self.swap_come, self.keep_sem = scratch[3:6]
        self.line = LineReduce(place, which, self.slot, up_buf, down_buf, scratch[6:])

    def slot(self, chip):
        return self.sums.at[self.which, :, chip]

    def first_swap(self):
        return send(
            self.part.at[self.which, :, :, 1 - self.place.core], self.sums.at[self.which],
            self.swap_out.at[self.which], self.swap_come.at[self.which], self.place.twin(),
        )

    def begin(self):
        self.first_swap().wait_recv()
        for sample in range(self.part.shape[1]):
            for chip in range(self.place.chips):
                mine = self.part[self.which, sample, chip, self.place.core].astype(F32)
                self.sums[self.which, sample, chip] = (
                    mine + self.sums[self.which, sample, chip].astype(F32)
                ).astype(BF16)

    def keep(self):
        return pltpu.make_async_copy(
            self.slot(self.place.chip), self.own.at[self.which], self.keep_sem.at[self.which]
        )

    def finish(self):
        self.line.finish()
        self.keep().start()

    def drain(self):
        self.first_swap().wait_send()
        self.keep().wait()


def reduce_rows_kernel(chips, samples, part_ref, own_ref, *scratch):
    place = Place(chips, samples)
    moves = [
        RowReduce(place, part_ref, own_ref, which, scratch) for which in range(part_ref.shape[0])
    ]
    place.barrier(False, True)
    for move in moves:
        move.first_swap().start()
    for move in moves:
        move.begin()
        move.line.advance(1)
    for t in range(2, chips):
        for move in moves:
            move.line.advance(t)
    for move in moves:
        move.finish()
    for move in moves:
        move.drain()


def reduce_rows(part, collective_id):
    samples, chips = lax.axis_size("sample"), lax.axis_size("row") // 2
    complexes, own, length, width = part.shape
    rows = length // (2 * chips)
    return pl.pallas_call(
        functools.partial(reduce_rows_kernel, chips, samples),
        in_specs=[pl.BlockSpec(memory_space=pltpu.VMEM)],
        out_specs=ANY,
        out_shape=jax.ShapeDtypeStruct((complexes, own, rows, width), part.dtype),
        scratch_shapes=RowReduce.scratch(complexes, own, length, rows, width, chips),
        compiler_params=params(collective_id=collective_id, has_side_effects=True),
        name="reduce_rows",
    )(part.reshape(complexes, own, chips, 2, rows, width))


class PlaneReduce:
    @staticmethod
    def scratch(samples, rows, width):
        dma = pltpu.SemaphoreType.DMA
        half = rows // 2
        return [
            pltpu.VMEM((samples, half, width), BF16),
            pltpu.VMEM((2 * samples - 2, half // 2, width), BF16),
            pltpu.VMEM((half, width), BF16),
        ] + [dma((samples,))] * 3 + [dma((2 * samples,))] * 2

    def __init__(self, place, grads, plane, scratch):
        self.place, self.grads, self.plane = place, grads, plane
        self.sums, self.come_buf, self.mine = scratch[:3]
        self.swap_out, self.swap_come, self.load_sem, self.out, self.come = scratch[3:]
        self.half = grads.shape[1] // 2
        self.relayed = place.samples == 4
        self.order = [3, 1, 2, 0] if self.relayed else list(range(1, place.samples)) + [0]

    def shard(self, k):
        return jnp.bitwise_xor(self.place.sample, k)

    def half_rows(self, core):
        return pl.ds(pl.multiple_of(core * self.half, 16), self.half)

    def part(self, k, which):
        return self.sums.at[self.shard(k), pl.ds(which * (self.half // 2), self.half // 2)]

    def swap(self, k):
        return send(
            self.grads.at[self.shard(k), self.half_rows(1 - self.place.core)],
            self.sums.at[self.shard(k)],
            self.swap_out.at[k], self.swap_come.at[k], self.place.twin(),
        )

    def load(self, k):
        return pltpu.make_async_copy(
            self.grads.at[self.shard(k), self.half_rows(self.place.core)],
            self.mine, self.load_sem.at[k],
        )

    def copy(self, k, which, peer, slot):
        return send(
            self.part(k, which), self.come_buf.at[slot], self.out.at[slot], self.come.at[slot],
            self.place.peer(peer),
        )

    def copies(self, k):
        if not self.relayed:
            return [self.copy(k, which, k, 2 * (k - 1) + which) for which in range(2)] if k else []
        return {
            3: lambda: [self.copy(3, 0, 1, 1), self.copy(3, 1, 2, 4)],
            1: lambda: [self.copy(1, 0, 1, 0)],
            2: lambda: [self.copy(2, 1, 2, 3)],
            0: lambda: [],
        }[k]()

    def onward(self):
        return [(self.copy(2, 0, 2, 2), 1, (2, 0)), (self.copy(1, 1, 1, 5), 4, (1, 1))]

    def arrived(self, slot):
        self.copy(0, 0, 1, slot).wait_recv()
        return self.come_buf[slot].astype(F32)

    def start(self):
        for k in self.order:
            self.swap(k).start()
        self.load(self.order[0]).start()

    def depart(self, k):
        place = self.order.index(k)
        self.load(k).wait()
        self.swap(k).wait_recv()
        slot = self.sums.at[self.shard(k)]
        slot[...] = (self.mine[...].astype(F32) + slot[...].astype(F32)).astype(BF16)
        for copy in self.copies(k):
            copy.start()
        if place + 1 < len(self.order):
            self.load(self.order[place + 1]).start()

    def hop(self):
        if self.relayed:
            for copy, slot, piece in self.onward():
                ref = self.part(*piece)
                ref[...] = (ref[...].astype(F32) + self.arrived(slot)).astype(BF16)
                copy.start()

    def finish(self):
        size = self.half // 2
        for which in range(2):
            value = self.part(0, which)[...].astype(F32)
            if self.relayed:
                slots = [3 * which, 3 * which + 2]
            else:
                slots = [2 * (k - 1) + which for k in range(1, self.place.samples)]
            for slot in slots:
                value = value + self.arrived(slot)
            self.plane[which * size : (which + 1) * size] = value.astype(BF16)

    def drain(self):
        for k in self.order:
            self.swap(k).wait_send()
            for copy in self.copies(k):
                copy.wait_send()
        if self.relayed:
            for copy, _, _ in self.onward():
                copy.wait_send()


class LineTotal:
    @staticmethod
    def scratch(size, width, chips):
        hop = pltpu.VMEM((1, chips - 1, size // chips, width), BF16)
        return [hop, hop] + LineReduce.sems(1, chips) + LineSpread.sems(1, chips)

    def __init__(self, place, plane, total, start, size, scratch):
        self.place, self.plane, self.total, self.start = place, plane, total, start
        self.half = total.shape[0] // 2
        self.size = size // place.chips
        self.reduce = LineReduce(place, 0, self.block, scratch[0], scratch[1], scratch[2:6])
        self.spread = LineSpread(place, 0, self.slot, scratch[6:])

    def block(self, chip):
        return self.plane.at[pl.ds(pl.multiple_of(self.start + chip * self.size, 16), self.size)]

    def slot(self, chip):
        start = self.place.core * self.half + self.start + chip * self.size
        return self.total.at[pl.ds(pl.multiple_of(start, 16), self.size)]

    @property
    def steps(self):
        return 2 * self.place.chips - 1

    def advance(self, t):
        if t < self.place.chips:
            self.reduce.advance(t)
            return
        t -= self.place.chips - 1
        if t == 1:
            self.reduce.finish()
            own = self.slot(self.place.chip)
            own[...] = self.block(self.place.chip)[...]
            self.spread.depart(1)
            self.spread.hand_over(self.place.chip).start()
        else:
            self.spread.advance(t - 1)

    def finish(self):
        self.spread.advance(self.place.chips - 1)
        self.spread.finish()
        self.spread.hand_over(self.place.chip).wait()


class DirectTotal:
    steps = 4

    @staticmethod
    def scratch(size, width, chips):
        dma = pltpu.SemaphoreType.DMA
        return [pltpu.VMEM((chips - 1, size // chips, width), BF16)] + [dma((chips,))] * 6

    def __init__(self, place, plane, total, start, size, scratch):
        self.place, self.plane, self.total, self.start = place, plane, total, start
        self.half = total.shape[0] // 2
        self.size = size // place.chips
        self.buf = scratch[0]
        self.out, self.come, self.back_out, self.back_come, self.swap_out, self.swap_come = scratch[1:]

    def chip(self, k):
        return jnp.bitwise_xor(self.place.chip, k)

    def block(self, chip):
        return self.plane.at[pl.ds(pl.multiple_of(self.start + chip * self.size, 16), self.size)]

    def slot(self, chip):
        start = self.place.core * self.half + self.start + chip * self.size
        return self.total.at[pl.ds(pl.multiple_of(start, 16), self.size)]

    def there(self, k):
        return send(
            self.block(self.chip(k)), self.buf.at[k - 1], self.out.at[k], self.come.at[k],
            self.place.along(k),
        )

    def back(self, k):
        own = self.slot(self.place.chip)
        return send(own, own, self.back_out.at[k], self.back_come.at[k], self.place.along(k))

    def swap(self, k):
        slot = self.slot(self.chip(k))
        return send(slot, slot, self.swap_out.at[k], self.swap_come.at[k], self.place.twin())

    def advance(self, t):
        peers = range(1, self.place.chips)
        if t == 1:
            for k in peers:
                self.there(k).start()
        elif t == 2:
            value = self.block(self.place.chip)[...].astype(F32)
            for k in peers:
                self.there(k).wait_recv()
                value = value + self.buf[k - 1].astype(F32)
            own = self.slot(self.place.chip)
            own[...] = value.astype(BF16)
            for k in peers:
                self.back(k).start()
            self.swap(0).start()
        else:
            for k in peers:
                self.back(k).wait_recv()
                self.swap(k).start()

    def finish(self):
        for k in range(1, self.place.chips):
            self.there(k).wait_send()
            self.back(k).wait_send()
        for k in range(self.place.chips):
            self.swap(k).wait()


def reduce_grads_kernel(chips, samples, grads_ref, total_ref, *scratch):
    place = Place(chips, samples)
    count = len(PlaneReduce.scratch(samples, 64, 128))
    plane_buf = scratch[0]
    plane = PlaneReduce(place, grads_ref, plane_buf, scratch[1 : 1 + count])
    line = LineTotal(place, plane_buf, total_ref, 0, plane_buf.shape[0], scratch[1 + count :])
    place.barrier(True, True)
    plane.start()
    for k in plane.order:
        plane.depart(k)
    plane.hop()
    plane.finish()
    for t in range(1, 2 * chips - 1):
        line.advance(t)
    line.finish()
    plane.drain()


def reduce_grads(grads, collective_id):
    chips = lax.axis_size("row") // 2
    samples, rows, width = grads.shape
    return pl.pallas_call(
        functools.partial(reduce_grads_kernel, chips, samples),
        in_specs=[pl.BlockSpec(memory_space=pltpu.VMEM)],
        out_specs=pl.BlockSpec(memory_space=pltpu.VMEM),
        out_shape=jax.ShapeDtypeStruct((rows, width), BF16),
        scratch_shapes=[pltpu.VMEM((rows // 2, width), BF16)]
        + PlaneReduce.scratch(samples, rows, width)
        + LineTotal.scratch(rows // 2, width, chips),
        compiler_params=params(collective_id=collective_id, has_side_effects=True),
        name="reduce_grads",
    )(grads)


def joined(ref, which=0):
    samples, _, rows, cols = ref.shape
    return ref[:, which].reshape(samples * rows, cols)


def head_windows(heads, head_dim):
    windows, head = [], 0
    while head < heads:
        start = head * head_dim // 128 * 128
        start = min(start, heads * head_dim - 256)
        inside = []
        while head < heads and (head + 1) * head_dim <= start + 256:
            inside.append(head)
            head += 1
        windows.append((start, inside))
    return windows


def head_mask(start, head, head_dim):
    lane = lax.broadcasted_iota(jnp.int32, (1, 256), 1) + start
    return (lane >= head * head_dim) & (lane < (head + 1) * head_dim)


def stack_heads(rows, start, inside, head_dim):
    zero = jnp.zeros_like(rows)
    return jnp.concatenate(
        [jnp.where(head_mask(start, head, head_dim), rows, zero) for head in inside], axis=0
    )


def unstack_heads(stacked, start, inside, head_dim):
    rows = stacked.shape[0] // len(inside)
    total = None
    for place, head in enumerate(inside):
        piece = jnp.where(
            head_mask(start, head, head_dim), stacked[place * rows : (place + 1) * rows], 0.0
        )
        total = piece if total is None else total + piece
    return total


def join_windows(parts, width):
    tiles = [None] * (width // 128)
    for start, value in parts:
        for half in range(2):
            place = start // 128 + half
            piece = value[:, half * 128 : (half + 1) * 128]
            tiles[place] = piece if tiles[place] is None else tiles[place] + piece
    return jnp.concatenate(tiles, axis=1)


PACK_ROWS, PACK_LANES = 64, 256


def pack_small(cond_gain, ada_bias, zero_bias, query_bias, pair_gain, pair_weight):
    line = lambda ref: jnp.pad(
        ref[...].astype(F32), ((0, 0), (0, PACK_LANES - ref.shape[1]))
    )
    rows = [line(ref) for ref in (cond_gain, ada_bias, zero_bias, query_bias, pair_gain, pair_weight)]
    left = PACK_ROWS - 8 - pair_weight.shape[0]
    return jnp.concatenate(rows + [jnp.zeros((left, PACK_LANES), F32)], axis=0).astype(BF16)


def unpack_small(packed, narrow, width, pair_width, heads):
    samples = packed.shape[0]
    thin = pair_width // samples

    def spread(size):
        count = size // samples
        total = None
        for sample in range(samples):
            lane = lax.broadcasted_iota(jnp.int32, (PACK_LANES, size), 0)
            spot = lax.broadcasted_iota(jnp.int32, (PACK_LANES, size), 1)
            move = ((spot == lane + count * sample) & (lane < count)).astype(BF16)
            piece = dot(packed[sample, 0:16], move)
            total = piece if total is None else total + piece
        return total

    gains = jnp.pad(spread(narrow)[0:2], ((0, 0), (0, width - narrow)))
    vec = jnp.concatenate([gains, spread(width)[2:7], jnp.zeros((1, width), F32)], axis=0)
    weight = [packed[sample].astype(F32)[8 : 8 + thin, 0:128] for sample in range(samples)]
    return vec, spread(pair_width)[7:8], jnp.concatenate(weight, axis=0).T[0:heads]


def pair_block(count_ref, first_row, complex_id, start, pair_ref, mask_ref, gain, weight, low_ref, bias_ref):
    rows, length = pair_ref.shape[1], pair_ref.shape[2]
    count = count_ref[complex_id]
    lines = []
    for row in range(rows):
        normed, _ = center_rows(pair_ref[0, row].astype(F32))
        low = (normed * gain).astype(BF16)
        low_ref[0, row] = low
        lines.append(dot_nt(weight, low))
    bias = jnp.stack(lines, axis=1)
    own = first_row + start + lax.broadcasted_iota(jnp.int32, (rows, length), 0)
    key = lax.broadcasted_iota(jnp.int32, (rows, length), 1)
    allowed = (key < count) & ((mask_ref[0] == 1) | (own == key) | (own >= count))
    bias_ref[0] = jnp.where(allowed[None], bias, MASKED)


PAIR_ROWS = 8


def enter_kernel(arrays, chips, samples, count_ref, tok_ref, single_ref, pair_ref, mask_ref, *refs):
    small, refs = refs[:6], refs[6:]
    shards, refs = refs[: arrays - 1], refs[arrays - 1 :]
    fulls, refs = refs[:arrays], refs[arrays:]
    full_ref, normed_ref, vec_ref, pairw_ref, low_ref, bias_ref = refs[:6]
    own_pack, packed, ada_buf, load_sem = refs[6:10]
    sems = refs[10:]
    place = Place(chips, samples)
    own_pack[0] = pack_small(*small)
    shards = (own_pack, shards[0].at[pl.ds(0, 2)]) + shards[1:] + (shards[0].at[pl.ds(2, 2)],)
    ada_full = fulls[1]
    fulls = (fulls[0], ada_full.at[:, pl.ds(0, 2)]) + fulls[2:] + (ada_full.at[:, pl.ds(2, 2)],)
    arrays += 1
    count = len(PlaneGather.sems(arrays, samples))
    move = PlaneGather(place, shards, fulls, sems[:count])
    complexes, own = normed_ref.shape[:2]
    lines = [
        RowGather(place, normed_ref, full_ref, line, sems[count:]) for line in range(complexes * own)
    ]
    rows_dev, width = normed_ref.shape[2:]
    narrow = single_ref.shape[1]
    place.barrier(True, True)
    move.start(0)
    move.start(1)
    move.relay(0)
    move.settle(0)
    move.relay(1)
    for i in range(2, arrays):
        move.start(i)
    move.arrive(0)
    load = pltpu.make_async_copy(fulls[0].at[:, 0], packed, load_sem.at[0])
    load.start()
    load.wait()
    heads = bias_ref.shape[1]
    vec, pair_gain, pair_weight = unpack_small(packed, narrow, width, pair_ref.shape[3], heads)
    vec_ref[...] = vec
    pairw_ref[0:1] = pair_gain
    pairw_ref[8 : 8 + heads] = pair_weight
    per = rows_dev // PAIR_ROWS

    def pair_part(first, last):
        def body(pair_block_ref, mask_block_ref, low_block_ref, bias_block_ref):
            step = first + pl.program_id(0)
            pair_block(
                count_ref, place.row * rows_dev, step // per, step % per * PAIR_ROWS, pair_block_ref, mask_block_ref,
                pairw_ref[0:1], pairw_ref[8 : 8 + heads].astype(BF16), low_block_ref, bias_block_ref,
            )

        length = pair_ref.shape[2]
        spot = lambda b: ((first + b) // per, (first + b) % per)
        block = pl.BlockSpec((1, PAIR_ROWS, length, pair_ref.shape[3]), lambda b: spot(b) + (0, 0))
        pltpu.emit_pipeline(
            body,
            grid=(last - first,),
            in_specs=[block, pl.BlockSpec((1, PAIR_ROWS, length), lambda b: spot(b) + (0,))],
            out_specs=[
                block,
                pl.BlockSpec((1, heads, PAIR_ROWS, length), lambda b: (spot(b)[0], 0, spot(b)[1], 0)),
            ],
        )(pair_ref, mask_ref, low_ref, bias_ref)

    total = complexes * per
    move.settle(1)
    move.arrive(1)
    load = pltpu.make_async_copy(fulls[1], ada_buf, load_sem.at[0])
    load.start()
    load.wait()
    cond, _ = center_rows(single_ref[...].astype(F32))
    cond = (cond * vec_ref[0:1, 0:narrow]).astype(BF16)
    pre = dot(cond, joined(ada_buf, 0)) + vec_ref[2:3]
    shift = dot(cond, joined(ada_buf, 1))
    normed, _ = center_rows(tok_ref[...].astype(F32))
    normed_in = (jax.nn.sigmoid(pre) * normed + shift).astype(BF16)
    normed_ref[...] = normed_in.reshape(normed_ref.shape)
    for line in lines:
        line.start()
    for line in lines:
        line.begin()
    pair_part(0, total // 4)
    between = {
        0: lambda: (pair_part(total // 4, total // 2), move.relay(2), move.relay(3), move.relay(4)),
        1: lambda: (pair_part(total // 2, total * 3 // 4), move.settle(2), move.relay(5)),
        2: lambda: (
            pair_part(total * 3 // 4, total), move.relay(6), move.settle(3), move.settle(4),
            move.settle(5),
        ),
    }
    for t in range(chips):
        if t:
            for line in lines:
                line.line.advance(t)
        if t in between:
            between[t]()
    move.settle(6)
    for line in lines:
        line.finish()
    move.finish(arrived=(0, 1))


def enter(token_count, tok, single, pair, pair_mask, small, shards, complexes, heads):
    samples, chips = lax.axis_size("sample"), lax.axis_size("row") // 2
    pack = jax.ShapeDtypeStruct((1, PACK_ROWS, PACK_LANES), BF16)
    parts = [pack] + list(shards)
    arrays = len(parts)
    width, narrow = tok.shape[1], single.shape[1]
    _, rows, length, pair_width = pair.shape
    own = tok.shape[0] // complexes // rows
    vmem = pl.BlockSpec(memory_space=pltpu.VMEM)
    fulls = [jax.ShapeDtypeStruct((samples,) + s.shape, s.dtype) for s in parts]
    out = pl.pallas_call(
        functools.partial(enter_kernel, arrays, chips, samples),
        in_specs=[pl.BlockSpec(memory_space=pltpu.SMEM), vmem, vmem, ANY, ANY]
        + [vmem] * 6
        + [ANY] * (arrays - 1),
        out_specs=[ANY] * arrays + [ANY, vmem, vmem, vmem, ANY, ANY],
        out_shape=fulls
        + [
            jax.ShapeDtypeStruct((complexes, own, length, width), BF16),
            jax.ShapeDtypeStruct((complexes, own, rows, width), BF16),
            jax.ShapeDtypeStruct((8, width), F32),
            jax.ShapeDtypeStruct((8 + heads, pair_width), F32),
            jax.ShapeDtypeStruct(pair.shape, BF16),
            jax.ShapeDtypeStruct((complexes, heads, rows, length), F32),
        ],
        scratch_shapes=[
            pltpu.VMEM(pack.shape, BF16),
            pltpu.VMEM((samples,) + pack.shape[1:], BF16),
            pltpu.VMEM((samples, 2) + shards[0].shape[1:], BF16),
            pltpu.SemaphoreType.DMA((1,)),
        ]
        + PlaneGather.sems(arrays + 1, samples)
        + RowGather.sems(complexes * own, chips),
        compiler_params=params(collective_id=0, has_side_effects=True),
        name="enter",
    )(token_count, tok, single, pair, pair_mask, *small, *shards)
    return out[:arrays], out[arrays:]


def pair_grad_kernel(dbias_ref, low_ref, out_ref):
    first = (pl.program_id(0) == 0) & (pl.program_id(1) == 0)

    @pl.when(first)
    def _():
        out_ref[...] = jnp.zeros_like(out_ref)

    total = out_ref[...]
    for row in range(low_ref.shape[1]):
        total = total + dot(dbias_ref[0, :, row, :].astype(BF16), low_ref[0, row])
    out_ref[...] = total


def pair_grad(dbias, pair_low):
    complexes, rows, length, width = pair_low.shape
    heads = dbias.shape[1]
    block = 8
    return pl.pallas_call(
        pair_grad_kernel,
        grid=(complexes, rows // block),
        in_specs=[
            pl.BlockSpec((1, heads, block, length), lambda c, b: (c, 0, b, 0)),
            pl.BlockSpec((1, block, length, width), lambda c, b: (c, b, 0, 0)),
        ],
        out_specs=pl.BlockSpec((heads, width), lambda c, b: (0, 0)),
        out_shape=jax.ShapeDtypeStruct((heads, width), F32),
        compiler_params=params(),
        name="pair_grad",
    )(dbias, pair_low)


def attend_step(
    heads, own, full_ref, attn_ref, vec_ref, bias_ref, out_ref, prob_ref, query_ref, gate_ref,
    key_ref, value_ref,
):
    rows, width = own.shape
    length = full_ref.shape[0]
    head_dim = width // heads
    scale = head_dim ** (-0.5)
    query_ref[...] = (dot(own, joined(attn_ref, 0)) + vec_ref[6:7]).astype(BF16)
    gate_ref[...] = jax.nn.sigmoid(dot(own, joined(attn_ref, 3)))
    full = full_ref[...]
    key_ref[...] = dot(full, joined(attn_ref, 1)).astype(BF16)
    value_ref[...] = dot(full, joined(attn_ref, 2)).astype(BF16)
    parts = []
    for start, inside in head_windows(heads, head_dim):
        count = len(inside)
        lanes = slice(start, start + 256)
        span = slice(inside[0], inside[-1] + 1)
        stacked = stack_heads(query_ref[:, lanes], start, inside, head_dim)
        scores = dot_nt(stacked, key_ref[:, lanes]) * scale
        scores = scores + bias_ref[span].reshape(count * rows, length)
        weight = jnp.exp(scores - jnp.max(scores, axis=-1, keepdims=True))
        prob = weight * (1.0 / jnp.sum(weight, axis=-1, keepdims=True))
        low = prob.astype(BF16)
        prob_ref[span] = low.reshape(count, rows, length)
        mixed = dot(low, value_ref[:, lanes])
        parts.append((start, unstack_heads(mixed, start, inside, head_dim)))
    out_ref[...] = join_windows(parts, width)


def attend_kernel(
    heads, chips, samples, shard_ref, normed_ref, full_ref, attn_ref, vec_ref, bias_ref,
    whole_ref, att_ref, prob_ref, query_ref, gate_ref, keyval_ref, attn_buf, load_sem, *sems,
):
    place = Place(chips, samples)
    complexes, own, rows, width = normed_ref.shape
    length = full_ref.shape[2]
    move = PlaneGather(place, (shard_ref,), (whole_ref,), sems)
    load = pltpu.make_async_copy(attn_ref, attn_buf, load_sem.at[0])
    load.start()
    place.barrier(True, False)
    move.start(0)
    load.wait()
    steps = complexes * own

    def body(full_block, bias_block, att_block, prob_block, query_block, gate_block, keyval_block):
        at = pl.program_id(0)
        attend_step(
            heads, normed_ref[at // own, at % own], full_block.at[0, 0], attn_buf, vec_ref,
            bias_block.at[0], att_block.at[0, 0], prob_block.at[0, 0], query_block.at[0, 0],
            gate_block.at[0, 0], keyval_block.at[0, 0, 0], keyval_block.at[1, 0, 0],
        )

        @pl.when(at == steps // 2)
        def _():
            move.relay(0)

    spot = lambda b: (b // own, b % own)
    rows_block = pl.BlockSpec((1, 1, rows, width), lambda b: spot(b) + (0, 0))
    pltpu.emit_pipeline(
        body,
        grid=(steps,),
        in_specs=[
            pl.BlockSpec((1, 1, length, width), lambda b: spot(b) + (0, 0)),
            pl.BlockSpec((1, heads, rows, length), lambda b: (b // own, 0, 0, 0)),
        ],
        out_specs=[
            rows_block,
            pl.BlockSpec((1, 1, heads, rows, length), lambda b: spot(b) + (0, 0, 0)),
            rows_block,
            rows_block,
            pl.BlockSpec((2, 1, 1, length, width), lambda b: (0,) + spot(b) + (0, 0)),
        ],
    )(full_ref, bias_ref, att_ref, prob_ref, query_ref, gate_ref, keyval_ref)
    move.settle(0)
    move.finish()


def attend(shard, normed, full, attn, vec, bias):
    samples_all, chips = lax.axis_size("sample"), lax.axis_size("row") // 2
    complexes, samples, rows, width = normed.shape
    heads, length = bias.shape[1], bias.shape[3]
    vmem = pl.BlockSpec(memory_space=pltpu.VMEM)
    return pl.pallas_call(
        functools.partial(attend_kernel, heads, chips, samples_all),
        in_specs=[ANY, vmem, ANY, ANY, vmem, ANY],
        out_specs=[ANY] * 6,
        out_shape=[
            jax.ShapeDtypeStruct((samples_all,) + shard.shape, BF16),
            jax.ShapeDtypeStruct((complexes, samples, rows, width), F32),
            jax.ShapeDtypeStruct((complexes, samples, heads, rows, length), BF16),
            jax.ShapeDtypeStruct((complexes, samples, rows, width), BF16),
            jax.ShapeDtypeStruct((complexes, samples, rows, width), F32),
            jax.ShapeDtypeStruct((2, complexes, samples, length, width), BF16),
        ],
        scratch_shapes=[pltpu.VMEM(attn.shape, BF16), pltpu.SemaphoreType.DMA((1,))]
        + PlaneGather.sems(1, samples_all),
        compiler_params=params(collective_id=7, has_side_effects=True),
        name="attend",
    )(shard, normed, full, attn, vec, bias)


def attend_back_step(
    heads, prob_ref, grad_ref, query_ref, key_ref, value_ref, full_ref, key_w, value_w,
    dq_ref, dfull_ref, dbias_ref, dkey_w_ref, dvalue_w_ref,
):
    rows, width = query_ref.shape
    length = key_ref.shape[0]
    head_dim = width // heads
    scale = head_dim ** (-0.5)
    dq_parts, dk_parts, dv_parts = [], [], []
    for start, inside in head_windows(heads, head_dim):
        count = len(inside)
        lanes = slice(start, start + 256)
        queries = stack_heads(query_ref[:, lanes], start, inside, head_dim)
        grads = stack_heads(grad_ref[:, lanes], start, inside, head_dim)
        span = slice(inside[0], inside[-1] + 1)
        low = prob_ref[span].reshape(count * rows, length)
        prob = low.astype(F32)
        dprob = dot_nt(grads, value_ref[:, lanes])
        inner = jnp.sum(prob * dprob, axis=-1, keepdims=True)
        dscore = (prob * (dprob - inner)).astype(BF16)
        dbias_ref[span] += dscore.astype(F32).reshape(count, rows, length)
        mixed = dot(dscore, key_ref[:, lanes])
        dq_parts.append((start, unstack_heads(mixed, start, inside, head_dim)))
        dk_parts.append((start, dot_tn(dscore, queries)))
        dv_parts.append((start, dot_tn(low, grads)))
    dq_ref[...] = (join_windows(dq_parts, width) * scale).astype(BF16)
    dkey = (join_windows(dk_parts, width) * scale).astype(BF16)
    dvalue = join_windows(dv_parts, width).astype(BF16)
    dfull_ref[...] = (dot_nt(dkey, key_w) + dot_nt(dvalue, value_w)).astype(BF16).reshape(
        dfull_ref.shape
    )
    turned = full_ref[...].T
    dkey_w_ref[...] += dot(turned, dkey)
    dvalue_w_ref[...] += dot(turned, dvalue)


def attend_back_kernel(
    heads, prob_ref, grad_ref, query_ref, keyval_ref, full_ref, key_w_ref, value_w_ref,
    dq_ref, dfull_ref, dbias_ref, dkey_w_ref, dvalue_w_ref,
):
    @pl.when(pl.program_id(1) == 0)
    def _():
        dbias_ref[...] = jnp.zeros_like(dbias_ref)

    @pl.when((pl.program_id(0) == 0) & (pl.program_id(1) == 0))
    def _():
        dkey_w_ref[...] = jnp.zeros_like(dkey_w_ref)
        dvalue_w_ref[...] = jnp.zeros_like(dvalue_w_ref)

    attend_back_step(
        heads, prob_ref.at[0, 0], grad_ref.at[0, 0], query_ref.at[0, 0], keyval_ref.at[0, 0, 0],
        keyval_ref.at[1, 0, 0], full_ref.at[0, 0], joined(key_w_ref), joined(value_w_ref),
        dq_ref.at[0, 0], dfull_ref.at[0, 0], dbias_ref.at[0], dkey_w_ref, dvalue_w_ref,
    )


def attend_back(prob, grad, query, keyval, full, attn):
    complexes, samples, rows, width = query.shape
    heads, length = prob.shape[2], prob.shape[4]
    own = pl.BlockSpec((1, 1, rows, width), lambda c, s: (c, s, 0, 0))
    long = pl.BlockSpec((1, 1, length, width), lambda c, s: (c, s, 0, 0))
    weight = lambda which: pl.BlockSpec(
        (attn.shape[0], 1) + attn.shape[2:], lambda c, s: (0, which, 0, 0),
        pipeline_mode=pl.Buffered(1),
    )
    square = pl.BlockSpec((width, width), lambda c, s: (0, 0))
    return pl.pallas_call(
        functools.partial(attend_back_kernel, heads),
        grid=(complexes, samples),
        in_specs=[
            pl.BlockSpec((1, 1, heads, rows, length), lambda c, s: (c, s, 0, 0, 0)),
            own,
            own,
            pl.BlockSpec((2, 1, 1, length, width), lambda c, s: (0, c, s, 0, 0)),
            long,
            weight(1),
            weight(2),
        ],
        out_specs=[
            own,
            long,
            pl.BlockSpec((1, heads, rows, length), lambda c, s: (c, 0, 0, 0)),
            square,
            square,
        ],
        out_shape=[
            jax.ShapeDtypeStruct((complexes, samples, rows, width), BF16),
            jax.ShapeDtypeStruct((complexes, samples, length, width), BF16),
            jax.ShapeDtypeStruct((complexes, heads, rows, length), F32),
            jax.ShapeDtypeStruct((width, width), F32),
            jax.ShapeDtypeStruct((width, width), F32),
        ],
        compiler_params=params(),
        name="attend_back",
    )(prob, grad, query, keyval, full, attn, attn)


def middle_kernel(
    rows_dev, count_ref,
    att_ref, gate_ref, tok_ref, single_ref, cot_ref,
    vec_ref, ada_ref, zero_ref, out_w_ref, tin_ref, tout_ref,
    out_ref, dmid_ref, datt_ref, dglogit_ref,
    gated_ref, dabranch_ref, dza_ref, dzb_ref, tcond_ref, dtpre_ref, dtin_ref,
    tinput_ref, dfirst_ref, dsecond_ref, hidden_ref, dtbranch_ref, small_ref,
):
    step = pl.program_id(0)
    rows = att_ref.shape[0]
    count = count_ref[step]
    place = lax.broadcasted_iota(jnp.int32, (rows, 1), 0) % rows_dev
    place = place + lax.axis_index("row") * rows_dev
    valid = (place < count).astype(F32)
    att = att_ref[...]
    gate = gate_ref[...]
    single = single_ref[...]
    gated = (att * gate).astype(BF16)
    gated_ref[...] = gated
    branch = dot(gated, joined(out_w_ref))
    attn_zero = jax.nn.sigmoid(dot(single, joined(zero_ref, 0)) + vec_ref[4:5])
    middle = tok_ref[...].astype(F32) + valid * attn_zero * branch
    cond, _ = center_rows(single.astype(F32))
    tcond = (cond * vec_ref[1:2, 0 : single.shape[1]]).astype(BF16)
    tcond_ref[...] = tcond
    scale = jax.nn.sigmoid(dot(tcond, joined(ada_ref, 0)) + vec_ref[3:4])
    shift = dot(tcond, joined(ada_ref, 1))
    normed, rstd = center_rows(middle)
    tinput = (scale * normed + shift).astype(BF16)
    tinput_ref[...] = tinput
    first = dot(tinput, joined(tin_ref, 0))
    second = dot(tinput, joined(tin_ref, 1))
    sig = jax.nn.sigmoid(first)
    hidden = (first * sig * second).astype(BF16)
    hidden_ref[...] = hidden
    tbranch = dot(hidden, joined(tout_ref))
    trans_zero = jax.nn.sigmoid(dot(single, joined(zero_ref, 1)) + vec_ref[5:6])
    out_ref[...] = (middle + valid * trans_zero * tbranch).astype(BF16)
    grad_out = cot_ref[...].astype(F32)
    gated_out = grad_out * valid
    dtbranch = (gated_out * trans_zero).astype(BF16)
    dtbranch_ref[...] = dtbranch
    dzb = (gated_out * tbranch * trans_zero * (1.0 - trans_zero)).astype(BF16)
    dzb_ref[...] = dzb
    dhidden = dot_nt(dtbranch, joined(tout_ref))
    dfirst = (dhidden * second * sig * (1.0 + first * (1.0 - sig))).astype(BF16)
    dsecond = (dhidden * first * sig).astype(BF16)
    dfirst_ref[...] = dfirst
    dsecond_ref[...] = dsecond
    dtin = (dot_nt(dfirst, joined(tin_ref, 0)) + dot_nt(dsecond, joined(tin_ref, 1))).astype(BF16)
    dtin_ref[...] = dtin
    dtin_full = dtin.astype(F32)
    dtpre = (dtin_full * normed * scale * (1.0 - scale)).astype(BF16)
    dtpre_ref[...] = dtpre
    grad_norm = dtin_full * scale
    tail = grad_norm - jnp.mean(grad_norm, axis=-1, keepdims=True)
    tail = tail - normed * jnp.mean(grad_norm * normed, axis=-1, keepdims=True)
    dmid = grad_out + tail * rstd
    dmid_ref[...] = dmid
    dtcond = dot_nt(dtpre, joined(ada_ref, 0)) + dot_nt(dtin, joined(ada_ref, 1))
    gated_mid = dmid * valid
    dabranch = (gated_mid * attn_zero).astype(BF16)
    dabranch_ref[...] = dabranch
    dza = (gated_mid * branch * attn_zero * (1.0 - attn_zero)).astype(BF16)
    dza_ref[...] = dza
    dgated = dot_nt(dabranch, joined(out_w_ref))
    datt_ref[...] = (dgated * gate).astype(BF16)
    dglogit_ref[...] = (dgated * att * gate * (1.0 - gate)).astype(BF16)

    @pl.when(step == 0)
    def _():
        small_ref[...] = jnp.zeros_like(small_ref)

    width, narrow = att.shape[1], single.shape[1]
    total = lambda value: jnp.sum(value.astype(F32), axis=0, keepdims=True)
    small_ref[0:1, :] += total(dtpre)
    small_ref[1:2, :] += total(dza)
    small_ref[2:3, :] += total(dzb)
    small_ref[3:4, 0:narrow] += total(dtcond * cond)


def middle_pass(
    token_count, att, gate, tok, single, cot, vec, ada, zero, out_w, trans_in, trans_out, complexes,
    rows_dev,
):
    rows, width = tok.shape
    narrow = single.shape[1]
    hidden = trans_out.shape[0] * trans_out.shape[2]
    part = rows // complexes
    wide = pl.BlockSpec((part, width), lambda c, m: (c, 0))
    slim = pl.BlockSpec((part, narrow), lambda c, m: (c, 0))
    long = pl.BlockSpec((part, hidden), lambda c, m: (c, 0))
    once = lambda shape: pl.BlockSpec(
        shape, lambda c, m: (0,) * len(shape), pipeline_mode=pl.Buffered(1)
    )
    shape = lambda cols, kind: jax.ShapeDtypeStruct((rows, cols), kind)
    return pl.pallas_call(
        functools.partial(middle_kernel, rows_dev),
        grid_spec=pltpu.PrefetchScalarGridSpec(
            num_scalar_prefetch=1,
            grid=(complexes,),
            in_specs=[
                wide, wide, wide, slim, wide,
                once(vec.shape),
                pl.BlockSpec(
                    (ada.shape[0], 2) + ada.shape[2:], lambda c, m: (0, 1, 0, 0),
                    pipeline_mode=pl.Buffered(1),
                ),
                once(zero.shape),
                once(out_w.shape),
                once(trans_in.shape),
                once(trans_out.shape),
            ],
            out_specs=[
                wide, wide, wide, wide,
                wide, wide, wide, wide, slim, wide, wide,
                wide, long, long, long, wide,
                once((8, width)),
            ],
        ),
        out_shape=[
            shape(width, BF16), shape(width, F32), shape(width, BF16), shape(width, BF16),
            shape(width, BF16), shape(width, BF16), shape(width, BF16), shape(width, BF16),
            shape(narrow, BF16), shape(width, BF16), shape(width, BF16),
            shape(width, BF16), shape(hidden, BF16), shape(hidden, BF16), shape(hidden, BF16),
            shape(width, BF16),
            jax.ShapeDtypeStruct((8, width), F32),
        ],
        compiler_params=params(),
        name="middle_pass",
    )(token_count, att, gate, tok, single, cot, vec, ada, zero, out_w, trans_in, trans_out)


def last_kernel(
    dquery_ref, dfull_ref, dglogit_ref, tok_ref, single_ref, dmid_ref,
    vec_ref, ada_ref, query_w_ref, gate_w_ref,
    tgrad_ref, dnormed_ref, dapre_ref, cond_ref, small_ref,
):
    total = lambda value: jnp.sum(value.astype(F32), axis=0, keepdims=True)
    dnormed = (
        dot_nt(dquery_ref[...], joined(query_w_ref))
        + dot_nt(dglogit_ref[...], joined(gate_w_ref))
        + dfull_ref[...].astype(F32)
    ).astype(BF16)
    dnormed_ref[...] = dnormed
    cond, _ = center_rows(single_ref[...].astype(F32))
    cond_low = (cond * vec_ref[0:1, 0 : cond.shape[1]]).astype(BF16)
    cond_ref[...] = cond_low
    scale = jax.nn.sigmoid(dot(cond_low, joined(ada_ref, 0)) + vec_ref[2:3])
    normed, rstd = center_rows(tok_ref[...].astype(F32))
    full = dnormed.astype(F32)
    dapre = (full * normed * scale * (1.0 - scale)).astype(BF16)
    dapre_ref[...] = dapre
    grad_norm = full * scale
    tail = grad_norm - jnp.mean(grad_norm, axis=-1, keepdims=True)
    tail = tail - normed * jnp.mean(grad_norm * normed, axis=-1, keepdims=True)
    tgrad_ref[...] = dmid_ref[...] + tail * rstd
    dcond = dot_nt(dapre, joined(ada_ref, 0)) + dot_nt(dnormed, joined(ada_ref, 1))
    narrow = cond.shape[1]
    small_ref[...] = jnp.zeros_like(small_ref)
    small_ref[0:1, :] = total(dapre)
    small_ref[1:2, :] = total(dquery_ref[...])
    small_ref[2:3, 0:narrow] = total(dcond * cond)


def last_pass(dquery, dfull, dglogit, tok, single, dmid, vec, ada, attn):
    rows, width = tok.shape
    narrow = single.shape[1]
    whole = lambda shape: pl.BlockSpec(shape, lambda w: (0,) * len(shape))
    wide = whole((rows, width))
    shape = lambda cols, kind: jax.ShapeDtypeStruct((rows, cols), kind)
    weight = lambda which: pl.BlockSpec(
        (attn.shape[0], 1) + attn.shape[2:], lambda w: (0, which, 0, 0)
    )
    return pl.pallas_call(
        last_kernel,
        grid=(1,),
        in_specs=[
            wide, wide, wide, wide, whole((rows, narrow)), wide,
            whole(vec.shape),
            pl.BlockSpec((ada.shape[0], 2) + ada.shape[2:], lambda w: (0, 0, 0, 0)),
            weight(0),
            weight(3),
        ],
        out_specs=[wide, wide, wide, whole((rows, narrow)), whole((8, width))],
        out_shape=[
            shape(width, F32), shape(width, BF16), shape(width, BF16), shape(narrow, BF16),
            jax.ShapeDtypeStruct((8, width), F32),
        ],
        compiler_params=params(),
        name="last_pass",
    )(dquery, dfull, dglogit, tok, single, dmid, vec, ada, attn, attn)


def return_kernel(
    heads, chips, samples, grads_ref, prob_ref, grad_ref, query_ref, keyval_ref, full_ref, attn_ref,
    low_ref, normed_ref,
    dq_ref, own_ref, pair_ref, wide_plane, plane_ref, query_plane_ref,
    dfull, dbias, weight_buf, dkey_w_ref, dvalue_w_ref, query_grads_buf, pair_acc,
    load_sem, *scratch,
):
    place = Place(chips, samples)
    complexes, own = query_ref.shape[:2]
    rows, width = query_ref.shape[2:]
    length = full_ref.shape[2]
    count = len(PlaneReduce.scratch(samples, 64, 128))
    cut = 2 * wide_plane.shape[0]
    wide = PlaneReduce(place, grads_ref.at[:, pl.ds(0, cut)], wide_plane, scratch[:count])
    rest = grads_ref.shape[1] - cut
    plane = PlaneReduce(
        place, grads_ref.at[:, pl.ds(cut, rest)], plane_ref, scratch[count : 2 * count]
    )
    query_plane = PlaneReduce(
        place, query_grads_buf, query_plane_ref, scratch[2 * count : 3 * count]
    )
    scratch = scratch[3 * count :]
    moves = [
        RowReduce(place, dfull, own_ref, which, scratch) for which in range(complexes)
    ]
    place.barrier(True, True)
    wide.start()
    plane.start()
    load = pltpu.make_async_copy(attn_ref.at[:, 1:3], weight_buf, load_sem.at[0])
    load.start()
    dkey_w_ref[...] = jnp.zeros_like(dkey_w_ref)
    dvalue_w_ref[...] = jnp.zeros_like(dvalue_w_ref)
    dbias[...] = jnp.zeros_like(dbias)
    load.wait()

    def hooked(step, hooks):
        for at, actions in hooks.items():

            @pl.when(step == at)
            def _():
                for action in actions:
                    action()

    def back(prob_block, grad_block, query_block, keyval_block, full_block):
        step = pl.program_id(0)
        which, sample = step // own, step % own
        attend_back_step(
            heads, prob_block.at[0, 0], grad_block.at[0, 0], query_block.at[0, 0],
            keyval_block.at[0, 0, 0], keyval_block.at[1, 0, 0], full_block.at[0, 0],
            joined(weight_buf, 0), joined(weight_buf, 1), dq_ref.at[which, sample],
            dfull.at[which, sample], dbias.at[which], dkey_w_ref, dvalue_w_ref,
        )
        hooked(step, back_hooks)

    back_hooks = {}
    final = complexes * own - 1

    def then(at, action):
        back_hooks.setdefault(min(at, final), []).append(action)

    half_order = (len(plane.order) + 1) // 2
    for at, k in enumerate(plane.order):
        if at < half_order:
            wide.depart(k)
        else:
            then(0, functools.partial(wide.depart, k))
        then(own - 2 + at // half_order, functools.partial(plane.depart, k))
    then(own - 1, lambda: moves[0].first_swap().start())
    then(own, moves[0].begin)
    for t in range(1, chips):
        then(own + t - 1, functools.partial(moves[0].line.advance, t))
    then(own + 1, wide.hop)
    then(final, lambda: moves[1].first_swap().start())

    spot = lambda b: (b // own, b % own)
    rows_block = pl.BlockSpec((1, 1, rows, width), lambda b: spot(b) + (0, 0))
    pltpu.emit_pipeline(
        back,
        grid=(complexes * own,),
        in_specs=[
            pl.BlockSpec((1, 1, heads, rows, length), lambda b: spot(b) + (0, 0, 0)),
            rows_block,
            rows_block,
            pl.BlockSpec((2, 1, 1, length, width), lambda b: (0,) + spot(b) + (0, 0)),
            pl.BlockSpec((1, 1, length, width), lambda b: spot(b) + (0, 0)),
        ],
    )(prob_ref, grad_ref, query_ref, keyval_ref, full_ref)
    query_grads(
        normed_ref[...], dq_ref[...].reshape(complexes * own * rows, width), dkey_w_ref[...],
        dvalue_w_ref[...], query_grads_buf,
    )
    query_plane.start()

    pair_acc[...] = jnp.zeros_like(pair_acc)
    per = rows // PAIR_ROWS

    def pair_part(first, last):
        def body(low_block):
            step = first + pl.program_id(0)
            which, start = step // per, pl.multiple_of(step % per * PAIR_ROWS, PAIR_ROWS)
            lines = dbias[which, :, pl.ds(start, PAIR_ROWS), :]
            lines = lines.reshape(heads * PAIR_ROWS, length).astype(BF16)
            line = lax.broadcasted_iota(jnp.int32, (heads * PAIR_ROWS, 1), 0) % PAIR_ROWS
            total = pair_acc[...]
            for row in range(PAIR_ROWS):
                total = total + jnp.where(line == row, dot(lines, low_block[0, row]), 0.0)
            pair_acc[...] = total

        pltpu.emit_pipeline(
            body,
            grid=(last - first,),
            in_specs=[
                pl.BlockSpec(
                    (1, PAIR_ROWS, length, low_ref.shape[3]),
                    lambda b: ((first + b) // per, (first + b) % per, 0, 0),
                )
            ],
        )(low_ref)

    total = complexes * per
    marks = [total * t // chips for t in range(chips + 1)]
    moves[1].begin()
    moves[1].line.advance(1)
    plane.hop()
    for k in query_plane.order:
        query_plane.depart(k)
    wide.finish()
    moves[0].finish()
    for t in range(chips):
        pair_part(marks[t], marks[t + 1])
        if t + 2 < chips:
            moves[1].line.advance(t + 2)
        if t == 1:
            query_plane.hop()
    pair_ref[...] = jnp.sum(pair_acc[...].reshape(heads, PAIR_ROWS, pair_acc.shape[1]), axis=1)
    plane.finish()
    moves[1].finish()
    query_plane.finish()
    for move in moves:
        move.drain()
    for part in (wide, plane, query_plane):
        part.drain()


def return_pass(grads, cut, prob, grad, query, keyval, full, attn, pair_low, normed, query_rows):
    samples, chips = lax.axis_size("sample"), lax.axis_size("row") // 2
    complexes, own, rows, width = query.shape
    heads, length = prob.shape[2], prob.shape[4]
    vmem = pl.BlockSpec(memory_space=pltpu.VMEM)
    half = (grads.shape[1] - cut) // 2
    return pl.pallas_call(
        functools.partial(return_kernel, heads, chips, samples),
        in_specs=[ANY] * 8 + [vmem],
        out_specs=[vmem, ANY, vmem, vmem, vmem, vmem],
        out_shape=[
            jax.ShapeDtypeStruct(query.shape, BF16),
            jax.ShapeDtypeStruct(query.shape, BF16),
            jax.ShapeDtypeStruct((heads, pair_low.shape[3]), F32),
            jax.ShapeDtypeStruct((cut // 2, width), BF16),
            jax.ShapeDtypeStruct((half, width), BF16),
            jax.ShapeDtypeStruct((query_rows // 2, width), BF16),
        ],
        scratch_shapes=[
            pltpu.VMEM((complexes, own, chips, 2, rows, width), BF16),
            pltpu.VMEM((complexes, heads, rows, length), F32),
            pltpu.VMEM((attn.shape[0], 2) + attn.shape[2:], BF16),
            pltpu.VMEM((width, width), F32),
            pltpu.VMEM((width, width), F32),
            pltpu.VMEM((samples, query_rows, width), BF16),
            pltpu.VMEM((heads * PAIR_ROWS, pair_low.shape[3]), F32),
            pltpu.SemaphoreType.DMA((1,)),
        ]
        + PlaneReduce.scratch(samples, cut, width)
        + PlaneReduce.scratch(samples, 2 * half, width)
        + PlaneReduce.scratch(samples, query_rows, width)
        + RowReduce.scratch(complexes, own, length, rows, width, chips),
        compiler_params=params(collective_id=5, has_side_effects=True),
        name="return_pass",
    )(grads, prob, grad, query, keyval, full, attn, pair_low, normed)


def leave_kernel(
    chips, samples, most_ref, late_ref, query_ref, dquery_ref, dfull_ref, dglogit_ref, tok_ref, single_ref,
    dmid_ref, vec_ref, ada_ref, attn_ref, small_mid, pair_sum,
    tgrad_ref, most_total, late_total, query_total, last_total,
    most_plane, late_plane, query_plane, last_grads_buf, last_plane, dnormed_ref, dapre_ref, cond_ref,
    small_ref, load_sem, *scratch,
):
    place = Place(chips, samples)
    count = len(PlaneReduce.scratch(samples, 64, 128))
    plane = PlaneReduce(place, last_grads_buf, last_plane, scratch[:count])
    scratch = scratch[count:]
    pieces = [
        (LineTotal, most_plane, most_total), (LineTotal, late_plane, late_total),
        (LineTotal, query_plane, query_total),
        (DirectTotal, last_plane, last_total),
    ]
    lines = []
    for kind, buf, total in pieces:
        count = len(kind.scratch(16 * chips, 128, chips))
        lines.append(kind(place, buf, total, 0, buf.shape[0], scratch[:count]))
        scratch = scratch[count:]
    most, late, query, last = lines
    loads = [
        pltpu.make_async_copy(late_ref, late_plane, load_sem.at[0]),
        pltpu.make_async_copy(query_ref, query_plane, load_sem.at[1]),
        pltpu.make_async_copy(most_ref, most_plane, load_sem.at[2]),
    ]
    for load in loads:
        load.start()
    place.barrier(True, True, True)
    for load in loads:
        load.wait()
    groups = [(most, 0), (late, 1), (query, 2), (last, 4)]
    clock = [0]

    def tick():
        t = clock[0] = clock[0] + 1
        for line, behind in groups:
            step = t - behind
            if 1 <= step < line.steps:
                line.advance(step)
            elif step == line.steps:
                line.finish()

    tick()
    last_kernel(
        dquery_ref, dfull_ref, dglogit_ref, tok_ref, single_ref, dmid_ref, vec_ref, ada_ref,
        attn_ref.at[:, 0:1], attn_ref.at[:, 3:4], tgrad_ref, dnormed_ref, dapre_ref, cond_ref,
        small_ref,
    )
    tick()
    last_grads(
        cond_ref[...], dapre_ref[...], dnormed_ref[...], small_mid[...], small_ref[...],
        pair_sum[...], last_grads_buf,
    )
    plane.start()
    tick()
    for k in plane.order:
        plane.depart(k)
    tick()
    plane.hop()
    plane.finish()
    while clock[0] < max(line.steps + behind for line, behind in groups):
        tick()
    plane.drain()


def leave(most, late, query, dquery, dfull, dglogit, tok, single, dmid, vec, ada, attn, small_mid, pair_sum,
          last_rows):
    samples, chips = lax.axis_size("sample"), lax.axis_size("row") // 2
    rows, width = tok.shape
    narrow = single.shape[1]
    halves = [most.shape[0], late.shape[0], query.shape[0], last_rows // 2]
    vmem = pl.BlockSpec(memory_space=pltpu.VMEM)
    return pl.pallas_call(
        functools.partial(leave_kernel, chips, samples),
        in_specs=[ANY] * 3 + [vmem] * 11,
        out_specs=[vmem] * 5,
        out_shape=[jax.ShapeDtypeStruct((rows, width), F32)]
        + [jax.ShapeDtypeStruct((2 * half, width), BF16) for half in halves],
        scratch_shapes=[
            pltpu.VMEM(most.shape, BF16),
            pltpu.VMEM(late.shape, BF16),
            pltpu.VMEM(query.shape, BF16),
            pltpu.VMEM((samples, last_rows, width), BF16),
            pltpu.VMEM((last_rows // 2, width), BF16),
            pltpu.VMEM((rows, width), BF16),
            pltpu.VMEM((rows, width), BF16),
            pltpu.VMEM((rows, narrow), BF16),
            pltpu.VMEM((8, width), F32),
            pltpu.SemaphoreType.DMA((3,)),
        ]
        + PlaneReduce.scratch(samples, last_rows, width)
        + LineTotal.scratch(halves[0], width, chips)
        + LineTotal.scratch(halves[1], width, chips)
        + LineTotal.scratch(halves[2], width, chips)
        + DirectTotal.scratch(halves[3], width, chips),
        compiler_params=params(collective_id=6, has_side_effects=True),
        name="leave",
    )(most, late, query, dquery, dfull, dglogit, tok, single, dmid, vec, ada, attn, small_mid, pair_sum)


def grad_rows(samples, chips, parts):
    unit = 32 * chips
    return -(-sum(parts) // unit) * unit


def store_grads(out_ref, start, left, grads):
    samples, _, width = out_ref.shape
    turned = left.T
    rows = turned.shape[0] // samples
    for grad in grads:
        value = dot(turned, grad).astype(BF16)
        out_ref[:, start : start + rows] = value.reshape(samples, rows, width)
        start += rows
    return start


def pad_grads(out_ref, start):
    samples, rows, width = out_ref.shape
    if start < rows:
        out_ref[:, start:] = jnp.zeros((samples, rows - start, width), BF16)


LATE_OPERANDS = 15


def late_grads_kernel(*refs):
    ins, out_ref, refs = refs[:LATE_OPERANDS], refs[LATE_OPERANDS], refs[LATE_OPERANDS + 1 :]
    bufs, grads, in_sem, out_sem = refs[:LATE_OPERANDS], *refs[LATE_OPERANDS:]
    loads = [
        pltpu.make_async_copy(ref, buf, in_sem.at[i]) for i, (ref, buf) in enumerate(zip(ins, bufs))
    ]
    for load in loads:
        load.start()
    width = out_ref.shape[2]
    stores = []

    def take(i):
        loads[i].wait()
        return bufs[i]

    def put(start, left, right):
        end = store_grads(grads, start, left, right)
        spot = pl.ds(start, end - start)
        store = pltpu.make_async_copy(grads.at[:, spot], out_ref.at[:, spot], out_sem.at[len(stores)])
        store.start()
        stores.append(store)
        return end

    tinput = take(0)[...]
    start = 0
    for i in (1, 2):
        ref = take(i)
        halves = [ref[:, lane : lane + width] for lane in range(0, ref.shape[1], width)]
        start = put(start, tinput, halves)
    start = put(start, take(3)[...], [take(4)[...]])
    start = put(start, take(5)[...], [take(6)[...], take(7)[...]])
    start = put(start, take(8)[...], [take(9)[...], take(10)[...]])
    start = put(start, take(11)[...], [take(12)[...]])
    start = put(start, take(13)[...], [take(14)[...]])
    rows = out_ref.shape[1]
    if start < rows:
        pad_grads(grads, start)
        spot = pl.ds(start, rows - start)
        store = pltpu.make_async_copy(grads.at[:, spot], out_ref.at[:, spot], out_sem.at[len(stores)])
        store.start()
        stores.append(store)
    for store in stores:
        store.wait()


def late_grads(samples, rows, width, operands):
    return pl.pallas_call(
        late_grads_kernel,
        in_specs=[ANY] * LATE_OPERANDS,
        out_specs=ANY,
        out_shape=jax.ShapeDtypeStruct((samples, rows, width), BF16),
        scratch_shapes=[pltpu.VMEM(value.shape, BF16) for value in operands]
        + [
            pltpu.VMEM((samples, rows, width), BF16),
            pltpu.SemaphoreType.DMA((LATE_OPERANDS,)),
            pltpu.SemaphoreType.DMA((8,)),
        ],
        compiler_params=params(),
        name="late_grads",
    )(*operands)


def store_ready(out_ref, start, ready):
    samples, _, width = out_ref.shape
    for value in ready:
        size = value.shape[0] // samples
        out_ref[:, start : start + size] = value.astype(BF16).reshape(samples, size, width)
        start += size
    return start


def query_grads(normed_in, dquery, dkey_w, dvalue_w, out_ref):
    start = store_grads(out_ref, 0, normed_in, [dquery])
    pad_grads(out_ref, store_ready(out_ref, start, [dkey_w, dvalue_w]))


def last_grads(cond, dapre, dnormed, small_mid, small_last, pair_sum, out_ref):
    samples, rows, width = out_ref.shape
    start = store_grads(out_ref, 0, cond, [dapre, dnormed])
    pairs = jnp.concatenate(
        [pair_sum, jnp.zeros((pair_sum.shape[0], width - pair_sum.shape[1]), F32)], axis=1
    )
    small = jnp.concatenate([small_mid, small_last, pairs], axis=0).astype(BF16)
    for sample in range(samples):
        out_ref[sample, start : start + small.shape[0]] = small
    pad_grads(out_ref, start + small.shape[0])


def query_grads_kernel(normed_in, dquery, dkey_w, dvalue_w, out_ref):
    query_grads(normed_in[...], dquery[...], dkey_w[...], dvalue_w[...], out_ref)


def last_grads_kernel(cond, dapre, dnormed, small_mid, small_last, pair_sum, out_ref):
    last_grads(
        cond[...], dapre[...], dnormed[...], small_mid[...], small_last[...], pair_sum[...], out_ref
    )


def grads_call(kernel, samples, rows, width, operands, name):
    return pl.pallas_call(
        kernel,
        out_shape=jax.ShapeDtypeStruct((samples, rows, width), BF16),
        compiler_params=params(),
        name=name,
    )(*operands)


def deal_kernel(
    most, late, early, last, pairw,
    gain_ref, ada_ref, ada_bias_ref, zero_ref, zero_bias_ref, attn_ref, query_bias_ref, out_ref,
    pair_gain_ref, pair_weight_ref, tin_ref, tout_ref,
):
    slim, wide = ada_ref.shape[1], attn_ref.shape[1]
    width = ada_ref.shape[2]
    spot = lax.axis_index("sample")
    part = lambda ref, start, size: ref[start : start + size].astype(F32)
    for which in range(2):
        for lane in range(2):
            tin_ref[which, :, lane * width : (lane + 1) * width] = part(
                most, (2 * which + lane) * wide, wide
            )
    tout_ref[...] = part(most, 4 * wide, tout_ref.shape[0])
    for which in range(2):
        ada_ref[which] = part(last, which * slim, slim)
        ada_ref[2 + which] = part(late, which * slim, slim)
        zero_ref[which] = part(late, (2 + which) * slim, slim)
    out_ref[...] = part(late, 4 * slim, wide)
    for which in range(3):
        attn_ref[which] = part(early, which * wide, wide)
    attn_ref[3] = part(late, 4 * slim + wide, wide)
    heads, thin = pair_weight_ref.shape[1], pair_weight_ref.shape[0]
    small = last[2 * slim : 2 * slim + 16]
    pairs = last[2 * slim + 16 : 2 * slim + 16 + heads, 0 : pairw.shape[1]]

    def choose(size, count):
        row = lax.broadcasted_iota(jnp.int32, (size, count), 0)
        lane = lax.broadcasted_iota(jnp.int32, (size, count), 1)
        return (row == lane + spot * count).astype(BF16)

    lines = dot(small, choose(width, wide))
    narrow = slim * (width // wide)
    slims = dot(small[:, 0:narrow], choose(narrow, slim))
    ada_bias_ref[0:1] = lines[8:9]
    ada_bias_ref[1:2] = lines[0:1]
    zero_bias_ref[...] = lines[1:3]
    query_bias_ref[...] = lines[9:10]
    gain_ref[0:1] = slims[10:11]
    gain_ref[1:2] = slims[3:4]
    turn = lax.broadcasted_iota(jnp.int32, (thin, pairw.shape[1]), 0)
    lane = lax.broadcasted_iota(jnp.int32, (thin, pairw.shape[1]), 1)
    pair_weight_ref[...] = dot_nt((lane == turn + spot * thin).astype(BF16), pairs)
    gains = jnp.sum(pairw[8 : 8 + heads] * pairs.astype(F32), axis=0, keepdims=True) / pairw[0:1]
    pair_gain_ref[...] = lax.dot_general(
        gains, choose(pairw.shape[1], thin).astype(F32), (((1,), (0,)), ((), ())),
        precision=lax.Precision.HIGHEST, preferred_element_type=F32,
    )


def deal(most, late, early, last, pairw, shapes):
    return pl.pallas_call(
        deal_kernel,
        out_shape=[jax.ShapeDtypeStruct(shape, F32) for shape in shapes],
        compiler_params=params(),
        name="deal",
    )(most, late, early, last, pairw)


def local(
    tokens, single, pair, token_count, pair_mask, cotangent, cond_gain, ada_weight, ada_bias,
    zero_weight, zero_bias, attn_weight, query_bias, out_weight, pair_gain, pair_weight,
    trans_in, trans_out,
):
    complexes, samples_own, rows_dev, width = tokens.shape
    narrow = single.shape[3]
    heads, length = pair_weight.shape[1], pair.shape[2]
    samples, chips = lax.axis_size("sample"), lax.axis_size("row") // 2
    rows = complexes * samples_own * rows_dev
    flat = lambda value: value.reshape(rows, value.shape[-1])
    block = lambda value: value.reshape(complexes, samples_own, rows_dev, width)
    tok, sing, cot = flat(tokens), flat(single), flat(cotangent)
    small = (cond_gain, ada_bias, zero_bias, query_bias[None], pair_gain[None], pair_weight)
    weights, (full, normed_in, vec, pairw, pair_low, bias) = enter(
        token_count, tok, sing, pair, pair_mask, small,
        [ada_weight, attn_weight, zero_weight, out_weight[None], trans_out[None]],
        complexes, heads,
    )
    _, ada, attn, zero, out_w, tout = weights
    tin, att, prob, query, gate, keyval = attend(trans_in, normed_in, full, attn, vec, bias)
    normed_in = flat(normed_in)
    (
        output, dmid, datt, dglogit, gated, dabranch, dza, dzb, tcond, dtpre, dtin, tinput,
        dfirst, dsecond, hidden, dtbranch, small_mid,
    ) = middle_pass(
        token_count, flat(att), flat(gate), tok, sing, cot, vec, ada, zero, out_w, tin, tout,
        complexes, rows_dev,
    )
    slim, wide = narrow // samples, width // samples
    late_parts = [wide] * 4 + [tout.shape[2]] + [slim] * 4 + [wide] * 2
    query_parts = [wide] * 3
    last_parts = [slim] * 2 + [16 + heads]
    late_rows, query_rows, last_rows = (
        grad_rows(samples, chips, parts) for parts in (late_parts, query_parts, last_parts)
    )
    late = late_grads(
        samples, late_rows, width,
        (tinput, dfirst, dsecond, hidden, dtbranch, tcond, dtpre, dtin, sing, dza, dzb, gated,
         dabranch, normed_in, dglogit),
    )
    datt = block(datt)
    if length <= 512:
        dquery, dfull, pair_sum, most, late, early = return_pass(
            late, sum(late_parts[:5]), prob, datt, query, keyval, full, attn, pair_low, normed_in, query_rows
        )
        tgrad, most, late, early, last = leave(
            most, late, early, flat(dquery), flat(dfull), dglogit, tok, sing, dmid, vec, ada, attn,
            small_mid, pair_sum, last_rows,
        )
    else:
        dquery, dfull, dbias, dkey_w, dvalue_w = attend_back(prob, datt, query, keyval, full, attn)
        dfull = flat(reduce_rows(dfull, 2))
        pair_sum = pair_grad(dbias, pair_low)
        dquery = flat(dquery)
        tgrad, dnormed, dapre, cond, small_last = last_pass(
            dquery, dfull, dglogit, tok, sing, dmid, vec, ada, attn
        )
        early = grads_call(
            query_grads_kernel, samples, query_rows, width, (normed_in, dquery, dkey_w, dvalue_w),
            "query_grads",
        )
        last = grads_call(
            last_grads_kernel, samples, last_rows, width,
            (cond, dapre, dnormed, small_mid, small_last, pair_sum), "last_grads",
        )
        late = reduce_grads(late, 3)
        most, late = late[: sum(late_parts[:5])], late[sum(late_parts[:5]) :]
        early = reduce_grads(early, 4)
        last = reduce_grads(last, 2)

    shapes = [
        cond_gain.shape, ada_weight.shape, ada_bias.shape, zero_weight.shape, zero_bias.shape,
        attn_weight.shape, (1,) + query_bias.shape, out_weight.shape, (1,) + pair_gain.shape,
        pair_weight.shape, trans_in.shape, trans_out.shape,
    ]
    grads = list(deal(most, late, early, last, pairw, shapes))
    for place in (6, 8):
        grads[place] = grads[place][0]
    return (output.reshape(tokens.shape), tgrad.reshape(tokens.shape), *grads)


def solution(mesh):
    rowwise = P(None, "sample", "row", None)
    return jax.shard_map(
        local,
        mesh=mesh,
        in_specs=(
            rowwise,
            rowwise,
            P(None, "row", None, None),
            P(),
            P(None, "row", None),
            rowwise,
            P(None, "sample"),
            P(None, "sample", None),
            P(None, "sample"),
            P(None, "sample", None),
            P(None, "sample"),
            P(None, "sample", None),
            P("sample"),
            P("sample", None),
            P("sample"),
            P("sample", None),
            P(None, "sample", None),
            P("sample", None),
        ),
        out_specs=(
            rowwise,
            rowwise,
            P(None, "sample"),
            P(None, "sample", None),
            P(None, "sample"),
            P(None, "sample", None),
            P(None, "sample"),
            P(None, "sample", None),
            P("sample"),
            P("sample", None),
            P("sample"),
            P("sample", None),
            P(None, "sample", None),
            P("sample", None),
        ),
        check_vma=False,
    )
```

```python
import functools

import jax
import jax.numpy as jnp
from jax import lax
from jax.experimental import pallas as pl
from jax.experimental.pallas import tpu as pltpu
from jax.sharding import PartitionSpec as P

EPSILON = 1e-05
MASKED = -1000000000.0
F32 = jnp.float32
BF16 = jnp.bfloat16
VMEM_LIMIT = 60 << 20


def center_rows(value):
    center = value - jnp.mean(value, axis=-1, keepdims=True)
    rstd = lax.rsqrt(jnp.mean(center * center, axis=-1, keepdims=True) + EPSILON)
    return center * rstd, rstd


def dot(left, right):
    return lax.dot_general(left, right, (((1,), (0,)), ((), ())), preferred_element_type=F32)


def dot_nt(left, right):
    return lax.dot_general(left, right, (((1,), (1,)), ((), ())), preferred_element_type=F32)


def dot_tn(left, right):
    return lax.dot_general(left, right, (((0,), (0,)), ((), ())), preferred_element_type=F32)


def params(**extra):
    return pltpu.CompilerParams(vmem_limit_bytes=VMEM_LIMIT, **extra)


MESH = pl.DeviceIdType.MESH
ANY = pl.BlockSpec(memory_space=pl.ANY)


class Place:
    def __init__(self, chips, samples):
        self.row = lax.axis_index("row")
        self.chip = self.row // 2
        self.core = self.row % 2
        self.sample = lax.axis_index("sample")
        self.chips, self.samples = chips, samples

    def twin(self):
        return (self.row + 1 - 2 * self.core, self.sample)

    def peer(self, k):
        return (self.row, jnp.bitwise_xor(self.sample, k))

    def up(self):
        return (self.row + 2, self.sample)

    def down(self):
        return (self.row - 2, self.sample)

    def along(self, k):
        return (jnp.bitwise_xor(self.row, 2 * k), self.sample)

    def barrier(self, plane, line, whole_line=False):
        bar = pltpu.get_barrier_semaphore()

        def greet(device):
            pl.semaphore_signal(bar, inc=1, device_id=device, device_id_type=MESH)

        greet(self.twin())
        if plane:
            for k in range(1, self.samples):
                greet(self.peer(k))
        if line and not whole_line:

            @pl.when(self.chip > 0)
            def _():
                greet(self.down())

            @pl.when(self.chip < self.chips - 1)
            def _():
                greet(self.up())

        count = 1 + (self.samples - 1 if plane else 0)
        if whole_line:
            for k in range(1, self.chips):
                greet(self.along(k))
            count = count + self.chips - 1
        elif line:
            count = count + jnp.minimum(self.chip, 1) + jnp.minimum(self.chips - 1 - self.chip, 1)
        pl.semaphore_wait(bar, count)


def send(source, target, send_sem, recv_sem, device):
    return pltpu.make_async_remote_copy(
        source, target, send_sem, recv_sem, device_id=device, device_id_type=MESH
    )


def half_of(ref, core):
    if ref.shape[0] > 1:
        size = ref.shape[0] // 2
        return ref.at[pl.ds(core * size, size)]
    size = ref.shape[1] // 2
    return ref.at[:, pl.ds(pl.multiple_of(core * size, 16), size)]


class PlaneGather:
    @staticmethod
    def sems(arrays, samples):
        dma = pltpu.SemaphoreType.DMA
        return [dma((arrays, samples))] * 4 + [dma((arrays, 2))] * 2

    def __init__(self, place, shards, fulls, sems):
        self.place, self.shards, self.fulls = place, shards, fulls
        self.out, self.come, self.swap_out, self.swap_come, self.hop_out, self.hop_come = sems
        self.relayed = place.samples == 4
        self.direct = [1, 2] if self.relayed else list(range(1, place.samples))

    def owner(self, k):
        return jnp.bitwise_xor(self.place.sample, k)

    def half(self, i, k):
        return half_of(self.fulls[i].at[self.owner(k)], self.place.core)

    def copy(self, i, k):
        slot = self.half(i, 0)
        return send(
            half_of(self.shards[i], self.place.core), slot, self.out.at[i, k], self.come.at[i, k],
            self.place.peer(k),
        )

    def hop(self, i, k):
        slot = self.half(i, k)
        size = slot.shape[1] // 2
        piece = slot.at[:, pl.ds((k - 1) * size, size)]
        return send(piece, piece, self.hop_out.at[i, k - 1], self.hop_come.at[i, k - 1], self.place.peer(3 - k))

    def swap(self, i, k):
        slot = self.half(i, k)
        return send(slot, slot, self.swap_out.at[i, k], self.swap_come.at[i, k], self.place.twin())

    def keep(self, i):
        return send(
            self.shards[i], self.fulls[i].at[self.place.sample], self.swap_out.at[i, 0],
            self.swap_come.at[i, 0], self.place.twin(),
        )

    def start(self, i):
        for k in self.direct:
            self.copy(i, k).start()
        self.keep(i).start()

    def relay(self, i):
        for k in self.direct:
            self.copy(i, k).wait_recv()
            if self.relayed:
                self.hop(i, k).start()
            self.swap(i, k).start()

    def settle(self, i):
        if self.relayed:
            for k in self.direct:
                self.hop(i, k).wait_recv()
            self.swap(i, 3).start()

    def arrive(self, i):
        self.keep(i).wait_recv()
        for k in range(1, self.place.samples):
            self.swap(i, k).wait_recv()

    def finish(self, arrived=()):
        for i in range(len(self.shards)):
            if i not in arrived:
                self.arrive(i)
            self.keep(i).wait_send()
            for k in self.direct:
                self.copy(i, k).wait_send()
                if self.relayed:
                    self.hop(i, k).wait_send()
            for k in range(1, self.place.samples):
                self.swap(i, k).wait_send()


class LineSpread:
    @staticmethod
    def sems(lines, chips):
        dma = pltpu.SemaphoreType.DMA
        return [dma((lines, chips))] * 6

    def __init__(self, place, line, slot, sems):
        self.place, self.line, self.slot = place, line, slot
        self.up_out, self.up_come, self.down_out, self.down_come, self.swap_out, self.swap_come = sems

    def step(self, upward, t):
        place, last = self.place, self.place.chips - 1
        z = place.chip
        if upward:
            out_chip, has_out = z - t + 1, (z >= t - 1) & (z < last)
            in_chip, has_in = z - t, z >= t
            sems, device = (self.up_out, self.up_come), place.up()
        else:
            out_chip, has_out = z + t - 1, (z + t - 1 <= last) & (z > 0)
            in_chip, has_in = z + t, z + t <= last
            sems, device = (self.down_out, self.down_come), place.down()
        make = lambda chip: send(
            self.slot(chip), self.slot(chip),
            sems[0].at[self.line, t], sems[1].at[self.line, t], device,
        )
        return (has_out, lambda: make(out_chip)), (has_in, in_chip, lambda: make(in_chip))

    def hand_over(self, chip):
        slot = self.slot(chip)
        return send(
            slot, slot, self.swap_out.at[self.line, chip], self.swap_come.at[self.line, chip],
            self.place.twin(),
        )

    def depart(self, t):
        for upward in (True, False):
            (has_out, copy), _ = self.step(upward, t)

            @pl.when(has_out)
            def _():
                copy().start()

    def advance(self, t):
        for upward in (True, False):
            _, (has_in, chip, copy) = self.step(upward, t)

            @pl.when(has_in)
            def _():
                copy().wait_recv()

        if t + 1 < self.place.chips:
            self.depart(t + 1)
        for upward in (True, False):
            _, (has_in, chip, copy) = self.step(upward, t)

            @pl.when(has_in)
            def _():
                self.hand_over(chip).start()

    def finish(self):
        for t in range(1, self.place.chips):
            for upward in (True, False):
                (has_out, copy), (has_in, chip, _) = self.step(upward, t)

                @pl.when(has_out)
                def _():
                    copy().wait_send()

                @pl.when(has_in)
                def _():
                    self.hand_over(chip).wait()


class LineReduce:
    @staticmethod
    def sems(lines, chips):
        dma = pltpu.SemaphoreType.DMA
        return [dma((lines, chips))] * 4

    def __init__(self, place, line, slot, up_buf, down_buf, sems):
        self.place, self.line, self.slot = place, line, slot
        self.bufs = (up_buf, down_buf)
        self.up_out, self.up_come, self.down_out, self.down_come = sems

    def step(self, upward, t):
        place, last = self.place, self.place.chips - 1
        z, distance = place.chip, place.chips - t
        buf = self.bufs[0 if upward else 1]
        if upward:
            block, has_out, has_before = z + distance, z + distance <= last, z > 0
            has_in = (z > 0) & (z - 1 + distance <= last)
            sems, device = (self.up_out, self.up_come), place.up()
        else:
            block, has_out, has_before = z - distance, z - distance >= 0, z < last
            has_in = (z < last) & (z + 1 - distance >= 0)
            sems, device = (self.down_out, self.down_come), place.down()
        copy = lambda chip: send(
            self.slot(chip), buf.at[self.line, t - 1],
            sems[0].at[self.line, t], sems[1].at[self.line, t], device,
        )
        return block, has_out, has_before, has_in, copy, buf

    def advance(self, t):
        for upward in (True, False):
            block, has_out, has_before, _, copy, buf = self.step(upward, t)
            before = self.step(upward, t - 1)[4] if t > 1 else None

            @pl.when(has_out)
            def _():
                if t > 1:

                    @pl.when(has_before)
                    def _():
                        before(block).wait_recv()
                        slot = self.slot(block)
                        slot[...] = (
                            slot[...].astype(F32) + buf[self.line, t - 2].astype(F32)
                        ).astype(slot.dtype)

                copy(block).start()

    def finish(self):
        last_step = self.place.chips - 1
        slot = self.slot(self.place.chip)
        for upward in (True, False):
            _, _, _, has_in, copy, buf = self.step(upward, last_step)

            @pl.when(has_in)
            def _():
                copy(self.place.chip).wait_recv()
                slot[...] = (
                    slot[...].astype(F32) + buf[self.line, last_step - 1].astype(F32)
                ).astype(slot.dtype)

        for t in range(1, self.place.chips):
            for upward in (True, False):
                block, has_out, _, _, copy, _ = self.step(upward, t)

                @pl.when(has_out)
                def _():
                    copy(block).wait_send()


class RowGather:
    @staticmethod
    def sems(lines, chips):
        return [pltpu.SemaphoreType.DMA((lines,))] + LineSpread.sems(lines, chips)

    def __init__(self, place, part, full, line, sems):
        self.place, self.part, self.full, self.index = place, part, full, line
        self.spot = (line // part.shape[1], line % part.shape[1])
        self.keep_sem = sems[0]
        self.rows = part.shape[2]
        self.line = LineSpread(place, line, self.slot, sems[1:])

    def slot(self, chip):
        start = (2 * chip + self.place.core) * self.rows
        return self.full.at[self.spot + (pl.ds(pl.multiple_of(start, 16), self.rows),)]

    def keep(self):
        return pltpu.make_async_copy(
            self.part.at[self.spot], self.slot(self.place.chip), self.keep_sem.at[self.index]
        )

    def start(self):
        self.keep().start()

    def begin(self):
        self.keep().wait()
        self.line.depart(1)
        self.line.hand_over(self.place.chip).start()

    def finish(self):
        self.line.finish()
        self.line.hand_over(self.place.chip).wait()


class RowReduce:
    @staticmethod
    def scratch(complexes, samples_own, length, rows, width, chips):
        dma = pltpu.SemaphoreType.DMA
        hop = pltpu.VMEM((complexes, chips - 1, samples_own, rows, width), BF16)
        return [
            pltpu.VMEM((complexes, samples_own, chips, rows, width), BF16), hop, hop,
        ] + [dma((complexes,))] * 3 + LineReduce.sems(complexes, chips)

    def __init__(self, place, part, own, which, scratch):
        self.place, self.part, self.own, self.which = place, part, own, which
        self.sums, up_buf, down_buf = scratch[:3]
        self.swap_out, self.swap_come, self.keep_sem = scratch[3:6]
        self.line = LineReduce(place, which, self.slot, up_buf, down_buf, scratch[6:])

    def slot(self, chip):
        return self.sums.at[self.which, :, chip]

    def first_swap(self):
        return send(
            self.part.at[self.which, :, :, 1 - self.place.core], self.sums.at[self.which],
            self.swap_out.at[self.which], self.swap_come.at[self.which], self.place.twin(),
        )

    def begin(self):
        self.first_swap().wait_recv()
        for sample in range(self.part.shape[1]):
            for chip in range(self.place.chips):
                mine = self.part[self.which, sample, chip, self.place.core].astype(F32)
                self.sums[self.which, sample, chip] = (
                    mine + self.sums[self.which, sample, chip].astype(F32)
                ).astype(BF16)

    def keep(self):
        return pltpu.make_async_copy(
            self.slot(self.place.chip), self.own.at[self.which], self.keep_sem.at[self.which]
        )

    def finish(self):
        self.line.finish()
        self.keep().start()

    def drain(self):
        self.first_swap().wait_send()
        self.keep().wait()


def reduce_rows_kernel(chips, samples, part_ref, own_ref, *scratch):
    place = Place(chips, samples)
    moves = [
        RowReduce(place, part_ref, own_ref, which, scratch) for which in range(part_ref.shape[0])
    ]
    place.barrier(False, True)
    for move in moves:
        move.first_swap().start()
    for move in moves:
        move.begin()
        move.line.advance(1)
    for t in range(2, chips):
        for move in moves:
            move.line.advance(t)
    for move in moves:
        move.finish()
    for move in moves:
        move.drain()


def reduce_rows(part, collective_id):
    samples, chips = lax.axis_size("sample"), lax.axis_size("row") // 2
    complexes, own, length, width = part.shape
    rows = length // (2 * chips)
    return pl.pallas_call(
        functools.partial(reduce_rows_kernel, chips, samples),
        in_specs=[pl.BlockSpec(memory_space=pltpu.VMEM)],
        out_specs=ANY,
        out_shape=jax.ShapeDtypeStruct((complexes, own, rows, width), part.dtype),
        scratch_shapes=RowReduce.scratch(complexes, own, length, rows, width, chips),
        compiler_params=params(collective_id=collective_id, has_side_effects=True),
        name="reduce_rows",
    )(part.reshape(complexes, own, chips, 2, rows, width))


class PlaneReduce:
    @staticmethod
    def scratch(samples, rows, width):
        dma = pltpu.SemaphoreType.DMA
        half = rows // 2
        return [
            pltpu.VMEM((samples, half, width), BF16),
            pltpu.VMEM((2 * samples - 2, half // 2, width), BF16),
            pltpu.VMEM((half, width), BF16),
        ] + [dma((samples,))] * 3 + [dma((2 * samples,))] * 2

    def __init__(self, place, grads, plane, scratch):
        self.place, self.grads, self.plane = place, grads, plane
        self.sums, self.come_buf, self.mine = scratch[:3]
        self.swap_out, self.swap_come, self.load_sem, self.out, self.come = scratch[3:]
        self.half = grads.shape[1] // 2
        self.relayed = place.samples == 4
        self.order = [3, 1, 2, 0] if self.relayed else list(range(1, place.samples)) + [0]

    def shard(self, k):
        return jnp.bitwise_xor(self.place.sample, k)

    def half_rows(self, core):
        return pl.ds(pl.multiple_of(core * self.half, 16), self.half)

    def part(self, k, which):
        return self.sums.at[self.shard(k), pl.ds(which * (self.half // 2), self.half // 2)]

    def swap(self, k):
        return send(
            self.grads.at[self.shard(k), self.half_rows(1 - self.place.core)],
            self.sums.at[self.shard(k)],
            self.swap_out.at[k], self.swap_come.at[k], self.place.twin(),
        )

    def load(self, k):
        return pltpu.make_async_copy(
            self.grads.at[self.shard(k), self.half_rows(self.place.core)],
            self.mine, self.load_sem.at[k],
        )

    def copy(self, k, which, peer, slot):
        return send(
            self.part(k, which), self.come_buf.at[slot], self.out.at[slot], self.come.at[slot],
            self.place.peer(peer),
        )

    def copies(self, k):
        if not self.relayed:
            return [self.copy(k, which, k, 2 * (k - 1) + which) for which in range(2)] if k else []
        return {
            3: lambda: [self.copy(3, 0, 1, 1), self.copy(3, 1, 2, 4)],
            1: lambda: [self.copy(1, 0, 1, 0)],
            2: lambda: [self.copy(2, 1, 2, 3)],
            0: lambda: [],
        }[k]()

    def onward(self):
        return [(self.copy(2, 0, 2, 2), 1, (2, 0)), (self.copy(1, 1, 1, 5), 4, (1, 1))]

    def arrived(self, slot):
        self.copy(0, 0, 1, slot).wait_recv()
        return self.come_buf[slot].astype(F32)

    def start(self):
        for k in self.order:
            self.swap(k).start()
        self.load(self.order[0]).start()

    def depart(self, k):
        place = self.order.index(k)
        self.load(k).wait()
        self.swap(k).wait_recv()
        slot = self.sums.at[self.shard(k)]
        slot[...] = (self.mine[...].astype(F32) + slot[...].astype(F32)).astype(BF16)
        for copy in self.copies(k):
            copy.start()
        if place + 1 < len(self.order):
            self.load(self.order[place + 1]).start()

    def hop(self):
        if self.relayed:
            for copy, slot, piece in self.onward():
                ref = self.part(*piece)
                ref[...] = (ref[...].astype(F32) + self.arrived(slot)).astype(BF16)
                copy.start()

    def finish(self):
        size = self.half // 2
        for which in range(2):
            value = self.part(0, which)[...].astype(F32)
            if self.relayed:
                slots = [3 * which, 3 * which + 2]
            else:
                slots = [2 * (k - 1) + which for k in range(1, self.place.samples)]
            for slot in slots:
                value = value + self.arrived(slot)
            self.plane[which * size : (which + 1) * size] = value.astype(BF16)

    def drain(self):
        for k in self.order:
            self.swap(k).wait_send()
            for copy in self.copies(k):
                copy.wait_send()
        if self.relayed:
            for copy, _, _ in self.onward():
                copy.wait_send()


class LineTotal:
    @staticmethod
    def scratch(size, width, chips):
        hop = pltpu.VMEM((1, chips - 1, size // chips, width), BF16)
        return [hop, hop] + LineReduce.sems(1, chips) + LineSpread.sems(1, chips)

    def __init__(self, place, plane, total, start, size, scratch):
        self.place, self.plane, self.total, self.start = place, plane, total, start
        self.half = total.shape[0] // 2
        self.size = size // place.chips
        self.reduce = LineReduce(place, 0, self.block, scratch[0], scratch[1], scratch[2:6])
        self.spread = LineSpread(place, 0, self.slot, scratch[6:])

    def block(self, chip):
        return self.plane.at[pl.ds(pl.multiple_of(self.start + chip * self.size, 16), self.size)]

    def slot(self, chip):
        start = self.place.core * self.half + self.start + chip * self.size
        return self.total.at[pl.ds(pl.multiple_of(start, 16), self.size)]

    @property
    def steps(self):
        return 2 * self.place.chips - 1

    def advance(self, t):
        if t < self.place.chips:
            self.reduce.advance(t)
            return
        t -= self.place.chips - 1
        if t == 1:
            self.reduce.finish()
            own = self.slot(self.place.chip)
            own[...] = self.block(self.place.chip)[...]
            self.spread.depart(1)
            self.spread.hand_over(self.place.chip).start()
        else:
            self.spread.advance(t - 1)

    def finish(self):
        self.spread.advance(self.place.chips - 1)
        self.spread.finish()
        self.spread.hand_over(self.place.chip).wait()


class DirectTotal:
    steps = 4

    @staticmethod
    def scratch(size, width, chips):
        dma = pltpu.SemaphoreType.DMA
        return [pltpu.VMEM((chips - 1, size // chips, width), BF16)] + [dma((chips,))] * 6

    def __init__(self, place, plane, total, start, size, scratch):
        self.place, self.plane, self.total, self.start = place, plane, total, start
        self.half = total.shape[0] // 2
        self.size = size // place.chips
        self.buf = scratch[0]
        self.out, self.come, self.back_out, self.back_come, self.swap_out, self.swap_come = scratch[1:]

    def chip(self, k):
        return jnp.bitwise_xor(self.place.chip, k)

    def block(self, chip):
        return self.plane.at[pl.ds(pl.multiple_of(self.start + chip * self.size, 16), self.size)]

    def slot(self, chip):
        start = self.place.core * self.half + self.start + chip * self.size
        return self.total.at[pl.ds(pl.multiple_of(start, 16), self.size)]

    def there(self, k):
        return send(
            self.block(self.chip(k)), self.buf.at[k - 1], self.out.at[k], self.come.at[k],
            self.place.along(k),
        )

    def back(self, k):
        own = self.slot(self.place.chip)
        return send(own, own, self.back_out.at[k], self.back_come.at[k], self.place.along(k))

    def swap(self, k):
        slot = self.slot(self.chip(k))
        return send(slot, slot, self.swap_out.at[k], self.swap_come.at[k], self.place.twin())

    def advance(self, t):
        peers = range(1, self.place.chips)
        if t == 1:
            for k in peers:
                self.there(k).start()
        elif t == 2:
            value = self.block(self.place.chip)[...].astype(F32)
            for k in peers:
                self.there(k).wait_recv()
                value = value + self.buf[k - 1].astype(F32)
            own = self.slot(self.place.chip)
            own[...] = value.astype(BF16)
            for k in peers:
                self.back(k).start()
            self.swap(0).start()
        else:
            for k in peers:
                self.back(k).wait_recv()
                self.swap(k).start()

    def finish(self):
        for k in range(1, self.place.chips):
            self.there(k).wait_send()
            self.back(k).wait_send()
        for k in range(self.place.chips):
            self.swap(k).wait()


def reduce_grads_kernel(chips, samples, grads_ref, total_ref, *scratch):
    place = Place(chips, samples)
    count = len(PlaneReduce.scratch(samples, 64, 128))
    plane_buf = scratch[0]
    plane = PlaneReduce(place, grads_ref, plane_buf, scratch[1 : 1 + count])
    line = LineTotal(place, plane_buf, total_ref, 0, plane_buf.shape[0], scratch[1 + count :])
    place.barrier(True, True)
    plane.start()
    for k in plane.order:
        plane.depart(k)
    plane.hop()
    plane.finish()
    for t in range(1, 2 * chips - 1):
        line.advance(t)
    line.finish()
    plane.drain()


def reduce_grads(grads, collective_id):
    chips = lax.axis_size("row") // 2
    samples, rows, width = grads.shape
    return pl.pallas_call(
        functools.partial(reduce_grads_kernel, chips, samples),
        in_specs=[pl.BlockSpec(memory_space=pltpu.VMEM)],
        out_specs=pl.BlockSpec(memory_space=pltpu.VMEM),
        out_shape=jax.ShapeDtypeStruct((rows, width), BF16),
        scratch_shapes=[pltpu.VMEM((rows // 2, width), BF16)]
        + PlaneReduce.scratch(samples, rows, width)
        + LineTotal.scratch(rows // 2, width, chips),
        compiler_params=params(collective_id=collective_id, has_side_effects=True),
        name="reduce_grads",
    )(grads)


def joined(ref, which=0):
    samples, _, rows, cols = ref.shape
    return ref[:, which].reshape(samples * rows, cols)


def head_windows(heads, head_dim):
    windows, head = [], 0
    while head < heads:
        start = head * head_dim // 128 * 128
        start = min(start, heads * head_dim - 256)
        inside = []
        while head < heads and (head + 1) * head_dim <= start + 256:
            inside.append(head)
            head += 1
        windows.append((start, inside))
    return windows


def head_mask(start, head, head_dim):
    lane = lax.broadcasted_iota(jnp.int32, (1, 256), 1) + start
    return (lane >= head * head_dim) & (lane < (head + 1) * head_dim)


def stack_heads(rows, start, inside, head_dim):
    zero = jnp.zeros_like(rows)
    return jnp.concatenate(
        [jnp.where(head_mask(start, head, head_dim), rows, zero) for head in inside], axis=0
    )


def unstack_heads(stacked, start, inside, head_dim):
    rows = stacked.shape[0] // len(inside)
    total = None
    for place, head in enumerate(inside):
        piece = jnp.where(
            head_mask(start, head, head_dim), stacked[place * rows : (place + 1) * rows], 0.0
        )
        total = piece if total is None else total + piece
    return total


def join_windows(parts, width):
    tiles = [None] * (width // 128)
    for start, value in parts:
        for half in range(2):
            place = start // 128 + half
            piece = value[:, half * 128 : (half + 1) * 128]
            tiles[place] = piece if tiles[place] is None else tiles[place] + piece
    return jnp.concatenate(tiles, axis=1)


PACK_ROWS, PACK_LANES = 64, 256


def pack_small(cond_gain, ada_bias, zero_bias, query_bias, pair_gain, pair_weight):
    def line(ref):
        value = ref[...].astype(F32)
        value = value.reshape(-1, value.shape[-1])
        return jnp.pad(value, ((0, 0), (0, PACK_LANES - value.shape[1])))

    rows = [line(ref) for ref in (cond_gain, ada_bias, zero_bias, query_bias, pair_gain, pair_weight)]
    left = PACK_ROWS - 8 - pair_weight.shape[0]
    return jnp.concatenate(rows + [jnp.zeros((left, PACK_LANES), F32)], axis=0).astype(BF16)


def unpack_small(packed, narrow, width, pair_width, heads):
    samples = packed.shape[0]

    def spread(size):
        count = size // samples
        total = None
        for sample in range(samples):
            lane = lax.broadcasted_iota(jnp.int32, (PACK_LANES, size), 0)
            spot = lax.broadcasted_iota(jnp.int32, (PACK_LANES, size), 1)
            move = ((spot == lane + count * sample) & (lane < count)).astype(BF16)
            piece = dot(packed[sample, 0:32], move)
            total = piece if total is None else total + piece
        return total

    gains = jnp.pad(spread(narrow)[0:2], ((0, 0), (0, width - narrow)))
    vec = jnp.concatenate([gains, spread(width)[2:7], jnp.zeros((1, width), F32)], axis=0)
    pairs = spread(pair_width)
    return vec, pairs[7:8], pairs[8 : 8 + heads]


def pair_block(count_ref, first_row, complex_id, start, pair_ref, mask_ref, gain, weight, low_ref, bias_ref):
    rows, length = pair_ref.shape[1], pair_ref.shape[2]
    count = count_ref[complex_id]
    lines = []
    for row in range(rows):
        normed, _ = center_rows(pair_ref[0, row].astype(F32))
        low = (normed * gain).astype(BF16)
        low_ref[0, row] = low
        lines.append(dot_nt(weight, low))
    bias = jnp.stack(lines, axis=1)
    own = first_row + start + lax.broadcasted_iota(jnp.int32, (rows, length), 0)
    key = lax.broadcasted_iota(jnp.int32, (rows, length), 1)
    allowed = (key < count) & ((mask_ref[0] == 1) | (own == key) | (own >= count))
    bias_ref[0] = jnp.where(allowed[None], bias, MASKED)


PAIR_ROWS = 8


def enter_kernel(arrays, chips, samples, count_ref, tok_ref, single_ref, pair_ref, mask_ref, *refs):
    small, refs = refs[:6], refs[6:]
    shards, refs = refs[: arrays - 1], refs[arrays - 1 :]
    fulls, refs = refs[:arrays], refs[arrays:]
    full_ref, normed_ref, vec_ref, pairw_ref, low_ref, bias_ref = refs[:6]
    own_pack, packed, ada_buf, load_sem = refs[6:10]
    sems = refs[10:]
    place = Place(chips, samples)
    own_pack[0] = pack_small(*small)
    shards = (own_pack, shards[0].at[pl.ds(0, 2)]) + shards[1:] + (shards[0].at[pl.ds(2, 2)],)
    ada_full = fulls[1]
    fulls = (fulls[0], ada_full.at[:, pl.ds(0, 2)]) + fulls[2:] + (ada_full.at[:, pl.ds(2, 2)],)
    arrays += 1
    count = len(PlaneGather.sems(arrays, samples))
    move = PlaneGather(place, shards, fulls, sems[:count])
    complexes, own = normed_ref.shape[:2]
    lines = [
        RowGather(place, normed_ref, full_ref, line, sems[count:]) for line in range(complexes * own)
    ]
    rows_dev, width = normed_ref.shape[2:]
    narrow = single_ref.shape[1]
    place.barrier(True, True)
    move.start(0)
    move.start(1)
    move.relay(0)
    move.settle(0)
    move.relay(1)
    for i in range(2, arrays):
        move.start(i)
    move.arrive(0)
    load = pltpu.make_async_copy(fulls[0].at[:, 0], packed, load_sem.at[0])
    load.start()
    load.wait()
    heads = bias_ref.shape[1]
    vec, pair_gain, pair_weight = unpack_small(packed, narrow, width, pair_ref.shape[3], heads)
    vec_ref[...] = vec
    pairw_ref[0:1] = pair_gain
    pairw_ref[8 : 8 + heads] = pair_weight
    per = rows_dev // PAIR_ROWS

    def pair_part(first, last):
        def body(pair_block_ref, mask_block_ref, low_block_ref, bias_block_ref):
            step = first + pl.program_id(0)
            pair_block(
                count_ref, place.row * rows_dev, step // per, step % per * PAIR_ROWS, pair_block_ref, mask_block_ref,
                pairw_ref[0:1], pairw_ref[8 : 8 + heads].astype(BF16), low_block_ref, bias_block_ref,
            )

        length = pair_ref.shape[2]
        spot = lambda b: ((first + b) // per, (first + b) % per)
        block = pl.BlockSpec((1, PAIR_ROWS, length, pair_ref.shape[3]), lambda b: spot(b) + (0, 0))
        pltpu.emit_pipeline(
            body,
            grid=(last - first,),
            in_specs=[block, pl.BlockSpec((1, PAIR_ROWS, length), lambda b: spot(b) + (0,))],
            out_specs=[
                block,
                pl.BlockSpec((1, heads, PAIR_ROWS, length), lambda b: (spot(b)[0], 0, spot(b)[1], 0)),
            ],
        )(pair_ref, mask_ref, low_ref, bias_ref)

    total = complexes * per
    move.settle(1)
    move.arrive(1)
    load = pltpu.make_async_copy(fulls[1], ada_buf, load_sem.at[0])
    load.start()
    load.wait()
    cond, _ = center_rows(single_ref[...].astype(F32))
    cond = (cond * vec_ref[0:1, 0:narrow]).astype(BF16)
    pre = dot(cond, joined(ada_buf, 0)) + vec_ref[2:3]
    shift = dot(cond, joined(ada_buf, 1))
    normed, _ = center_rows(tok_ref[...].astype(F32))
    normed_in = (jax.nn.sigmoid(pre) * normed + shift).astype(BF16)
    normed_ref[...] = normed_in.reshape(normed_ref.shape)
    for line in lines:
        line.start()
    for line in lines:
        line.begin()
    pair_part(0, total // 4)
    between = {
        0: lambda: (pair_part(total // 4, total // 2), move.relay(2), move.relay(3), move.relay(4)),
        1: lambda: (pair_part(total // 2, total * 3 // 4), move.settle(2), move.relay(5)),
        2: lambda: (
            pair_part(total * 3 // 4, total), move.relay(6), move.settle(3), move.settle(4),
            move.settle(5),
        ),
    }
    for t in range(chips):
        if t:
            for line in lines:
                line.line.advance(t)
        if t in between:
            between[t]()
    move.settle(6)
    for line in lines:
        line.finish()
    move.finish(arrived=(0, 1))


def enter(token_count, tok, single, pair, pair_mask, small, shards, complexes, heads):
    samples, chips = lax.axis_size("sample"), lax.axis_size("row") // 2
    pack = jax.ShapeDtypeStruct((1, PACK_ROWS, PACK_LANES), BF16)
    parts = [pack] + list(shards)
    arrays = len(parts)
    width, narrow = tok.shape[1], single.shape[1]
    _, rows, length, pair_width = pair.shape
    own = tok.shape[0] // complexes // rows
    vmem = pl.BlockSpec(memory_space=pltpu.VMEM)
    fulls = [jax.ShapeDtypeStruct((samples,) + s.shape, s.dtype) for s in parts]
    out = pl.pallas_call(
        functools.partial(enter_kernel, arrays, chips, samples),
        in_specs=[pl.BlockSpec(memory_space=pltpu.SMEM), vmem, vmem, ANY, ANY]
        + [vmem] * 6
        + [ANY] * (arrays - 1),
        out_specs=[ANY] * arrays + [ANY, vmem, vmem, vmem, ANY, ANY],
        out_shape=fulls
        + [
            jax.ShapeDtypeStruct((complexes, own, length, width), BF16),
            jax.ShapeDtypeStruct((complexes, own, rows, width), BF16),
            jax.ShapeDtypeStruct((8, width), F32),
            jax.ShapeDtypeStruct((8 + heads, pair_width), F32),
            jax.ShapeDtypeStruct(pair.shape, BF16),
            jax.ShapeDtypeStruct((complexes, heads, rows, length), F32),
        ],
        scratch_shapes=[
            pltpu.VMEM(pack.shape, BF16),
            pltpu.VMEM((samples,) + pack.shape[1:], BF16),
            pltpu.VMEM((samples, 2) + shards[0].shape[1:], BF16),
            pltpu.SemaphoreType.DMA((1,)),
        ]
        + PlaneGather.sems(arrays + 1, samples)
        + RowGather.sems(complexes * own, chips),
        compiler_params=params(collective_id=0, has_side_effects=True),
        name="enter",
    )(token_count, tok, single, pair, pair_mask, *small, *shards)
    return out[:arrays], out[arrays:]


def pair_grad_kernel(dbias_ref, low_ref, out_ref):
    first = (pl.program_id(0) == 0) & (pl.program_id(1) == 0)

    @pl.when(first)
    def _():
        out_ref[...] = jnp.zeros_like(out_ref)

    total = out_ref[...]
    for row in range(low_ref.shape[1]):
        total = total + dot(dbias_ref[0, :, row, :].astype(BF16), low_ref[0, row])
    out_ref[...] = total


def pair_grad(dbias, pair_low):
    complexes, rows, length, width = pair_low.shape
    heads = dbias.shape[1]
    block = 8
    return pl.pallas_call(
        pair_grad_kernel,
        grid=(complexes, rows // block),
        in_specs=[
            pl.BlockSpec((1, heads, block, length), lambda c, b: (c, 0, b, 0)),
            pl.BlockSpec((1, block, length, width), lambda c, b: (c, b, 0, 0)),
        ],
        out_specs=pl.BlockSpec((heads, width), lambda c, b: (0, 0)),
        out_shape=jax.ShapeDtypeStruct((heads, width), F32),
        compiler_params=params(),
        name="pair_grad",
    )(dbias, pair_low)


def attend_step(
    heads, own, full_ref, attn_ref, vec_ref, bias_ref, out_ref, prob_ref, query_ref, gate_ref,
    key_ref, value_ref,
):
    rows, width = own.shape
    length = full_ref.shape[0]
    head_dim = width // heads
    scale = head_dim ** (-0.5)
    query_ref[...] = (dot(own, joined(attn_ref, 0)) + vec_ref[6:7]).astype(BF16)
    gate_ref[...] = jax.nn.sigmoid(dot(own, joined(attn_ref, 3)))
    full = full_ref[...]
    key_ref[...] = dot(full, joined(attn_ref, 1)).astype(BF16)
    value_ref[...] = dot(full, joined(attn_ref, 2)).astype(BF16)
    parts = []
    for start, inside in head_windows(heads, head_dim):
        count = len(inside)
        lanes = slice(start, start + 256)
        span = slice(inside[0], inside[-1] + 1)
        stacked = stack_heads(query_ref[:, lanes], start, inside, head_dim)
        scores = dot_nt(stacked, key_ref[:, lanes]) * scale
        scores = scores + bias_ref[span].reshape(count * rows, length)
        weight = jnp.exp(scores - jnp.max(scores, axis=-1, keepdims=True))
        prob = weight * (1.0 / jnp.sum(weight, axis=-1, keepdims=True))
        low = prob.astype(BF16)
        prob_ref[span] = low.reshape(count, rows, length)
        mixed = dot(low, value_ref[:, lanes])
        parts.append((start, unstack_heads(mixed, start, inside, head_dim)))
    out_ref[...] = join_windows(parts, width)


def attend_kernel(
    heads, chips, samples, shard_ref, normed_ref, full_ref, attn_ref, vec_ref, bias_ref,
    whole_ref, att_ref, prob_ref, query_ref, gate_ref, keyval_ref, attn_buf, load_sem, *sems,
):
    place = Place(chips, samples)
    complexes, own, rows, width = normed_ref.shape
    length = full_ref.shape[2]
    move = PlaneGather(place, (shard_ref,), (whole_ref,), sems)
    load = pltpu.make_async_copy(attn_ref, attn_buf, load_sem.at[0])
    load.start()
    place.barrier(True, False)
    move.start(0)
    load.wait()
    steps = complexes * own

    def body(full_block, bias_block, att_block, prob_block, query_block, gate_block, keyval_block):
        at = pl.program_id(0)
        attend_step(
            heads, normed_ref[at // own, at % own], full_block.at[0, 0], attn_buf, vec_ref,
            bias_block.at[0], att_block.at[0, 0], prob_block.at[0, 0], query_block.at[0, 0],
            gate_block.at[0, 0], keyval_block.at[0, 0, 0], keyval_block.at[1, 0, 0],
        )

        @pl.when(at == steps // 2)
        def _():
            move.relay(0)

    spot = lambda b: (b // own, b % own)
    rows_block = pl.BlockSpec((1, 1, rows, width), lambda b: spot(b) + (0, 0))
    pltpu.emit_pipeline(
        body,
        grid=(steps,),
        in_specs=[
            pl.BlockSpec((1, 1, length, width), lambda b: spot(b) + (0, 0)),
            pl.BlockSpec((1, heads, rows, length), lambda b: (b // own, 0, 0, 0)),
        ],
        out_specs=[
            rows_block,
            pl.BlockSpec((1, 1, heads, rows, length), lambda b: spot(b) + (0, 0, 0)),
            rows_block,
            rows_block,
            pl.BlockSpec((2, 1, 1, length, width), lambda b: (0,) + spot(b) + (0, 0)),
        ],
    )(full_ref, bias_ref, att_ref, prob_ref, query_ref, gate_ref, keyval_ref)
    move.settle(0)
    move.finish()


def attend(shard, normed, full, attn, vec, bias):
    samples_all, chips = lax.axis_size("sample"), lax.axis_size("row") // 2
    complexes, samples, rows, width = normed.shape
    heads, length = bias.shape[1], bias.shape[3]
    vmem = pl.BlockSpec(memory_space=pltpu.VMEM)
    return pl.pallas_call(
        functools.partial(attend_kernel, heads, chips, samples_all),
        in_specs=[ANY, vmem, ANY, ANY, vmem, ANY],
        out_specs=[ANY] * 6,
        out_shape=[
            jax.ShapeDtypeStruct((samples_all,) + shard.shape, BF16),
            jax.ShapeDtypeStruct((complexes, samples, rows, width), F32),
            jax.ShapeDtypeStruct((complexes, samples, heads, rows, length), BF16),
            jax.ShapeDtypeStruct((complexes, samples, rows, width), BF16),
            jax.ShapeDtypeStruct((complexes, samples, rows, width), F32),
            jax.ShapeDtypeStruct((2, complexes, samples, length, width), BF16),
        ],
        scratch_shapes=[pltpu.VMEM(attn.shape, BF16), pltpu.SemaphoreType.DMA((1,))]
        + PlaneGather.sems(1, samples_all),
        compiler_params=params(collective_id=7, has_side_effects=True),
        name="attend",
    )(shard, normed, full, attn, vec, bias)


def attend_back_step(
    heads, prob_ref, grad_ref, query_ref, key_ref, value_ref, full_ref, key_w, value_w,
    dq_ref, dfull_ref, dbias_ref, dkey_w_ref, dvalue_w_ref,
):
    rows, width = query_ref.shape
    length = key_ref.shape[0]
    head_dim = width // heads
    scale = head_dim ** (-0.5)
    dq_parts, dk_parts, dv_parts = [], [], []
    for start, inside in head_windows(heads, head_dim):
        count = len(inside)
        lanes = slice(start, start + 256)
        queries = stack_heads(query_ref[:, lanes], start, inside, head_dim)
        grads = stack_heads(grad_ref[:, lanes], start, inside, head_dim)
        span = slice(inside[0], inside[-1] + 1)
        low = prob_ref[span].reshape(count * rows, length)
        prob = low.astype(F32)
        dprob = dot_nt(grads, value_ref[:, lanes])
        inner = jnp.sum(prob * dprob, axis=-1, keepdims=True)
        dscore = (prob * (dprob - inner)).astype(BF16)
        dbias_ref[span] += dscore.astype(F32).reshape(count, rows, length)
        mixed = dot(dscore, key_ref[:, lanes])
        dq_parts.append((start, unstack_heads(mixed, start, inside, head_dim)))
        dk_parts.append((start, dot_tn(dscore, queries)))
        dv_parts.append((start, dot_tn(low, grads)))
    dq_ref[...] = (join_windows(dq_parts, width) * scale).astype(BF16)
    dkey = (join_windows(dk_parts, width) * scale).astype(BF16)
    dvalue = join_windows(dv_parts, width).astype(BF16)
    dfull_ref[...] = (dot_nt(dkey, key_w) + dot_nt(dvalue, value_w)).astype(BF16).reshape(
        dfull_ref.shape
    )
    turned = full_ref[...].T
    dkey_w_ref[...] += dot(turned, dkey)
    dvalue_w_ref[...] += dot(turned, dvalue)


def attend_back_kernel(
    heads, prob_ref, grad_ref, query_ref, keyval_ref, full_ref, key_w_ref, value_w_ref,
    dq_ref, dfull_ref, dbias_ref, dkey_w_ref, dvalue_w_ref,
):
    @pl.when(pl.program_id(1) == 0)
    def _():
        dbias_ref[...] = jnp.zeros_like(dbias_ref)

    @pl.when((pl.program_id(0) == 0) & (pl.program_id(1) == 0))
    def _():
        dkey_w_ref[...] = jnp.zeros_like(dkey_w_ref)
        dvalue_w_ref[...] = jnp.zeros_like(dvalue_w_ref)

    attend_back_step(
        heads, prob_ref.at[0, 0], grad_ref.at[0, 0], query_ref.at[0, 0], keyval_ref.at[0, 0, 0],
        keyval_ref.at[1, 0, 0], full_ref.at[0, 0], joined(key_w_ref), joined(value_w_ref),
        dq_ref.at[0, 0], dfull_ref.at[0, 0], dbias_ref.at[0], dkey_w_ref, dvalue_w_ref,
    )


def attend_back(prob, grad, query, keyval, full, attn):
    complexes, samples, rows, width = query.shape
    heads, length = prob.shape[2], prob.shape[4]
    own = pl.BlockSpec((1, 1, rows, width), lambda c, s: (c, s, 0, 0))
    long = pl.BlockSpec((1, 1, length, width), lambda c, s: (c, s, 0, 0))
    weight = lambda which: pl.BlockSpec(
        (attn.shape[0], 1) + attn.shape[2:], lambda c, s: (0, which, 0, 0),
        pipeline_mode=pl.Buffered(1),
    )
    square = pl.BlockSpec((width, width), lambda c, s: (0, 0))
    return pl.pallas_call(
        functools.partial(attend_back_kernel, heads),
        grid=(complexes, samples),
        in_specs=[
            pl.BlockSpec((1, 1, heads, rows, length), lambda c, s: (c, s, 0, 0, 0)),
            own,
            own,
            pl.BlockSpec((2, 1, 1, length, width), lambda c, s: (0, c, s, 0, 0)),
            long,
            weight(1),
            weight(2),
        ],
        out_specs=[
            own,
            long,
            pl.BlockSpec((1, heads, rows, length), lambda c, s: (c, 0, 0, 0)),
            square,
            square,
        ],
        out_shape=[
            jax.ShapeDtypeStruct((complexes, samples, rows, width), BF16),
            jax.ShapeDtypeStruct((complexes, samples, length, width), BF16),
            jax.ShapeDtypeStruct((complexes, heads, rows, length), F32),
            jax.ShapeDtypeStruct((width, width), F32),
            jax.ShapeDtypeStruct((width, width), F32),
        ],
        compiler_params=params(),
        name="attend_back",
    )(prob, grad, query, keyval, full, attn, attn)


def middle_kernel(
    rows_dev, count_ref,
    att_ref, gate_ref, tok_ref, single_ref, cot_ref,
    vec_ref, ada_ref, zero_ref, out_w_ref, tin_ref, tout_ref,
    out_ref, dmid_ref, datt_ref, dglogit_ref,
    gated_ref, dabranch_ref, dza_ref, dzb_ref, tcond_ref, dtpre_ref, dtin_ref,
    tinput_ref, dfirst_ref, dsecond_ref, hidden_ref, dtbranch_ref, small_ref,
):
    step = pl.program_id(0)
    rows = att_ref.shape[0]
    count = count_ref[step]
    place = lax.broadcasted_iota(jnp.int32, (rows, 1), 0) % rows_dev
    place = place + lax.axis_index("row") * rows_dev
    valid = (place < count).astype(F32)
    att = att_ref[...]
    gate = gate_ref[...]
    single = single_ref[...]
    gated = (att * gate).astype(BF16)
    gated_ref[...] = gated
    branch = dot(gated, joined(out_w_ref))
    attn_zero = jax.nn.sigmoid(dot(single, joined(zero_ref, 0)) + vec_ref[4:5])
    middle = tok_ref[...].astype(F32) + valid * attn_zero * branch
    cond, _ = center_rows(single.astype(F32))
    tcond = (cond * vec_ref[1:2, 0 : single.shape[1]]).astype(BF16)
    tcond_ref[...] = tcond
    scale = jax.nn.sigmoid(dot(tcond, joined(ada_ref, 0)) + vec_ref[3:4])
    shift = dot(tcond, joined(ada_ref, 1))
    normed, rstd = center_rows(middle)
    tinput = (scale * normed + shift).astype(BF16)
    tinput_ref[...] = tinput
    first = dot(tinput, joined(tin_ref, 0))
    second = dot(tinput, joined(tin_ref, 1))
    sig = jax.nn.sigmoid(first)
    hidden = (first * sig * second).astype(BF16)
    hidden_ref[...] = hidden
    tbranch = dot(hidden, joined(tout_ref))
    trans_zero = jax.nn.sigmoid(dot(single, joined(zero_ref, 1)) + vec_ref[5:6])
    out_ref[...] = (middle + valid * trans_zero * tbranch).astype(BF16)
    grad_out = cot_ref[...].astype(F32)
    gated_out = grad_out * valid
    dtbranch = (gated_out * trans_zero).astype(BF16)
    dtbranch_ref[...] = dtbranch
    dzb = (gated_out * tbranch * trans_zero * (1.0 - trans_zero)).astype(BF16)
    dzb_ref[...] = dzb
    dhidden = dot_nt(dtbranch, joined(tout_ref))
    dfirst = (dhidden * second * sig * (1.0 + first * (1.0 - sig))).astype(BF16)
    dsecond = (dhidden * first * sig).astype(BF16)
    dfirst_ref[...] = dfirst
    dsecond_ref[...] = dsecond
    dtin = (dot_nt(dfirst, joined(tin_ref, 0)) + dot_nt(dsecond, joined(tin_ref, 1))).astype(BF16)
    dtin_ref[...] = dtin
    dtin_full = dtin.astype(F32)
    dtpre = (dtin_full * normed * scale * (1.0 - scale)).astype(BF16)
    dtpre_ref[...] = dtpre
    grad_norm = dtin_full * scale
    tail = grad_norm - jnp.mean(grad_norm, axis=-1, keepdims=True)
    tail = tail - normed * jnp.mean(grad_norm * normed, axis=-1, keepdims=True)
    dmid = grad_out + tail * rstd
    dmid_ref[...] = dmid
    dtcond = dot_nt(dtpre, joined(ada_ref, 0)) + dot_nt(dtin, joined(ada_ref, 1))
    gated_mid = dmid * valid
    dabranch = (gated_mid * attn_zero).astype(BF16)
    dabranch_ref[...] = dabranch
    dza = (gated_mid * branch * attn_zero * (1.0 - attn_zero)).astype(BF16)
    dza_ref[...] = dza
    dgated = dot_nt(dabranch, joined(out_w_ref))
    datt_ref[...] = (dgated * gate).astype(BF16)
    dglogit_ref[...] = (dgated * att * gate * (1.0 - gate)).astype(BF16)

    @pl.when(step == 0)
    def _():
        small_ref[...] = jnp.zeros_like(small_ref)

    width, narrow = att.shape[1], single.shape[1]
    total = lambda value: jnp.sum(value.astype(F32), axis=0, keepdims=True)
    small_ref[0:1, :] += total(dtpre)
    small_ref[1:2, :] += total(dza)
    small_ref[2:3, :] += total(dzb)
    small_ref[3:4, 0:narrow] += total(dtcond * cond)


def middle_pass(
    token_count, att, gate, tok, single, cot, vec, ada, zero, out_w, trans_in, trans_out, complexes,
    rows_dev,
):
    rows, width = tok.shape
    narrow = single.shape[1]
    hidden = trans_out.shape[0] * trans_out.shape[2]
    part = rows // complexes
    wide = pl.BlockSpec((part, width), lambda c, m: (c, 0))
    slim = pl.BlockSpec((part, narrow), lambda c, m: (c, 0))
    long = pl.BlockSpec((part, hidden), lambda c, m: (c, 0))
    once = lambda shape: pl.BlockSpec(
        shape, lambda c, m: (0,) * len(shape), pipeline_mode=pl.Buffered(1)
    )
    shape = lambda cols, kind: jax.ShapeDtypeStruct((rows, cols), kind)
    return pl.pallas_call(
        functools.partial(middle_kernel, rows_dev),
        grid_spec=pltpu.PrefetchScalarGridSpec(
            num_scalar_prefetch=1,
            grid=(complexes,),
            in_specs=[
                wide, wide, wide, slim, wide,
                once(vec.shape),
                pl.BlockSpec(
                    (ada.shape[0], 2) + ada.shape[2:], lambda c, m: (0, 1, 0, 0),
                    pipeline_mode=pl.Buffered(1),
                ),
                once(zero.shape),
                once(out_w.shape),
                once(trans_in.shape),
                once(trans_out.shape),
            ],
            out_specs=[
                wide, wide, wide, wide,
                wide, wide, wide, wide, slim, wide, wide,
                wide, long, long, long, wide,
                once((8, width)),
            ],
        ),
        out_shape=[
            shape(width, BF16), shape(width, F32), shape(width, BF16), shape(width, BF16),
            shape(width, BF16), shape(width, BF16), shape(width, BF16), shape(width, BF16),
            shape(narrow, BF16), shape(width, BF16), shape(width, BF16),
            shape(width, BF16), shape(hidden, BF16), shape(hidden, BF16), shape(hidden, BF16),
            shape(width, BF16),
            jax.ShapeDtypeStruct((8, width), F32),
        ],
        compiler_params=params(),
        name="middle_pass",
    )(token_count, att, gate, tok, single, cot, vec, ada, zero, out_w, trans_in, trans_out)


def last_kernel(
    dquery_ref, dfull_ref, dglogit_ref, tok_ref, single_ref, dmid_ref,
    vec_ref, ada_ref, query_w_ref, gate_w_ref,
    tgrad_ref, dnormed_ref, dapre_ref, cond_ref, small_ref,
):
    total = lambda value: jnp.sum(value.astype(F32), axis=0, keepdims=True)
    dnormed = (
        dot_nt(dquery_ref[...], joined(query_w_ref))
        + dot_nt(dglogit_ref[...], joined(gate_w_ref))
        + dfull_ref[...].astype(F32)
    ).astype(BF16)
    dnormed_ref[...] = dnormed
    cond, _ = center_rows(single_ref[...].astype(F32))
    cond_low = (cond * vec_ref[0:1, 0 : cond.shape[1]]).astype(BF16)
    cond_ref[...] = cond_low
    scale = jax.nn.sigmoid(dot(cond_low, joined(ada_ref, 0)) + vec_ref[2:3])
    normed, rstd = center_rows(tok_ref[...].astype(F32))
    full = dnormed.astype(F32)
    dapre = (full * normed * scale * (1.0 - scale)).astype(BF16)
    dapre_ref[...] = dapre
    grad_norm = full * scale
    tail = grad_norm - jnp.mean(grad_norm, axis=-1, keepdims=True)
    tail = tail - normed * jnp.mean(grad_norm * normed, axis=-1, keepdims=True)
    tgrad_ref[...] = dmid_ref[...] + tail * rstd
    dcond = dot_nt(dapre, joined(ada_ref, 0)) + dot_nt(dnormed, joined(ada_ref, 1))
    narrow = cond.shape[1]
    small_ref[...] = jnp.zeros_like(small_ref)
    small_ref[0:1, :] = total(dapre)
    small_ref[1:2, :] = total(dquery_ref[...])
    small_ref[2:3, 0:narrow] = total(dcond * cond)


def last_pass(dquery, dfull, dglogit, tok, single, dmid, vec, ada, attn):
    rows, width = tok.shape
    narrow = single.shape[1]
    whole = lambda shape: pl.BlockSpec(shape, lambda w: (0,) * len(shape))
    wide = whole((rows, width))
    shape = lambda cols, kind: jax.ShapeDtypeStruct((rows, cols), kind)
    weight = lambda which: pl.BlockSpec(
        (attn.shape[0], 1) + attn.shape[2:], lambda w: (0, which, 0, 0)
    )
    return pl.pallas_call(
        last_kernel,
        grid=(1,),
        in_specs=[
            wide, wide, wide, wide, whole((rows, narrow)), wide,
            whole(vec.shape),
            pl.BlockSpec((ada.shape[0], 2) + ada.shape[2:], lambda w: (0, 0, 0, 0)),
            weight(0),
            weight(3),
        ],
        out_specs=[wide, wide, wide, whole((rows, narrow)), whole((8, width))],
        out_shape=[
            shape(width, F32), shape(width, BF16), shape(width, BF16), shape(narrow, BF16),
            jax.ShapeDtypeStruct((8, width), F32),
        ],
        compiler_params=params(),
        name="last_pass",
    )(dquery, dfull, dglogit, tok, single, dmid, vec, ada, attn, attn)


def return_kernel(
    heads, chips, samples, grads_ref, prob_ref, grad_ref, query_ref, keyval_ref, full_ref, attn_ref,
    low_ref, normed_ref,
    dq_ref, own_ref, pair_ref, wide_plane, plane_ref, query_plane_ref,
    dfull, dbias, weight_buf, dkey_w_ref, dvalue_w_ref, query_grads_buf, pair_acc,
    load_sem, *scratch,
):
    place = Place(chips, samples)
    complexes, own = query_ref.shape[:2]
    rows, width = query_ref.shape[2:]
    length = full_ref.shape[2]
    count = len(PlaneReduce.scratch(samples, 64, 128))
    cut = 2 * wide_plane.shape[0]
    wide = PlaneReduce(place, grads_ref.at[:, pl.ds(0, cut)], wide_plane, scratch[:count])
    rest = grads_ref.shape[1] - cut
    plane = PlaneReduce(
        place, grads_ref.at[:, pl.ds(cut, rest)], plane_ref, scratch[count : 2 * count]
    )
    query_plane = PlaneReduce(
        place, query_grads_buf, query_plane_ref, scratch[2 * count : 3 * count]
    )
    scratch = scratch[3 * count :]
    moves = [
        RowReduce(place, dfull, own_ref, which, scratch) for which in range(complexes)
    ]
    place.barrier(True, True)
    wide.start()
    plane.start()
    load = pltpu.make_async_copy(attn_ref.at[:, 1:3], weight_buf, load_sem.at[0])
    load.start()
    dkey_w_ref[...] = jnp.zeros_like(dkey_w_ref)
    dvalue_w_ref[...] = jnp.zeros_like(dvalue_w_ref)
    dbias[...] = jnp.zeros_like(dbias)
    load.wait()

    def hooked(step, hooks):
        for at, actions in hooks.items():

            @pl.when(step == at)
            def _():
                for action in actions:
                    action()

    def back(prob_block, grad_block, query_block, keyval_block, full_block):
        step = pl.program_id(0)
        which, sample = step // own, step % own
        attend_back_step(
            heads, prob_block.at[0, 0], grad_block.at[0, 0], query_block.at[0, 0],
            keyval_block.at[0, 0, 0], keyval_block.at[1, 0, 0], full_block.at[0, 0],
            joined(weight_buf, 0), joined(weight_buf, 1), dq_ref.at[which, sample],
            dfull.at[which, sample], dbias.at[which], dkey_w_ref, dvalue_w_ref,
        )
        hooked(step, back_hooks)

    back_hooks = {}
    final = complexes * own - 1

    def then(at, action):
        back_hooks.setdefault(min(at, final), []).append(action)

    half_order = (len(plane.order) + 1) // 2
    for at, k in enumerate(plane.order):
        if at < half_order:
            wide.depart(k)
        else:
            then(0, functools.partial(wide.depart, k))
        then(own - 2 + at // half_order, functools.partial(plane.depart, k))
    then(own - 1, lambda: moves[0].first_swap().start())
    then(own, moves[0].begin)
    for t in range(1, chips):
        then(own + t - 1, functools.partial(moves[0].line.advance, t))
    then(own + 1, wide.hop)
    then(final, lambda: moves[1].first_swap().start())

    spot = lambda b: (b // own, b % own)
    rows_block = pl.BlockSpec((1, 1, rows, width), lambda b: spot(b) + (0, 0))
    pltpu.emit_pipeline(
        back,
        grid=(complexes * own,),
        in_specs=[
            pl.BlockSpec((1, 1, heads, rows, length), lambda b: spot(b) + (0, 0, 0)),
            rows_block,
            rows_block,
            pl.BlockSpec((2, 1, 1, length, width), lambda b: (0,) + spot(b) + (0, 0)),
            pl.BlockSpec((1, 1, length, width), lambda b: spot(b) + (0, 0)),
        ],
    )(prob_ref, grad_ref, query_ref, keyval_ref, full_ref)
    query_grads(
        normed_ref[...], dq_ref[...].reshape(complexes * own * rows, width), dkey_w_ref[...],
        dvalue_w_ref[...], query_grads_buf,
    )
    query_plane.start()

    pair_acc[...] = jnp.zeros_like(pair_acc)
    per = rows // PAIR_ROWS

    def pair_part(first, last):
        def body(low_block):
            step = first + pl.program_id(0)
            which, start = step // per, pl.multiple_of(step % per * PAIR_ROWS, PAIR_ROWS)
            lines = dbias[which, :, pl.ds(start, PAIR_ROWS), :]
            lines = lines.reshape(heads * PAIR_ROWS, length).astype(BF16)
            line = lax.broadcasted_iota(jnp.int32, (heads * PAIR_ROWS, 1), 0) % PAIR_ROWS
            total = pair_acc[...]
            for row in range(PAIR_ROWS):
                total = total + jnp.where(line == row, dot(lines, low_block[0, row]), 0.0)
            pair_acc[...] = total

        pltpu.emit_pipeline(
            body,
            grid=(last - first,),
            in_specs=[
                pl.BlockSpec(
                    (1, PAIR_ROWS, length, low_ref.shape[3]),
                    lambda b: ((first + b) // per, (first + b) % per, 0, 0),
                )
            ],
        )(low_ref)

    total = complexes * per
    marks = [total * t // chips for t in range(chips + 1)]
    moves[1].begin()
    moves[1].line.advance(1)
    plane.hop()
    for k in query_plane.order:
        query_plane.depart(k)
    wide.finish()
    moves[0].finish()
    for t in range(chips):
        pair_part(marks[t], marks[t + 1])
        if t + 2 < chips:
            moves[1].line.advance(t + 2)
        if t == 1:
            query_plane.hop()
    pair_ref[...] = jnp.sum(pair_acc[...].reshape(heads, PAIR_ROWS, pair_acc.shape[1]), axis=1)
    plane.finish()
    moves[1].finish()
    query_plane.finish()
    for move in moves:
        move.drain()
    for part in (wide, plane, query_plane):
        part.drain()


def return_pass(grads, cut, prob, grad, query, keyval, full, attn, pair_low, normed, query_rows):
    samples, chips = lax.axis_size("sample"), lax.axis_size("row") // 2
    complexes, own, rows, width = query.shape
    heads, length = prob.shape[2], prob.shape[4]
    vmem = pl.BlockSpec(memory_space=pltpu.VMEM)
    half = (grads.shape[1] - cut) // 2
    return pl.pallas_call(
        functools.partial(return_kernel, heads, chips, samples),
        in_specs=[ANY] * 8 + [vmem],
        out_specs=[vmem, ANY, vmem, vmem, vmem, vmem],
        out_shape=[
            jax.ShapeDtypeStruct(query.shape, BF16),
            jax.ShapeDtypeStruct(query.shape, BF16),
            jax.ShapeDtypeStruct((heads, pair_low.shape[3]), F32),
            jax.ShapeDtypeStruct((cut // 2, width), BF16),
            jax.ShapeDtypeStruct((half, width), BF16),
            jax.ShapeDtypeStruct((query_rows // 2, width), BF16),
        ],
        scratch_shapes=[
            pltpu.VMEM((complexes, own, chips, 2, rows, width), BF16),
            pltpu.VMEM((complexes, heads, rows, length), F32),
            pltpu.VMEM((attn.shape[0], 2) + attn.shape[2:], BF16),
            pltpu.VMEM((width, width), F32),
            pltpu.VMEM((width, width), F32),
            pltpu.VMEM((samples, query_rows, width), BF16),
            pltpu.VMEM((heads * PAIR_ROWS, pair_low.shape[3]), F32),
            pltpu.SemaphoreType.DMA((1,)),
        ]
        + PlaneReduce.scratch(samples, cut, width)
        + PlaneReduce.scratch(samples, 2 * half, width)
        + PlaneReduce.scratch(samples, query_rows, width)
        + RowReduce.scratch(complexes, own, length, rows, width, chips),
        compiler_params=params(collective_id=5, has_side_effects=True),
        name="return_pass",
    )(grads, prob, grad, query, keyval, full, attn, pair_low, normed)


def leave_kernel(
    chips, samples, most_ref, late_ref, query_ref, dquery_ref, dfull_ref, dglogit_ref, tok_ref, single_ref,
    dmid_ref, vec_ref, ada_ref, attn_ref, small_mid, pair_sum,
    tgrad_ref, most_total, late_total, query_total, last_total,
    most_plane, late_plane, query_plane, last_grads_buf, last_plane, dnormed_ref, dapre_ref, cond_ref,
    small_ref, load_sem, *scratch,
):
    place = Place(chips, samples)
    count = len(PlaneReduce.scratch(samples, 64, 128))
    plane = PlaneReduce(place, last_grads_buf, last_plane, scratch[:count])
    scratch = scratch[count:]
    pieces = [
        (LineTotal, most_plane, most_total), (LineTotal, late_plane, late_total),
        (LineTotal, query_plane, query_total),
        (DirectTotal, last_plane, last_total),
    ]
    lines = []
    for kind, buf, total in pieces:
        count = len(kind.scratch(16 * chips, 128, chips))
        lines.append(kind(place, buf, total, 0, buf.shape[0], scratch[:count]))
        scratch = scratch[count:]
    most, late, query, last = lines
    loads = [
        pltpu.make_async_copy(late_ref, late_plane, load_sem.at[0]),
        pltpu.make_async_copy(query_ref, query_plane, load_sem.at[1]),
        pltpu.make_async_copy(most_ref, most_plane, load_sem.at[2]),
    ]
    for load in loads:
        load.start()
    place.barrier(True, True, True)
    for load in loads:
        load.wait()
    groups = [(most, 0), (late, 1), (query, 2), (last, 4)]
    clock = [0]

    def tick():
        t = clock[0] = clock[0] + 1
        for line, behind in groups:
            step = t - behind
            if 1 <= step < line.steps:
                line.advance(step)
            elif step == line.steps:
                line.finish()

    tick()
    last_kernel(
        dquery_ref, dfull_ref, dglogit_ref, tok_ref, single_ref, dmid_ref, vec_ref, ada_ref,
        attn_ref.at[:, 0:1], attn_ref.at[:, 3:4], tgrad_ref, dnormed_ref, dapre_ref, cond_ref,
        small_ref,
    )
    tick()
    last_grads(
        cond_ref[...], dapre_ref[...], dnormed_ref[...], small_mid[...], small_ref[...],
        pair_sum[...], last_grads_buf,
    )
    plane.start()
    tick()
    for k in plane.order:
        plane.depart(k)
    tick()
    plane.hop()
    plane.finish()
    while clock[0] < max(line.steps + behind for line, behind in groups):
        tick()
    plane.drain()


def leave(most, late, query, dquery, dfull, dglogit, tok, single, dmid, vec, ada, attn, small_mid, pair_sum,
          last_rows):
    samples, chips = lax.axis_size("sample"), lax.axis_size("row") // 2
    rows, width = tok.shape
    narrow = single.shape[1]
    halves = [most.shape[0], late.shape[0], query.shape[0], last_rows // 2]
    vmem = pl.BlockSpec(memory_space=pltpu.VMEM)
    return pl.pallas_call(
        functools.partial(leave_kernel, chips, samples),
        in_specs=[ANY] * 3 + [vmem] * 11,
        out_specs=[vmem] * 5,
        out_shape=[jax.ShapeDtypeStruct((rows, width), F32)]
        + [jax.ShapeDtypeStruct((2 * half, width), BF16) for half in halves],
        scratch_shapes=[
            pltpu.VMEM(most.shape, BF16),
            pltpu.VMEM(late.shape, BF16),
            pltpu.VMEM(query.shape, BF16),
            pltpu.VMEM((samples, last_rows, width), BF16),
            pltpu.VMEM((last_rows // 2, width), BF16),
            pltpu.VMEM((rows, width), BF16),
            pltpu.VMEM((rows, width), BF16),
            pltpu.VMEM((rows, narrow), BF16),
            pltpu.VMEM((8, width), F32),
            pltpu.SemaphoreType.DMA((3,)),
        ]
        + PlaneReduce.scratch(samples, last_rows, width)
        + LineTotal.scratch(halves[0], width, chips)
        + LineTotal.scratch(halves[1], width, chips)
        + LineTotal.scratch(halves[2], width, chips)
        + DirectTotal.scratch(halves[3], width, chips),
        compiler_params=params(collective_id=6, has_side_effects=True),
        name="leave",
    )(most, late, query, dquery, dfull, dglogit, tok, single, dmid, vec, ada, attn, small_mid, pair_sum)


def grad_rows(samples, chips, parts):
    unit = 32 * chips
    return -(-sum(parts) // unit) * unit


def store_grads(out_ref, start, left, grads):
    samples, _, width = out_ref.shape
    turned = left.T
    rows = turned.shape[0] // samples
    for grad in grads:
        value = dot(turned, grad).astype(BF16)
        out_ref[:, start : start + rows] = value.reshape(samples, rows, width)
        start += rows
    return start


def pad_grads(out_ref, start):
    samples, rows, width = out_ref.shape
    if start < rows:
        out_ref[:, start:] = jnp.zeros((samples, rows - start, width), BF16)


LATE_OPERANDS = 15


def late_grads_kernel(*refs):
    ins, out_ref, refs = refs[:LATE_OPERANDS], refs[LATE_OPERANDS], refs[LATE_OPERANDS + 1 :]
    bufs, grads, in_sem, out_sem = refs[:LATE_OPERANDS], *refs[LATE_OPERANDS:]
    loads = [
        pltpu.make_async_copy(ref, buf, in_sem.at[i]) for i, (ref, buf) in enumerate(zip(ins, bufs))
    ]
    for load in loads:
        load.start()
    width = out_ref.shape[2]
    stores = []

    def take(i):
        loads[i].wait()
        return bufs[i]

    def put(start, left, right):
        end = store_grads(grads, start, left, right)
        spot = pl.ds(start, end - start)
        store = pltpu.make_async_copy(grads.at[:, spot], out_ref.at[:, spot], out_sem.at[len(stores)])
        store.start()
        stores.append(store)
        return end

    tinput = take(0)[...]
    start = 0
    for i in (1, 2):
        ref = take(i)
        halves = [ref[:, lane : lane + width] for lane in range(0, ref.shape[1], width)]
        start = put(start, tinput, halves)
    start = put(start, take(3)[...], [take(4)[...]])
    start = put(start, take(5)[...], [take(6)[...], take(7)[...]])
    start = put(start, take(8)[...], [take(9)[...], take(10)[...]])
    start = put(start, take(11)[...], [take(12)[...]])
    start = put(start, take(13)[...], [take(14)[...]])
    rows = out_ref.shape[1]
    if start < rows:
        pad_grads(grads, start)
        spot = pl.ds(start, rows - start)
        store = pltpu.make_async_copy(grads.at[:, spot], out_ref.at[:, spot], out_sem.at[len(stores)])
        store.start()
        stores.append(store)
    for store in stores:
        store.wait()


def late_grads(samples, rows, width, operands):
    return pl.pallas_call(
        late_grads_kernel,
        in_specs=[ANY] * LATE_OPERANDS,
        out_specs=ANY,
        out_shape=jax.ShapeDtypeStruct((samples, rows, width), BF16),
        scratch_shapes=[pltpu.VMEM(value.shape, BF16) for value in operands]
        + [
            pltpu.VMEM((samples, rows, width), BF16),
            pltpu.SemaphoreType.DMA((LATE_OPERANDS,)),
            pltpu.SemaphoreType.DMA((8,)),
        ],
        compiler_params=params(),
        name="late_grads",
    )(*operands)


def store_ready(out_ref, start, ready):
    samples, _, width = out_ref.shape
    for value in ready:
        size = value.shape[0] // samples
        out_ref[:, start : start + size] = value.astype(BF16).reshape(samples, size, width)
        start += size
    return start


def query_grads(normed_in, dquery, dkey_w, dvalue_w, out_ref):
    start = store_grads(out_ref, 0, normed_in, [dquery])
    pad_grads(out_ref, store_ready(out_ref, start, [dkey_w, dvalue_w]))


def last_grads(cond, dapre, dnormed, small_mid, small_last, pair_sum, out_ref):
    samples, rows, width = out_ref.shape
    start = store_grads(out_ref, 0, cond, [dapre, dnormed])
    pairs = jnp.concatenate(
        [pair_sum, jnp.zeros((pair_sum.shape[0], width - pair_sum.shape[1]), F32)], axis=1
    )
    small = jnp.concatenate([small_mid, small_last, pairs], axis=0).astype(BF16)
    for sample in range(samples):
        out_ref[sample, start : start + small.shape[0]] = small
    pad_grads(out_ref, start + small.shape[0])


def query_grads_kernel(normed_in, dquery, dkey_w, dvalue_w, out_ref):
    query_grads(normed_in[...], dquery[...], dkey_w[...], dvalue_w[...], out_ref)


def last_grads_kernel(cond, dapre, dnormed, small_mid, small_last, pair_sum, out_ref):
    last_grads(
        cond[...], dapre[...], dnormed[...], small_mid[...], small_last[...], pair_sum[...], out_ref
    )


def grads_call(kernel, samples, rows, width, operands, name):
    return pl.pallas_call(
        kernel,
        out_shape=jax.ShapeDtypeStruct((samples, rows, width), BF16),
        compiler_params=params(),
        name=name,
    )(*operands)


def deal_kernel(
    most, late, early, last, pairw,
    gain_ref, ada_ref, ada_bias_ref, zero_ref, zero_bias_ref, attn_ref, query_bias_ref, out_ref,
    pair_gain_ref, pair_weight_ref, tin_ref, tout_ref,
):
    slim, wide = ada_ref.shape[1], attn_ref.shape[1]
    width = ada_ref.shape[2]
    spot = lax.axis_index("sample")
    part = lambda ref, start, size: ref[start : start + size].astype(F32)
    for which in range(2):
        for lane in range(2):
            tin_ref[which, :, lane * width : (lane + 1) * width] = part(
                most, (2 * which + lane) * wide, wide
            )
    tout_ref[...] = part(most, 4 * wide, tout_ref.shape[0])
    for which in range(2):
        ada_ref[which] = part(last, which * slim, slim)
        ada_ref[2 + which] = part(late, which * slim, slim)
        zero_ref[which] = part(late, (2 + which) * slim, slim)
    out_ref[...] = part(late, 4 * slim, wide)
    for which in range(3):
        attn_ref[which] = part(early, which * wide, wide)
    attn_ref[3] = part(late, 4 * slim + wide, wide)
    heads, thin = pair_weight_ref.shape
    small = last[2 * slim : 2 * slim + 16]
    pairs = last[2 * slim + 16 : 2 * slim + 16 + heads, 0 : pairw.shape[1]]

    def choose(size, count):
        row = lax.broadcasted_iota(jnp.int32, (size, count), 0)
        lane = lax.broadcasted_iota(jnp.int32, (size, count), 1)
        return (row == lane + spot * count).astype(BF16)

    lines = dot(small, choose(width, wide))
    narrow = slim * (width // wide)
    slims = dot(small[:, 0:narrow], choose(narrow, slim))
    ada_bias_ref[0:1] = lines[8:9]
    ada_bias_ref[1:2] = lines[0:1]
    zero_bias_ref[...] = lines[1:3]
    query_bias_ref[...] = lines[9:10]
    gain_ref[0:1] = slims[10:11]
    gain_ref[1:2] = slims[3:4]
    pair_weight_ref[...] = dot(pairs, choose(pairw.shape[1], thin))
    gains = jnp.sum(pairw[8 : 8 + heads] * pairs.astype(F32), axis=0, keepdims=True) / pairw[0:1]
    pair_gain_ref[...] = lax.dot_general(
        gains, choose(pairw.shape[1], thin).astype(F32), (((1,), (0,)), ((), ())),
        precision=lax.Precision.HIGHEST, preferred_element_type=F32,
    )


def deal(most, late, early, last, pairw, shapes):
    return pl.pallas_call(
        deal_kernel,
        out_shape=[jax.ShapeDtypeStruct(shape, F32) for shape in shapes],
        compiler_params=params(),
        name="deal",
    )(most, late, early, last, pairw)


def local(
    tokens, single, pair, token_count, pair_mask, cotangent, cond_gain, ada_weight, ada_bias,
    zero_weight, zero_bias, attn_weight, query_bias, out_weight, pair_gain, pair_weight,
    trans_in, trans_out,
):
    complexes, samples_own, rows_dev, width = tokens.shape
    narrow = single.shape[3]
    heads, length = pair_weight.shape[1], pair.shape[2]
    samples, chips = lax.axis_size("sample"), lax.axis_size("row") // 2
    rows = complexes * samples_own * rows_dev
    flat = lambda value: value.reshape(rows, value.shape[-1])
    block = lambda value: value.reshape(complexes, samples_own, rows_dev, width)
    tok, sing, cot = flat(tokens), flat(single), flat(cotangent)
    small = (cond_gain, ada_bias, zero_bias, query_bias, pair_gain, pair_weight.T)
    weights, (full, normed_in, vec, pairw, pair_low, bias) = enter(
        token_count, tok, sing, pair, pair_mask, small,
        [ada_weight, attn_weight, zero_weight, out_weight[None], trans_out[None]],
        complexes, heads,
    )
    _, ada, attn, zero, out_w, tout = weights
    tin, att, prob, query, gate, keyval = attend(trans_in, normed_in, full, attn, vec, bias)
    normed_in = flat(normed_in)
    (
        output, dmid, datt, dglogit, gated, dabranch, dza, dzb, tcond, dtpre, dtin, tinput,
        dfirst, dsecond, hidden, dtbranch, small_mid,
    ) = middle_pass(
        token_count, flat(att), flat(gate), tok, sing, cot, vec, ada, zero, out_w, tin, tout,
        complexes, rows_dev,
    )
    slim, wide = narrow // samples, width // samples
    late_parts = [wide] * 4 + [tout.shape[2]] + [slim] * 4 + [wide] * 2
    query_parts = [wide] * 3
    last_parts = [slim] * 2 + [16 + heads]
    late_rows, query_rows, last_rows = (
        grad_rows(samples, chips, parts) for parts in (late_parts, query_parts, last_parts)
    )
    late = late_grads(
        samples, late_rows, width,
        (tinput, dfirst, dsecond, hidden, dtbranch, tcond, dtpre, dtin, sing, dza, dzb, gated,
         dabranch, normed_in, dglogit),
    )
    datt = block(datt)
    if length <= 512:
        dquery, dfull, pair_sum, most, late, early = return_pass(
            late, sum(late_parts[:5]), prob, datt, query, keyval, full, attn, pair_low, normed_in, query_rows
        )
        tgrad, most, late, early, last = leave(
            most, late, early, flat(dquery), flat(dfull), dglogit, tok, sing, dmid, vec, ada, attn,
            small_mid, pair_sum, last_rows,
        )
    else:
        dquery, dfull, dbias, dkey_w, dvalue_w = attend_back(prob, datt, query, keyval, full, attn)
        dfull = flat(reduce_rows(dfull, 2))
        pair_sum = pair_grad(dbias, pair_low)
        dquery = flat(dquery)
        tgrad, dnormed, dapre, cond, small_last = last_pass(
            dquery, dfull, dglogit, tok, sing, dmid, vec, ada, attn
        )
        early = grads_call(
            query_grads_kernel, samples, query_rows, width, (normed_in, dquery, dkey_w, dvalue_w),
            "query_grads",
        )
        last = grads_call(
            last_grads_kernel, samples, last_rows, width,
            (cond, dapre, dnormed, small_mid, small_last, pair_sum), "last_grads",
        )
        late = reduce_grads(late, 3)
        most, late = late[: sum(late_parts[:5])], late[sum(late_parts[:5]) :]
        early = reduce_grads(early, 4)
        last = reduce_grads(last, 2)

    shapes = [
        cond_gain.shape, ada_weight.shape, ada_bias.shape, zero_weight.shape, zero_bias.shape,
        attn_weight.shape, (1,) + query_bias.shape, out_weight.shape, (1,) + pair_gain.shape,
        pair_weight.T.shape, trans_in.shape, trans_out.shape,
    ]
    grads = list(deal(most, late, early, last, pairw, shapes))
    grads[9] = grads[9].T
    for place in (6, 8):
        grads[place] = grads[place][0]
    return (output.reshape(tokens.shape), tgrad.reshape(tokens.shape), *grads)


def solution(mesh):
    rowwise = P(None, "sample", "row", None)
    return jax.shard_map(
        local,
        mesh=mesh,
        in_specs=(
            rowwise,
            rowwise,
            P(None, "row", None, None),
            P(),
            P(None, "row", None),
            rowwise,
            P(None, "sample"),
            P(None, "sample", None),
            P(None, "sample"),
            P(None, "sample", None),
            P(None, "sample"),
            P(None, "sample", None),
            P("sample"),
            P("sample", None),
            P("sample"),
            P("sample", None),
            P(None, "sample", None),
            P("sample", None),
        ),
        out_specs=(
            rowwise,
            rowwise,
            P(None, "sample"),
            P(None, "sample", None),
            P(None, "sample"),
            P(None, "sample", None),
            P(None, "sample"),
            P(None, "sample", None),
            P("sample"),
            P("sample", None),
            P("sample"),
            P("sample", None),
            P(None, "sample", None),
            P("sample", None),
        ),
        check_vma=False,
    )
```

```python
import functools

import jax
import jax.numpy as jnp
from jax import lax
from jax.experimental import pallas as pl
from jax.experimental.pallas import tpu as pltpu
from jax.sharding import PartitionSpec as P

EPSILON = 1e-05
MASKED = -1000000000.0
F32 = jnp.float32
BF16 = jnp.bfloat16
VMEM_LIMIT = 60 << 20


def center_rows(value):
    center = value - jnp.mean(value, axis=-1, keepdims=True)
    rstd = lax.rsqrt(jnp.mean(center * center, axis=-1, keepdims=True) + EPSILON)
    return center * rstd, rstd


def dot(left, right):
    return lax.dot_general(left, right, (((1,), (0,)), ((), ())), preferred_element_type=F32)


def dot_nt(left, right):
    return lax.dot_general(left, right, (((1,), (1,)), ((), ())), preferred_element_type=F32)


def dot_tn(left, right):
    return lax.dot_general(left, right, (((0,), (0,)), ((), ())), preferred_element_type=F32)


def params(**extra):
    return pltpu.CompilerParams(vmem_limit_bytes=VMEM_LIMIT, **extra)


MESH = pl.DeviceIdType.MESH
ANY = pl.BlockSpec(memory_space=pl.ANY)


class Place:
    def __init__(self, chips, samples):
        self.row = lax.axis_index("row")
        self.chip = self.row // 2
        self.core = self.row % 2
        self.sample = lax.axis_index("sample")
        self.chips, self.samples = chips, samples

    def twin(self):
        return (self.row + 1 - 2 * self.core, self.sample)

    def peer(self, k):
        return (self.row, jnp.bitwise_xor(self.sample, k))

    def up(self):
        return (self.row + 2, self.sample)

    def down(self):
        return (self.row - 2, self.sample)

    def along(self, k):
        return (jnp.bitwise_xor(self.row, 2 * k), self.sample)

    def barrier(self, plane, line, whole_line=False):
        bar = pltpu.get_barrier_semaphore()

        def greet(device):
            pl.semaphore_signal(bar, inc=1, device_id=device, device_id_type=MESH)

        greet(self.twin())
        if plane:
            for k in range(1, self.samples):
                greet(self.peer(k))
        if line and not whole_line:

            @pl.when(self.chip > 0)
            def _():
                greet(self.down())

            @pl.when(self.chip < self.chips - 1)
            def _():
                greet(self.up())

        count = 1 + (self.samples - 1 if plane else 0)
        if whole_line:
            for k in range(1, self.chips):
                greet(self.along(k))
            count = count + self.chips - 1
        elif line:
            count = count + jnp.minimum(self.chip, 1) + jnp.minimum(self.chips - 1 - self.chip, 1)
        pl.semaphore_wait(bar, count)


def send(source, target, send_sem, recv_sem, device):
    return pltpu.make_async_remote_copy(
        source, target, send_sem, recv_sem, device_id=device, device_id_type=MESH
    )


def half_of(ref, core):
    if ref.shape[0] > 1:
        size = ref.shape[0] // 2
        return ref.at[pl.ds(core * size, size)]
    size = ref.shape[1] // 2
    return ref.at[:, pl.ds(pl.multiple_of(core * size, 16), size)]


class PlaneGather:
    @staticmethod
    def sems(arrays, samples):
        dma = pltpu.SemaphoreType.DMA
        return [dma((arrays, samples))] * 4 + [dma((arrays, 2))] * 2

    def __init__(self, place, shards, fulls, sems):
        self.place, self.shards, self.fulls = place, shards, fulls
        self.out, self.come, self.swap_out, self.swap_come, self.hop_out, self.hop_come = sems
        self.relayed = place.samples == 4
        self.direct = [1, 2] if self.relayed else list(range(1, place.samples))

    def owner(self, k):
        return jnp.bitwise_xor(self.place.sample, k)

    def half(self, i, k):
        return half_of(self.fulls[i].at[self.owner(k)], self.place.core)

    def copy(self, i, k):
        slot = self.half(i, 0)
        return send(
            half_of(self.shards[i], self.place.core), slot, self.out.at[i, k], self.come.at[i, k],
            self.place.peer(k),
        )

    def hop(self, i, k):
        slot = self.half(i, k)
        size = slot.shape[1] // 2
        piece = slot.at[:, pl.ds((k - 1) * size, size)]
        return send(piece, piece, self.hop_out.at[i, k - 1], self.hop_come.at[i, k - 1], self.place.peer(3 - k))

    def swap(self, i, k):
        slot = self.half(i, k)
        return send(slot, slot, self.swap_out.at[i, k], self.swap_come.at[i, k], self.place.twin())

    def keep(self, i):
        return send(
            self.shards[i], self.fulls[i].at[self.place.sample], self.swap_out.at[i, 0],
            self.swap_come.at[i, 0], self.place.twin(),
        )

    def start(self, i):
        for k in self.direct:
            self.copy(i, k).start()
        self.keep(i).start()

    def relay(self, i):
        for k in self.direct:
            self.copy(i, k).wait_recv()
            if self.relayed:
                self.hop(i, k).start()
            self.swap(i, k).start()

    def settle(self, i):
        if self.relayed:
            for k in self.direct:
                self.hop(i, k).wait_recv()
            self.swap(i, 3).start()

    def arrive(self, i):
        self.keep(i).wait_recv()
        for k in range(1, self.place.samples):
            self.swap(i, k).wait_recv()

    def finish(self, arrived=()):
        for i in range(len(self.shards)):
            if i not in arrived:
                self.arrive(i)
            self.keep(i).wait_send()
            for k in self.direct:
                self.copy(i, k).wait_send()
                if self.relayed:
                    self.hop(i, k).wait_send()
            for k in range(1, self.place.samples):
                self.swap(i, k).wait_send()


class LineSpread:
    @staticmethod
    def sems(lines, chips):
        dma = pltpu.SemaphoreType.DMA
        return [dma((lines, chips))] * 6

    def __init__(self, place, line, slot, sems):
        self.place, self.line, self.slot = place, line, slot
        self.up_out, self.up_come, self.down_out, self.down_come, self.swap_out, self.swap_come = sems

    def step(self, upward, t):
        place, last = self.place, self.place.chips - 1
        z = place.chip
        if upward:
            out_chip, has_out = z - t + 1, (z >= t - 1) & (z < last)
            in_chip, has_in = z - t, z >= t
            sems, device = (self.up_out, self.up_come), place.up()
        else:
            out_chip, has_out = z + t - 1, (z + t - 1 <= last) & (z > 0)
            in_chip, has_in = z + t, z + t <= last
            sems, device = (self.down_out, self.down_come), place.down()
        make = lambda chip: send(
            self.slot(chip), self.slot(chip),
            sems[0].at[self.line, t], sems[1].at[self.line, t], device,
        )
        return (has_out, lambda: make(out_chip)), (has_in, in_chip, lambda: make(in_chip))

    def hand_over(self, chip):
        slot = self.slot(chip)
        return send(
            slot, slot, self.swap_out.at[self.line, chip], self.swap_come.at[self.line, chip],
            self.place.twin(),
        )

    def depart(self, t):
        for upward in (True, False):
            (has_out, copy), _ = self.step(upward, t)

            @pl.when(has_out)
            def _():
                copy().start()

    def advance(self, t):
        for upward in (True, False):
            _, (has_in, chip, copy) = self.step(upward, t)

            @pl.when(has_in)
            def _():
                copy().wait_recv()

        if t + 1 < self.place.chips:
            self.depart(t + 1)
        for upward in (True, False):
            _, (has_in, chip, copy) = self.step(upward, t)

            @pl.when(has_in)
            def _():
                self.hand_over(chip).start()

    def finish(self):
        for t in range(1, self.place.chips):
            for upward in (True, False):
                (has_out, copy), (has_in, chip, _) = self.step(upward, t)

                @pl.when(has_out)
                def _():
                    copy().wait_send()

                @pl.when(has_in)
                def _():
                    self.hand_over(chip).wait()


class LineReduce:
    @staticmethod
    def sems(lines, chips):
        dma = pltpu.SemaphoreType.DMA
        return [dma((lines, chips))] * 4

    def __init__(self, place, line, slot, up_buf, down_buf, sems):
        self.place, self.line, self.slot = place, line, slot
        self.bufs = (up_buf, down_buf)
        self.up_out, self.up_come, self.down_out, self.down_come = sems

    def step(self, upward, t):
        place, last = self.place, self.place.chips - 1
        z, distance = place.chip, place.chips - t
        buf = self.bufs[0 if upward else 1]
        if upward:
            block, has_out, has_before = z + distance, z + distance <= last, z > 0
            has_in = (z > 0) & (z - 1 + distance <= last)
            sems, device = (self.up_out, self.up_come), place.up()
        else:
            block, has_out, has_before = z - distance, z - distance >= 0, z < last
            has_in = (z < last) & (z + 1 - distance >= 0)
            sems, device = (self.down_out, self.down_come), place.down()
        copy = lambda chip: send(
            self.slot(chip), buf.at[self.line, t - 1],
            sems[0].at[self.line, t], sems[1].at[self.line, t], device,
        )
        return block, has_out, has_before, has_in, copy, buf

    def advance(self, t):
        for upward in (True, False):
            block, has_out, has_before, _, copy, buf = self.step(upward, t)
            before = self.step(upward, t - 1)[4] if t > 1 else None

            @pl.when(has_out)
            def _():
                if t > 1:

                    @pl.when(has_before)
                    def _():
                        before(block).wait_recv()
                        slot = self.slot(block)
                        slot[...] = (
                            slot[...].astype(F32) + buf[self.line, t - 2].astype(F32)
                        ).astype(slot.dtype)

                copy(block).start()

    def finish(self):
        last_step = self.place.chips - 1
        slot = self.slot(self.place.chip)
        for upward in (True, False):
            _, _, _, has_in, copy, buf = self.step(upward, last_step)

            @pl.when(has_in)
            def _():
                copy(self.place.chip).wait_recv()
                slot[...] = (
                    slot[...].astype(F32) + buf[self.line, last_step - 1].astype(F32)
                ).astype(slot.dtype)

        for t in range(1, self.place.chips):
            for upward in (True, False):
                block, has_out, _, _, copy, _ = self.step(upward, t)

                @pl.when(has_out)
                def _():
                    copy(block).wait_send()


class RowGather:
    @staticmethod
    def sems(lines, chips):
        return [pltpu.SemaphoreType.DMA((lines,))] + LineSpread.sems(lines, chips)

    def __init__(self, place, part, full, line, sems):
        self.place, self.part, self.full, self.index = place, part, full, line
        self.spot = (line // part.shape[1], line % part.shape[1])
        self.keep_sem = sems[0]
        self.rows = part.shape[2]
        self.line = LineSpread(place, line, self.slot, sems[1:])

    def slot(self, chip):
        start = (2 * chip + self.place.core) * self.rows
        return self.full.at[self.spot + (pl.ds(pl.multiple_of(start, 16), self.rows),)]

    def keep(self):
        return pltpu.make_async_copy(
            self.part.at[self.spot], self.slot(self.place.chip), self.keep_sem.at[self.index]
        )

    def start(self):
        self.keep().start()

    def begin(self):
        self.keep().wait()
        self.line.depart(1)
        self.line.hand_over(self.place.chip).start()

    def finish(self):
        self.line.finish()
        self.line.hand_over(self.place.chip).wait()


class RowReduce:
    @staticmethod
    def scratch(complexes, samples_own, length, rows, width, chips):
        dma = pltpu.SemaphoreType.DMA
        hop = pltpu.VMEM((complexes, chips - 1, samples_own, rows, width), BF16)
        return [
            pltpu.VMEM((complexes, samples_own, chips, rows, width), BF16), hop, hop,
        ] + [dma((complexes,))] * 3 + LineReduce.sems(complexes, chips)

    def __init__(self, place, part, own, which, scratch):
        self.place, self.part, self.own, self.which = place, part, own, which
        self.sums, up_buf, down_buf = scratch[:3]
        self.swap_out, self.swap_come, self.keep_sem = scratch[3:6]
        self.line = LineReduce(place, which, self.slot, up_buf, down_buf, scratch[6:])

    def slot(self, chip):
        return self.sums.at[self.which, :, chip]

    def first_swap(self):
        return send(
            self.part.at[self.which, :, :, 1 - self.place.core], self.sums.at[self.which],
            self.swap_out.at[self.which], self.swap_come.at[self.which], self.place.twin(),
        )

    def begin(self):
        self.first_swap().wait_recv()
        for sample in range(self.part.shape[1]):
            for chip in range(self.place.chips):
                mine = self.part[self.which, sample, chip, self.place.core].astype(F32)
                self.sums[self.which, sample, chip] = (
                    mine + self.sums[self.which, sample, chip].astype(F32)
                ).astype(BF16)

    def keep(self):
        return pltpu.make_async_copy(
            self.slot(self.place.chip), self.own.at[self.which], self.keep_sem.at[self.which]
        )

    def finish(self):
        self.line.finish()
        self.keep().start()

    def drain(self):
        self.first_swap().wait_send()
        self.keep().wait()


def reduce_rows_kernel(chips, samples, part_ref, own_ref, *scratch):
    place = Place(chips, samples)
    moves = [
        RowReduce(place, part_ref, own_ref, which, scratch) for which in range(part_ref.shape[0])
    ]
    place.barrier(False, True)
    for move in moves:
        move.first_swap().start()
    for move in moves:
        move.begin()
        move.line.advance(1)
    for t in range(2, chips):
        for move in moves:
            move.line.advance(t)
    for move in moves:
        move.finish()
    for move in moves:
        move.drain()


def reduce_rows(part, collective_id):
    samples, chips = lax.axis_size("sample"), lax.axis_size("row") // 2
    complexes, own, length, width = part.shape
    rows = length // (2 * chips)
    return pl.pallas_call(
        functools.partial(reduce_rows_kernel, chips, samples),
        in_specs=[pl.BlockSpec(memory_space=pltpu.VMEM)],
        out_specs=ANY,
        out_shape=jax.ShapeDtypeStruct((complexes, own, rows, width), part.dtype),
        scratch_shapes=RowReduce.scratch(complexes, own, length, rows, width, chips),
        compiler_params=params(collective_id=collective_id, has_side_effects=True),
        name="reduce_rows",
    )(part.reshape(complexes, own, chips, 2, rows, width))


class PlaneReduce:
    @staticmethod
    def scratch(samples, rows, width):
        dma = pltpu.SemaphoreType.DMA
        half = rows // 2
        return [
            pltpu.VMEM((samples, half, width), BF16),
            pltpu.VMEM((2 * samples - 2, half // 2, width), BF16),
            pltpu.VMEM((half, width), BF16),
        ] + [dma((samples,))] * 3 + [dma((2 * samples,))] * 2

    def __init__(self, place, grads, plane, scratch):
        self.place, self.grads, self.plane = place, grads, plane
        self.sums, self.come_buf, self.mine = scratch[:3]
        self.swap_out, self.swap_come, self.load_sem, self.out, self.come = scratch[3:]
        self.half = grads.shape[1] // 2
        self.relayed = place.samples == 4
        self.order = [3, 1, 2, 0] if self.relayed else list(range(1, place.samples)) + [0]

    def shard(self, k):
        return jnp.bitwise_xor(self.place.sample, k)

    def half_rows(self, core):
        return pl.ds(pl.multiple_of(core * self.half, 16), self.half)

    def part(self, k, which):
        return self.sums.at[self.shard(k), pl.ds(which * (self.half // 2), self.half // 2)]

    def swap(self, k):
        return send(
            self.grads.at[self.shard(k), self.half_rows(1 - self.place.core)],
            self.sums.at[self.shard(k)],
            self.swap_out.at[k], self.swap_come.at[k], self.place.twin(),
        )

    def load(self, k):
        return pltpu.make_async_copy(
            self.grads.at[self.shard(k), self.half_rows(self.place.core)],
            self.mine, self.load_sem.at[k],
        )

    def copy(self, k, which, peer, slot):
        return send(
            self.part(k, which), self.come_buf.at[slot], self.out.at[slot], self.come.at[slot],
            self.place.peer(peer),
        )

    def copies(self, k):
        if not self.relayed:
            return [self.copy(k, which, k, 2 * (k - 1) + which) for which in range(2)] if k else []
        return {
            3: lambda: [self.copy(3, 0, 1, 1), self.copy(3, 1, 2, 4)],
            1: lambda: [self.copy(1, 0, 1, 0)],
            2: lambda: [self.copy(2, 1, 2, 3)],
            0: lambda: [],
        }[k]()

    def onward(self):
        return [(self.copy(2, 0, 2, 2), 1, (2, 0)), (self.copy(1, 1, 1, 5), 4, (1, 1))]

    def arrived(self, slot):
        self.copy(0, 0, 1, slot).wait_recv()
        return self.come_buf[slot].astype(F32)

    def start(self):
        for k in self.order:
            self.swap(k).start()
        self.load(self.order[0]).start()

    def depart(self, k):
        place = self.order.index(k)
        self.load(k).wait()
        self.swap(k).wait_recv()
        slot = self.sums.at[self.shard(k)]
        slot[...] = (self.mine[...].astype(F32) + slot[...].astype(F32)).astype(BF16)
        for copy in self.copies(k):
            copy.start()
        if place + 1 < len(self.order):
            self.load(self.order[place + 1]).start()

    def hop(self):
        if self.relayed:
            for copy, slot, piece in self.onward():
                ref = self.part(*piece)
                ref[...] = (ref[...].astype(F32) + self.arrived(slot)).astype(BF16)
                copy.start()

    def finish(self):
        size = self.half // 2
        for which in range(2):
            value = self.part(0, which)[...].astype(F32)
            if self.relayed:
                slots = [3 * which, 3 * which + 2]
            else:
                slots = [2 * (k - 1) + which for k in range(1, self.place.samples)]
            for slot in slots:
                value = value + self.arrived(slot)
            self.plane[which * size : (which + 1) * size] = value.astype(BF16)

    def drain(self):
        for k in self.order:
            self.swap(k).wait_send()
            for copy in self.copies(k):
                copy.wait_send()
        if self.relayed:
            for copy, _, _ in self.onward():
                copy.wait_send()


class LineTotal:
    @staticmethod
    def scratch(size, width, chips):
        hop = pltpu.VMEM((1, chips - 1, size // chips, width), BF16)
        return [hop, hop] + LineReduce.sems(1, chips) + LineSpread.sems(1, chips)

    def __init__(self, place, plane, total, start, size, scratch):
        self.place, self.plane, self.total, self.start = place, plane, total, start
        self.half = total.shape[0] // 2
        self.size = size // place.chips
        self.reduce = LineReduce(place, 0, self.block, scratch[0], scratch[1], scratch[2:6])
        self.spread = LineSpread(place, 0, self.slot, scratch[6:])

    def block(self, chip):
        return self.plane.at[pl.ds(pl.multiple_of(self.start + chip * self.size, 16), self.size)]

    def slot(self, chip):
        start = self.place.core * self.half + self.start + chip * self.size
        return self.total.at[pl.ds(pl.multiple_of(start, 16), self.size)]

    @property
    def steps(self):
        return 2 * self.place.chips - 1

    def advance(self, t):
        if t < self.place.chips:
            self.reduce.advance(t)
            return
        t -= self.place.chips - 1
        if t == 1:
            self.reduce.finish()
            own = self.slot(self.place.chip)
            own[...] = self.block(self.place.chip)[...]
            self.spread.depart(1)
            self.spread.hand_over(self.place.chip).start()
        else:
            self.spread.advance(t - 1)

    def finish(self):
        self.spread.advance(self.place.chips - 1)
        self.spread.finish()
        self.spread.hand_over(self.place.chip).wait()


class DirectTotal:
    steps = 4

    @staticmethod
    def scratch(size, width, chips):
        dma = pltpu.SemaphoreType.DMA
        return [pltpu.VMEM((chips - 1, size // chips, width), BF16)] + [dma((chips,))] * 6

    def __init__(self, place, plane, total, start, size, scratch):
        self.place, self.plane, self.total, self.start = place, plane, total, start
        self.half = total.shape[0] // 2
        self.size = size // place.chips
        self.buf = scratch[0]
        self.out, self.come, self.back_out, self.back_come, self.swap_out, self.swap_come = scratch[1:]

    def chip(self, k):
        return jnp.bitwise_xor(self.place.chip, k)

    def block(self, chip):
        return self.plane.at[pl.ds(pl.multiple_of(self.start + chip * self.size, 16), self.size)]

    def slot(self, chip):
        start = self.place.core * self.half + self.start + chip * self.size
        return self.total.at[pl.ds(pl.multiple_of(start, 16), self.size)]

    def there(self, k):
        return send(
            self.block(self.chip(k)), self.buf.at[k - 1], self.out.at[k], self.come.at[k],
            self.place.along(k),
        )

    def back(self, k):
        own = self.slot(self.place.chip)
        return send(own, own, self.back_out.at[k], self.back_come.at[k], self.place.along(k))

    def swap(self, k):
        slot = self.slot(self.chip(k))
        return send(slot, slot, self.swap_out.at[k], self.swap_come.at[k], self.place.twin())

    def advance(self, t):
        peers = range(1, self.place.chips)
        if t == 1:
            for k in peers:
                self.there(k).start()
        elif t == 2:
            value = self.block(self.place.chip)[...].astype(F32)
            for k in peers:
                self.there(k).wait_recv()
                value = value + self.buf[k - 1].astype(F32)
            own = self.slot(self.place.chip)
            own[...] = value.astype(BF16)
            for k in peers:
                self.back(k).start()
            self.swap(0).start()
        else:
            for k in peers:
                self.back(k).wait_recv()
                self.swap(k).start()

    def finish(self):
        for k in range(1, self.place.chips):
            self.there(k).wait_send()
            self.back(k).wait_send()
        for k in range(self.place.chips):
            self.swap(k).wait()


def reduce_grads_kernel(chips, samples, grads_ref, total_ref, *scratch):
    place = Place(chips, samples)
    count = len(PlaneReduce.scratch(samples, 64, 128))
    plane_buf = scratch[0]
    plane = PlaneReduce(place, grads_ref, plane_buf, scratch[1 : 1 + count])
    line = LineTotal(place, plane_buf, total_ref, 0, plane_buf.shape[0], scratch[1 + count :])
    place.barrier(True, True)
    plane.start()
    for k in plane.order:
        plane.depart(k)
    plane.hop()
    plane.finish()
    for t in range(1, 2 * chips - 1):
        line.advance(t)
    line.finish()
    plane.drain()


def reduce_grads(grads, collective_id):
    chips = lax.axis_size("row") // 2
    samples, rows, width = grads.shape
    return pl.pallas_call(
        functools.partial(reduce_grads_kernel, chips, samples),
        in_specs=[pl.BlockSpec(memory_space=pltpu.VMEM)],
        out_specs=pl.BlockSpec(memory_space=pltpu.VMEM),
        out_shape=jax.ShapeDtypeStruct((rows, width), BF16),
        scratch_shapes=[pltpu.VMEM((rows // 2, width), BF16)]
        + PlaneReduce.scratch(samples, rows, width)
        + LineTotal.scratch(rows // 2, width, chips),
        compiler_params=params(collective_id=collective_id, has_side_effects=True),
        name="reduce_grads",
    )(grads)


def joined(ref, which=0):
    samples, _, rows, cols = ref.shape
    return ref[:, which].reshape(samples * rows, cols)


def head_windows(heads, head_dim):
    windows, head = [], 0
    while head < heads:
        start = head * head_dim // 128 * 128
        start = min(start, heads * head_dim - 256)
        inside = []
        while head < heads and (head + 1) * head_dim <= start + 256:
            inside.append(head)
            head += 1
        windows.append((start, inside))
    return windows


def head_mask(start, head, head_dim):
    lane = lax.broadcasted_iota(jnp.int32, (1, 256), 1) + start
    return (lane >= head * head_dim) & (lane < (head + 1) * head_dim)


def stack_heads(rows, start, inside, head_dim):
    zero = jnp.zeros_like(rows)
    return jnp.concatenate(
        [jnp.where(head_mask(start, head, head_dim), rows, zero) for head in inside], axis=0
    )


def unstack_heads(stacked, start, inside, head_dim):
    rows = stacked.shape[0] // len(inside)
    total = None
    for place, head in enumerate(inside):
        piece = jnp.where(
            head_mask(start, head, head_dim), stacked[place * rows : (place + 1) * rows], 0.0
        )
        total = piece if total is None else total + piece
    return total


def join_windows(parts, width):
    tiles = [None] * (width // 128)
    for start, value in parts:
        for half in range(2):
            place = start // 128 + half
            piece = value[:, half * 128 : (half + 1) * 128]
            tiles[place] = piece if tiles[place] is None else tiles[place] + piece
    return jnp.concatenate(tiles, axis=1)


PACK_ROWS, PACK_LANES = 64, 256


def pack_small(cond_gain, ada_bias, zero_bias, query_bias, pair_gain, pair_weight):
    def line(ref):
        value = ref[...].astype(F32)
        value = value.reshape(-1, value.shape[-1])
        return jnp.pad(value, ((0, 0), (0, PACK_LANES - value.shape[1])))

    rows = [line(ref) for ref in (cond_gain, ada_bias, zero_bias, query_bias, pair_gain, pair_weight)]
    left = PACK_ROWS - 8 - pair_weight.shape[0]
    return jnp.concatenate(rows + [jnp.zeros((left, PACK_LANES), F32)], axis=0).astype(BF16)


def unpack_small(packed, narrow, width, pair_width, heads):
    samples = packed.shape[0]

    def spread(size):
        count = size // samples
        total = None
        for sample in range(samples):
            lane = lax.broadcasted_iota(jnp.int32, (PACK_LANES, size), 0)
            spot = lax.broadcasted_iota(jnp.int32, (PACK_LANES, size), 1)
            move = ((spot == lane + count * sample) & (lane < count)).astype(BF16)
            piece = dot(packed[sample, 0:32], move)
            total = piece if total is None else total + piece
        return total

    gains = jnp.pad(spread(narrow)[0:2], ((0, 0), (0, width - narrow)))
    vec = jnp.concatenate([gains, spread(width)[2:7], jnp.zeros((1, width), F32)], axis=0)
    pairs = spread(pair_width)
    return vec, pairs[7:8], pairs[8 : 8 + heads]


def pair_block(count_ref, first_row, complex_id, start, pair_ref, mask_ref, gain, weight, low_ref, bias_ref):
    rows, length = pair_ref.shape[1], pair_ref.shape[2]
    count = count_ref[complex_id]
    lines = []
    for row in range(rows):
        normed, _ = center_rows(pair_ref[0, row].astype(F32))
        low = (normed * gain).astype(BF16)
        low_ref[0, row] = low
        lines.append(dot_nt(weight, low))
    bias = jnp.stack(lines, axis=1)
    own = first_row + start + lax.broadcasted_iota(jnp.int32, (rows, length), 0)
    key = lax.broadcasted_iota(jnp.int32, (rows, length), 1)
    allowed = (key < count) & ((mask_ref[0] == 1) | (own == key) | (own >= count))
    bias_ref[0] = jnp.where(allowed[None], bias, MASKED)


PAIR_ROWS = 8


def enter_kernel(arrays, chips, samples, count_ref, tok_ref, single_ref, pair_ref, mask_ref, *refs):
    small, refs = refs[:6], refs[6:]
    shards, refs = refs[: arrays - 1], refs[arrays - 1 :]
    fulls, refs = refs[:arrays], refs[arrays:]
    full_ref, normed_ref, vec_ref, pairw_ref, low_ref, bias_ref = refs[:6]
    own_pack, packed, ada_buf, load_sem = refs[6:10]
    sems = refs[10:]
    place = Place(chips, samples)
    own_pack[0] = pack_small(*small)
    shards = (own_pack, shards[0].at[pl.ds(0, 2)]) + shards[1:] + (shards[0].at[pl.ds(2, 2)],)
    ada_full = fulls[1]
    fulls = (fulls[0], ada_full.at[:, pl.ds(0, 2)]) + fulls[2:] + (ada_full.at[:, pl.ds(2, 2)],)
    arrays += 1
    count = len(PlaneGather.sems(arrays, samples))
    move = PlaneGather(place, shards, fulls, sems[:count])
    complexes, own = normed_ref.shape[:2]
    lines = [
        RowGather(place, normed_ref, full_ref, line, sems[count:]) for line in range(complexes * own)
    ]
    rows_dev, width = normed_ref.shape[2:]
    narrow = single_ref.shape[1]
    place.barrier(True, True)
    move.start(0)
    move.start(1)
    move.relay(0)
    move.settle(0)
    move.relay(1)
    for i in range(2, arrays):
        move.start(i)
    move.arrive(0)
    load = pltpu.make_async_copy(fulls[0].at[:, 0], packed, load_sem.at[0])
    load.start()
    load.wait()
    heads = bias_ref.shape[1]
    vec, pair_gain, pair_weight = unpack_small(packed, narrow, width, pair_ref.shape[3], heads)
    vec_ref[...] = vec
    pairw_ref[0:1] = pair_gain
    pairw_ref[8 : 8 + heads] = pair_weight
    per = rows_dev // PAIR_ROWS

    def pair_part(first, last):
        def body(pair_block_ref, mask_block_ref, low_block_ref, bias_block_ref):
            step = first + pl.program_id(0)
            pair_block(
                count_ref, place.row * rows_dev, step // per, step % per * PAIR_ROWS, pair_block_ref, mask_block_ref,
                pairw_ref[0:1], pairw_ref[8 : 8 + heads].astype(BF16), low_block_ref, bias_block_ref,
            )

        length = pair_ref.shape[2]
        spot = lambda b: ((first + b) // per, (first + b) % per)
        block = pl.BlockSpec((1, PAIR_ROWS, length, pair_ref.shape[3]), lambda b: spot(b) + (0, 0))
        pltpu.emit_pipeline(
            body,
            grid=(last - first,),
            in_specs=[block, pl.BlockSpec((1, PAIR_ROWS, length), lambda b: spot(b) + (0,))],
            out_specs=[
                block,
                pl.BlockSpec((1, heads, PAIR_ROWS, length), lambda b: (spot(b)[0], 0, spot(b)[1], 0)),
            ],
        )(pair_ref, mask_ref, low_ref, bias_ref)

    total = complexes * per
    move.settle(1)
    move.arrive(1)
    load = pltpu.make_async_copy(fulls[1], ada_buf, load_sem.at[0])
    load.start()
    load.wait()
    cond, _ = center_rows(single_ref[...].astype(F32))
    cond = (cond * vec_ref[0:1, 0:narrow]).astype(BF16)
    pre = dot(cond, joined(ada_buf, 0)) + vec_ref[2:3]
    shift = dot(cond, joined(ada_buf, 1))
    normed, _ = center_rows(tok_ref[...].astype(F32))
    normed_in = (jax.nn.sigmoid(pre) * normed + shift).astype(BF16)
    normed_ref[...] = normed_in.reshape(normed_ref.shape)
    for line in lines:
        line.start()
    for line in lines:
        line.begin()
    pair_part(0, total // 4)
    between = {
        0: lambda: (pair_part(total // 4, total // 2), move.relay(2), move.relay(3), move.relay(4)),
        1: lambda: (pair_part(total // 2, total * 3 // 4), move.settle(2), move.relay(5)),
        2: lambda: (
            pair_part(total * 3 // 4, total), move.relay(6), move.settle(3), move.settle(4),
            move.settle(5),
        ),
    }
    for t in range(chips):
        if t:
            for line in lines:
                line.line.advance(t)
        if t in between:
            between[t]()
    move.settle(6)
    for line in lines:
        line.finish()
    move.finish(arrived=(0, 1))


def enter(token_count, tok, single, pair, pair_mask, small, shards, complexes, heads):
    samples, chips = lax.axis_size("sample"), lax.axis_size("row") // 2
    pack = jax.ShapeDtypeStruct((1, PACK_ROWS, PACK_LANES), BF16)
    parts = [pack] + list(shards)
    arrays = len(parts)
    width, narrow = tok.shape[1], single.shape[1]
    _, rows, length, pair_width = pair.shape
    own = tok.shape[0] // complexes // rows
    vmem = pl.BlockSpec(memory_space=pltpu.VMEM)
    fulls = [jax.ShapeDtypeStruct((samples,) + s.shape, s.dtype) for s in parts]
    out = pl.pallas_call(
        functools.partial(enter_kernel, arrays, chips, samples),
        in_specs=[pl.BlockSpec(memory_space=pltpu.SMEM), vmem, vmem, ANY, ANY]
        + [vmem] * 6
        + [ANY] * (arrays - 1),
        out_specs=[ANY] * arrays + [ANY, vmem, vmem, vmem, ANY, ANY],
        out_shape=fulls
        + [
            jax.ShapeDtypeStruct((complexes, own, length, width), BF16),
            jax.ShapeDtypeStruct((complexes, own, rows, width), BF16),
            jax.ShapeDtypeStruct((8, width), F32),
            jax.ShapeDtypeStruct((8 + heads, pair_width), F32),
            jax.ShapeDtypeStruct(pair.shape, BF16),
            jax.ShapeDtypeStruct((complexes, heads, rows, length), F32),
        ],
        scratch_shapes=[
            pltpu.VMEM(pack.shape, BF16),
            pltpu.VMEM((samples,) + pack.shape[1:], BF16),
            pltpu.VMEM((samples, 2) + shards[0].shape[1:], BF16),
            pltpu.SemaphoreType.DMA((1,)),
        ]
        + PlaneGather.sems(arrays + 1, samples)
        + RowGather.sems(complexes * own, chips),
        compiler_params=params(collective_id=0, has_side_effects=True),
        name="enter",
    )(token_count, tok, single, pair, pair_mask, *small, *shards)
    return out[:arrays], out[arrays:]


def pair_grad_kernel(dbias_ref, low_ref, out_ref):
    first = (pl.program_id(0) == 0) & (pl.program_id(1) == 0)

    @pl.when(first)
    def _():
        out_ref[...] = jnp.zeros_like(out_ref)

    total = out_ref[...]
    for row in range(low_ref.shape[1]):
        total = total + dot(dbias_ref[0, :, row, :].astype(BF16), low_ref[0, row])
    out_ref[...] = total


def pair_grad(dbias, pair_low):
    complexes, rows, length, width = pair_low.shape
    heads = dbias.shape[1]
    block = 8
    return pl.pallas_call(
        pair_grad_kernel,
        grid=(complexes, rows // block),
        in_specs=[
            pl.BlockSpec((1, heads, block, length), lambda c, b: (c, 0, b, 0)),
            pl.BlockSpec((1, block, length, width), lambda c, b: (c, b, 0, 0)),
        ],
        out_specs=pl.BlockSpec((heads, width), lambda c, b: (0, 0)),
        out_shape=jax.ShapeDtypeStruct((heads, width), F32),
        compiler_params=params(),
        name="pair_grad",
    )(dbias, pair_low)


def attend_step(
    heads, own, full_ref, attn_ref, vec_ref, bias_ref, out_ref, prob_ref, query_ref, gate_ref,
    key_ref, value_ref,
):
    rows, width = own.shape
    length = full_ref.shape[0]
    head_dim = width // heads
    scale = head_dim ** (-0.5)
    query_ref[...] = (dot(own, joined(attn_ref, 0)) + vec_ref[6:7]).astype(BF16)
    gate_ref[...] = jax.nn.sigmoid(dot(own, joined(attn_ref, 3)))
    full = full_ref[...]
    key_ref[...] = dot(full, joined(attn_ref, 1)).astype(BF16)
    value_ref[...] = dot(full, joined(attn_ref, 2)).astype(BF16)
    parts = []
    for start, inside in head_windows(heads, head_dim):
        count = len(inside)
        lanes = slice(start, start + 256)
        span = slice(inside[0], inside[-1] + 1)
        stacked = stack_heads(query_ref[:, lanes], start, inside, head_dim)
        scores = dot_nt(stacked, key_ref[:, lanes]) * scale
        scores = scores + bias_ref[span].reshape(count * rows, length)
        weight = jnp.exp(scores - jnp.max(scores, axis=-1, keepdims=True))
        prob = weight * (1.0 / jnp.sum(weight, axis=-1, keepdims=True))
        low = prob.astype(BF16)
        prob_ref[span] = low.reshape(count, rows, length)
        mixed = dot(low, value_ref[:, lanes])
        parts.append((start, unstack_heads(mixed, start, inside, head_dim)))
    out_ref[...] = join_windows(parts, width)


def attend_kernel(
    heads, chips, samples, shard_ref, normed_ref, full_ref, attn_ref, vec_ref, bias_ref,
    whole_ref, att_ref, prob_ref, query_ref, gate_ref, keyval_ref, attn_buf, load_sem, *sems,
):
    place = Place(chips, samples)
    complexes, own, rows, width = normed_ref.shape
    length = full_ref.shape[2]
    move = PlaneGather(place, (shard_ref,), (whole_ref,), sems)
    load = pltpu.make_async_copy(attn_ref, attn_buf, load_sem.at[0])
    load.start()
    place.barrier(True, False)
    move.start(0)
    load.wait()
    steps = complexes * own

    def body(full_block, bias_block, att_block, prob_block, query_block, gate_block, keyval_block):
        at = pl.program_id(0)
        attend_step(
            heads, normed_ref[at // own, at % own], full_block.at[0, 0], attn_buf, vec_ref,
            bias_block.at[0], att_block.at[0, 0], prob_block.at[0, 0], query_block.at[0, 0],
            gate_block.at[0, 0], keyval_block.at[0, 0, 0], keyval_block.at[1, 0, 0],
        )

        @pl.when(at == steps // 2)
        def _():
            move.relay(0)

    spot = lambda b: (b // own, b % own)
    rows_block = pl.BlockSpec((1, 1, rows, width), lambda b: spot(b) + (0, 0))
    pltpu.emit_pipeline(
        body,
        grid=(steps,),
        in_specs=[
            pl.BlockSpec((1, 1, length, width), lambda b: spot(b) + (0, 0)),
            pl.BlockSpec((1, heads, rows, length), lambda b: (b // own, 0, 0, 0)),
        ],
        out_specs=[
            rows_block,
            pl.BlockSpec((1, 1, heads, rows, length), lambda b: spot(b) + (0, 0, 0)),
            rows_block,
            rows_block,
            pl.BlockSpec((2, 1, 1, length, width), lambda b: (0,) + spot(b) + (0, 0)),
        ],
    )(full_ref, bias_ref, att_ref, prob_ref, query_ref, gate_ref, keyval_ref)
    move.settle(0)
    move.finish()


def attend(shard, normed, full, attn, vec, bias):
    samples_all, chips = lax.axis_size("sample"), lax.axis_size("row") // 2
    complexes, samples, rows, width = normed.shape
    heads, length = bias.shape[1], bias.shape[3]
    vmem = pl.BlockSpec(memory_space=pltpu.VMEM)
    return pl.pallas_call(
        functools.partial(attend_kernel, heads, chips, samples_all),
        in_specs=[ANY, vmem, ANY, ANY, vmem, ANY],
        out_specs=[ANY] * 6,
        out_shape=[
            jax.ShapeDtypeStruct((samples_all,) + shard.shape, BF16),
            jax.ShapeDtypeStruct((complexes, samples, rows, width), F32),
            jax.ShapeDtypeStruct((complexes, samples, heads, rows, length), BF16),
            jax.ShapeDtypeStruct((complexes, samples, rows, width), BF16),
            jax.ShapeDtypeStruct((complexes, samples, rows, width), F32),
            jax.ShapeDtypeStruct((2, complexes, samples, length, width), BF16),
        ],
        scratch_shapes=[pltpu.VMEM(attn.shape, BF16), pltpu.SemaphoreType.DMA((1,))]
        + PlaneGather.sems(1, samples_all),
        compiler_params=params(collective_id=7, has_side_effects=True),
        name="attend",
    )(shard, normed, full, attn, vec, bias)


def attend_back_step(
    heads, prob_ref, grad_ref, query_ref, key_ref, value_ref, full_ref, key_w, value_w,
    dq_ref, dfull_ref, dbias_ref, dkey_w_ref, dvalue_w_ref,
):
    rows, width = query_ref.shape
    length = key_ref.shape[0]
    head_dim = width // heads
    scale = head_dim ** (-0.5)
    dq_parts, dk_parts, dv_parts = [], [], []
    for start, inside in head_windows(heads, head_dim):
        count = len(inside)
        lanes = slice(start, start + 256)
        queries = stack_heads(query_ref[:, lanes], start, inside, head_dim)
        grads = stack_heads(grad_ref[:, lanes], start, inside, head_dim)
        span = slice(inside[0], inside[-1] + 1)
        low = prob_ref[span].reshape(count * rows, length)
        prob = low.astype(F32)
        dprob = dot_nt(grads, value_ref[:, lanes])
        inner = jnp.sum(prob * dprob, axis=-1, keepdims=True)
        dscore = (prob * (dprob - inner)).astype(BF16)
        dbias_ref[span] += dscore.astype(F32).reshape(count, rows, length)
        mixed = dot(dscore, key_ref[:, lanes])
        dq_parts.append((start, unstack_heads(mixed, start, inside, head_dim)))
        dk_parts.append((start, dot_tn(dscore, queries)))
        dv_parts.append((start, dot_tn(low, grads)))
    dq_ref[...] = (join_windows(dq_parts, width) * scale).astype(BF16)
    dkey = (join_windows(dk_parts, width) * scale).astype(BF16)
    dvalue = join_windows(dv_parts, width).astype(BF16)
    dfull_ref[...] = (dot_nt(dkey, key_w) + dot_nt(dvalue, value_w)).astype(BF16).reshape(
        dfull_ref.shape
    )
    turned = full_ref[...].T
    dkey_w_ref[...] += dot(turned, dkey)
    dvalue_w_ref[...] += dot(turned, dvalue)


def attend_back_kernel(
    heads, prob_ref, grad_ref, query_ref, keyval_ref, full_ref, key_w_ref, value_w_ref,
    dq_ref, dfull_ref, dbias_ref, dkey_w_ref, dvalue_w_ref,
):
    @pl.when(pl.program_id(1) == 0)
    def _():
        dbias_ref[...] = jnp.zeros_like(dbias_ref)

    @pl.when((pl.program_id(0) == 0) & (pl.program_id(1) == 0))
    def _():
        dkey_w_ref[...] = jnp.zeros_like(dkey_w_ref)
        dvalue_w_ref[...] = jnp.zeros_like(dvalue_w_ref)

    attend_back_step(
        heads, prob_ref.at[0, 0], grad_ref.at[0, 0], query_ref.at[0, 0], keyval_ref.at[0, 0, 0],
        keyval_ref.at[1, 0, 0], full_ref.at[0, 0], joined(key_w_ref), joined(value_w_ref),
        dq_ref.at[0, 0], dfull_ref.at[0, 0], dbias_ref.at[0], dkey_w_ref, dvalue_w_ref,
    )


def attend_back(prob, grad, query, keyval, full, attn):
    complexes, samples, rows, width = query.shape
    heads, length = prob.shape[2], prob.shape[4]
    own = pl.BlockSpec((1, 1, rows, width), lambda c, s: (c, s, 0, 0))
    long = pl.BlockSpec((1, 1, length, width), lambda c, s: (c, s, 0, 0))
    weight = lambda which: pl.BlockSpec(
        (attn.shape[0], 1) + attn.shape[2:], lambda c, s: (0, which, 0, 0),
        pipeline_mode=pl.Buffered(1),
    )
    square = pl.BlockSpec((width, width), lambda c, s: (0, 0))
    return pl.pallas_call(
        functools.partial(attend_back_kernel, heads),
        grid=(complexes, samples),
        in_specs=[
            pl.BlockSpec((1, 1, heads, rows, length), lambda c, s: (c, s, 0, 0, 0)),
            own,
            own,
            pl.BlockSpec((2, 1, 1, length, width), lambda c, s: (0, c, s, 0, 0)),
            long,
            weight(1),
            weight(2),
        ],
        out_specs=[
            own,
            long,
            pl.BlockSpec((1, heads, rows, length), lambda c, s: (c, 0, 0, 0)),
            square,
            square,
        ],
        out_shape=[
            jax.ShapeDtypeStruct((complexes, samples, rows, width), BF16),
            jax.ShapeDtypeStruct((complexes, samples, length, width), BF16),
            jax.ShapeDtypeStruct((complexes, heads, rows, length), F32),
            jax.ShapeDtypeStruct((width, width), F32),
            jax.ShapeDtypeStruct((width, width), F32),
        ],
        compiler_params=params(),
        name="attend_back",
    )(prob, grad, query, keyval, full, attn, attn)


def middle_kernel(
    rows_dev, count_ref,
    att_ref, gate_ref, tok_ref, single_ref, cot_ref,
    vec_ref, ada_ref, zero_ref, out_w_ref, tin_ref, tout_ref,
    out_ref, dmid_ref, datt_ref, dglogit_ref,
    gated_ref, dabranch_ref, dza_ref, dzb_ref, tcond_ref, dtpre_ref, dtin_ref,
    tinput_ref, dfirst_ref, dsecond_ref, hidden_ref, dtbranch_ref, small_ref,
):
    step = pl.program_id(0)
    rows = att_ref.shape[0]
    count = count_ref[step]
    place = lax.broadcasted_iota(jnp.int32, (rows, 1), 0) % rows_dev
    place = place + lax.axis_index("row") * rows_dev
    valid = (place < count).astype(F32)
    att = att_ref[...]
    gate = gate_ref[...]
    single = single_ref[...]
    gated = (att * gate).astype(BF16)
    gated_ref[...] = gated
    branch = dot(gated, joined(out_w_ref))
    attn_zero = jax.nn.sigmoid(dot(single, joined(zero_ref, 0)) + vec_ref[4:5])
    middle = tok_ref[...].astype(F32) + valid * attn_zero * branch
    cond, _ = center_rows(single.astype(F32))
    tcond = (cond * vec_ref[1:2, 0 : single.shape[1]]).astype(BF16)
    tcond_ref[...] = tcond
    scale = jax.nn.sigmoid(dot(tcond, joined(ada_ref, 0)) + vec_ref[3:4])
    shift = dot(tcond, joined(ada_ref, 1))
    normed, rstd = center_rows(middle)
    tinput = (scale * normed + shift).astype(BF16)
    tinput_ref[...] = tinput
    first = dot(tinput, joined(tin_ref, 0))
    second = dot(tinput, joined(tin_ref, 1))
    sig = jax.nn.sigmoid(first)
    hidden = (first * sig * second).astype(BF16)
    hidden_ref[...] = hidden
    tbranch = dot(hidden, joined(tout_ref))
    trans_zero = jax.nn.sigmoid(dot(single, joined(zero_ref, 1)) + vec_ref[5:6])
    out_ref[...] = (middle + valid * trans_zero * tbranch).astype(BF16)
    grad_out = cot_ref[...].astype(F32)
    gated_out = grad_out * valid
    dtbranch = (gated_out * trans_zero).astype(BF16)
    dtbranch_ref[...] = dtbranch
    dzb = (gated_out * tbranch * trans_zero * (1.0 - trans_zero)).astype(BF16)
    dzb_ref[...] = dzb
    dhidden = dot_nt(dtbranch, joined(tout_ref))
    dfirst = (dhidden * second * sig * (1.0 + first * (1.0 - sig))).astype(BF16)
    dsecond = (dhidden * first * sig).astype(BF16)
    dfirst_ref[...] = dfirst
    dsecond_ref[...] = dsecond
    dtin = (dot_nt(dfirst, joined(tin_ref, 0)) + dot_nt(dsecond, joined(tin_ref, 1))).astype(BF16)
    dtin_ref[...] = dtin
    dtin_full = dtin.astype(F32)
    dtpre = (dtin_full * normed * scale * (1.0 - scale)).astype(BF16)
    dtpre_ref[...] = dtpre
    grad_norm = dtin_full * scale
    tail = grad_norm - jnp.mean(grad_norm, axis=-1, keepdims=True)
    tail = tail - normed * jnp.mean(grad_norm * normed, axis=-1, keepdims=True)
    dmid = grad_out + tail * rstd
    dmid_ref[...] = dmid
    dtcond = dot_nt(dtpre, joined(ada_ref, 0)) + dot_nt(dtin, joined(ada_ref, 1))
    gated_mid = dmid * valid
    dabranch = (gated_mid * attn_zero).astype(BF16)
    dabranch_ref[...] = dabranch
    dza = (gated_mid * branch * attn_zero * (1.0 - attn_zero)).astype(BF16)
    dza_ref[...] = dza
    dgated = dot_nt(dabranch, joined(out_w_ref))
    datt_ref[...] = (dgated * gate).astype(BF16)
    dglogit_ref[...] = (dgated * att * gate * (1.0 - gate)).astype(BF16)

    @pl.when(step == 0)
    def _():
        small_ref[...] = jnp.zeros_like(small_ref)

    width, narrow = att.shape[1], single.shape[1]
    total = lambda value: jnp.sum(value.astype(F32), axis=0, keepdims=True)
    small_ref[0:1, :] += total(dtpre)
    small_ref[1:2, :] += total(dza)
    small_ref[2:3, :] += total(dzb)
    small_ref[3:4, 0:narrow] += total(dtcond * cond)


def middle_pass(
    token_count, att, gate, tok, single, cot, vec, ada, zero, out_w, trans_in, trans_out, complexes,
    rows_dev,
):
    rows, width = tok.shape
    narrow = single.shape[1]
    hidden = trans_out.shape[0] * trans_out.shape[2]
    part = rows // complexes
    wide = pl.BlockSpec((part, width), lambda c, m: (c, 0))
    slim = pl.BlockSpec((part, narrow), lambda c, m: (c, 0))
    long = pl.BlockSpec((part, hidden), lambda c, m: (c, 0))
    once = lambda shape: pl.BlockSpec(
        shape, lambda c, m: (0,) * len(shape), pipeline_mode=pl.Buffered(1)
    )
    shape = lambda cols, kind: jax.ShapeDtypeStruct((rows, cols), kind)
    return pl.pallas_call(
        functools.partial(middle_kernel, rows_dev),
        grid_spec=pltpu.PrefetchScalarGridSpec(
            num_scalar_prefetch=1,
            grid=(complexes,),
            in_specs=[
                wide, wide, wide, slim, wide,
                once(vec.shape),
                pl.BlockSpec(
                    (ada.shape[0], 2) + ada.shape[2:], lambda c, m: (0, 1, 0, 0),
                    pipeline_mode=pl.Buffered(1),
                ),
                once(zero.shape),
                once(out_w.shape),
                once(trans_in.shape),
                once(trans_out.shape),
            ],
            out_specs=[
                wide, wide, wide, wide,
                wide, wide, wide, wide, slim, wide, wide,
                wide, long, long, long, wide,
                once((8, width)),
            ],
        ),
        out_shape=[
            shape(width, BF16), shape(width, F32), shape(width, BF16), shape(width, BF16),
            shape(width, BF16), shape(width, BF16), shape(width, BF16), shape(width, BF16),
            shape(narrow, BF16), shape(width, BF16), shape(width, BF16),
            shape(width, BF16), shape(hidden, BF16), shape(hidden, BF16), shape(hidden, BF16),
            shape(width, BF16),
            jax.ShapeDtypeStruct((8, width), F32),
        ],
        compiler_params=params(),
        name="middle_pass",
    )(token_count, att, gate, tok, single, cot, vec, ada, zero, out_w, trans_in, trans_out)


def last_kernel(
    dquery_ref, dfull_ref, dglogit_ref, tok_ref, single_ref, dmid_ref,
    vec_ref, ada_ref, query_w_ref, gate_w_ref,
    tgrad_ref, dnormed_ref, dapre_ref, cond_ref, small_ref,
):
    total = lambda value: jnp.sum(value.astype(F32), axis=0, keepdims=True)
    dnormed = (
        dot_nt(dquery_ref[...], joined(query_w_ref))
        + dot_nt(dglogit_ref[...], joined(gate_w_ref))
        + dfull_ref[...].astype(F32)
    ).astype(BF16)
    dnormed_ref[...] = dnormed
    cond, _ = center_rows(single_ref[...].astype(F32))
    cond_low = (cond * vec_ref[0:1, 0 : cond.shape[1]]).astype(BF16)
    cond_ref[...] = cond_low
    scale = jax.nn.sigmoid(dot(cond_low, joined(ada_ref, 0)) + vec_ref[2:3])
    normed, rstd = center_rows(tok_ref[...].astype(F32))
    full = dnormed.astype(F32)
    dapre = (full * normed * scale * (1.0 - scale)).astype(BF16)
    dapre_ref[...] = dapre
    grad_norm = full * scale
    tail = grad_norm - jnp.mean(grad_norm, axis=-1, keepdims=True)
    tail = tail - normed * jnp.mean(grad_norm * normed, axis=-1, keepdims=True)
    tgrad_ref[...] = dmid_ref[...] + tail * rstd
    dcond = dot_nt(dapre, joined(ada_ref, 0)) + dot_nt(dnormed, joined(ada_ref, 1))
    narrow = cond.shape[1]
    small_ref[...] = jnp.zeros_like(small_ref)
    small_ref[0:1, :] = total(dapre)
    small_ref[1:2, :] = total(dquery_ref[...])
    small_ref[2:3, 0:narrow] = total(dcond * cond)


def last_pass(dquery, dfull, dglogit, tok, single, dmid, vec, ada, attn):
    rows, width = tok.shape
    narrow = single.shape[1]
    whole = lambda shape: pl.BlockSpec(shape, lambda w: (0,) * len(shape))
    wide = whole((rows, width))
    shape = lambda cols, kind: jax.ShapeDtypeStruct((rows, cols), kind)
    weight = lambda which: pl.BlockSpec(
        (attn.shape[0], 1) + attn.shape[2:], lambda w: (0, which, 0, 0)
    )
    return pl.pallas_call(
        last_kernel,
        grid=(1,),
        in_specs=[
            wide, wide, wide, wide, whole((rows, narrow)), wide,
            whole(vec.shape),
            pl.BlockSpec((ada.shape[0], 2) + ada.shape[2:], lambda w: (0, 0, 0, 0)),
            weight(0),
            weight(3),
        ],
        out_specs=[wide, wide, wide, whole((rows, narrow)), whole((8, width))],
        out_shape=[
            shape(width, F32), shape(width, BF16), shape(width, BF16), shape(narrow, BF16),
            jax.ShapeDtypeStruct((8, width), F32),
        ],
        compiler_params=params(),
        name="last_pass",
    )(dquery, dfull, dglogit, tok, single, dmid, vec, ada, attn, attn)


def return_kernel(
    heads, chips, samples, grads_ref, prob_ref, grad_ref, query_ref, keyval_ref, full_ref, attn_ref,
    low_ref, normed_ref,
    dq_ref, own_ref, pair_ref, wide_plane, plane_ref, query_plane_ref,
    dfull, dbias, weight_buf, dkey_w_ref, dvalue_w_ref, query_grads_buf, pair_acc,
    load_sem, *scratch,
):
    place = Place(chips, samples)
    complexes, own = query_ref.shape[:2]
    rows, width = query_ref.shape[2:]
    length = full_ref.shape[2]
    count = len(PlaneReduce.scratch(samples, 64, 128))
    cut = 2 * wide_plane.shape[0]
    wide = PlaneReduce(place, grads_ref.at[:, pl.ds(0, cut)], wide_plane, scratch[:count])
    rest = grads_ref.shape[1] - cut
    plane = PlaneReduce(
        place, grads_ref.at[:, pl.ds(cut, rest)], plane_ref, scratch[count : 2 * count]
    )
    query_plane = PlaneReduce(
        place, query_grads_buf, query_plane_ref, scratch[2 * count : 3 * count]
    )
    scratch = scratch[3 * count :]
    moves = [
        RowReduce(place, dfull, own_ref, which, scratch) for which in range(complexes)
    ]
    place.barrier(True, True)
    wide.start()
    plane.start()
    load = pltpu.make_async_copy(attn_ref.at[:, 1:3], weight_buf, load_sem.at[0])
    load.start()
    dkey_w_ref[...] = jnp.zeros_like(dkey_w_ref)
    dvalue_w_ref[...] = jnp.zeros_like(dvalue_w_ref)
    dbias[...] = jnp.zeros_like(dbias)
    load.wait()

    def hooked(step, hooks):
        for at, actions in hooks.items():

            @pl.when(step == at)
            def _():
                for action in actions:
                    action()

    def back(prob_block, grad_block, query_block, keyval_block, full_block):
        step = pl.program_id(0)
        which, sample = step // own, step % own
        attend_back_step(
            heads, prob_block.at[0, 0], grad_block.at[0, 0], query_block.at[0, 0],
            keyval_block.at[0, 0, 0], keyval_block.at[1, 0, 0], full_block.at[0, 0],
            joined(weight_buf, 0), joined(weight_buf, 1), dq_ref.at[which, sample],
            dfull.at[which, sample], dbias.at[which], dkey_w_ref, dvalue_w_ref,
        )
        hooked(step, back_hooks)

    back_hooks = {}
    final = complexes * own - 1

    def then(at, action):
        back_hooks.setdefault(min(at, final), []).append(action)

    half_order = (len(plane.order) + 1) // 2
    for at, k in enumerate(plane.order):
        if at < half_order:
            wide.depart(k)
        else:
            then(0, functools.partial(wide.depart, k))
        then(own - 2 + at // half_order, functools.partial(plane.depart, k))
    then(own - 1, lambda: moves[0].first_swap().start())
    then(own, moves[0].begin)
    for t in range(1, chips):
        then(own + t - 1, functools.partial(moves[0].line.advance, t))
    then(own + 1, wide.hop)
    then(final, lambda: moves[1].first_swap().start())

    spot = lambda b: (b // own, b % own)
    rows_block = pl.BlockSpec((1, 1, rows, width), lambda b: spot(b) + (0, 0))
    pltpu.emit_pipeline(
        back,
        grid=(complexes * own,),
        in_specs=[
            pl.BlockSpec((1, 1, heads, rows, length), lambda b: spot(b) + (0, 0, 0)),
            rows_block,
            rows_block,
            pl.BlockSpec((2, 1, 1, length, width), lambda b: (0,) + spot(b) + (0, 0)),
            pl.BlockSpec((1, 1, length, width), lambda b: spot(b) + (0, 0)),
        ],
    )(prob_ref, grad_ref, query_ref, keyval_ref, full_ref)
    query_grads(
        normed_ref[...], dq_ref[...].reshape(complexes * own * rows, width), dkey_w_ref[...],
        dvalue_w_ref[...], query_grads_buf,
    )
    query_plane.start()

    pair_acc[...] = jnp.zeros_like(pair_acc)
    per = rows // PAIR_ROWS

    def pair_part(first, last):
        def body(low_block):
            step = first + pl.program_id(0)
            which, start = step // per, pl.multiple_of(step % per * PAIR_ROWS, PAIR_ROWS)
            lines = dbias[which, :, pl.ds(start, PAIR_ROWS), :]
            lines = lines.reshape(heads * PAIR_ROWS, length).astype(BF16)
            line = lax.broadcasted_iota(jnp.int32, (heads * PAIR_ROWS, 1), 0) % PAIR_ROWS
            total = pair_acc[...]
            for row in range(PAIR_ROWS):
                total = total + jnp.where(line == row, dot(lines, low_block[0, row]), 0.0)
            pair_acc[...] = total

        pltpu.emit_pipeline(
            body,
            grid=(last - first,),
            in_specs=[
                pl.BlockSpec(
                    (1, PAIR_ROWS, length, low_ref.shape[3]),
                    lambda b: ((first + b) // per, (first + b) % per, 0, 0),
                )
            ],
        )(low_ref)

    total = complexes * per
    marks = [total * t // chips for t in range(chips + 1)]
    moves[1].begin()
    moves[1].line.advance(1)
    plane.hop()
    for k in query_plane.order:
        query_plane.depart(k)
    wide.finish()
    moves[0].finish()
    for t in range(chips):
        pair_part(marks[t], marks[t + 1])
        if t + 2 < chips:
            moves[1].line.advance(t + 2)
        if t == 1:
            query_plane.hop()
    pair_ref[...] = jnp.sum(pair_acc[...].reshape(heads, PAIR_ROWS, pair_acc.shape[1]), axis=1)
    plane.finish()
    moves[1].finish()
    query_plane.finish()
    for move in moves:
        move.drain()
    for part in (wide, plane, query_plane):
        part.drain()


def return_pass(grads, cut, prob, grad, query, keyval, full, attn, pair_low, normed, query_rows):
    samples, chips = lax.axis_size("sample"), lax.axis_size("row") // 2
    complexes, own, rows, width = query.shape
    heads, length = prob.shape[2], prob.shape[4]
    vmem = pl.BlockSpec(memory_space=pltpu.VMEM)
    half = (grads.shape[1] - cut) // 2
    return pl.pallas_call(
        functools.partial(return_kernel, heads, chips, samples),
        in_specs=[ANY] * 8 + [vmem],
        out_specs=[vmem, ANY, vmem, vmem, vmem, vmem],
        out_shape=[
            jax.ShapeDtypeStruct(query.shape, BF16),
            jax.ShapeDtypeStruct(query.shape, BF16),
            jax.ShapeDtypeStruct((heads, pair_low.shape[3]), F32),
            jax.ShapeDtypeStruct((cut // 2, width), BF16),
            jax.ShapeDtypeStruct((half, width), BF16),
            jax.ShapeDtypeStruct((query_rows // 2, width), BF16),
        ],
        scratch_shapes=[
            pltpu.VMEM((complexes, own, chips, 2, rows, width), BF16),
            pltpu.VMEM((complexes, heads, rows, length), F32),
            pltpu.VMEM((attn.shape[0], 2) + attn.shape[2:], BF16),
            pltpu.VMEM((width, width), F32),
            pltpu.VMEM((width, width), F32),
            pltpu.VMEM((samples, query_rows, width), BF16),
            pltpu.VMEM((heads * PAIR_ROWS, pair_low.shape[3]), F32),
            pltpu.SemaphoreType.DMA((1,)),
        ]
        + PlaneReduce.scratch(samples, cut, width)
        + PlaneReduce.scratch(samples, 2 * half, width)
        + PlaneReduce.scratch(samples, query_rows, width)
        + RowReduce.scratch(complexes, own, length, rows, width, chips),
        compiler_params=params(collective_id=5, has_side_effects=True),
        name="return_pass",
    )(grads, prob, grad, query, keyval, full, attn, pair_low, normed)


def leave_kernel(
    chips, samples, most_ref, late_ref, query_ref, dquery_ref, dfull_ref, dglogit_ref, tok_ref, single_ref,
    dmid_ref, vec_ref, ada_ref, attn_ref, small_mid, pair_sum,
    tgrad_ref, most_total, late_total, query_total, last_total,
    most_plane, late_plane, query_plane, last_grads_buf, last_plane, dnormed_ref, dapre_ref, cond_ref,
    small_ref, load_sem, *scratch,
):
    place = Place(chips, samples)
    count = len(PlaneReduce.scratch(samples, 64, 128))
    plane = PlaneReduce(place, last_grads_buf, last_plane, scratch[:count])
    scratch = scratch[count:]
    pieces = [
        (LineTotal, most_plane, most_total), (LineTotal, late_plane, late_total),
        (LineTotal, query_plane, query_total),
        (DirectTotal, last_plane, last_total),
    ]
    lines = []
    for kind, buf, total in pieces:
        count = len(kind.scratch(16 * chips, 128, chips))
        lines.append(kind(place, buf, total, 0, buf.shape[0], scratch[:count]))
        scratch = scratch[count:]
    most, late, query, last = lines
    loads = [
        pltpu.make_async_copy(late_ref, late_plane, load_sem.at[0]),
        pltpu.make_async_copy(query_ref, query_plane, load_sem.at[1]),
        pltpu.make_async_copy(most_ref, most_plane, load_sem.at[2]),
    ]
    for load in loads:
        load.start()
    place.barrier(True, True, True)
    for load in loads:
        load.wait()
    groups = [(most, 0), (late, 1), (query, 2), (last, 4)]
    clock = [0]

    def tick():
        t = clock[0] = clock[0] + 1
        for line, behind in groups:
            step = t - behind
            if 1 <= step < line.steps:
                line.advance(step)
            elif step == line.steps:
                line.finish()

    tick()
    last_kernel(
        dquery_ref, dfull_ref, dglogit_ref, tok_ref, single_ref, dmid_ref, vec_ref, ada_ref,
        attn_ref.at[:, 0:1], attn_ref.at[:, 3:4], tgrad_ref, dnormed_ref, dapre_ref, cond_ref,
        small_ref,
    )
    tick()
    last_grads(
        cond_ref[...], dapre_ref[...], dnormed_ref[...], small_mid[...], small_ref[...],
        pair_sum[...], last_grads_buf,
    )
    plane.start()
    tick()
    for k in plane.order:
        plane.depart(k)
    tick()
    plane.hop()
    plane.finish()
    while clock[0] < max(line.steps + behind for line, behind in groups):
        tick()
    plane.drain()


def leave(most, late, query, dquery, dfull, dglogit, tok, single, dmid, vec, ada, attn, small_mid, pair_sum,
          last_rows):
    samples, chips = lax.axis_size("sample"), lax.axis_size("row") // 2
    rows, width = tok.shape
    narrow = single.shape[1]
    halves = [most.shape[0], late.shape[0], query.shape[0], last_rows // 2]
    vmem = pl.BlockSpec(memory_space=pltpu.VMEM)
    return pl.pallas_call(
        functools.partial(leave_kernel, chips, samples),
        in_specs=[ANY] * 3 + [vmem] * 11,
        out_specs=[vmem] * 5,
        out_shape=[jax.ShapeDtypeStruct((rows, width), F32)]
        + [jax.ShapeDtypeStruct((2 * half, width), BF16) for half in halves],
        scratch_shapes=[
            pltpu.VMEM(most.shape, BF16),
            pltpu.VMEM(late.shape, BF16),
            pltpu.VMEM(query.shape, BF16),
            pltpu.VMEM((samples, last_rows, width), BF16),
            pltpu.VMEM((last_rows // 2, width), BF16),
            pltpu.VMEM((rows, width), BF16),
            pltpu.VMEM((rows, width), BF16),
            pltpu.VMEM((rows, narrow), BF16),
            pltpu.VMEM((8, width), F32),
            pltpu.SemaphoreType.DMA((3,)),
        ]
        + PlaneReduce.scratch(samples, last_rows, width)
        + LineTotal.scratch(halves[0], width, chips)
        + LineTotal.scratch(halves[1], width, chips)
        + LineTotal.scratch(halves[2], width, chips)
        + DirectTotal.scratch(halves[3], width, chips),
        compiler_params=params(collective_id=6, has_side_effects=True),
        name="leave",
    )(most, late, query, dquery, dfull, dglogit, tok, single, dmid, vec, ada, attn, small_mid, pair_sum)


def grad_rows(samples, chips, parts):
    unit = 32 * chips
    return -(-sum(parts) // unit) * unit


def store_grads(out_ref, start, left, grads):
    samples, _, width = out_ref.shape
    turned = left.T
    rows = turned.shape[0] // samples
    for grad in grads:
        value = dot(turned, grad).astype(BF16)
        out_ref[:, start : start + rows] = value.reshape(samples, rows, width)
        start += rows
    return start


def pad_grads(out_ref, start):
    samples, rows, width = out_ref.shape
    if start < rows:
        out_ref[:, start:] = jnp.zeros((samples, rows - start, width), BF16)


LATE_OPERANDS = 15


def late_grads_kernel(*refs):
    ins, out_ref, refs = refs[:LATE_OPERANDS], refs[LATE_OPERANDS], refs[LATE_OPERANDS + 1 :]
    bufs, grads, in_sem, out_sem = refs[:LATE_OPERANDS], *refs[LATE_OPERANDS:]
    loads = [
        pltpu.make_async_copy(ref, buf, in_sem.at[i]) for i, (ref, buf) in enumerate(zip(ins, bufs))
    ]
    for load in loads:
        load.start()
    width = out_ref.shape[2]
    stores = []

    def take(i):
        loads[i].wait()
        return bufs[i]

    def put(start, left, right):
        end = store_grads(grads, start, left, right)
        spot = pl.ds(start, end - start)
        store = pltpu.make_async_copy(grads.at[:, spot], out_ref.at[:, spot], out_sem.at[len(stores)])
        store.start()
        stores.append(store)
        return end

    tinput = take(0)[...]
    start = 0
    for i in (1, 2):
        ref = take(i)
        halves = [ref[:, lane : lane + width] for lane in range(0, ref.shape[1], width)]
        start = put(start, tinput, halves)
    start = put(start, take(3)[...], [take(4)[...]])
    start = put(start, take(5)[...], [take(6)[...], take(7)[...]])
    start = put(start, take(8)[...], [take(9)[...], take(10)[...]])
    start = put(start, take(11)[...], [take(12)[...]])
    start = put(start, take(13)[...], [take(14)[...]])
    rows = out_ref.shape[1]
    if start < rows:
        pad_grads(grads, start)
        spot = pl.ds(start, rows - start)
        store = pltpu.make_async_copy(grads.at[:, spot], out_ref.at[:, spot], out_sem.at[len(stores)])
        store.start()
        stores.append(store)
    for store in stores:
        store.wait()


def late_grads(samples, rows, width, operands):
    return pl.pallas_call(
        late_grads_kernel,
        in_specs=[ANY] * LATE_OPERANDS,
        out_specs=ANY,
        out_shape=jax.ShapeDtypeStruct((samples, rows, width), BF16),
        scratch_shapes=[pltpu.VMEM(value.shape, BF16) for value in operands]
        + [
            pltpu.VMEM((samples, rows, width), BF16),
            pltpu.SemaphoreType.DMA((LATE_OPERANDS,)),
            pltpu.SemaphoreType.DMA((8,)),
        ],
        compiler_params=params(),
        name="late_grads",
    )(*operands)


def store_ready(out_ref, start, ready):
    samples, _, width = out_ref.shape
    for value in ready:
        size = value.shape[0] // samples
        out_ref[:, start : start + size] = value.astype(BF16).reshape(samples, size, width)
        start += size
    return start


def query_grads(normed_in, dquery, dkey_w, dvalue_w, out_ref):
    start = store_grads(out_ref, 0, normed_in, [dquery])
    pad_grads(out_ref, store_ready(out_ref, start, [dkey_w, dvalue_w]))


def last_grads(cond, dapre, dnormed, small_mid, small_last, pair_sum, out_ref):
    samples, rows, width = out_ref.shape
    start = store_grads(out_ref, 0, cond, [dapre, dnormed])
    pairs = jnp.concatenate(
        [pair_sum, jnp.zeros((pair_sum.shape[0], width - pair_sum.shape[1]), F32)], axis=1
    )
    small = jnp.concatenate([small_mid, small_last, pairs], axis=0).astype(BF16)
    for sample in range(samples):
        out_ref[sample, start : start + small.shape[0]] = small
    pad_grads(out_ref, start + small.shape[0])


def query_grads_kernel(normed_in, dquery, dkey_w, dvalue_w, out_ref):
    query_grads(normed_in[...], dquery[...], dkey_w[...], dvalue_w[...], out_ref)


def last_grads_kernel(cond, dapre, dnormed, small_mid, small_last, pair_sum, out_ref):
    last_grads(
        cond[...], dapre[...], dnormed[...], small_mid[...], small_last[...], pair_sum[...], out_ref
    )


def grads_call(kernel, samples, rows, width, operands, name):
    return pl.pallas_call(
        kernel,
        out_shape=jax.ShapeDtypeStruct((samples, rows, width), BF16),
        compiler_params=params(),
        name=name,
    )(*operands)


def deal_kernel(
    most, late, early, last, pairw, tgrad,
    gain_ref, ada_ref, ada_bias_ref, zero_ref, zero_bias_ref, attn_ref, query_bias_ref, out_ref,
    pair_gain_ref, pair_weight_ref, tin_ref, tout_ref, tgrad_ref,
):
    tgrad_ref[...] = tgrad[...]
    slim, wide = ada_ref.shape[1], attn_ref.shape[1]
    width = ada_ref.shape[2]
    spot = lax.axis_index("sample")
    part = lambda ref, start, size: ref[start : start + size].astype(F32)
    for which in range(2):
        for lane in range(2):
            tin_ref[which, :, lane * width : (lane + 1) * width] = part(
                most, (2 * which + lane) * wide, wide
            )
    tout_ref[...] = part(most, 4 * wide, tout_ref.shape[0])
    for which in range(2):
        ada_ref[which] = part(last, which * slim, slim)
        ada_ref[2 + which] = part(late, which * slim, slim)
        zero_ref[which] = part(late, (2 + which) * slim, slim)
    out_ref[...] = part(late, 4 * slim, wide)
    for which in range(3):
        attn_ref[which] = part(early, which * wide, wide)
    attn_ref[3] = part(late, 4 * slim + wide, wide)
    heads, thin = pair_weight_ref.shape
    small = last[2 * slim : 2 * slim + 16]
    pairs = last[2 * slim + 16 : 2 * slim + 16 + heads, 0 : pairw.shape[1]]

    def choose(size, count):
        row = lax.broadcasted_iota(jnp.int32, (size, count), 0)
        lane = lax.broadcasted_iota(jnp.int32, (size, count), 1)
        return (row == lane + spot * count).astype(BF16)

    lines = dot(small, choose(width, wide))
    narrow = slim * (width // wide)
    slims = dot(small[:, 0:narrow], choose(narrow, slim))
    ada_bias_ref[0:1] = lines[8:9]
    ada_bias_ref[1:2] = lines[0:1]
    zero_bias_ref[...] = lines[1:3]
    query_bias_ref[...] = lines[9:10]
    gain_ref[0:1] = slims[10:11]
    gain_ref[1:2] = slims[3:4]
    pair_weight_ref[...] = dot(pairs, choose(pairw.shape[1], thin))
    gains = jnp.sum(pairw[8 : 8 + heads] * pairs.astype(F32), axis=0, keepdims=True) / pairw[0:1]
    pair_gain_ref[...] = lax.dot_general(
        gains, choose(pairw.shape[1], thin).astype(F32), (((1,), (0,)), ((), ())),
        precision=lax.Precision.HIGHEST, preferred_element_type=F32,
    )


def deal(most, late, early, last, pairw, tgrad, shapes):
    return pl.pallas_call(
        deal_kernel,
        out_shape=[jax.ShapeDtypeStruct(shape, F32) for shape in shapes],
        compiler_params=params(),
        name="deal",
    )(most, late, early, last, pairw, tgrad)


def local(
    tokens, single, pair, token_count, pair_mask, cotangent, cond_gain, ada_weight, ada_bias,
    zero_weight, zero_bias, attn_weight, query_bias, out_weight, pair_gain, pair_weight,
    trans_in, trans_out,
):
    complexes, samples_own, rows_dev, width = tokens.shape
    narrow = single.shape[3]
    heads, length = pair_weight.shape[1], pair.shape[2]
    samples, chips = lax.axis_size("sample"), lax.axis_size("row") // 2
    rows = complexes * samples_own * rows_dev
    flat = lambda value: value.reshape(rows, value.shape[-1])
    block = lambda value: value.reshape(complexes, samples_own, rows_dev, width)
    tok, sing, cot = flat(tokens), flat(single), flat(cotangent)
    small = (cond_gain, ada_bias, zero_bias, query_bias, pair_gain, pair_weight.T)
    weights, (full, normed_in, vec, pairw, pair_low, bias) = enter(
        token_count, tok, sing, pair, pair_mask, small,
        [ada_weight, attn_weight, zero_weight, out_weight[None], trans_out[None]],
        complexes, heads,
    )
    _, ada, attn, zero, out_w, tout = weights
    tin, att, prob, query, gate, keyval = attend(trans_in, normed_in, full, attn, vec, bias)
    normed_in = flat(normed_in)
    (
        output, dmid, datt, dglogit, gated, dabranch, dza, dzb, tcond, dtpre, dtin, tinput,
        dfirst, dsecond, hidden, dtbranch, small_mid,
    ) = middle_pass(
        token_count, flat(att), flat(gate), tok, sing, cot, vec, ada, zero, out_w, tin, tout,
        complexes, rows_dev,
    )
    slim, wide = narrow // samples, width // samples
    late_parts = [wide] * 4 + [tout.shape[2]] + [slim] * 4 + [wide] * 2
    query_parts = [wide] * 3
    last_parts = [slim] * 2 + [16 + heads]
    late_rows, query_rows, last_rows = (
        grad_rows(samples, chips, parts) for parts in (late_parts, query_parts, last_parts)
    )
    late = late_grads(
        samples, late_rows, width,
        (tinput, dfirst, dsecond, hidden, dtbranch, tcond, dtpre, dtin, sing, dza, dzb, gated,
         dabranch, normed_in, dglogit),
    )
    datt = block(datt)
    if length <= 512:
        dquery, dfull, pair_sum, most, late, early = return_pass(
            late, sum(late_parts[:5]), prob, datt, query, keyval, full, attn, pair_low, normed_in, query_rows
        )
        tgrad, most, late, early, last = leave(
            most, late, early, flat(dquery), flat(dfull), dglogit, tok, sing, dmid, vec, ada, attn,
            small_mid, pair_sum, last_rows,
        )
    else:
        dquery, dfull, dbias, dkey_w, dvalue_w = attend_back(prob, datt, query, keyval, full, attn)
        dfull = flat(reduce_rows(dfull, 2))
        pair_sum = pair_grad(dbias, pair_low)
        dquery = flat(dquery)
        tgrad, dnormed, dapre, cond, small_last = last_pass(
            dquery, dfull, dglogit, tok, sing, dmid, vec, ada, attn
        )
        early = grads_call(
            query_grads_kernel, samples, query_rows, width, (normed_in, dquery, dkey_w, dvalue_w),
            "query_grads",
        )
        last = grads_call(
            last_grads_kernel, samples, last_rows, width,
            (cond, dapre, dnormed, small_mid, small_last, pair_sum), "last_grads",
        )
        late = reduce_grads(late, 3)
        most, late = late[: sum(late_parts[:5])], late[sum(late_parts[:5]) :]
        early = reduce_grads(early, 4)
        last = reduce_grads(last, 2)

    shapes = [
        cond_gain.shape, ada_weight.shape, ada_bias.shape, zero_weight.shape, zero_bias.shape,
        attn_weight.shape, (1,) + query_bias.shape, out_weight.shape, (1,) + pair_gain.shape,
        pair_weight.T.shape, trans_in.shape, trans_out.shape, tgrad.shape,
    ]
    *grads, tgrad = deal(most, late, early, last, pairw, tgrad, shapes)
    grads[9] = grads[9].T
    for place in (6, 8):
        grads[place] = grads[place][0]
    return (output.reshape(tokens.shape), tgrad.reshape(tokens.shape), *grads)


def solution(mesh):
    rowwise = P(None, "sample", "row", None)
    return jax.shard_map(
        local,
        mesh=mesh,
        in_specs=(
            rowwise,
            rowwise,
            P(None, "row", None, None),
            P(),
            P(None, "row", None),
            rowwise,
            P(None, "sample"),
            P(None, "sample", None),
            P(None, "sample"),
            P(None, "sample", None),
            P(None, "sample"),
            P(None, "sample", None),
            P("sample"),
            P("sample", None),
            P("sample"),
            P("sample", None),
            P(None, "sample", None),
            P("sample", None),
        ),
        out_specs=(
            rowwise,
            rowwise,
            P(None, "sample"),
            P(None, "sample", None),
            P(None, "sample"),
            P(None, "sample", None),
            P(None, "sample"),
            P(None, "sample", None),
            P("sample"),
            P("sample", None),
            P("sample"),
            P("sample", None),
            P(None, "sample", None),
            P("sample", None),
        ),
        check_vma=False,
    )
```
